32 devices in a mesh: seq: 8 (over y, x, core), batch: 4 (over z).
Axes of the slice: x: 2, y: 2, z: 4, core: 2. Of those that a mesh axis runs over, the one named last changes fastest.
Arguments:
- stream_in: bfloat16 [16, 2048, 768], P('batch', 'seq'), may hold values from -6 to 6
- lengths: int32 [16], P('batch'), may hold values from 64 to 2048, as said below
- token_mask: int32 [16, 2048], P('batch', 'seq'), may hold values from 0 to 1, as said below
- norm1_gain: bfloat16 [768], replicated, may hold values from 0.5 to 1.5
- w_qkv: bfloat16 [768, 2304], replicated, may hold values from -0.21875 to 0.21875
- conv_taps: bfloat16 [3, 2304], replicated, may hold values from -3 to 3
- w_out: bfloat16 [768, 768], replicated, may hold values from -1.75 to 1.75
- norm2_gain: bfloat16 [768], replicated, may hold values from 0.5 to 1.5
- w_up: bfloat16 [768, 3072], replicated, may hold values from -0.21875 to 0.21875
- w_down: bfloat16 [3072, 768], replicated, may hold values from -0.109375 to 0.109375
- grad_output: bfloat16 [16, 2048, 768], P('batch', 'seq'), may hold values from -6 to 6
Outputs:
- stream_out: bfloat16 [16, 2048, 768], P('batch', 'seq')
- grad_input: float32 [16, 2048, 768], P('batch', 'seq')
- grad_norm1: float32 [768], P('batch')
- grad_qkv: float32 [768, 2304], P('batch')
- grad_taps: float32 [3, 2304], replicated
- grad_wout: float32 [768, 768], P('batch')
- grad_norm2: float32 [768], P('batch')
- grad_up: float32 [768, 3072], P('batch')
- grad_down: float32 [3072, 768], P('batch')
- block_rms: float32 [3], replicated
The draws below stay inside these ranges and needn't reach their ends.
Inputs may be any that keep to these rules, and one draw needn't show every extreme that they name: `lengths`: lengths are heavy tailed over 64 to 2048; some sequence has exactly 2048. `token_mask`: 0 or 1; the first position of every sequence is 1.
All inputs are finite; a program needn't handle non-finite values.
Results may differ from the reference program's by a relative error of at most 0.02.
Values may be sent and summed in bfloat16 or wider, within the bound.
A program may use at most 384 MiB of HBM per device.

```python
import math
import jax
import jax.numpy as jnp
from jax import lax

D = 768
HEADS = 12
HEAD = 64
FF = 3072
SEQ_LEN = 2048
MIN_LEN = 64
SEQS = 16


def draw_lengths(key, part):
    key_one, key_two, key_three, key_four = jax.random.split(jax.random.fold_in(key, 11), 4)
    levels = (SEQ_LEN // MIN_LEN).bit_length() - 1
    first_exp = jax.random.randint(key_one, (SEQS,), 0, levels + 1)
    second_exp = jax.random.randint(key_two, (SEQS,), 0, levels + 1)
    exponent = jnp.minimum(first_exp, second_exp).astype(jnp.int32)
    base_len = MIN_LEN * jnp.power(2, exponent).astype(jnp.int32)
    extra = jax.random.randint(key_three, (SEQS,), 0, 1 << 30) % base_len
    seq_lengths = jnp.minimum(base_len + extra, SEQ_LEN).astype(jnp.int32)
    chosen = jax.random.randint(key_four, (), 0, SEQS)
    return jnp.where(jnp.arange(SEQS) == chosen, SEQ_LEN, seq_lengths).astype(jnp.int32)


def draw_token_mask(key, part):
    levels = jax.random.randint(jax.random.fold_in(key, 23), (SEQS, SEQ_LEN), 0, 4)
    ones = (levels > 0).astype(jnp.int32)
    first = (jnp.arange(SEQ_LEN) == 0)[None, :]
    return jnp.where(first, 1, ones).astype(jnp.int32)


def shard_levels(stream_key, extent, cuts, smallest, top_value):
    def one(dim, parts):
        draws = jax.random.uniform(jax.random.fold_in(jax.random.fold_in(stream_key, 6), dim), (parts,), jnp.float32, smallest / len(cuts), top_value / len(cuts))
        return jnp.repeat(jnp.exp(draws), extent[dim] // parts).reshape((-1,) + (1,) * (len(extent) - dim - 1))

    gain = one(*cuts[0])
    for cut in cuts[1:]:
        gain = gain * one(*cut)
    return gain


def gaussian(own_key, shape, scale, reach, shards=(), kind=jnp.bfloat16):
    result = jax.random.normal(own_key, shape, jnp.float32) * scale
    if len(shards) > 0:
        result = shard_levels(own_key, shape, shards, -0.22, 0.18) * result
    return jnp.clip(result, min=-reach, max=reach).astype(kind)


def setup_inputs(seed: int = 0) -> dict:
    arg_keys = jax.random.split(jax.random.key(seed), 12)
    stream_in = gaussian(arg_keys[0], (SEQS, SEQ_LEN, D), 1.0, 6.0, ((0, 4), (1, 8)))
    lengths = draw_lengths(jax.random.fold_in(arg_keys[11], 71), 0)
    token_mask = draw_token_mask(jax.random.fold_in(arg_keys[11], 71), 0)
    norm1_gain = jnp.clip(1.0 + 0.1 * jax.random.normal(arg_keys[3], (D,), jnp.float32), 0.5, 1.5).astype(jnp.bfloat16)
    w_qkv = gaussian(arg_keys[4], (D, 3 * D), D ** -0.5, 0.21875)
    conv_taps = gaussian(arg_keys[5], (3, 3 * D), 0.6, 3.0)
    w_out = gaussian(arg_keys[6], (D, D), (D // 64) ** -0.5, 1.75)
    norm2_gain = jnp.clip(1.0 + 0.1 * jax.random.normal(arg_keys[7], (D,), jnp.float32), 0.5, 1.5).astype(jnp.bfloat16)
    w_up = gaussian(arg_keys[8], (D, FF), D ** -0.5, 0.21875)
    w_down = gaussian(arg_keys[9], (FF, D), FF ** -0.5, 0.109375)
    grad_output = gaussian(arg_keys[10], (SEQS, SEQ_LEN, D), 1.0, 6.0, ((0, 4), (1, 8)))
    return dict(stream_in=stream_in, lengths=lengths, token_mask=token_mask, norm1_gain=norm1_gain, w_qkv=w_qkv, conv_taps=conv_taps, w_out=w_out, norm2_gain=norm2_gain, w_up=w_up, w_down=w_down, grad_output=grad_output)


@jax.custom_vjp
def low(v):
    return lax.optimization_barrier(v.astype(jnp.bfloat16)).astype(jnp.float32)

@jax.custom_vjp
def low_back(v):
    return v

def low_keep(v):
    return (low(v), None)

def low_pass(kept, grad):
    return (grad,)

def back_keep(v):
    return (v, None)

def back_low(kept, grad):
    return (low(grad),)
low.defvjp(low_keep, low_pass)
low_back.defvjp(back_keep, back_low)

def matmul_high(left_op, right_op):
    return jnp.dot(left_op, right_op, precision=lax.Precision.HIGHEST, preferred_element_type=jnp.float32)

def rms_norm(values, gain_vec):
    factor = lax.rsqrt(lax.optimization_barrier(jnp.mean(values * values, axis=-1, keepdims=True)) + 1e-06)
    return values * factor * gain_vec

def causal_conv(projected, taps):
    padded = jnp.pad(projected, ((0, 0), (2, 0), (0, 0)))
    return taps[0] * padded[:, 2:] + taps[1] * padded[:, 1:-1] + taps[2] * padded[:, :-2]

def attention(query, key_rows, value_rows, seq_lengths):
    group_size = query.shape[0]
    q_heads = query.reshape(group_size, SEQ_LEN, HEADS, HEAD)
    k_heads = key_rows.reshape(group_size, SEQ_LEN, HEADS, HEAD)
    v_heads = value_rows.reshape(group_size, SEQ_LEN, HEADS, HEAD)
    block_rows = min(512, SEQ_LEN)
    key_pos = jnp.arange(SEQ_LEN, dtype=jnp.int32)
    factor = 1.0 / math.sqrt(HEAD)

    def one_block(block_index):
        begin_row = (block_index * block_rows).astype(jnp.int32)
        q_block = lax.dynamic_slice_in_dim(q_heads, begin_row, block_rows, 1)
        scores = jnp.einsum('gqhe,gkhe->ghqk', q_block, k_heads, precision=lax.Precision.HIGHEST) * factor
        scores = low_back(scores)
        q_pos = begin_row + jnp.arange(block_rows, dtype=jnp.int32)
        causal = key_pos[None, :] <= q_pos[:, None]
        inside = key_pos[None, :] < seq_lengths[:, None]
        allowed = causal[None, None, :, :] & inside[:, None, None, :]
        masked = jnp.where(allowed, scores, -1e+30)
        weights = low(jax.nn.softmax(masked, axis=-1))
        return jnp.einsum('ghqk,gkhe->gqhe', weights, v_heads, precision=lax.Precision.HIGHEST)
    blocks = lax.map(jax.checkpoint(one_block), jnp.arange(SEQ_LEN // block_rows, dtype=jnp.int32))
    return jnp.moveaxis(blocks, 0, 1).reshape(group_size, SEQ_LEN, HEADS * HEAD)

def forward(values, seq_lengths, gain_one, w_qkv, taps, w_out, gain_two, w_up, w_down):
    normed1 = low(rms_norm(values, gain_one))
    projected = low_back(matmul_high(normed1, w_qkv))
    mixed = low(causal_conv(projected, taps))
    width = values.shape[-1]
    query = mixed[..., :width]
    key_rows = mixed[..., width:2 * width]
    value_rows = mixed[..., 2 * width:]
    attended = low(low_back(attention(query, key_rows, value_rows, seq_lengths)))
    attn_branch = low_back(matmul_high(attended, w_out))
    hidden1 = values + attn_branch
    normed2 = low(rms_norm(hidden1, gain_two))
    up_proj = low_back(matmul_high(normed2, w_up))
    active = jax.nn.relu(up_proj)
    squared = low(active * active)
    ffn_branch = low_back(matmul_high(squared, w_down))
    return (hidden1 + ffn_branch, attn_branch, ffn_branch)

def reference(stream_in, lengths, token_mask, norm1_gain, w_qkv, conv_taps, w_out, norm2_gain, w_up, w_down, grad_output):
    weight_list = (norm1_gain.astype(jnp.float32), w_qkv.astype(jnp.float32), conv_taps.astype(jnp.float32), w_out.astype(jnp.float32), norm2_gain.astype(jnp.float32), w_up.astype(jnp.float32), w_down.astype(jnp.float32))
    group_size = math.gcd(SEQS, max(1, 4096 // SEQ_LEN))
    step_count = SEQS // group_size
    positions = jnp.arange(SEQ_LEN, dtype=jnp.int32)

    def regroup(array):
        return array.reshape((step_count, group_size) + array.shape[1:])

    def scan_step(running, inputs):
        grad_sums, stat_sums = running
        rows, seq_lengths, mask_rows, cotangent = inputs
        stat_weight = mask_rows.astype(jnp.float32) * (positions[None, :] < seq_lengths[:, None]).astype(jnp.float32)

        def forward_fn(values, *weights):
            stream_full, attn_branch, ffn_branch = forward(values, seq_lengths, *weights)
            return (stream_full, (attn_branch, ffn_branch))
        stream_full, pull, aux = jax.vjp(forward_fn, rows.astype(jnp.float32), *weight_list, has_aux=True)
        gradients = pull(cotangent.astype(jnp.float32) * stat_weight[..., None])

        def masked_square(values):
            return jnp.sum(stat_weight * lax.optimization_barrier(jnp.sum(values * values, axis=-1)))
        new_stats = stat_sums + jnp.stack([masked_square(stream_full), masked_square(aux[0]), masked_square(aux[1]), jnp.sum(stat_weight)])
        new_grads = tuple((old + new for old, new in zip(grad_sums, gradients[1:])))
        return ((new_grads, new_stats), (stream_full.astype(jnp.bfloat16), gradients[0]))
    start_grads = tuple((jnp.zeros(weight.shape, jnp.float32) for weight in weight_list))
    start_stats = jnp.zeros((4,), jnp.float32)
    (grad_sums, stat_sums), (streams, inputs_grad) = lax.scan(scan_step, (start_grads, start_stats), (regroup(stream_in), regroup(lengths), regroup(token_mask), regroup(grad_output)))
    stream_out = streams.reshape(SEQS, SEQ_LEN, D)
    grad_input = inputs_grad.reshape(SEQS, SEQ_LEN, D)
    block_rms = jnp.sqrt(stat_sums[:3] / (D * stat_sums[3]))
    return (stream_out, grad_input, grad_sums[0], grad_sums[1], grad_sums[2], grad_sums[3], grad_sums[4], grad_sums[5], grad_sums[6], block_rms)
```

```python
import functools
import math

import jax
import jax.numpy as jnp
from jax import lax
from jax.experimental import pallas as pl
from jax.experimental.pallas import tpu as pltpu
from jax.sharding import PartitionSpec as P

HEADS = 12
HEAD = 64
PAIRS = HEADS // 2
WIDE = 2 * HEAD
TILE = 256
NEG = -1e30
F32 = jnp.float32
BF16 = jnp.bfloat16


def mm(left_op, right_op):
    return jnp.dot(left_op, right_op, preferred_element_type=F32)


def mm_nt(left_op, right_op):
    return lax.dot_general(
        left_op, right_op, (((1,), (1,)), ((), ())), preferred_element_type=F32
    )


def mm_tn(left_op, right_op):
    return lax.dot_general(
        left_op, right_op, (((0,), (0,)), ((), ())), preferred_element_type=F32
    )


def params(limit):
    return pltpu.CompilerParams(vmem_limit_bytes=limit << 20)


def project_kernel(x_ref, gain_ref, w_ref, n_ref, p_ref):
    x = x_ref[0].astype(F32)
    factor = lax.rsqrt(jnp.mean(x * x, axis=-1, keepdims=True) + 1e-06)
    normed = (x * factor * gain_ref[...].astype(F32)).astype(BF16)
    n_ref[0] = normed
    width = x.shape[1]
    for part in range(3):
        cols = mm(normed, w_ref[:, part * width : (part + 1) * width])
        for pair in range(PAIRS):
            p_ref[pair, :, part * WIDE : (part + 1) * WIDE] = cols[
                :, pair * WIDE : (pair + 1) * WIDE
            ].astype(BF16)


def project(x, gain, w_qkv):
    groups, rows, width = x.shape
    return pl.pallas_call(
        project_kernel,
        grid=(groups,),
        in_specs=[
            pl.BlockSpec((1, rows, width), lambda s: (s, 0, 0)),
            pl.BlockSpec((1, width), lambda s: (0, 0)),
            pl.BlockSpec(w_qkv.shape, lambda s: (0, 0)),
        ],
        out_specs=[
            pl.BlockSpec((1, rows, width), lambda s: (s, 0, 0)),
            pl.BlockSpec((PAIRS, rows, 3 * WIDE), lambda s: (s, 0, 0)),
        ],
        out_shape=[
            jax.ShapeDtypeStruct(x.shape, BF16),
            jax.ShapeDtypeStruct((groups * PAIRS, rows, 3 * WIDE), BF16),
        ],
        compiler_params=params(40),
        name="project",
    )(x, gain.reshape(1, width), w_qkv)


def stack_heads(rows):
    lane = lax.broadcasted_iota(jnp.int32, rows.shape, 1)
    zero = jnp.zeros_like(rows)
    first = jnp.where(lane < HEAD, rows, zero)
    second = jnp.where(lane < HEAD, zero, rows)
    return jnp.concatenate([first, second], axis=0)


def unstack_heads(rows):
    half = rows.shape[0] // 2
    lane = lax.broadcasted_iota(jnp.int32, (half, rows.shape[1]), 1)
    return jnp.where(lane < HEAD, rows[:half], rows[half:])


def tile_rows(index):
    return pl.ds(pl.multiple_of(index * TILE, TILE), TILE)


def allowed_keys(key_tile, query_tile, length):
    shape = (TILE, 2 * TILE)
    k_pos = key_tile * TILE + lax.broadcasted_iota(jnp.int32, shape, 0)
    q_pos = query_tile * TILE + (lax.broadcasted_iota(jnp.int32, shape, 1) & (TILE - 1))
    return (k_pos <= q_pos) & (k_pos < length)


def over_key_tiles(query_tile, length, visit):
    full = jnp.minimum(query_tile, length // TILE)
    last = jnp.minimum(query_tile + 1, (length + TILE - 1) // TILE)

    def plain(key_tile, carry):
        visit(key_tile, False)
        return carry

    def edge(key_tile, carry):
        visit(key_tile, True)
        return carry

    lax.fori_loop(0, full, plain, 0)
    lax.fori_loop(full, last, edge, 0)


def convolve(wide_ref, taps_ref, tile):
    begin = 8 + tile * TILE
    total = taps_ref[0:1] * wide_ref[begin : begin + TILE]
    total += taps_ref[1:2] * wide_ref[begin - 1 : begin - 1 + TILE]
    total += taps_ref[2:3] * wide_ref[begin - 2 : begin - 2 + TILE]
    return total


def attend_kernel(info, p_ref, taps_ref, o_ref, lse_ref, wide, q_sc, k_sc, vt_sc, m_sc, acc):
    length = info[0]
    tiles = p_ref.shape[0] // TILE
    taps = taps_ref.at[0]
    wide[0:8] = jnp.zeros((8, wide.shape[1]), F32)
    wide[8:] = p_ref[...].astype(F32)
    for tile in range(tiles):
        rows = slice(tile * TILE, (tile + 1) * TILE)
        mixed = convolve(wide, taps, tile).astype(BF16)
        q_sc[rows] = mixed[:, :WIDE] * (1.0 / math.sqrt(HEAD))
        k_sc[rows] = mixed[:, WIDE : 2 * WIDE]
        vt_sc[tile, :WIDE] = mixed[:, 2 * WIDE :].astype(F32).T.astype(BF16)
        vt_sc[tile, WIDE:] = jnp.ones((vt_sc.shape[1] - WIDE, TILE), BF16)

    def query_tile(index, carry):
        q_stack = stack_heads(q_sc[tile_rows(index)])
        m_sc[...] = jnp.full(m_sc.shape, NEG, F32)
        acc[...] = jnp.zeros(acc.shape, F32)

        def visit(key_tile, masked):
            scores = mm_nt(k_sc[tile_rows(key_tile)], q_stack)
            if masked:
                scores = jnp.where(allowed_keys(key_tile, index, length), scores, NEG)
            old = m_sc[...]
            new = jnp.maximum(old, jnp.max(scores, axis=0, keepdims=True))
            probs = jnp.exp(scores - new)
            acc[...] = acc[...] * jnp.exp(old - new) + mm(vt_sc[key_tile], probs.astype(BF16))
            m_sc[...] = new

        over_key_tiles(index, length, visit)
        total = acc[WIDE : WIDE + 1]
        out = (acc[:WIDE] / total).T
        o_ref[tile_rows(index)] = unstack_heads(out).astype(BF16)
        lse_ref[pl.ds(index, 1)] = m_sc[...] + jnp.log(total)
        return carry

    lax.fori_loop(0, tiles, query_tile, 0)


def attend(info, proj, taps):
    rows = proj.shape[0]
    tiles = rows // TILE
    whole = lambda i, info: (0, 0)
    return pl.pallas_call(
        attend_kernel,
        grid_spec=pltpu.PrefetchScalarGridSpec(
            num_scalar_prefetch=1,
            grid=(1,),
            in_specs=[
                pl.BlockSpec((rows, 3 * WIDE), whole),
                pl.BlockSpec((1, 3, 3 * WIDE), lambda i, info: (info[1], 0, 0)),
            ],
            out_specs=[
                pl.BlockSpec((rows, WIDE), whole),
                pl.BlockSpec((tiles, 2 * TILE), whole),
            ],
            scratch_shapes=[
                pltpu.VMEM((rows + 8, 3 * WIDE), F32),
                pltpu.VMEM((rows, WIDE), BF16),
                pltpu.VMEM((rows, WIDE), BF16),
                pltpu.VMEM((tiles, WIDE + 16, TILE), BF16),
                pltpu.VMEM((1, 2 * TILE), F32),
                pltpu.VMEM((WIDE + 16, 2 * TILE), F32),
            ],
        ),
        out_shape=[
            jax.ShapeDtypeStruct((rows, WIDE), BF16),
            jax.ShapeDtypeStruct((tiles, 2 * TILE), F32),
        ],
        compiler_params=params(40),
        name="attend",
    )(info, proj, taps)


def attend_back_kernel(
    info, p_ref, taps_ref, o_ref, do_ref, lse_ref, dp_ref, gt_ref, wide, q_sc, k_sc, v_sc, kt_sc, dm, dqt
):
    length = info[0]
    tiles = p_ref.shape[0] // TILE
    taps = taps_ref.at[0]
    wide[0:8] = jnp.zeros((8, wide.shape[1]), F32)
    wide[8:] = p_ref[...].astype(F32)
    dm[...] = jnp.zeros(dm.shape, F32)
    for tile in range(tiles):
        rows = slice(tile * TILE, (tile + 1) * TILE)

        @pl.when(tile * TILE < length)
        def _():
            mixed = convolve(wide, taps, tile).astype(BF16)
            q_sc[rows] = mixed[:, :WIDE] * (1.0 / math.sqrt(HEAD))
            k_sc[rows] = mixed[:, WIDE : 2 * WIDE]
            v_sc[rows] = mixed[:, 2 * WIDE :]
            kt_sc[tile] = mixed[:, WIDE : 2 * WIDE].astype(F32).T.astype(BF16)

    lane = lax.broadcasted_iota(jnp.int32, (8, WIDE), 1)
    row = lax.broadcasted_iota(jnp.int32, (8, WIDE), 0)
    picks = jnp.where((lane < HEAD) == (row == 0), 1.0, 0.0).astype(BF16)

    def query_tile(index, carry):
        here = tile_rows(index)
        q_stack = stack_heads(q_sc[here])
        d_rows = do_ref[here]
        d_stack = stack_heads(d_rows)
        product = d_rows.astype(F32) * o_ref[here].astype(F32)
        upper = product.astype(BF16)
        lower = (product - upper.astype(F32)).astype(BF16)
        sums = mm_nt(picks, upper) + mm_nt(picks, lower)
        delta = jnp.concatenate([sums[0:1], sums[1:2]], axis=1)
        lse = lse_ref[pl.ds(index, 1)]
        dqt[...] = jnp.zeros(dqt.shape, F32)

        def visit(key_tile, masked):
            there = tile_rows(key_tile)
            scores = mm_nt(k_sc[there], q_stack)
            probs = jnp.exp(scores - lse)
            if masked:
                probs = jnp.where(allowed_keys(key_tile, index, length), probs, 0.0)
            d_probs = mm_nt(v_sc[there], d_stack)
            d_scores = (probs * (d_probs - delta)).astype(BF16)
            dm[there, 2 * WIDE :] += mm(probs.astype(BF16), d_stack)
            dm[there, WIDE : 2 * WIDE] += mm(d_scores, q_stack)
            dqt[...] += mm(kt_sc[key_tile], d_scores)

        over_key_tiles(index, length, visit)
        dm[here, :WIDE] = unstack_heads(dqt[...].T) * (1.0 / math.sqrt(HEAD))
        return carry

    lax.fori_loop(0, (length + TILE - 1) // TILE, query_tile, 0)
    gt_ref[...] = jnp.zeros(gt_ref.shape, F32)
    for tile in range(tiles):
        begin = tile * TILE
        total = taps[0:1] * dm[begin : begin + TILE]
        total += taps[1:2] * dm[begin + 1 : begin + 1 + TILE]
        total += taps[2:3] * dm[begin + 2 : begin + 2 + TILE]
        dp_ref[begin : begin + TILE] = total.astype(BF16)
        for tap in range(3):
            behind = wide[begin + 8 - tap : begin + 8 - tap + TILE]
            gt_ref[tap : tap + 1] += jnp.sum(
                dm[begin : begin + TILE] * behind, axis=0, keepdims=True
            )


def attend_back(info, proj, taps, attended, d_attended, lse):
    rows = proj.shape[0]
    tiles = rows // TILE
    whole = lambda i, info: (0, 0)
    return pl.pallas_call(
        attend_back_kernel,
        grid_spec=pltpu.PrefetchScalarGridSpec(
            num_scalar_prefetch=1,
            grid=(1,),
            in_specs=[
                pl.BlockSpec((rows, 3 * WIDE), whole),
                pl.BlockSpec((1, 3, 3 * WIDE), lambda i, info: (info[1], 0, 0)),
                pl.BlockSpec((rows, WIDE), whole),
                pl.BlockSpec((rows, WIDE), whole),
                pl.BlockSpec((tiles, 2 * TILE), whole),
            ],
            out_specs=[
                pl.BlockSpec((rows, 3 * WIDE), whole),
                pl.BlockSpec((8, 3 * WIDE), whole),
            ],
            scratch_shapes=[
                pltpu.VMEM((rows + 8, 3 * WIDE), F32),
                pltpu.VMEM((rows, WIDE), BF16),
                pltpu.VMEM((rows, WIDE), BF16),
                pltpu.VMEM((rows, WIDE), BF16),
                pltpu.VMEM((tiles, WIDE, TILE), BF16),
                pltpu.VMEM((rows + 8, 3 * WIDE), F32),
                pltpu.VMEM((WIDE, 2 * TILE), F32),
            ],
        ),
        out_shape=[
            jax.ShapeDtypeStruct((rows, 3 * WIDE), BF16),
            jax.ShapeDtypeStruct((8, 3 * WIDE), F32),
        ],
        compiler_params=params(48),
        name="attend_back",
    )(info, proj, taps, attended, d_attended, lse)


def norm_forward(values, gain_vec):
    factor = lax.rsqrt(jnp.mean(values * values, axis=-1, keepdims=True) + 1e-06)
    return (values * factor * gain_vec, factor)


def norm_backward(values, factor, gain_vec, upstream):
    weighted = upstream * gain_vec
    inner_mean = jnp.mean(weighted * values, axis=-1, keepdims=True)
    d_values = factor * weighted - values * (factor * factor * factor) * inner_mean
    d_gain = jnp.sum(upstream * values * factor, axis=(0, 1))
    return (d_values, d_gain)


def exchange(blocks):
    return lax.all_to_all(blocks, "seq", 0, 0, tiled=True)


def shards(
    stream_in,
    lengths,
    token_mask,
    norm1_gain,
    w_qkv,
    conv_taps,
    w_out,
    norm2_gain,
    w_up,
    w_down,
    grad_output,
):
    groups, block_len, width = stream_in.shape
    count = lax.axis_size("seq")
    place = lax.axis_index("seq")
    units = groups * PAIRS
    slots = -(-units // count)
    spare = slots * count - units
    offset = place * block_len
    gain_one = norm1_gain.astype(F32)
    gain_two = norm2_gain.astype(F32)
    taps = conv_taps.astype(F32).reshape(3, 3, PAIRS, WIDE).transpose(2, 0, 1, 3)
    taps = taps.reshape(PAIRS, 3, 3 * WIDE)

    def fill(blocks):
        return jnp.pad(blocks, ((0, spare), (0, 0), (0, 0))) if spare else blocks

    def to_heads(blocks, slot):
        got = exchange(blocks[slot * count : (slot + 1) * count])
        return got.reshape(count * block_len, blocks.shape[2])

    def to_tokens(per_slot):
        got = [exchange(rows.reshape(count, block_len, rows.shape[1])) for rows in per_slot]
        return jnp.concatenate(got, axis=0)[:units]

    infos = []
    for slot in range(slots):
        unit = slot * count + place
        sequence = jnp.minimum(unit // PAIRS, groups - 1)
        length = jnp.where(unit < units, lengths[sequence], 0)
        infos.append(jnp.stack([length, unit % PAIRS]).astype(jnp.int32))

    normed1, proj = project(stream_in, norm1_gain, w_qkv)
    proj = fill(proj)
    unit_proj, unit_out, unit_lse = [], [], []
    for slot in range(slots):
        rows = to_heads(proj, slot)
        out, lse = attend(infos[slot], rows, taps)
        unit_proj.append(rows)
        unit_out.append(out)
        unit_lse.append(lse)
    attended = to_tokens(unit_out).reshape(groups, PAIRS, block_len, WIDE)
    attended = attended.transpose(0, 2, 1, 3).reshape(groups, block_len, width)

    resid = stream_in.astype(F32)
    positions = offset + jnp.arange(block_len, dtype=jnp.int32)
    inside = (positions[None, :] < lengths[:, None]).astype(F32)
    stat_weight = token_mask.astype(F32) * inside
    cotangent = (grad_output.astype(F32) * stat_weight[..., None]).astype(BF16)
    branch_attn = mm(attended, w_out)
    hidden1 = resid + branch_attn
    normed2, factor_two = norm_forward(hidden1, gain_two)
    normed2_low = normed2.astype(BF16)
    up_proj = mm(normed2_low, w_up)
    active = jax.nn.relu(up_proj)
    squared = (active * active).astype(BF16)
    branch_ff = mm(squared, w_down)
    stream_full = hidden1 + branch_ff
    stream_out = stream_full.astype(BF16)

    def masked_square(values):
        return jnp.sum(stat_weight * jnp.sum(values * values, axis=-1))

    local_stats = jnp.stack(
        [
            masked_square(stream_full),
            masked_square(branch_attn),
            masked_square(branch_ff),
            jnp.sum(stat_weight),
        ]
    )
    grad_down = jnp.einsum("scf,scd->fd", squared, cotangent, preferred_element_type=F32)
    d_squared = jnp.einsum("scd,fd->scf", cotangent, w_down, preferred_element_type=F32)
    d_up = (2.0 * active * d_squared).astype(BF16)
    grad_up = jnp.einsum("scd,scf->df", normed2_low, d_up, preferred_element_type=F32)
    d_normed2 = jnp.einsum("scf,df->scd", d_up, w_up, preferred_element_type=F32)
    d_hidden_norm, grad_norm2 = norm_backward(hidden1, factor_two, gain_two, d_normed2)
    d_hidden1 = cotangent.astype(F32) + d_hidden_norm
    d_attn = d_hidden1.astype(BF16)
    grad_wout = jnp.einsum("scd,sce->de", attended, d_attn, preferred_element_type=F32)
    d_attended = jnp.einsum("sce,de->scd", d_attn, w_out, preferred_element_type=F32).astype(BF16)
    d_blocks = d_attended.reshape(groups, block_len, PAIRS, WIDE).transpose(0, 2, 1, 3)
    d_blocks = fill(d_blocks.reshape(units, block_len, WIDE))

    def reduce(gradient):
        share = lax.psum_scatter(
            gradient.astype(BF16), ("batch", "seq"), scatter_dimension=0, tiled=True
        )
        return lax.all_gather(share, "seq", axis=0, tiled=True).astype(F32)

    total_down, total_up, total_wout = reduce(grad_down), reduce(grad_up), reduce(grad_wout)

    back, unit_taps = [], jnp.zeros((PAIRS, 3, 3 * WIDE), F32)
    for slot in range(slots):
        d_rows = to_heads(d_blocks, slot)
        d_proj_rows, part = attend_back(
            infos[slot], unit_proj[slot], taps, unit_out[slot], d_rows, unit_lse[slot]
        )
        back.append(d_proj_rows)
        chosen = jnp.arange(PAIRS)[:, None, None] == infos[slot][1]
        unit_taps = unit_taps + jnp.where(chosen, part[None, :3], 0.0)
    grad_taps = unit_taps.reshape(PAIRS, 3, 3, WIDE).transpose(1, 2, 0, 3).reshape(3, 3 * width)
    d_proj = to_tokens(back).reshape(groups, PAIRS, block_len, 3, WIDE)
    d_proj = d_proj.transpose(0, 2, 3, 1, 4).reshape(groups, block_len, 3 * width)

    grad_qkv = jnp.einsum("scd,scn->dn", normed1, d_proj, preferred_element_type=F32)
    d_normed1 = jnp.einsum("scn,dn->scd", d_proj, w_qkv, preferred_element_type=F32)
    factor_one = lax.rsqrt(jnp.mean(resid * resid, axis=-1, keepdims=True) + 1e-06)
    d_input_norm, grad_norm1 = norm_backward(resid, factor_one, gain_one, d_normed1)
    grad_input = d_hidden1 + d_input_norm
    total_qkv = reduce(grad_qkv)
    small = lax.psum((grad_taps, local_stats, grad_norm1, grad_norm2), ("seq", "batch"))
    share = width // lax.axis_size("batch")
    begin = lax.axis_index("batch") * share
    block_rms = jnp.sqrt(small[1][:3] / (width * small[1][3]))
    return (
        stream_out,
        grad_input,
        lax.dynamic_slice_in_dim(small[2], begin, share),
        total_qkv,
        small[0],
        total_wout,
        lax.dynamic_slice_in_dim(small[3], begin, share),
        total_up,
        total_down,
        block_rms,
    )


def solution(mesh):
    tokens = P("batch", "seq", None)
    return jax.shard_map(
        shards,
        mesh=mesh,
        in_specs=(
            tokens,
            P("batch"),
            P("batch", "seq"),
            P(),
            P(),
            P(),
            P(),
            P(),
            P(),
            P(),
            tokens,
        ),
        out_specs=(
            tokens,
            tokens,
            P("batch"),
            P("batch", None),
            P(),
            P("batch", None),
            P("batch"),
            P("batch", None),
            P("batch", None),
            P(),
        ),
        check_vma=False,
    )
```

```python
import functools
import math

import jax
import jax.numpy as jnp
from jax import lax
from jax.experimental import pallas as pl
from jax.experimental.pallas import tpu as pltpu
from jax.sharding import PartitionSpec as P

HEADS = 12
HEAD = 64
PAIRS = HEADS // 2
WIDE = 2 * HEAD
TILE = 256
NEG = -1e30
F32 = jnp.float32
BF16 = jnp.bfloat16


def mm(left_op, right_op):
    return jnp.dot(left_op, right_op, preferred_element_type=F32)


def mm_nt(left_op, right_op):
    return lax.dot_general(
        left_op, right_op, (((1,), (1,)), ((), ())), preferred_element_type=F32
    )


def mm_tn(left_op, right_op):
    return lax.dot_general(
        left_op, right_op, (((0,), (0,)), ((), ())), preferred_element_type=F32
    )


def params(limit):
    return pltpu.CompilerParams(vmem_limit_bytes=limit << 20)


def project_kernel(x_ref, gain_ref, w_ref, n_ref, p_ref):
    x = x_ref[0].astype(F32)
    factor = lax.rsqrt(jnp.mean(x * x, axis=-1, keepdims=True) + 1e-06)
    normed = (x * factor * gain_ref[...].astype(F32)).astype(BF16)
    n_ref[0] = normed
    width = x.shape[1]
    for part in range(3):
        cols = mm(normed, w_ref[:, part * width : (part + 1) * width])
        for pair in range(PAIRS):
            p_ref[pair, :, part * WIDE : (part + 1) * WIDE] = cols[
                :, pair * WIDE : (pair + 1) * WIDE
            ].astype(BF16)


def project(x, gain, w_qkv):
    groups, rows, width = x.shape
    return pl.pallas_call(
        project_kernel,
        grid=(groups,),
        in_specs=[
            pl.BlockSpec((1, rows, width), lambda s: (s, 0, 0)),
            pl.BlockSpec((1, width), lambda s: (0, 0)),
            pl.BlockSpec(w_qkv.shape, lambda s: (0, 0)),
        ],
        out_specs=[
            pl.BlockSpec((1, rows, width), lambda s: (s, 0, 0)),
            pl.BlockSpec((PAIRS, rows, 3 * WIDE), lambda s: (s, 0, 0)),
        ],
        out_shape=[
            jax.ShapeDtypeStruct(x.shape, BF16),
            jax.ShapeDtypeStruct((groups * PAIRS, rows, 3 * WIDE), BF16),
        ],
        compiler_params=params(40),
        name="project",
    )(x, gain.reshape(1, width), w_qkv)


def stack_heads(rows):
    lane = lax.broadcasted_iota(jnp.int32, rows.shape, 1)
    zero = jnp.zeros_like(rows)
    first = jnp.where(lane < HEAD, rows, zero)
    second = jnp.where(lane < HEAD, zero, rows)
    return jnp.concatenate([first, second], axis=0)


def unstack_heads(rows):
    half = rows.shape[0] // 2
    lane = lax.broadcasted_iota(jnp.int32, (half, rows.shape[1]), 1)
    return jnp.where(lane < HEAD, rows[:half], rows[half:])


def tile_rows(index):
    return pl.ds(pl.multiple_of(index * TILE, TILE), TILE)


def allowed_keys(key_tile, query_tile, length):
    shape = (TILE, 2 * TILE)
    k_pos = key_tile * TILE + lax.broadcasted_iota(jnp.int32, shape, 0)
    q_pos = query_tile * TILE + (lax.broadcasted_iota(jnp.int32, shape, 1) & (TILE - 1))
    return (k_pos <= q_pos) & (k_pos < length)


def over_key_tiles(query_tile, length, visit):
    full = jnp.minimum(query_tile, length // TILE)
    last = jnp.minimum(query_tile + 1, (length + TILE - 1) // TILE)

    def plain(key_tile, carry):
        visit(key_tile, False)
        return carry

    def edge(key_tile, carry):
        visit(key_tile, True)
        return carry

    lax.fori_loop(0, full, plain, 0)
    lax.fori_loop(full, last, edge, 0)


def convolve(wide_ref, taps_ref, tile):
    begin = 8 + tile * TILE
    total = taps_ref[0:1] * wide_ref[begin : begin + TILE]
    total += taps_ref[1:2] * wide_ref[begin - 1 : begin - 1 + TILE]
    total += taps_ref[2:3] * wide_ref[begin - 2 : begin - 2 + TILE]
    return total


def attend_kernel(info, p_ref, taps_ref, o_ref, lse_ref, wide, q_sc, k_sc, vt_sc, m_sc, acc):
    length = info[0]
    tiles = p_ref.shape[0] // TILE
    taps = taps_ref.at[0]
    wide[0:8] = jnp.zeros((8, wide.shape[1]), F32)
    wide[8:] = p_ref[...].astype(F32)
    for tile in range(tiles):
        rows = slice(tile * TILE, (tile + 1) * TILE)
        mixed = convolve(wide, taps, tile).astype(BF16)
        q_sc[rows] = mixed[:, :WIDE] * (1.0 / math.sqrt(HEAD))
        k_sc[rows] = mixed[:, WIDE : 2 * WIDE]
        vt_sc[tile, :WIDE] = mixed[:, 2 * WIDE :].astype(F32).T.astype(BF16)
        vt_sc[tile, WIDE:] = jnp.ones((vt_sc.shape[1] - WIDE, TILE), BF16)

    def query_tile(index, carry):
        q_stack = stack_heads(q_sc[tile_rows(index)])
        m_sc[...] = jnp.full(m_sc.shape, NEG, F32)
        acc[...] = jnp.zeros(acc.shape, F32)

        def visit(key_tile, masked):
            scores = mm_nt(k_sc[tile_rows(key_tile)], q_stack)
            if masked:
                scores = jnp.where(allowed_keys(key_tile, index, length), scores, NEG)
            old = m_sc[...]
            new = jnp.maximum(old, jnp.max(scores, axis=0, keepdims=True))
            probs = jnp.exp(scores - new)
            acc[...] = acc[...] * jnp.exp(old - new) + mm(vt_sc[key_tile], probs.astype(BF16))
            m_sc[...] = new

        over_key_tiles(index, length, visit)
        total = acc[WIDE : WIDE + 1]
        out = (acc[:WIDE] / total).T
        o_ref[tile_rows(index)] = unstack_heads(out).astype(BF16)
        lse_ref[pl.ds(index, 1)] = m_sc[...] + jnp.log(total)
        return carry

    lax.fori_loop(0, tiles, query_tile, 0)


def attend(info, proj, taps):
    rows = proj.shape[0]
    tiles = rows // TILE
    whole = lambda i, info: (0, 0)
    return pl.pallas_call(
        attend_kernel,
        grid_spec=pltpu.PrefetchScalarGridSpec(
            num_scalar_prefetch=1,
            grid=(1,),
            in_specs=[
                pl.BlockSpec((rows, 3 * WIDE), whole),
                pl.BlockSpec((1, 3, 3 * WIDE), lambda i, info: (info[1], 0, 0)),
            ],
            out_specs=[
                pl.BlockSpec((rows, WIDE), whole),
                pl.BlockSpec((tiles, 2 * TILE), whole),
            ],
            scratch_shapes=[
                pltpu.VMEM((rows + 8, 3 * WIDE), F32),
                pltpu.VMEM((rows, WIDE), BF16),
                pltpu.VMEM((rows, WIDE), BF16),
                pltpu.VMEM((tiles, WIDE + 16, TILE), BF16),
                pltpu.VMEM((1, 2 * TILE), F32),
                pltpu.VMEM((WIDE + 16, 2 * TILE), F32),
            ],
        ),
        out_shape=[
            jax.ShapeDtypeStruct((rows, WIDE), BF16),
            jax.ShapeDtypeStruct((tiles, 2 * TILE), F32),
        ],
        compiler_params=params(40),
        name="attend",
    )(info, proj, taps)


def attend_back_kernel(
    info, p_ref, taps_ref, o_ref, do_ref, lse_ref, dp_ref, gt_ref, wide, q_sc, k_sc, v_sc, kt_sc, dm, dqt
):
    length = info[0]
    tiles = p_ref.shape[0] // TILE
    taps = taps_ref.at[0]
    wide[0:8] = jnp.zeros((8, wide.shape[1]), F32)
    wide[8:] = p_ref[...].astype(F32)
    dm[...] = jnp.zeros(dm.shape, F32)
    for tile in range(tiles):
        rows = slice(tile * TILE, (tile + 1) * TILE)

        @pl.when(tile * TILE < length)
        def _():
            mixed = convolve(wide, taps, tile).astype(BF16)
            q_sc[rows] = mixed[:, :WIDE] * (1.0 / math.sqrt(HEAD))
            k_sc[rows] = mixed[:, WIDE : 2 * WIDE]
            v_sc[rows] = mixed[:, 2 * WIDE :]
            kt_sc[tile] = mixed[:, WIDE : 2 * WIDE].astype(F32).T.astype(BF16)

    lane = lax.broadcasted_iota(jnp.int32, (8, WIDE), 1)
    row = lax.broadcasted_iota(jnp.int32, (8, WIDE), 0)
    picks = jnp.where((lane < HEAD) == (row == 0), 1.0, 0.0).astype(BF16)

    def query_tile(index, carry):
        here = tile_rows(index)
        q_stack = stack_heads(q_sc[here])
        d_rows = do_ref[here]
        d_stack = stack_heads(d_rows)
        product = d_rows.astype(F32) * o_ref[here].astype(F32)
        upper = product.astype(BF16)
        lower = (product - upper.astype(F32)).astype(BF16)
        sums = mm_nt(picks, upper) + mm_nt(picks, lower)
        delta = jnp.concatenate([sums[0:1], sums[1:2]], axis=1)
        lse = lse_ref[pl.ds(index, 1)]
        dqt[...] = jnp.zeros(dqt.shape, F32)

        def visit(key_tile, masked):
            there = tile_rows(key_tile)
            scores = mm_nt(k_sc[there], q_stack)
            probs = jnp.exp(scores - lse)
            if masked:
                probs = jnp.where(allowed_keys(key_tile, index, length), probs, 0.0)
            d_probs = mm_nt(v_sc[there], d_stack)
            d_scores = (probs * (d_probs - delta)).astype(BF16)
            dm[there, 2 * WIDE :] += mm(probs.astype(BF16), d_stack)
            dm[there, WIDE : 2 * WIDE] += mm(d_scores, q_stack)
            dqt[...] += mm(kt_sc[key_tile], d_scores)

        over_key_tiles(index, length, visit)
        dm[here, :WIDE] = unstack_heads(dqt[...].T) * (1.0 / math.sqrt(HEAD))
        return carry

    lax.fori_loop(0, (length + TILE - 1) // TILE, query_tile, 0)
    gt_ref[...] = jnp.zeros(gt_ref.shape, F32)
    for tile in range(tiles):
        begin = tile * TILE
        total = taps[0:1] * dm[begin : begin + TILE]
        total += taps[1:2] * dm[begin + 1 : begin + 1 + TILE]
        total += taps[2:3] * dm[begin + 2 : begin + 2 + TILE]
        dp_ref[begin : begin + TILE] = total.astype(BF16)
        for tap in range(3):
            behind = wide[begin + 8 - tap : begin + 8 - tap + TILE]
            gt_ref[tap : tap + 1] += jnp.sum(
                dm[begin : begin + TILE] * behind, axis=0, keepdims=True
            )


def attend_back(info, proj, taps, attended, d_attended, lse):
    rows = proj.shape[0]
    tiles = rows // TILE
    whole = lambda i, info: (0, 0)
    return pl.pallas_call(
        attend_back_kernel,
        grid_spec=pltpu.PrefetchScalarGridSpec(
            num_scalar_prefetch=1,
            grid=(1,),
            in_specs=[
                pl.BlockSpec((rows, 3 * WIDE), whole),
                pl.BlockSpec((1, 3, 3 * WIDE), lambda i, info: (info[1], 0, 0)),
                pl.BlockSpec((rows, WIDE), whole),
                pl.BlockSpec((rows, WIDE), whole),
                pl.BlockSpec((tiles, 2 * TILE), whole),
            ],
            out_specs=[
                pl.BlockSpec((rows, 3 * WIDE), whole),
                pl.BlockSpec((8, 3 * WIDE), whole),
            ],
            scratch_shapes=[
                pltpu.VMEM((rows + 8, 3 * WIDE), F32),
                pltpu.VMEM((rows, WIDE), BF16),
                pltpu.VMEM((rows, WIDE), BF16),
                pltpu.VMEM((rows, WIDE), BF16),
                pltpu.VMEM((tiles, WIDE, TILE), BF16),
                pltpu.VMEM((rows + 8, 3 * WIDE), F32),
                pltpu.VMEM((WIDE, 2 * TILE), F32),
            ],
        ),
        out_shape=[
            jax.ShapeDtypeStruct((rows, 3 * WIDE), BF16),
            jax.ShapeDtypeStruct((8, 3 * WIDE), F32),
        ],
        compiler_params=params(48),
        name="attend_back",
    )(info, proj, taps, attended, d_attended, lse)


def dense_kernel(
    x_ref, att_ref, cot_ref, weight_ref, gain_ref, wo_ref, wu_ref, wd_ref,
    out_ref, dh_ref, datt_ref, n2_ref, sq_ref, du_ref, da_ref, cz_ref, gain_grad_ref, stats_ref,
    act_sc, att_sc,
):
    rows, width = x_ref.shape[1:]
    hidden_units = wu_ref.shape[1]
    step = width
    for pair in range(PAIRS):
        att_sc[:, pair * WIDE : (pair + 1) * WIDE] = att_ref[pair]
    weight = weight_ref[0]
    gain = gain_ref[...].astype(F32)
    branch = mm(att_sc[...], wo_ref[...])
    hidden = x_ref[0].astype(F32) + branch
    factor = lax.rsqrt(jnp.mean(hidden * hidden, axis=-1, keepdims=True) + 1e-06)
    normed = (hidden * factor * gain).astype(BF16)
    n2_ref[0] = normed
    total = jnp.zeros((rows, width), F32)
    for begin in range(0, hidden_units, step):
        cols = slice(begin, begin + step)
        active = jnp.maximum(mm(normed, wu_ref[:, cols]), 0.0)
        act_sc[:, cols] = active
        squared = (active * active).astype(BF16)
        sq_ref[0, :, cols] = squared
        total += mm(squared, wd_ref[cols])
    full = hidden + total
    out_ref[0] = full.astype(BF16)

    def masked(values):
        per_row = jnp.sum(values * values, axis=-1, keepdims=True)
        return jnp.sum(weight * per_row, axis=0, keepdims=True)

    @pl.when(pl.program_id(0) == 0)
    def _():
        stats_ref[...] = jnp.zeros(stats_ref.shape, F32)
        gain_grad_ref[...] = jnp.zeros(gain_grad_ref.shape, F32)

    parts = [masked(full), masked(branch), masked(total), jnp.sum(weight, axis=0, keepdims=True)]
    for place, part in enumerate(parts):
        stats_ref[place : place + 1] += jnp.broadcast_to(part, (1, WIDE))
    cotangent = (cot_ref[0].astype(F32) * weight).astype(BF16)
    cz_ref[0] = cotangent
    d_normed = jnp.zeros((rows, width), F32)
    for begin in range(0, hidden_units, step):
        cols = slice(begin, begin + step)
        d_squared = mm_nt(cotangent, wd_ref[cols])
        d_up = (2.0 * act_sc[:, cols] * d_squared).astype(BF16)
        du_ref[0, :, cols] = d_up
        d_normed += mm_nt(d_up, wu_ref[:, cols])
    weighted = d_normed * gain
    inner = jnp.mean(weighted * hidden, axis=-1, keepdims=True)
    d_hidden = cotangent.astype(F32) + factor * weighted - hidden * (factor * factor * factor) * inner
    gain_grad_ref[...] += jnp.sum(d_normed * hidden * factor, axis=0, keepdims=True)
    dh_ref[0] = d_hidden
    d_attn = d_hidden.astype(BF16)
    da_ref[0] = d_attn
    d_att = mm_nt(d_attn, wo_ref[...]).astype(BF16)
    for pair in range(PAIRS):
        datt_ref[pair] = d_att[:, pair * WIDE : (pair + 1) * WIDE]


def dense(x, attended, grad_output, weight, gain, w_out, w_up, w_down):
    groups, rows, width = x.shape
    hidden_units = w_up.shape[1]
    per_group = lambda s: (s, 0, 0)
    fixed = lambda s: (0, 0)
    once = pl.Buffered(1)
    row_block = pl.BlockSpec((1, rows, width), per_group)
    wide_block = pl.BlockSpec((1, rows, hidden_units), per_group)
    unit_block = pl.BlockSpec((PAIRS, rows, WIDE), per_group)
    low = jax.ShapeDtypeStruct(x.shape, BF16)
    wide_low = jax.ShapeDtypeStruct((groups, rows, hidden_units), BF16)
    return pl.pallas_call(
        dense_kernel,
        grid=(groups,),
        in_specs=[
            row_block,
            unit_block,
            row_block,
            pl.BlockSpec((1, rows, 1), per_group),
            pl.BlockSpec((1, width), fixed),
            pl.BlockSpec(w_out.shape, fixed, pipeline_mode=once),
            pl.BlockSpec(w_up.shape, fixed, pipeline_mode=once),
            pl.BlockSpec(w_down.shape, fixed, pipeline_mode=once),
        ],
        out_specs=[
            row_block,
            row_block,
            unit_block,
            row_block,
            wide_block,
            wide_block,
            row_block,
            row_block,
            pl.BlockSpec((1, width), fixed),
            pl.BlockSpec((8, WIDE), fixed),
        ],
        out_shape=[
            low,
            jax.ShapeDtypeStruct(x.shape, F32),
            jax.ShapeDtypeStruct((groups * PAIRS, rows, WIDE), BF16),
            low,
            wide_low,
            wide_low,
            low,
            low,
            jax.ShapeDtypeStruct((1, width), F32),
            jax.ShapeDtypeStruct((8, WIDE), F32),
        ],
        scratch_shapes=[pltpu.VMEM((rows, hidden_units), F32), pltpu.VMEM((rows, width), BF16)],
        compiler_params=params(58),
        name="dense",
    )(x, attended, grad_output, weight, gain.reshape(1, width), w_out, w_up, w_down)


PART = 384


def feed_grads_kernel(sq_ref, cz_ref, n2_ref, du_ref, att_ref, da_ref, out_ref, n2_t):
    half, sub = pl.program_id(0), pl.program_id(1)
    groups, rows, width = n2_ref.shape
    tokens = groups * rows

    @pl.when((half == 0) & (sub == 0))
    def _():
        for group in range(groups):
            n2_t[:, group * rows : (group + 1) * rows] = n2_ref[group].astype(F32).T.astype(BF16)

    down = mm_tn(sq_ref[...].reshape(tokens, PART), cz_ref[...].reshape(tokens, width))
    for place in range(4):
        for side in range(2):
            out_ref[place, pl.ds(sub, 1), side * 96 : side * 96 + 96] = down[
                place * 96 : (place + 1) * 96, side * PART : (side + 1) * PART
            ].astype(BF16)[None]
    up = mm(n2_t[...], du_ref[...].reshape(tokens, PART))
    out_ref[pl.ds(sub, 1), :, 192:384] = up.astype(BF16).reshape(1, 4, 192, PART)

    @pl.when(sub == 0)
    def _():
        for pair in range(PAIRS):
            block = mm_tn(
                att_ref[:, pair].reshape(tokens, WIDE), da_ref[...].reshape(tokens, PART)
            ).astype(BF16)
            for low in range(0, WIDE, 16):
                row = pair * WIDE + low
                batch, inner = row // 192, row % 192
                out_ref[inner // 48, batch, 384 + inner % 48 : 400 + inner % 48] = block[low : low + 16]


def feed_grads(squared, cotangent, normed2, d_up, attended, d_attn):
    groups, rows, width = normed2.shape
    whole = lambda h, b: (0, 0, 0)
    return pl.pallas_call(
        feed_grads_kernel,
        grid=(2, 4),
        in_specs=[
            pl.BlockSpec((groups, rows, PART), lambda h, b: (0, 0, 2 * b + h)),
            pl.BlockSpec((groups, rows, width), whole, pipeline_mode=pl.Buffered(1)),
            pl.BlockSpec((groups, rows, width), whole, pipeline_mode=pl.Buffered(1)),
            pl.BlockSpec((groups, rows, PART), lambda h, b: (0, 0, 4 * h + b)),
            pl.BlockSpec(
                (groups, PAIRS, rows, WIDE), lambda h, b: (0, 0, 0, 0), pipeline_mode=pl.Buffered(1)
            ),
            pl.BlockSpec((groups, rows, PART), lambda h, b: (0, 0, h)),
        ],
        out_specs=pl.BlockSpec((4, 4, 432, PART), lambda h, b: (h, 0, 0, 0)),
        out_shape=jax.ShapeDtypeStruct((8, 4, 432, PART), BF16),
        scratch_shapes=[pltpu.VMEM((width, groups * rows), BF16)],
        compiler_params=params(58),
        name="feed_grads",
    )(squared, cotangent, normed2, d_up, attended.reshape(groups, PAIRS, rows, WIDE), d_attn)


def input_grads_kernel(
    dp_ref, n1_ref, x_ref, dh_ref, w_ref, gain_ref, out_ref, gx_ref, gain_grad_ref, n1_t, total, w_sc
):
    pair = pl.program_id(0)
    groups, rows, width = n1_ref.shape
    tokens = groups * rows

    @pl.when(pair == 0)
    def _():
        for group in range(groups):
            n1_t[:, group * rows : (group + 1) * rows] = n1_ref[group].astype(F32).T.astype(BF16)
        total[...] = jnp.zeros(total.shape, F32)

    d_proj = dp_ref[...].reshape(tokens, 3 * WIDE)
    grad = mm(n1_t[...], d_proj).astype(BF16)
    for batch in range(4):
        for chip in range(4):
            begin = batch * 192 + chip * 48
            out_ref[0, 0, chip, batch] = grad[begin : begin + 48]
    for part in range(3):
        cols = pl.ds(pl.multiple_of(part * width + pair * WIDE, WIDE), WIDE)
        w_sc[:, part * WIDE : (part + 1) * WIDE] = w_ref[:, cols]
    total[...] += mm_nt(d_proj, w_sc[...])

    @pl.when(pair == PAIRS - 1)
    def _():
        gain = gain_ref[...].astype(F32)
        gain_sum = jnp.zeros((1, width), F32)
        for group in range(groups):
            x = x_ref[group].astype(F32)
            d_normed = total[group * rows : (group + 1) * rows]
            factor = lax.rsqrt(jnp.mean(x * x, axis=-1, keepdims=True) + 1e-06)
            weighted = d_normed * gain
            inner = jnp.mean(weighted * x, axis=-1, keepdims=True)
            gx_ref[group] = (
                dh_ref[group] + factor * weighted - x * (factor * factor * factor) * inner
            )
            gain_sum += jnp.sum(d_normed * x * factor, axis=0, keepdims=True)
        gain_grad_ref[...] = gain_sum


def input_grads(d_proj, normed1, x, d_hidden, w_qkv, gain):
    groups, rows, width = x.shape
    whole = lambda p: (0, 0, 0)
    once = pl.Buffered(1)
    tokens = pl.BlockSpec((groups, rows, width), whole, pipeline_mode=once)
    return pl.pallas_call(
        input_grads_kernel,
        grid=(PAIRS,),
        in_specs=[
            pl.BlockSpec((groups, 1, rows, 3 * WIDE), lambda p: (0, p, 0, 0)),
            tokens,
            tokens,
            tokens,
            pl.BlockSpec(w_qkv.shape, lambda p: (0, 0), pipeline_mode=once),
            pl.BlockSpec((1, width), lambda p: (0, 0)),
        ],
        out_specs=[
            pl.BlockSpec((1, 1, 4, 4, 48, PART), lambda p: (p % 3, p // 3, 0, 0, 0, 0)),
            tokens,
            pl.BlockSpec((1, width), lambda p: (0, 0)),
        ],
        out_shape=[
            jax.ShapeDtypeStruct((3, 2, 4, 4, 48, PART), BF16),
            jax.ShapeDtypeStruct(x.shape, F32),
            jax.ShapeDtypeStruct((1, width), F32),
        ],
        scratch_shapes=[
            pltpu.VMEM((width, groups * rows), BF16),
            pltpu.VMEM((groups * rows, width), F32),
            pltpu.VMEM((width, 3 * WIDE), BF16),
        ],
        compiler_params=params(58),
        name="input_grads",
    )(d_proj.reshape(groups, PAIRS, rows, 3 * WIDE), normed1, x, d_hidden, w_qkv, gain.reshape(1, width))


MESH = pl.DeviceIdType.MESH


def sum_kernel(
    g_ref, feed_ref, small_ref, qkv_out, feed_out, small_out,
    core_in, here, chip_in, mine, z_in, qkv_all, feed_in, feed_all, row_in, row_sum, col_in,
    core_s, core_r, chip_s, chip_r, z_s, z_r, qkv_s, qkv_r, fz_s, fz_r, fa_s, fa_r,
    row_s, row_r, col_s, col_r,
):
    me = lax.axis_index("seq")
    z = lax.axis_index("batch")
    core, chip = lax.rem(me, 2), me // 2
    barrier = pltpu.get_barrier_semaphore()
    for bit in range(1, 8):
        pl.semaphore_signal(barrier, inc=1, device_id={"seq": me ^ bit}, device_id_type=MESH)
    for bit in range(1, 4):
        pl.semaphore_signal(barrier, inc=1, device_id={"batch": z ^ bit}, device_id_type=MESH)
    pl.semaphore_wait(barrier, 10)

    def send(source, target, sems, axis, peer):
        copy = pltpu.make_async_remote_copy(
            src_ref=source,
            dst_ref=target,
            send_sem=sems[0],
            recv_sem=sems[1],
            device_id={axis: peer},
            device_id_type=MESH,
        )
        copy.start()
        return copy

    def spread(ref, s, r):
        return [
            send(ref.at[me], ref.at[me], (s.at[step], r.at[step]), "seq", me ^ max(2 * step, 1))
            for step in range(4)
        ]

    def relay(ref, first, s, r):
        more = []
        for step in range(1, 4):
            first[step].wait()
            slot = me ^ (2 * step)
            more.append(
                send(ref.at[slot], ref.at[slot], (s.at[3 + step], r.at[3 + step]), "seq", me ^ 1)
            )
        return [first[0]] + more

    chunks = g_ref.shape[0]
    rows = feed_ref.shape[1] // chunks
    to_core = [
        send(g_ref.at[c, 1 - core], core_in.at[c], (core_s.at[c], core_r.at[c]), "seq", me ^ 1)
        for c in range(chunks)
    ]
    feed_z = [
        [
            send(
                feed_ref.at[z ^ bit, c * rows : (c + 1) * rows],
                feed_in.at[c, bit - 1],
                (fz_s.at[c, bit - 1], fz_r.at[c, bit - 1]),
                "batch",
                z ^ bit,
            )
            for bit in range(1, 4)
        ]
        for c in range(chunks)
    ]
    row_in[pl.ds(me, 1)] = small_ref[...][None]
    rows_out = [
        send(small_ref, row_in.at[me], (row_s.at[bit - 1], row_r.at[bit - 1]), "seq", me ^ bit)
        for bit in range(1, 8)
    ]
    to_chip = []
    for c in range(chunks):
        to_core[c].wait()
        for q in range(4):
            both = g_ref[c, core, q].astype(F32) + core_in[c, q].astype(F32)
            here[c, q] = both.astype(BF16)
        to_chip.append(
            [
                send(
                    here.at[c, chip ^ bit],
                    chip_in.at[c, bit - 1],
                    (chip_s.at[c, bit - 1], chip_r.at[c, bit - 1]),
                    "seq",
                    me ^ (2 * bit),
                )
                for bit in range(1, 4)
            ]
        )
    for copy in rows_out:
        copy.wait()
    total = row_in[0]
    for place in range(1, 8):
        total = total + row_in[place]
    row_sum[...] = total
    col_in[pl.ds(z, 1)] = total[None]
    cols_out = [
        send(row_sum, col_in.at[z], (col_s.at[bit - 1], col_r.at[bit - 1]), "batch", z ^ bit)
        for bit in range(1, 4)
    ]
    to_z = []
    for c in range(chunks):
        for copy in to_chip[c]:
            copy.wait()
        both = here[c, chip].astype(F32)
        for bit in range(3):
            both = both + chip_in[c, bit].astype(F32)
        mine[c] = both.astype(BF16)
        to_z.append(
            [
                send(
                    mine.at[c, z ^ bit],
                    z_in.at[c, bit - 1],
                    (z_s.at[c, bit - 1], z_r.at[c, bit - 1]),
                    "batch",
                    z ^ bit,
                )
                for bit in range(1, 4)
            ]
        )
    feed_first = []
    for c in range(chunks):
        for copy in feed_z[c]:
            copy.wait()
        both = feed_ref[z, c * rows : (c + 1) * rows].astype(F32)
        for bit in range(3):
            both = both + feed_in[c, bit].astype(F32)
        feed_all[c, pl.ds(me, 1)] = both.astype(BF16)[None]
        feed_first.append(spread(feed_all.at[c], fa_s.at[c], fa_r.at[c]))
    qkv_first = []
    for c in range(chunks):
        for copy in to_z[c]:
            copy.wait()
        both = mine[c, z].astype(F32)
        for bit in range(3):
            both = both + z_in[c, bit].astype(F32)
        qkv_all[c, pl.ds(me, 1)] = both.astype(BF16)[None]
        qkv_first.append(spread(qkv_all.at[c], qkv_s.at[c], qkv_r.at[c]))
    last = []
    for c in range(chunks):
        last += relay(feed_all.at[c], feed_first[c], fa_s.at[c], fa_r.at[c])
    for c in range(chunks):
        last += relay(qkv_all.at[c], qkv_first[c], qkv_s.at[c], qkv_r.at[c])
    for copy in cols_out:
        copy.wait()
    small_out[...] = ((col_in[0] + col_in[1]) + col_in[2]) + col_in[3]
    for copy in last:
        copy.wait()
    qkv_out[...] = qkv_all[...]
    feed_out[...] = feed_all[...]


def sum_over_devices(pieces, feed, small):
    chunks, rows = pieces.shape[0], pieces.shape[4]
    feed_rows = feed.shape[1] // chunks
    vmem = pl.BlockSpec(memory_space=pltpu.VMEM)
    dma = pltpu.SemaphoreType.DMA
    pairs = []
    for shape in [(), (3,), (3,), (7,), (3,), (7,)]:
        pairs += [dma((chunks,) + shape), dma((chunks,) + shape)]
    return pl.pallas_call(
        sum_kernel,
        in_specs=[vmem, vmem, vmem],
        out_specs=[vmem, vmem, vmem],
        out_shape=[
            jax.ShapeDtypeStruct((chunks, 8, rows, PART), BF16),
            jax.ShapeDtypeStruct((chunks, 8, feed_rows, PART), BF16),
            jax.ShapeDtypeStruct(small.shape, F32),
        ],
        scratch_shapes=[
            pltpu.VMEM((chunks, 4, 4, rows, PART), BF16),
            pltpu.VMEM((chunks, 4, 4, rows, PART), BF16),
            pltpu.VMEM((chunks, 3, 4, rows, PART), BF16),
            pltpu.VMEM((chunks, 4, rows, PART), BF16),
            pltpu.VMEM((chunks, 3, rows, PART), BF16),
            pltpu.VMEM((chunks, 8, rows, PART), BF16),
            pltpu.VMEM((chunks, 3, feed_rows, PART), BF16),
            pltpu.VMEM((chunks, 8, feed_rows, PART), BF16),
            pltpu.VMEM((8,) + small.shape, F32),
            pltpu.VMEM(small.shape, F32),
            pltpu.VMEM((4,) + small.shape, F32),
        ]
        + pairs
        + [dma((7,)), dma((7,)), dma((3,)), dma((3,))],
        compiler_params=pltpu.CompilerParams(
            collective_id=0, has_side_effects=True, vmem_limit_bytes=56 << 20
        ),
        name="sum_over_devices",
    )(pieces, feed, small)


def unpack_kernel(feed_ref, qkv_ref, down_ref, up_ref, out_ref, grad_ref):
    down_ref[:, :PART] = feed_ref[0, 0, :96].astype(F32)
    down_ref[:48, PART:] = feed_ref[0, 0, 96:].astype(F32)
    down_ref[48:, PART:] = feed_ref[1, 0, :48].astype(F32)
    up_ref[:96] = feed_ref[1, 0, 48:].astype(F32)
    up_ref[96:] = feed_ref[2, 0, :96].astype(F32)
    out_ref[...] = feed_ref[2, 0, 96:].astype(F32)
    place = pl.program_id(0)

    def put(core):
        for c in range(3):
            for part in range(3):
                begin = part * PAIRS * WIDE + (core * 3 + c) * WIDE
                grad_ref[:, begin : begin + WIDE] = qkv_ref[
                    c, 0, :, part * WIDE : (part + 1) * WIDE
                ].astype(F32)

    for core in range(2):
        pl.when(place % 2 == core)(functools.partial(put, core))


def unpack(feed, qkv):
    return pl.pallas_call(
        unpack_kernel,
        grid=(8,),
        in_specs=[
            pl.BlockSpec((3, 1, 144, PART), lambda r: (0, r, 0, 0)),
            pl.BlockSpec((3, 1, 48, PART), lambda r: (0, r, 0, 0)),
        ],
        out_specs=[
            pl.BlockSpec((96, 2 * PART), lambda r: (r, 0)),
            pl.BlockSpec((192, PART), lambda r: (0, r)),
            pl.BlockSpec((48, PART), lambda r: (r % 4, r // 4)),
            pl.BlockSpec((48, 3 * PAIRS * WIDE), lambda r: (r // 2, 0)),
        ],
        out_shape=[
            jax.ShapeDtypeStruct((768, 2 * PART), F32),
            jax.ShapeDtypeStruct((192, 8 * PART), F32),
            jax.ShapeDtypeStruct((192, 2 * PART), F32),
            jax.ShapeDtypeStruct((192, 3 * PAIRS * WIDE), F32),
        ],
        compiler_params=params(32),
        name="unpack",
    )(feed, qkv)


def exchange(blocks):
    return lax.all_to_all(blocks, "seq", 0, 0, tiled=True)


def plain_gradients(feed, qkv):
    down = feed[:, :, :192].reshape(8, 4, 2, 96, PART).transpose(1, 0, 3, 2, 4)
    up = feed[:, :, 192:384].transpose(1, 2, 0, 3)
    out = feed[:, :, 384:].reshape(2, 4, 4, 48, PART).transpose(2, 1, 3, 0, 4)
    grad = qkv.reshape(3, 2, 4, 4, 48, 3, WIDE).transpose(3, 2, 4, 5, 1, 0, 6)
    return (
        down.reshape(3072, 768),
        up.reshape(768, 3072),
        out.reshape(768, 768),
        grad.reshape(768, 2304),
    )


def shards(
    stream_in,
    lengths,
    token_mask,
    norm1_gain,
    w_qkv,
    conv_taps,
    w_out,
    norm2_gain,
    w_up,
    w_down,
    grad_output,
):
    groups, block_len, width = stream_in.shape
    count = lax.axis_size("seq")
    batches = lax.axis_size("batch")
    place = lax.axis_index("seq")
    units = groups * PAIRS
    slots = -(-units // count)
    spare = slots * count - units
    offset = place * block_len
    taps = conv_taps.astype(F32).reshape(3, 3, PAIRS, WIDE).transpose(2, 0, 1, 3)
    taps = taps.reshape(PAIRS, 3, 3 * WIDE)

    def fill(blocks):
        return jnp.pad(blocks, ((0, spare), (0, 0), (0, 0))) if spare else blocks

    def to_heads(blocks, slot):
        got = exchange(blocks[slot * count : (slot + 1) * count])
        return got.reshape(count * block_len, blocks.shape[2])

    def to_tokens(per_slot):
        got = [exchange(rows.reshape(count, block_len, rows.shape[1])) for rows in per_slot]
        return jnp.concatenate(got, axis=0)[:units]

    infos = []
    for slot in range(slots):
        unit = slot * count + place
        sequence = jnp.minimum(unit // PAIRS, groups - 1)
        length = jnp.where(unit < units, lengths[sequence], 0)
        infos.append(jnp.stack([length, unit % PAIRS]).astype(jnp.int32))

    normed1, proj = project(stream_in, norm1_gain, w_qkv)
    proj = fill(proj)
    unit_proj, unit_out, unit_lse = [], [], []
    for slot in range(slots):
        rows = to_heads(proj, slot)
        out, lse = attend(infos[slot], rows, taps)
        unit_proj.append(rows)
        unit_out.append(out)
        unit_lse.append(lse)
    attended = to_tokens(unit_out)

    positions = offset + jnp.arange(block_len, dtype=jnp.int32)
    inside = (positions[None, :] < lengths[:, None]).astype(F32)
    stat_weight = (token_mask.astype(F32) * inside)[..., None]
    (
        stream_out,
        d_hidden,
        d_blocks,
        normed2,
        squared,
        d_up,
        d_attn,
        cotangent,
        grad_norm2,
        local_stats,
    ) = dense(stream_in, attended, grad_output, stat_weight, norm2_gain, w_out, w_up, w_down)
    d_blocks = fill(d_blocks)
    feed = feed_grads(squared, cotangent, normed2, d_up, attended, d_attn)
    fitted = count == 8 and batches == 4
    if fitted:
        feed = lax.psum_scatter(feed, "seq", scatter_dimension=0, tiled=False)

    back, unit_taps = [], jnp.zeros((PAIRS, 3, 3 * WIDE), F32)
    for slot in range(slots):
        d_rows = to_heads(d_blocks, slot)
        d_proj_rows, part = attend_back(
            infos[slot], unit_proj[slot], taps, unit_out[slot], d_rows, unit_lse[slot]
        )
        back.append(d_proj_rows)
        chosen = jnp.arange(PAIRS)[:, None, None] == infos[slot][1]
        unit_taps = unit_taps + jnp.where(chosen, part[None, :3], 0.0)
    grad_taps = unit_taps.reshape(PAIRS, 3, 3, WIDE).transpose(1, 2, 0, 3).reshape(9, width)
    d_proj = to_tokens(back)
    pieces, grad_input, grad_norm1 = input_grads(
        d_proj, normed1, stream_in, d_hidden, w_qkv, norm1_gain
    )
    stats_row = jnp.pad(local_stats[:4, 0], (0, width - 4)).reshape(1, width)
    small = jnp.concatenate(
        [grad_taps, grad_norm1, grad_norm2, stats_row, jnp.zeros((4, width), F32)], axis=0
    )
    if fitted:
        qkv, feed, small = sum_over_devices(pieces, feed, small)
        total_down, total_up, total_wout, total_qkv = unpack(feed, qkv)
    else:

        def reduce(gradient):
            share = lax.psum_scatter(
                gradient, ("batch", "seq"), scatter_dimension=0, tiled=True
            )
            return lax.all_gather(share, "seq", axis=0, tiled=True).astype(F32)

        total_down, total_up, total_wout, total_qkv = map(reduce, plain_gradients(feed, pieces))
        small = lax.psum(small, ("seq", "batch"))
    share = width // batches
    begin = lax.axis_index("batch") * share
    block_rms = jnp.sqrt(small[11, :3] / (width * small[11, 3]))
    return (
        stream_out,
        grad_input,
        lax.dynamic_slice_in_dim(small[9], begin, share),
        total_qkv,
        small[:9].reshape(3, 3 * width),
        total_wout,
        lax.dynamic_slice_in_dim(small[10], begin, share),
        total_up,
        total_down,
        block_rms,
    )


def solution(mesh):
    tokens = P("batch", "seq", None)
    return jax.shard_map(
        shards,
        mesh=mesh,
        in_specs=(
            tokens,
            P("batch"),
            P("batch", "seq"),
            P(),
            P(),
            P(),
            P(),
            P(),
            P(),
            P(),
            tokens,
        ),
        out_specs=(
            tokens,
            tokens,
            P("batch"),
            P("batch", None),
            P(),
            P("batch", None),
            P("batch"),
            P("batch", None),
            P("batch", None),
            P(),
        ),
        check_vma=False,
    )
```

```python
import functools
import math

import jax
import jax.numpy as jnp
from jax import lax
from jax.experimental import pallas as pl
from jax.experimental.pallas import tpu as pltpu
from jax.sharding import PartitionSpec as P

HEADS = 12
HEAD = 64
PAIRS = HEADS // 2
WIDE = 2 * HEAD
TILE = 256
NEG = -1e30
F32 = jnp.float32
BF16 = jnp.bfloat16


def mm(left_op, right_op):
    return jnp.dot(left_op, right_op, preferred_element_type=F32)


def mm_nt(left_op, right_op):
    return lax.dot_general(
        left_op, right_op, (((1,), (1,)), ((), ())), preferred_element_type=F32
    )


def mm_tn(left_op, right_op):
    return lax.dot_general(
        left_op, right_op, (((0,), (0,)), ((), ())), preferred_element_type=F32
    )


def params(limit):
    return pltpu.CompilerParams(vmem_limit_bytes=limit << 20)


MESH = pl.DeviceIdType.MESH
GROUP = 8
DMA = pltpu.SemaphoreType.DMA


def remote(source, target, sems, axis, peer):
    return pltpu.make_async_remote_copy(
        src_ref=source,
        dst_ref=target,
        send_sem=sems[0],
        recv_sem=sems[1],
        device_id={axis: peer},
        device_id_type=MESH,
    )


def meet_group():
    me = lax.axis_index("seq")
    barrier = pltpu.get_barrier_semaphore()
    for bit in range(1, GROUP):
        pl.semaphore_signal(barrier, inc=1, device_id={"seq": me ^ bit}, device_id_type=MESH)
    pl.semaphore_wait(barrier, GROUP - 1)


def unit_copy(blocks, inbox, sems, unit):
    me = lax.axis_index("seq")
    owner, slot = lax.rem(unit, GROUP), unit // GROUP
    return owner, remote(
        blocks.at[unit],
        inbox.at[slot, me],
        (sems[0].at[unit], sems[1].at[slot, me ^ owner]),
        "seq",
        owner,
    )


def send_unit(blocks, inbox, sems, unit):
    me = lax.axis_index("seq")
    owner, copy = unit_copy(blocks, inbox, sems, unit)

    @pl.when(owner != me)
    def _():
        copy.start()

    @pl.when(owner == me)
    def _():
        slot = unit // GROUP
        pltpu.make_async_copy(blocks.at[unit], inbox.at[slot, me], sems[1].at[slot, 0]).start()


def wait_units(blocks, inbox, sems):
    me = lax.axis_index("seq")
    units = blocks.shape[0]
    for slot in range(units // GROUP):
        unit = slot * GROUP + me
        pltpu.make_async_copy(blocks.at[unit], inbox.at[slot, me], sems[1].at[slot, 0]).wait()
        for bit in range(1, GROUP):
            remote(
                blocks.at[unit],
                inbox.at[slot, me ^ bit],
                (sems[0].at[unit], sems[1].at[slot, bit]),
                "seq",
                me ^ bit,
            ).wait_recv()
    for unit in range(units):
        owner, copy = unit_copy(blocks, inbox, sems, unit)
        pl.when(owner != me)(copy.wait_send)


def block_copies(units, inbox, sems, slot):
    me = lax.axis_index("seq")
    return [
        remote(
            units.at[slot, me ^ bit],
            inbox.at[slot * GROUP + me],
            (sems[0].at[slot, bit], sems[1].at[slot, bit]),
            "seq",
            me ^ bit,
        )
        for bit in range(1, GROUP)
    ]


def own_block(units, inbox, sems, slot):
    me = lax.axis_index("seq")
    return pltpu.make_async_copy(
        units.at[slot, me], inbox.at[slot * GROUP + me], sems[1].at[slot, 0]
    )


def send_blocks(units, inbox, sems, slot):
    own_block(units, inbox, sems, slot).start()
    for copy in block_copies(units, inbox, sems, slot):
        copy.start()


def wait_blocks(units, inbox, sems, slot):
    own_block(units, inbox, sems, slot).wait()
    for copy in block_copies(units, inbox, sems, slot):
        copy.wait()


def group_params(number, limit):
    return pltpu.CompilerParams(
        collective_id=number, has_side_effects=True, vmem_limit_bytes=limit << 20
    )


def project_kernel(x_ref, gain_ref, w_ref, n_ref, p_ref):
    x = x_ref[0].astype(F32)
    factor = lax.rsqrt(jnp.mean(x * x, axis=-1, keepdims=True) + 1e-06)
    normed = (x * factor * gain_ref[...].astype(F32)).astype(BF16)
    n_ref[0] = normed
    width = x.shape[1]
    for part in range(3):
        cols = mm(normed, w_ref[:, part * width : (part + 1) * width])
        for pair in range(PAIRS):
            p_ref[pair, :, part * WIDE : (part + 1) * WIDE] = cols[
                :, pair * WIDE : (pair + 1) * WIDE
            ].astype(BF16)


def project_send_kernel(x_ref, gain_ref, w_ref, n_ref, inbox, blocks, send_sems, recv_sems):
    group = pl.program_id(0)
    sems = (send_sems, recv_sems)
    pl.when(group == 0)(meet_group)
    project_kernel(x_ref, gain_ref, w_ref, n_ref, blocks.at[pl.ds(group * PAIRS, PAIRS)])
    for pair in range(PAIRS):
        send_unit(blocks, inbox, sems, group * PAIRS + pair)
    pl.when(group == pl.num_programs(0) - 1)(lambda: wait_units(blocks, inbox, sems))


def project_send(x, gain, w_qkv):
    groups, rows, width = x.shape
    slots = groups * PAIRS // GROUP
    return pl.pallas_call(
        project_send_kernel,
        grid=(groups,),
        in_specs=[
            pl.BlockSpec((1, rows, width), lambda s: (s, 0, 0)),
            pl.BlockSpec((1, width), lambda s: (0, 0)),
            pl.BlockSpec(w_qkv.shape, lambda s: (0, 0), pipeline_mode=pl.Buffered(1)),
        ],
        out_specs=[
            pl.BlockSpec((1, rows, width), lambda s: (s, 0, 0)),
            pl.BlockSpec(memory_space=pl.ANY),
        ],
        out_shape=[
            jax.ShapeDtypeStruct(x.shape, BF16),
            jax.ShapeDtypeStruct((slots, GROUP, rows, 3 * WIDE), BF16),
        ],
        scratch_shapes=[
            pltpu.VMEM((groups * PAIRS, rows, 3 * WIDE), BF16),
            DMA((groups * PAIRS,)),
            DMA((slots, GROUP)),
        ],
        compiler_params=group_params(1, 40),
        name="project_send",
    )(x, gain.reshape(1, width), w_qkv)


def project(x, gain, w_qkv):
    groups, rows, width = x.shape
    return pl.pallas_call(
        project_kernel,
        grid=(groups,),
        in_specs=[
            pl.BlockSpec((1, rows, width), lambda s: (s, 0, 0)),
            pl.BlockSpec((1, width), lambda s: (0, 0)),
            pl.BlockSpec(w_qkv.shape, lambda s: (0, 0)),
        ],
        out_specs=[
            pl.BlockSpec((1, rows, width), lambda s: (s, 0, 0)),
            pl.BlockSpec((PAIRS, rows, 3 * WIDE), lambda s: (s, 0, 0)),
        ],
        out_shape=[
            jax.ShapeDtypeStruct(x.shape, BF16),
            jax.ShapeDtypeStruct((groups * PAIRS, rows, 3 * WIDE), BF16),
        ],
        compiler_params=params(40),
        name="project",
    )(x, gain.reshape(1, width), w_qkv)


def stack_heads(rows):
    lane = lax.broadcasted_iota(jnp.int32, rows.shape, 1)
    zero = jnp.zeros_like(rows)
    first = jnp.where(lane < HEAD, rows, zero)
    second = jnp.where(lane < HEAD, zero, rows)
    return jnp.concatenate([first, second], axis=0)


def unstack_heads(rows):
    half = rows.shape[0] // 2
    lane = lax.broadcasted_iota(jnp.int32, (half, rows.shape[1]), 1)
    return jnp.where(lane < HEAD, rows[:half], rows[half:])


def tile_rows(index):
    return pl.ds(pl.multiple_of(index * TILE, TILE), TILE)


def allowed_keys(key_tile, query_tile, length):
    shape = (TILE, 2 * TILE)
    k_pos = key_tile * TILE + lax.broadcasted_iota(jnp.int32, shape, 0)
    q_pos = query_tile * TILE + (lax.broadcasted_iota(jnp.int32, shape, 1) & (TILE - 1))
    return (k_pos <= q_pos) & (k_pos < length)


def over_key_tiles(query_tile, length, visit):
    full = jnp.minimum(query_tile, length // TILE)
    last = jnp.minimum(query_tile + 1, (length + TILE - 1) // TILE)

    def plain(key_tile, carry):
        visit(key_tile, False)
        return carry

    def edge(key_tile, carry):
        visit(key_tile, True)
        return carry

    lax.fori_loop(0, full, plain, 0)
    lax.fori_loop(full, last, edge, 0)


def convolve(wide_ref, taps_ref, tile):
    begin = 8 + tile * TILE
    total = taps_ref[0:1] * wide_ref[begin : begin + TILE]
    total += taps_ref[1:2] * wide_ref[begin - 1 : begin - 1 + TILE]
    total += taps_ref[2:3] * wide_ref[begin - 2 : begin - 2 + TILE]
    return total


def attend_kernel(info, p_ref, taps_ref, o_ref, lse_ref, wide, q_sc, k_sc, vt_sc, m_sc, acc):
    p_ref, o_ref, lse_ref = p_ref.at[0], o_ref.at[0], lse_ref.at[0]
    length = info[pl.program_id(0), 0]
    tiles = p_ref.shape[0] // TILE
    taps = taps_ref.at[0]
    wide[0:8] = jnp.zeros((8, wide.shape[1]), F32)
    wide[8:] = p_ref[...].astype(F32)
    for tile in range(tiles):
        rows = slice(tile * TILE, (tile + 1) * TILE)
        mixed = convolve(wide, taps, tile).astype(BF16)
        q_sc[rows] = mixed[:, :WIDE] * (1.0 / math.sqrt(HEAD))
        k_sc[rows] = mixed[:, WIDE : 2 * WIDE]
        vt_sc[tile, :WIDE] = mixed[:, 2 * WIDE :].astype(F32).T.astype(BF16)
        vt_sc[tile, WIDE:] = jnp.ones((vt_sc.shape[1] - WIDE, TILE), BF16)

    def query_tile(index, carry):
        q_stack = stack_heads(q_sc[tile_rows(index)])
        m_sc[...] = jnp.full(m_sc.shape, NEG, F32)
        acc[...] = jnp.zeros(acc.shape, F32)

        def visit(key_tile, masked):
            scores = mm_nt(k_sc[tile_rows(key_tile)], q_stack)
            if masked:
                scores = jnp.where(allowed_keys(key_tile, index, length), scores, NEG)
            old = m_sc[...]
            new = jnp.maximum(old, jnp.max(scores, axis=0, keepdims=True))
            probs = jnp.exp(scores - new)
            acc[...] = acc[...] * jnp.exp(old - new) + mm(vt_sc[key_tile], probs.astype(BF16))
            m_sc[...] = new

        over_key_tiles(index, length, visit)
        total = acc[WIDE : WIDE + 1]
        out = (acc[:WIDE] / total).T
        o_ref[tile_rows(index)] = unstack_heads(out).astype(BF16)
        lse_ref[pl.ds(index, 1)] = m_sc[...] + jnp.log(total)
        return carry

    lax.fori_loop(0, tiles, query_tile, 0)


def attend(info, proj, taps):
    slots, rows = proj.shape[:2]
    tiles = rows // TILE
    own = lambda i, info: (i, 0, 0)
    return pl.pallas_call(
        attend_kernel,
        grid_spec=pltpu.PrefetchScalarGridSpec(
            num_scalar_prefetch=1,
            grid=(slots,),
            in_specs=[
                pl.BlockSpec((1, rows, 3 * WIDE), own),
                pl.BlockSpec((1, 3, 3 * WIDE), lambda i, info: (info[i, 1], 0, 0)),
            ],
            out_specs=[
                pl.BlockSpec((1, rows, WIDE), own),
                pl.BlockSpec((1, tiles, 2 * TILE), own),
            ],
            scratch_shapes=[
                pltpu.VMEM((rows + 8, 3 * WIDE), F32),
                pltpu.VMEM((rows, WIDE), BF16),
                pltpu.VMEM((rows, WIDE), BF16),
                pltpu.VMEM((tiles, WIDE + 16, TILE), BF16),
                pltpu.VMEM((1, 2 * TILE), F32),
                pltpu.VMEM((WIDE + 16, 2 * TILE), F32),
            ],
        ),
        out_shape=[
            jax.ShapeDtypeStruct((slots, rows, WIDE), BF16),
            jax.ShapeDtypeStruct((slots, tiles, 2 * TILE), F32),
        ],
        compiler_params=params(40),
        name="attend",
    )(info, proj, taps)


def attend_back_kernel(
    info, p_ref, taps_ref, o_ref, do_ref, lse_ref, dp_ref, gt_ref, wide, q_sc, k_sc, v_sc, kt_sc, dm, dqt
):
    p_ref, o_ref, do_ref, lse_ref = p_ref.at[0], o_ref.at[0], do_ref.at[0], lse_ref.at[0]
    dp_ref, gt_ref = dp_ref.at[0], gt_ref.at[0]
    length = info[pl.program_id(0), 0]
    tiles = p_ref.shape[0] // TILE
    taps = taps_ref.at[0]
    wide[0:8] = jnp.zeros((8, wide.shape[1]), F32)
    wide[8:] = p_ref[...].astype(F32)
    dm[...] = jnp.zeros(dm.shape, F32)
    for tile in range(tiles):
        rows = slice(tile * TILE, (tile + 1) * TILE)

        @pl.when(tile * TILE < length)
        def _():
            mixed = convolve(wide, taps, tile).astype(BF16)
            q_sc[rows] = mixed[:, :WIDE] * (1.0 / math.sqrt(HEAD))
            k_sc[rows] = mixed[:, WIDE : 2 * WIDE]
            v_sc[rows] = mixed[:, 2 * WIDE :]
            kt_sc[tile] = mixed[:, WIDE : 2 * WIDE].astype(F32).T.astype(BF16)

    lane = lax.broadcasted_iota(jnp.int32, (8, WIDE), 1)
    row = lax.broadcasted_iota(jnp.int32, (8, WIDE), 0)
    picks = jnp.where((lane < HEAD) == (row == 0), 1.0, 0.0).astype(BF16)

    def query_tile(index, carry):
        here = tile_rows(index)
        q_stack = stack_heads(q_sc[here])
        d_rows = do_ref[here]
        d_stack = stack_heads(d_rows)
        product = d_rows.astype(F32) * o_ref[here].astype(F32)
        upper = product.astype(BF16)
        lower = (product - upper.astype(F32)).astype(BF16)
        sums = mm_nt(picks, upper) + mm_nt(picks, lower)
        delta = jnp.concatenate([sums[0:1], sums[1:2]], axis=1)
        lse = lse_ref[pl.ds(index, 1)]
        dqt[...] = jnp.zeros(dqt.shape, F32)

        def visit(key_tile, masked):
            there = tile_rows(key_tile)
            scores = mm_nt(k_sc[there], q_stack)
            probs = jnp.exp(scores - lse)
            if masked:
                probs = jnp.where(allowed_keys(key_tile, index, length), probs, 0.0)
            d_probs = mm_nt(v_sc[there], d_stack)
            d_scores = (probs * (d_probs - delta)).astype(BF16)
            dm[there, 2 * WIDE :] += mm(probs.astype(BF16), d_stack)
            dm[there, WIDE : 2 * WIDE] += mm(d_scores, q_stack)
            dqt[...] += mm(kt_sc[key_tile], d_scores)

        over_key_tiles(index, length, visit)
        dm[here, :WIDE] = unstack_heads(dqt[...].T) * (1.0 / math.sqrt(HEAD))
        return carry

    lax.fori_loop(0, (length + TILE - 1) // TILE, query_tile, 0)
    gt_ref[...] = jnp.zeros(gt_ref.shape, F32)
    for tile in range(tiles):
        begin = tile * TILE
        total = taps[0:1] * dm[begin : begin + TILE]
        total += taps[1:2] * dm[begin + 1 : begin + 1 + TILE]
        total += taps[2:3] * dm[begin + 2 : begin + 2 + TILE]
        dp_ref[begin : begin + TILE] = total.astype(BF16)
        for tap in range(3):
            behind = wide[begin + 8 - tap : begin + 8 - tap + TILE]
            gt_ref[tap : tap + 1] += jnp.sum(
                dm[begin : begin + TILE] * behind, axis=0, keepdims=True
            )


def attend_back(info, proj, taps, attended, d_attended, lse):
    slots, rows = proj.shape[:2]
    tiles = rows // TILE
    own = lambda i, info: (i, 0, 0)
    return pl.pallas_call(
        attend_back_kernel,
        grid_spec=pltpu.PrefetchScalarGridSpec(
            num_scalar_prefetch=1,
            grid=(slots,),
            in_specs=[
                pl.BlockSpec((1, rows, 3 * WIDE), own),
                pl.BlockSpec((1, 3, 3 * WIDE), lambda i, info: (info[i, 1], 0, 0)),
                pl.BlockSpec((1, rows, WIDE), own),
                pl.BlockSpec((1, rows, WIDE), own),
                pl.BlockSpec((1, tiles, 2 * TILE), own),
            ],
            out_specs=[
                pl.BlockSpec((1, rows, 3 * WIDE), own),
                pl.BlockSpec((1, 8, 3 * WIDE), own),
            ],
            scratch_shapes=[
                pltpu.VMEM((rows + 8, 3 * WIDE), F32),
                pltpu.VMEM((rows, WIDE), BF16),
                pltpu.VMEM((rows, WIDE), BF16),
                pltpu.VMEM((rows, WIDE), BF16),
                pltpu.VMEM((tiles, WIDE, TILE), BF16),
                pltpu.VMEM((rows + 8, 3 * WIDE), F32),
                pltpu.VMEM((WIDE, 2 * TILE), F32),
            ],
        ),
        out_shape=[
            jax.ShapeDtypeStruct((slots, rows, 3 * WIDE), BF16),
            jax.ShapeDtypeStruct((slots, 8, 3 * WIDE), F32),
        ],
        compiler_params=params(48),
        name="attend_back",
    )(info, proj, taps, attended, d_attended, lse)


def dense_kernel(
    x_ref, att_ref, cot_ref, weight_ref, gain_ref, wo_ref, wu_ref, wd_ref,
    out_ref, dh_ref, datt_ref, n2_ref, sq_ref, du_ref, da_ref, cz_ref, gain_grad_ref, stats_ref,
    act_sc, att_sc,
):
    rows, width = x_ref.shape[1:]
    hidden_units = wu_ref.shape[1]
    step = width
    for pair in range(PAIRS):
        att_sc[:, pair * WIDE : (pair + 1) * WIDE] = att_ref[pair]
    weight = weight_ref[0]
    gain = gain_ref[...].astype(F32)
    branch = mm(att_sc[...], wo_ref[...])
    hidden = x_ref[0].astype(F32) + branch
    factor = lax.rsqrt(jnp.mean(hidden * hidden, axis=-1, keepdims=True) + 1e-06)
    normed = (hidden * factor * gain).astype(BF16)
    n2_ref[0] = normed
    total = jnp.zeros((rows, width), F32)
    for begin in range(0, hidden_units, step):
        cols = slice(begin, begin + step)
        active = jnp.maximum(mm(normed, wu_ref[:, cols]), 0.0)
        act_sc[:, cols] = active
        squared = (active * active).astype(BF16)
        sq_ref[0, :, cols] = squared
        total += mm(squared, wd_ref[cols])
    full = hidden + total
    out_ref[0] = full.astype(BF16)

    def masked(values):
        per_row = jnp.sum(values * values, axis=-1, keepdims=True)
        return jnp.sum(weight * per_row, axis=0, keepdims=True)

    @pl.when(pl.program_id(0) == 0)
    def _():
        stats_ref[...] = jnp.zeros(stats_ref.shape, F32)
        gain_grad_ref[...] = jnp.zeros(gain_grad_ref.shape, F32)

    parts = [masked(full), masked(branch), masked(total), jnp.sum(weight, axis=0, keepdims=True)]
    for place, part in enumerate(parts):
        stats_ref[place : place + 1] += jnp.broadcast_to(part, (1, WIDE))
    cotangent = (cot_ref[0].astype(F32) * weight).astype(BF16)
    cz_ref[0] = cotangent
    d_normed = jnp.zeros((rows, width), F32)
    for begin in range(0, hidden_units, step):
        cols = slice(begin, begin + step)
        d_squared = mm_nt(cotangent, wd_ref[cols])
        d_up = (2.0 * act_sc[:, cols] * d_squared).astype(BF16)
        du_ref[0, :, cols] = d_up
        d_normed += mm_nt(d_up, wu_ref[:, cols])
    weighted = d_normed * gain
    inner = jnp.mean(weighted * hidden, axis=-1, keepdims=True)
    d_hidden = cotangent.astype(F32) + factor * weighted - hidden * (factor * factor * factor) * inner
    gain_grad_ref[...] += jnp.sum(d_normed * hidden * factor, axis=0, keepdims=True)
    dh_ref[0] = d_hidden
    d_attn = d_hidden.astype(BF16)
    da_ref[0] = d_attn
    d_att = mm_nt(d_attn, wo_ref[...]).astype(BF16)
    for pair in range(PAIRS):
        datt_ref[pair] = d_att[:, pair * WIDE : (pair + 1) * WIDE]


def dense_send_kernel(
    x_ref, units_ref, cot_ref, weight_ref, gain_ref, wo_ref, wu_ref, wd_ref,
    out_ref, dh_ref, inbox, att_ref, n2_ref, sq_ref, du_ref, da_ref, cz_ref, gain_grad_ref, stats_ref,
    act_sc, att_sc, att_in, d_blocks, in_s, in_r, out_s, out_r,
):
    group = pl.program_id(0)
    in_sems, out_sems = (in_s, in_r), (out_s, out_r)
    slots = units_ref.shape[0]

    @pl.when(group == 0)
    def _():
        meet_group()
        for slot in range(slots):
            send_blocks(units_ref, att_in, in_sems, slot)

    for slot in range(slots):
        first = slot * GROUP // PAIRS
        pl.when(group == first)(lambda slot=slot: wait_blocks(units_ref, att_in, in_sems, slot))
    here = pl.ds(group * PAIRS, PAIRS)
    att_ref[...] = att_in[here]
    dense_kernel(
        x_ref, att_in.at[here], cot_ref, weight_ref, gain_ref, wo_ref, wu_ref, wd_ref,
        out_ref, dh_ref, d_blocks.at[here], n2_ref, sq_ref, du_ref, da_ref, cz_ref, gain_grad_ref,
        stats_ref, act_sc, att_sc,
    )
    for pair in range(PAIRS):
        send_unit(d_blocks, inbox, out_sems, group * PAIRS + pair)
    pl.when(group == pl.num_programs(0) - 1)(lambda: wait_units(d_blocks, inbox, out_sems))


def dense_send(x, units, grad_output, weight, gain, w_out, w_up, w_down):
    groups, rows, width = x.shape
    hidden_units = w_up.shape[1]
    slots = groups * PAIRS // GROUP
    per_group = lambda s: (s, 0, 0)
    fixed = lambda s: (0, 0)
    once = pl.Buffered(1)
    anywhere = pl.BlockSpec(memory_space=pl.ANY)
    row_block = pl.BlockSpec((1, rows, width), per_group)
    wide_block = pl.BlockSpec((1, rows, hidden_units), per_group)
    low = jax.ShapeDtypeStruct(x.shape, BF16)
    wide_low = jax.ShapeDtypeStruct((groups, rows, hidden_units), BF16)
    unit_rows = (groups * PAIRS, rows, WIDE)
    return pl.pallas_call(
        dense_send_kernel,
        grid=(groups,),
        in_specs=[
            row_block,
            anywhere,
            row_block,
            pl.BlockSpec((1, rows, 1), per_group),
            pl.BlockSpec((1, width), fixed),
            pl.BlockSpec(w_out.shape, fixed, pipeline_mode=once),
            pl.BlockSpec(w_up.shape, fixed, pipeline_mode=once),
            pl.BlockSpec(w_down.shape, fixed, pipeline_mode=once),
        ],
        out_specs=[
            row_block,
            row_block,
            anywhere,
            pl.BlockSpec((PAIRS, rows, WIDE), per_group),
            row_block,
            wide_block,
            wide_block,
            row_block,
            row_block,
            pl.BlockSpec((1, width), fixed),
            pl.BlockSpec((8, WIDE), fixed),
        ],
        out_shape=[
            low,
            jax.ShapeDtypeStruct(x.shape, F32),
            jax.ShapeDtypeStruct((slots, GROUP, rows, WIDE), BF16),
            jax.ShapeDtypeStruct(unit_rows, BF16),
            low,
            wide_low,
            wide_low,
            low,
            low,
            jax.ShapeDtypeStruct((1, width), F32),
            jax.ShapeDtypeStruct((8, WIDE), F32),
        ],
        scratch_shapes=[
            pltpu.VMEM((rows, hidden_units), F32),
            pltpu.VMEM((rows, width), BF16),
            pltpu.VMEM(unit_rows, BF16),
            pltpu.VMEM(unit_rows, BF16),
            DMA((slots, GROUP)),
            DMA((slots, GROUP)),
            DMA((groups * PAIRS,)),
            DMA((slots, GROUP)),
        ],
        compiler_params=group_params(2, 58),
        name="dense_send",
    )(x, units, grad_output, weight, gain.reshape(1, width), w_out, w_up, w_down)


def dense(x, attended, grad_output, weight, gain, w_out, w_up, w_down):
    groups, rows, width = x.shape
    hidden_units = w_up.shape[1]
    per_group = lambda s: (s, 0, 0)
    fixed = lambda s: (0, 0)
    once = pl.Buffered(1)
    row_block = pl.BlockSpec((1, rows, width), per_group)
    wide_block = pl.BlockSpec((1, rows, hidden_units), per_group)
    unit_block = pl.BlockSpec((PAIRS, rows, WIDE), per_group)
    low = jax.ShapeDtypeStruct(x.shape, BF16)
    wide_low = jax.ShapeDtypeStruct((groups, rows, hidden_units), BF16)
    return pl.pallas_call(
        dense_kernel,
        grid=(groups,),
        in_specs=[
            row_block,
            unit_block,
            row_block,
            pl.BlockSpec((1, rows, 1), per_group),
            pl.BlockSpec((1, width), fixed),
            pl.BlockSpec(w_out.shape, fixed, pipeline_mode=once),
            pl.BlockSpec(w_up.shape, fixed, pipeline_mode=once),
            pl.BlockSpec(w_down.shape, fixed, pipeline_mode=once),
        ],
        out_specs=[
            row_block,
            row_block,
            unit_block,
            row_block,
            wide_block,
            wide_block,
            row_block,
            row_block,
            pl.BlockSpec((1, width), fixed),
            pl.BlockSpec((8, WIDE), fixed),
        ],
        out_shape=[
            low,
            jax.ShapeDtypeStruct(x.shape, F32),
            jax.ShapeDtypeStruct((groups * PAIRS, rows, WIDE), BF16),
            low,
            wide_low,
            wide_low,
            low,
            low,
            jax.ShapeDtypeStruct((1, width), F32),
            jax.ShapeDtypeStruct((8, WIDE), F32),
        ],
        scratch_shapes=[pltpu.VMEM((rows, hidden_units), F32), pltpu.VMEM((rows, width), BF16)],
        compiler_params=params(58),
        name="dense",
    )(x, attended, grad_output, weight, gain.reshape(1, width), w_out, w_up, w_down)


PART = 384


def feed_grads_kernel(sq_ref, cz_ref, n2_ref, du_ref, att_ref, da_ref, out_ref, n2_t):
    half, sub = pl.program_id(0), pl.program_id(1)
    groups, rows, width = n2_ref.shape
    tokens = groups * rows

    @pl.when((half == 0) & (sub == 0))
    def _():
        for group in range(groups):
            n2_t[:, group * rows : (group + 1) * rows] = n2_ref[group].astype(F32).T.astype(BF16)

    down = mm_tn(sq_ref[...].reshape(tokens, PART), cz_ref[...].reshape(tokens, width))
    for place in range(4):
        for side in range(2):
            out_ref[place, pl.ds(sub, 1), side * 96 : side * 96 + 96] = down[
                place * 96 : (place + 1) * 96, side * PART : (side + 1) * PART
            ].astype(BF16)[None]
    up = mm(n2_t[...], du_ref[...].reshape(tokens, PART))
    out_ref[pl.ds(sub, 1), :, 192:384] = up.astype(BF16).reshape(1, 4, 192, PART)

    @pl.when(sub == 0)
    def _():
        for pair in range(PAIRS):
            block = mm_tn(
                att_ref[:, pair].reshape(tokens, WIDE), da_ref[...].reshape(tokens, PART)
            ).astype(BF16)
            for low in range(0, WIDE, 16):
                row = pair * WIDE + low
                batch, inner = row // 192, row % 192
                out_ref[inner // 48, batch, 384 + inner % 48 : 400 + inner % 48] = block[low : low + 16]


def feed_grads(squared, cotangent, normed2, d_up, attended, d_attn):
    groups, rows, width = normed2.shape
    whole = lambda h, b: (0, 0, 0)
    return pl.pallas_call(
        feed_grads_kernel,
        grid=(2, 4),
        in_specs=[
            pl.BlockSpec((groups, rows, PART), lambda h, b: (0, 0, 2 * b + h)),
            pl.BlockSpec((groups, rows, width), whole, pipeline_mode=pl.Buffered(1)),
            pl.BlockSpec((groups, rows, width), whole, pipeline_mode=pl.Buffered(1)),
            pl.BlockSpec((groups, rows, PART), lambda h, b: (0, 0, 4 * h + b)),
            pl.BlockSpec(
                (groups, PAIRS, rows, WIDE), lambda h, b: (0, 0, 0, 0), pipeline_mode=pl.Buffered(1)
            ),
            pl.BlockSpec((groups, rows, PART), lambda h, b: (0, 0, h)),
        ],
        out_specs=pl.BlockSpec((4, 4, 432, PART), lambda h, b: (h, 0, 0, 0)),
        out_shape=jax.ShapeDtypeStruct((8, 4, 432, PART), BF16),
        scratch_shapes=[pltpu.VMEM((width, groups * rows), BF16)],
        compiler_params=params(58),
        name="feed_grads",
    )(squared, cotangent, normed2, d_up, attended.reshape(groups, PAIRS, rows, WIDE), d_attn)


def input_grads_kernel(
    dp_ref, n1_ref, x_ref, dh_ref, w_ref, gain_ref, out_ref, gx_ref, gain_grad_ref, n1_t, total, w_sc
):
    pair = pl.program_id(0)
    groups, rows, width = n1_ref.shape
    tokens = groups * rows

    @pl.when(pair == 0)
    def _():
        for group in range(groups):
            n1_t[:, group * rows : (group + 1) * rows] = n1_ref[group].astype(F32).T.astype(BF16)
        total[...] = jnp.zeros(total.shape, F32)

    d_proj = dp_ref[...].reshape(tokens, 3 * WIDE)
    grad = mm(n1_t[...], d_proj).astype(BF16)
    for batch in range(4):
        for chip in range(4):
            begin = batch * 192 + chip * 48
            out_ref[0, 0, chip, batch] = grad[begin : begin + 48]
    for part in range(3):
        cols = pl.ds(pl.multiple_of(part * width + pair * WIDE, WIDE), WIDE)
        w_sc[:, part * WIDE : (part + 1) * WIDE] = w_ref[:, cols]
    total[...] += mm_nt(d_proj, w_sc[...])

    @pl.when(pair == PAIRS - 1)
    def _():
        gain = gain_ref[...].astype(F32)
        gain_sum = jnp.zeros((1, width), F32)
        for group in range(groups):
            x = x_ref[group].astype(F32)
            d_normed = total[group * rows : (group + 1) * rows]
            factor = lax.rsqrt(jnp.mean(x * x, axis=-1, keepdims=True) + 1e-06)
            weighted = d_normed * gain
            inner = jnp.mean(weighted * x, axis=-1, keepdims=True)
            gx_ref[group] = (
                dh_ref[group] + factor * weighted - x * (factor * factor * factor) * inner
            )
            gain_sum += jnp.sum(d_normed * x * factor, axis=0, keepdims=True)
        gain_grad_ref[...] = gain_sum


def input_grads(d_proj, normed1, x, d_hidden, w_qkv, gain):
    groups, rows, width = x.shape
    whole = lambda p: (0, 0, 0)
    once = pl.Buffered(1)
    tokens = pl.BlockSpec((groups, rows, width), whole, pipeline_mode=once)
    return pl.pallas_call(
        input_grads_kernel,
        grid=(PAIRS,),
        in_specs=[
            pl.BlockSpec((groups, 1, rows, 3 * WIDE), lambda p: (0, p, 0, 0)),
            tokens,
            tokens,
            tokens,
            pl.BlockSpec(w_qkv.shape, lambda p: (0, 0), pipeline_mode=once),
            pl.BlockSpec((1, width), lambda p: (0, 0)),
        ],
        out_specs=[
            pl.BlockSpec((1, 1, 4, 4, 48, PART), lambda p: (p % 3, p // 3, 0, 0, 0, 0)),
            tokens,
            pl.BlockSpec((1, width), lambda p: (0, 0)),
        ],
        out_shape=[
            jax.ShapeDtypeStruct((3, 2, 4, 4, 48, PART), BF16),
            jax.ShapeDtypeStruct(x.shape, F32),
            jax.ShapeDtypeStruct((1, width), F32),
        ],
        scratch_shapes=[
            pltpu.VMEM((width, groups * rows), BF16),
            pltpu.VMEM((groups * rows, width), F32),
            pltpu.VMEM((width, 3 * WIDE), BF16),
        ],
        compiler_params=params(58),
        name="input_grads",
    )(d_proj.reshape(groups, PAIRS, rows, 3 * WIDE), normed1, x, d_hidden, w_qkv, gain.reshape(1, width))


def sum_kernel(
    g_ref, feed_ref, small_ref, qkv_out, feed_out, small_out,
    core_in, here, chip_in, mine, z_in, qkv_all, feed_in, feed_all, row_in, row_sum, col_in,
    core_s, core_r, chip_s, chip_r, z_s, z_r, qkv_s, qkv_r, fz_s, fz_r, fa_s, fa_r,
    row_s, row_r, col_s, col_r,
):
    me = lax.axis_index("seq")
    z = lax.axis_index("batch")
    core, chip = lax.rem(me, 2), me // 2
    barrier = pltpu.get_barrier_semaphore()
    for bit in range(1, 8):
        pl.semaphore_signal(barrier, inc=1, device_id={"seq": me ^ bit}, device_id_type=MESH)
    for bit in range(1, 4):
        pl.semaphore_signal(barrier, inc=1, device_id={"batch": z ^ bit}, device_id_type=MESH)
    pl.semaphore_wait(barrier, 10)

    def send(source, target, sems, axis, peer):
        copy = pltpu.make_async_remote_copy(
            src_ref=source,
            dst_ref=target,
            send_sem=sems[0],
            recv_sem=sems[1],
            device_id={axis: peer},
            device_id_type=MESH,
        )
        copy.start()
        return copy

    def spread(ref, s, r):
        return [
            send(ref.at[me], ref.at[me], (s.at[step], r.at[step]), "seq", me ^ max(2 * step, 1))
            for step in range(4)
        ]

    def relay(ref, first, s, r):
        more = []
        for step in range(1, 4):
            first[step].wait()
            slot = me ^ (2 * step)
            more.append(
                send(ref.at[slot], ref.at[slot], (s.at[3 + step], r.at[3 + step]), "seq", me ^ 1)
            )
        return [first[0]] + more

    chunks = g_ref.shape[0]
    rows = feed_ref.shape[1] // chunks
    to_core = [
        send(g_ref.at[c, 1 - core], core_in.at[c], (core_s.at[c], core_r.at[c]), "seq", me ^ 1)
        for c in range(chunks)
    ]
    feed_z = [
        [
            send(
                feed_ref.at[z ^ bit, c * rows : (c + 1) * rows],
                feed_in.at[c, bit - 1],
                (fz_s.at[c, bit - 1], fz_r.at[c, bit - 1]),
                "batch",
                z ^ bit,
            )
            for bit in range(1, 4)
        ]
        for c in range(chunks)
    ]
    row_in[pl.ds(me, 1)] = small_ref[...][None]
    rows_out = [
        send(small_ref, row_in.at[me], (row_s.at[bit - 1], row_r.at[bit - 1]), "seq", me ^ bit)
        for bit in range(1, 8)
    ]
    to_chip = []
    for c in range(chunks):
        to_core[c].wait()
        for q in range(4):
            both = g_ref[c, core, q].astype(F32) + core_in[c, q].astype(F32)
            here[c, q] = both.astype(BF16)
        to_chip.append(
            [
                send(
                    here.at[c, chip ^ bit],
                    chip_in.at[c, bit - 1],
                    (chip_s.at[c, bit - 1], chip_r.at[c, bit - 1]),
                    "seq",
                    me ^ (2 * bit),
                )
                for bit in range(1, 4)
            ]
        )
    for copy in rows_out:
        copy.wait()
    total = row_in[0]
    for place in range(1, 8):
        total = total + row_in[place]
    row_sum[...] = total
    col_in[pl.ds(z, 1)] = total[None]
    cols_out = [
        send(row_sum, col_in.at[z], (col_s.at[bit - 1], col_r.at[bit - 1]), "batch", z ^ bit)
        for bit in range(1, 4)
    ]
    to_z = []
    for c in range(chunks):
        for copy in to_chip[c]:
            copy.wait()
        both = here[c, chip].astype(F32)
        for bit in range(3):
            both = both + chip_in[c, bit].astype(F32)
        mine[c] = both.astype(BF16)
        to_z.append(
            [
                send(
                    mine.at[c, z ^ bit],
                    z_in.at[c, bit - 1],
                    (z_s.at[c, bit - 1], z_r.at[c, bit - 1]),
                    "batch",
                    z ^ bit,
                )
                for bit in range(1, 4)
            ]
        )
    feed_first = []
    for c in range(chunks):
        for copy in feed_z[c]:
            copy.wait()
        both = feed_ref[z, c * rows : (c + 1) * rows].astype(F32)
        for bit in range(3):
            both = both + feed_in[c, bit].astype(F32)
        feed_all[c, pl.ds(me, 1)] = both.astype(BF16)[None]
        feed_first.append(spread(feed_all.at[c], fa_s.at[c], fa_r.at[c]))
    qkv_first = []
    for c in range(chunks):
        for copy in to_z[c]:
            copy.wait()
        both = mine[c, z].astype(F32)
        for bit in range(3):
            both = both + z_in[c, bit].astype(F32)
        qkv_all[c, pl.ds(me, 1)] = both.astype(BF16)[None]
        qkv_first.append(spread(qkv_all.at[c], qkv_s.at[c], qkv_r.at[c]))
    last = []
    for c in range(chunks):
        last += relay(feed_all.at[c], feed_first[c], fa_s.at[c], fa_r.at[c])
    for c in range(chunks):
        last += relay(qkv_all.at[c], qkv_first[c], qkv_s.at[c], qkv_r.at[c])
    for copy in cols_out:
        copy.wait()
    small_out[...] = ((col_in[0] + col_in[1]) + col_in[2]) + col_in[3]
    for copy in last:
        copy.wait()
    qkv_out[...] = qkv_all[...]
    feed_out[...] = feed_all[...]


def sum_over_devices(pieces, feed, small):
    chunks, rows = pieces.shape[0], pieces.shape[4]
    feed_rows = feed.shape[1] // chunks
    vmem = pl.BlockSpec(memory_space=pltpu.VMEM)
    dma = pltpu.SemaphoreType.DMA
    pairs = []
    for shape in [(), (3,), (3,), (7,), (3,), (7,)]:
        pairs += [dma((chunks,) + shape), dma((chunks,) + shape)]
    return pl.pallas_call(
        sum_kernel,
        in_specs=[vmem, vmem, vmem],
        out_specs=[vmem, vmem, vmem],
        out_shape=[
            jax.ShapeDtypeStruct((chunks, 8, rows, PART), BF16),
            jax.ShapeDtypeStruct((chunks, 8, feed_rows, PART), BF16),
            jax.ShapeDtypeStruct(small.shape, F32),
        ],
        scratch_shapes=[
            pltpu.VMEM((chunks, 4, 4, rows, PART), BF16),
            pltpu.VMEM((chunks, 4, 4, rows, PART), BF16),
            pltpu.VMEM((chunks, 3, 4, rows, PART), BF16),
            pltpu.VMEM((chunks, 4, rows, PART), BF16),
            pltpu.VMEM((chunks, 3, rows, PART), BF16),
            pltpu.VMEM((chunks, 8, rows, PART), BF16),
            pltpu.VMEM((chunks, 3, feed_rows, PART), BF16),
            pltpu.VMEM((chunks, 8, feed_rows, PART), BF16),
            pltpu.VMEM((8,) + small.shape, F32),
            pltpu.VMEM(small.shape, F32),
            pltpu.VMEM((4,) + small.shape, F32),
        ]
        + pairs
        + [dma((7,)), dma((7,)), dma((3,)), dma((3,))],
        compiler_params=pltpu.CompilerParams(
            collective_id=0, has_side_effects=True, vmem_limit_bytes=56 << 20
        ),
        name="sum_over_devices",
    )(pieces, feed, small)


def unpack_kernel(feed_ref, qkv_ref, down_ref, up_ref, out_ref, grad_ref):
    down_ref[:, :PART] = feed_ref[0, 0, :96].astype(F32)
    down_ref[:48, PART:] = feed_ref[0, 0, 96:].astype(F32)
    down_ref[48:, PART:] = feed_ref[1, 0, :48].astype(F32)
    up_ref[:96] = feed_ref[1, 0, 48:].astype(F32)
    up_ref[96:] = feed_ref[2, 0, :96].astype(F32)
    out_ref[...] = feed_ref[2, 0, 96:].astype(F32)
    place = pl.program_id(0)

    def put(core):
        for c in range(3):
            for part in range(3):
                begin = part * PAIRS * WIDE + (core * 3 + c) * WIDE
                grad_ref[:, begin : begin + WIDE] = qkv_ref[
                    c, 0, :, part * WIDE : (part + 1) * WIDE
                ].astype(F32)

    for core in range(2):
        pl.when(place % 2 == core)(functools.partial(put, core))


def unpack(feed, qkv):
    return pl.pallas_call(
        unpack_kernel,
        grid=(8,),
        in_specs=[
            pl.BlockSpec((3, 1, 144, PART), lambda r: (0, r, 0, 0)),
            pl.BlockSpec((3, 1, 48, PART), lambda r: (0, r, 0, 0)),
        ],
        out_specs=[
            pl.BlockSpec((96, 2 * PART), lambda r: (r, 0)),
            pl.BlockSpec((192, PART), lambda r: (0, r)),
            pl.BlockSpec((48, PART), lambda r: (r % 4, r // 4)),
            pl.BlockSpec((48, 3 * PAIRS * WIDE), lambda r: (r // 2, 0)),
        ],
        out_shape=[
            jax.ShapeDtypeStruct((768, 2 * PART), F32),
            jax.ShapeDtypeStruct((192, 8 * PART), F32),
            jax.ShapeDtypeStruct((192, 2 * PART), F32),
            jax.ShapeDtypeStruct((192, 3 * PAIRS * WIDE), F32),
        ],
        compiler_params=params(32),
        name="unpack",
    )(feed, qkv)


def exchange(blocks):
    return lax.all_to_all(blocks, "seq", 0, 0, tiled=True)


def plain_gradients(feed, qkv):
    down = feed[:, :, :192].reshape(8, 4, 2, 96, PART).transpose(1, 0, 3, 2, 4)
    up = feed[:, :, 192:384].transpose(1, 2, 0, 3)
    out = feed[:, :, 384:].reshape(2, 4, 4, 48, PART).transpose(2, 1, 3, 0, 4)
    grad = qkv.reshape(3, 2, 4, 4, 48, 3, WIDE).transpose(3, 2, 4, 5, 1, 0, 6)
    return (
        down.reshape(3072, 768),
        up.reshape(768, 3072),
        out.reshape(768, 768),
        grad.reshape(768, 2304),
    )


def shards(
    stream_in,
    lengths,
    token_mask,
    norm1_gain,
    w_qkv,
    conv_taps,
    w_out,
    norm2_gain,
    w_up,
    w_down,
    grad_output,
):
    groups, block_len, width = stream_in.shape
    count = lax.axis_size("seq")
    batches = lax.axis_size("batch")
    place = lax.axis_index("seq")
    units = groups * PAIRS
    slots = -(-units // count)
    spare = slots * count - units
    offset = place * block_len
    taps = conv_taps.astype(F32).reshape(3, 3, PAIRS, WIDE).transpose(2, 0, 1, 3)
    taps = taps.reshape(PAIRS, 3, 3 * WIDE)

    fitted = count == GROUP and batches == 4 and units % GROUP == 0

    def to_heads(blocks):
        blocks = jnp.pad(blocks, ((0, spare), (0, 0), (0, 0)))
        blocks = blocks.reshape((slots, count) + blocks.shape[1:])
        return jnp.stack([exchange(blocks[slot]) for slot in range(slots)])

    def to_tokens(rows):
        rows = rows.reshape(slots, count, block_len, rows.shape[2])
        return jnp.concatenate([exchange(rows[slot]) for slot in range(slots)])[:units]

    unit = jnp.arange(slots) * count + place
    sequence = jnp.minimum(unit // PAIRS, groups - 1)
    info = jnp.stack([jnp.where(unit < units, lengths[sequence], 0), unit % PAIRS], axis=1)
    info = info.astype(jnp.int32)

    if fitted:
        normed1, proj = project_send(stream_in, norm1_gain, w_qkv)
    else:
        normed1, proj = project(stream_in, norm1_gain, w_qkv)
        proj = to_heads(proj)
    proj = proj.reshape(slots, count * block_len, 3 * WIDE)
    unit_out, unit_lse = attend(info, proj, taps)

    positions = offset + jnp.arange(block_len, dtype=jnp.int32)
    inside = (positions[None, :] < lengths[:, None]).astype(F32)
    stat_weight = (token_mask.astype(F32) * inside)[..., None]
    rest = (grad_output, stat_weight, norm2_gain, w_out, w_up, w_down)
    if fitted:
        blocks = unit_out.reshape(slots, count, block_len, WIDE)
        stream_out, d_hidden, d_units, attended, *saved = dense_send(stream_in, blocks, *rest)
    else:
        attended = to_tokens(unit_out)
        stream_out, d_hidden, d_units, *saved = dense(stream_in, attended, *rest)
        d_units = to_heads(d_units)
    normed2, squared, d_up, d_attn, cotangent, grad_norm2, local_stats = saved
    d_units = d_units.reshape(slots, count * block_len, WIDE)
    feed = feed_grads(squared, cotangent, normed2, d_up, attended, d_attn)
    if fitted:
        feed = lax.psum_scatter(feed, "seq", scatter_dimension=0, tiled=False)

    back, parts = attend_back(info, proj, taps, unit_out, d_units, unit_lse)
    unit_taps = jnp.zeros((PAIRS, 3, 3 * WIDE), F32)
    for slot in range(slots):
        chosen = jnp.arange(PAIRS)[:, None, None] == info[slot, 1]
        unit_taps = unit_taps + jnp.where(chosen, parts[slot, None, :3], 0.0)
    grad_taps = unit_taps.reshape(PAIRS, 3, 3, WIDE).transpose(1, 2, 0, 3).reshape(9, width)
    d_proj = to_tokens(back)
    pieces, grad_input, grad_norm1 = input_grads(
        d_proj, normed1, stream_in, d_hidden, w_qkv, norm1_gain
    )
    stats_row = jnp.pad(local_stats[:4, 0], (0, width - 4)).reshape(1, width)
    small = jnp.concatenate(
        [grad_taps, grad_norm1, grad_norm2, stats_row, jnp.zeros((4, width), F32)], axis=0
    )
    if fitted:
        qkv, feed, small = sum_over_devices(pieces, feed, small)
        total_down, total_up, total_wout, total_qkv = unpack(feed, qkv)
    else:

        def reduce(gradient):
            share = lax.psum_scatter(
                gradient, ("batch", "seq"), scatter_dimension=0, tiled=True
            )
            return lax.all_gather(share, "seq", axis=0, tiled=True).astype(F32)

        total_down, total_up, total_wout, total_qkv = map(reduce, plain_gradients(feed, pieces))
        small = lax.psum(small, ("seq", "batch"))
    share = width // batches
    begin = lax.axis_index("batch") * share
    block_rms = jnp.sqrt(small[11, :3] / (width * small[11, 3]))
    return (
        stream_out,
        grad_input,
        lax.dynamic_slice_in_dim(small[9], begin, share),
        total_qkv,
        small[:9].reshape(3, 3 * width),
        total_wout,
        lax.dynamic_slice_in_dim(small[10], begin, share),
        total_up,
        total_down,
        block_rms,
    )


def solution(mesh):
    tokens = P("batch", "seq", None)
    return jax.shard_map(
        shards,
        mesh=mesh,
        in_specs=(
            tokens,
            P("batch"),
            P("batch", "seq"),
            P(),
            P(),
            P(),
            P(),
            P(),
            P(),
            P(),
            tokens,
        ),
        out_specs=(
            tokens,
            tokens,
            P("batch"),
            P("batch", None),
            P(),
            P("batch", None),
            P("batch"),
            P("batch", None),
            P("batch", None),
            P(),
        ),
        check_vma=False,
    )
```

```python
import functools
import math

import jax
import jax.numpy as jnp
from jax import lax
from jax.experimental import pallas as pl
from jax.experimental.pallas import tpu as pltpu
from jax.sharding import PartitionSpec as P

HEADS = 12
HEAD = 64
PAIRS = HEADS // 2
WIDE = 2 * HEAD
TILE = 256
NEG = -1e30
F32 = jnp.float32
BF16 = jnp.bfloat16


def mm(left_op, right_op):
    return jnp.dot(left_op, right_op, preferred_element_type=F32)


def mm_nt(left_op, right_op):
    return lax.dot_general(
        left_op, right_op, (((1,), (1,)), ((), ())), preferred_element_type=F32
    )


def mm_tn(left_op, right_op):
    return lax.dot_general(
        left_op, right_op, (((0,), (0,)), ((), ())), preferred_element_type=F32
    )


def params(limit):
    return pltpu.CompilerParams(vmem_limit_bytes=limit << 20)


MESH = pl.DeviceIdType.MESH
GROUP = 8
DMA = pltpu.SemaphoreType.DMA


def remote(source, target, sems, axis, peer):
    return pltpu.make_async_remote_copy(
        src_ref=source,
        dst_ref=target,
        send_sem=sems[0],
        recv_sem=sems[1],
        device_id={axis: peer},
        device_id_type=MESH,
    )


def meet_group():
    me = lax.axis_index("seq")
    barrier = pltpu.get_barrier_semaphore()
    for bit in range(1, GROUP):
        pl.semaphore_signal(barrier, inc=1, device_id={"seq": me ^ bit}, device_id_type=MESH)
    pl.semaphore_wait(barrier, GROUP - 1)


def unit_copy(blocks, inbox, sems, unit):
    me = lax.axis_index("seq")
    owner, slot = lax.rem(unit, GROUP), unit // GROUP
    return owner, remote(
        blocks.at[unit],
        inbox.at[slot, me],
        (sems[0].at[unit], sems[1].at[slot, me ^ owner]),
        "seq",
        owner,
    )


def send_unit(blocks, inbox, sems, unit):
    me = lax.axis_index("seq")
    owner, copy = unit_copy(blocks, inbox, sems, unit)

    @pl.when(owner != me)
    def _():
        copy.start()

    @pl.when(owner == me)
    def _():
        slot = unit // GROUP
        pltpu.make_async_copy(blocks.at[unit], inbox.at[slot, me], sems[1].at[slot, 0]).start()


def wait_units(blocks, inbox, sems):
    me = lax.axis_index("seq")
    units = blocks.shape[0]
    for slot in range(units // GROUP):
        unit = slot * GROUP + me
        pltpu.make_async_copy(blocks.at[unit], inbox.at[slot, me], sems[1].at[slot, 0]).wait()
        for bit in range(1, GROUP):
            remote(
                blocks.at[unit],
                inbox.at[slot, me ^ bit],
                (sems[0].at[unit], sems[1].at[slot, bit]),
                "seq",
                me ^ bit,
            ).wait_recv()
    for unit in range(units):
        owner, copy = unit_copy(blocks, inbox, sems, unit)
        pl.when(owner != me)(copy.wait_send)


def block_copies(units, inbox, sems, slot):
    me = lax.axis_index("seq")
    return [
        remote(
            units.at[slot, me ^ bit],
            inbox.at[slot * GROUP + me],
            (sems[0].at[slot, bit], sems[1].at[slot, bit]),
            "seq",
            me ^ bit,
        )
        for bit in range(1, GROUP)
    ]


def own_block(units, inbox, sems, slot):
    me = lax.axis_index("seq")
    return pltpu.make_async_copy(
        units.at[slot, me], inbox.at[slot * GROUP + me], sems[1].at[slot, 0]
    )


def send_blocks(units, inbox, sems, slot):
    own_block(units, inbox, sems, slot).start()
    for copy in block_copies(units, inbox, sems, slot):
        copy.start()


def wait_blocks(units, inbox, sems, slot):
    own_block(units, inbox, sems, slot).wait()
    for copy in block_copies(units, inbox, sems, slot):
        copy.wait()


def group_params(number, limit):
    return pltpu.CompilerParams(
        collective_id=number, has_side_effects=True, vmem_limit_bytes=limit << 20
    )


def project_kernel(x_ref, gain_ref, w_ref, n_ref, p_ref):
    x = x_ref[0].astype(F32)
    factor = lax.rsqrt(jnp.mean(x * x, axis=-1, keepdims=True) + 1e-06)
    normed = (x * factor * gain_ref[...].astype(F32)).astype(BF16)
    n_ref[0] = normed
    width = x.shape[1]
    for part in range(3):
        cols = mm(normed, w_ref[:, part * width : (part + 1) * width])
        for pair in range(PAIRS):
            p_ref[pair, :, part * WIDE : (part + 1) * WIDE] = cols[
                :, pair * WIDE : (pair + 1) * WIDE
            ].astype(BF16)


def project_send_kernel(x_ref, gain_ref, w_ref, n_ref, inbox, blocks, send_sems, recv_sems):
    group = pl.program_id(0)
    sems = (send_sems, recv_sems)
    pl.when(group == 0)(meet_group)
    project_kernel(x_ref, gain_ref, w_ref, n_ref, blocks.at[pl.ds(group * PAIRS, PAIRS)])
    for pair in range(PAIRS):
        send_unit(blocks, inbox, sems, group * PAIRS + pair)
    pl.when(group == pl.num_programs(0) - 1)(lambda: wait_units(blocks, inbox, sems))


def project_send(x, gain, w_qkv):
    groups, rows, width = x.shape
    slots = groups * PAIRS // GROUP
    return pl.pallas_call(
        project_send_kernel,
        grid=(groups,),
        in_specs=[
            pl.BlockSpec((1, rows, width), lambda s: (s, 0, 0)),
            pl.BlockSpec((1, width), lambda s: (0, 0)),
            pl.BlockSpec(w_qkv.shape, lambda s: (0, 0), pipeline_mode=pl.Buffered(1)),
        ],
        out_specs=[
            pl.BlockSpec((1, rows, width), lambda s: (s, 0, 0)),
            pl.BlockSpec(memory_space=pl.ANY),
        ],
        out_shape=[
            jax.ShapeDtypeStruct(x.shape, BF16),
            jax.ShapeDtypeStruct((slots, GROUP, rows, 3 * WIDE), BF16),
        ],
        scratch_shapes=[
            pltpu.VMEM((groups * PAIRS, rows, 3 * WIDE), BF16),
            DMA((groups * PAIRS,)),
            DMA((slots, GROUP)),
        ],
        compiler_params=group_params(1, 40),
        name="project_send",
    )(x, gain.reshape(1, width), w_qkv)


def project(x, gain, w_qkv):
    groups, rows, width = x.shape
    return pl.pallas_call(
        project_kernel,
        grid=(groups,),
        in_specs=[
            pl.BlockSpec((1, rows, width), lambda s: (s, 0, 0)),
            pl.BlockSpec((1, width), lambda s: (0, 0)),
            pl.BlockSpec(w_qkv.shape, lambda s: (0, 0)),
        ],
        out_specs=[
            pl.BlockSpec((1, rows, width), lambda s: (s, 0, 0)),
            pl.BlockSpec((PAIRS, rows, 3 * WIDE), lambda s: (s, 0, 0)),
        ],
        out_shape=[
            jax.ShapeDtypeStruct(x.shape, BF16),
            jax.ShapeDtypeStruct((groups * PAIRS, rows, 3 * WIDE), BF16),
        ],
        compiler_params=params(40),
        name="project",
    )(x, gain.reshape(1, width), w_qkv)


def stack_heads(rows):
    lane = lax.broadcasted_iota(jnp.int32, rows.shape, 1)
    zero = jnp.zeros_like(rows)
    first = jnp.where(lane < HEAD, rows, zero)
    second = jnp.where(lane < HEAD, zero, rows)
    return jnp.concatenate([first, second], axis=0)


def unstack_heads(rows):
    half = rows.shape[0] // 2
    lane = lax.broadcasted_iota(jnp.int32, (half, rows.shape[1]), 1)
    return jnp.where(lane < HEAD, rows[:half], rows[half:])


def tile_rows(index):
    return pl.ds(pl.multiple_of(index * TILE, TILE), TILE)


def allowed_keys(key_tile, query_tile, length):
    shape = (TILE, 2 * TILE)
    k_pos = key_tile * TILE + lax.broadcasted_iota(jnp.int32, shape, 0)
    q_pos = query_tile * TILE + (lax.broadcasted_iota(jnp.int32, shape, 1) & (TILE - 1))
    return (k_pos <= q_pos) & (k_pos < length)


def over_key_tiles(query_tile, length, visit):
    full = jnp.minimum(query_tile, length // TILE)
    last = jnp.minimum(query_tile + 1, (length + TILE - 1) // TILE)

    def plain(key_tile, carry):
        visit(key_tile, False)
        return carry

    def edge(key_tile, carry):
        visit(key_tile, True)
        return carry

    lax.fori_loop(0, full, plain, 0)
    lax.fori_loop(full, last, edge, 0)


def convolve(wide_ref, taps_ref, tile):
    begin = 8 + tile * TILE
    total = taps_ref[0:1] * wide_ref[begin : begin + TILE]
    total += taps_ref[1:2] * wide_ref[begin - 1 : begin - 1 + TILE]
    total += taps_ref[2:3] * wide_ref[begin - 2 : begin - 2 + TILE]
    return total


def attend_kernel(info, p_ref, taps_ref, o_ref, lse_ref, wide, q_sc, k_sc, vt_sc, m_sc, acc):
    p_ref, o_ref, lse_ref = p_ref.at[0], o_ref.at[0], lse_ref.at[0]
    length = info[pl.program_id(0), 0]
    tiles = p_ref.shape[0] // TILE
    taps = taps_ref.at[0]
    wide[0:8] = jnp.zeros((8, wide.shape[1]), F32)
    wide[8:] = p_ref[...].astype(F32)
    for tile in range(tiles):
        rows = slice(tile * TILE, (tile + 1) * TILE)
        mixed = convolve(wide, taps, tile).astype(BF16)
        q_sc[rows] = mixed[:, :WIDE] * (1.0 / math.sqrt(HEAD))
        k_sc[rows] = mixed[:, WIDE : 2 * WIDE]
        vt_sc[tile, :WIDE] = mixed[:, 2 * WIDE :].astype(F32).T.astype(BF16)
        vt_sc[tile, WIDE:] = jnp.ones((vt_sc.shape[1] - WIDE, TILE), BF16)

    def query_tile(index, carry):
        q_stack = stack_heads(q_sc[tile_rows(index)])
        m_sc[...] = jnp.full(m_sc.shape, NEG, F32)
        acc[...] = jnp.zeros(acc.shape, F32)

        def visit(key_tile, masked):
            scores = mm_nt(k_sc[tile_rows(key_tile)], q_stack)
            if masked:
                scores = jnp.where(allowed_keys(key_tile, index, length), scores, NEG)
            old = m_sc[...]
            new = jnp.maximum(old, jnp.max(scores, axis=0, keepdims=True))
            probs = jnp.exp(scores - new)
            acc[...] = acc[...] * jnp.exp(old - new) + mm(vt_sc[key_tile], probs.astype(BF16))
            m_sc[...] = new

        over_key_tiles(index, length, visit)
        total = acc[WIDE : WIDE + 1]
        out = (acc[:WIDE] / total).T
        o_ref[tile_rows(index)] = unstack_heads(out).astype(BF16)
        lse_ref[pl.ds(index, 1)] = m_sc[...] + jnp.log(total)
        return carry

    lax.fori_loop(0, tiles, query_tile, 0)


def attend(info, proj, taps):
    slots, rows = proj.shape[:2]
    tiles = rows // TILE
    own = lambda i, info: (i, 0, 0)
    return pl.pallas_call(
        attend_kernel,
        grid_spec=pltpu.PrefetchScalarGridSpec(
            num_scalar_prefetch=1,
            grid=(slots,),
            in_specs=[
                pl.BlockSpec((1, rows, 3 * WIDE), own),
                pl.BlockSpec((1, 3, 3 * WIDE), lambda i, info: (info[i, 1], 0, 0)),
            ],
            out_specs=[
                pl.BlockSpec((1, rows, WIDE), own),
                pl.BlockSpec((1, tiles, 2 * TILE), own),
            ],
            scratch_shapes=[
                pltpu.VMEM((rows + 8, 3 * WIDE), F32),
                pltpu.VMEM((rows, WIDE), BF16),
                pltpu.VMEM((rows, WIDE), BF16),
                pltpu.VMEM((tiles, WIDE + 16, TILE), BF16),
                pltpu.VMEM((1, 2 * TILE), F32),
                pltpu.VMEM((WIDE + 16, 2 * TILE), F32),
            ],
        ),
        out_shape=[
            jax.ShapeDtypeStruct((slots, rows, WIDE), BF16),
            jax.ShapeDtypeStruct((slots, tiles, 2 * TILE), F32),
        ],
        compiler_params=params(40),
        name="attend",
    )(info, proj, taps)


def attend_back_kernel(
    info, p_ref, taps_ref, o_ref, do_ref, lse_ref, dp_ref, gt_ref, wide, q_sc, k_sc, v_sc, kt_sc, dm, dqt
):
    p_ref, o_ref, do_ref, lse_ref = p_ref.at[0], o_ref.at[0], do_ref.at[0], lse_ref.at[0]
    dp_ref, gt_ref = dp_ref.at[0], gt_ref.at[0]
    length = info[pl.program_id(0), 0]
    tiles = p_ref.shape[0] // TILE
    taps = taps_ref.at[0]
    wide[0:8] = jnp.zeros((8, wide.shape[1]), F32)
    wide[8:] = p_ref[...].astype(F32)
    dm[...] = jnp.zeros(dm.shape, F32)
    for tile in range(tiles):
        rows = slice(tile * TILE, (tile + 1) * TILE)

        @pl.when(tile * TILE < length)
        def _():
            mixed = convolve(wide, taps, tile).astype(BF16)
            q_sc[rows] = mixed[:, :WIDE] * (1.0 / math.sqrt(HEAD))
            k_sc[rows] = mixed[:, WIDE : 2 * WIDE]
            v_sc[rows] = mixed[:, 2 * WIDE :]
            kt_sc[tile] = mixed[:, WIDE : 2 * WIDE].astype(F32).T.astype(BF16)

    lane = lax.broadcasted_iota(jnp.int32, (8, WIDE), 1)
    row = lax.broadcasted_iota(jnp.int32, (8, WIDE), 0)
    picks = jnp.where((lane < HEAD) == (row == 0), 1.0, 0.0).astype(BF16)

    def query_tile(index, carry):
        here = tile_rows(index)
        q_stack = stack_heads(q_sc[here])
        d_rows = do_ref[here]
        d_stack = stack_heads(d_rows)
        product = d_rows.astype(F32) * o_ref[here].astype(F32)
        upper = product.astype(BF16)
        lower = (product - upper.astype(F32)).astype(BF16)
        sums = mm_nt(picks, upper) + mm_nt(picks, lower)
        delta = jnp.concatenate([sums[0:1], sums[1:2]], axis=1)
        lse = lse_ref[pl.ds(index, 1)]
        dqt[...] = jnp.zeros(dqt.shape, F32)

        def visit(key_tile, masked):
            there = tile_rows(key_tile)
            scores = mm_nt(k_sc[there], q_stack)
            probs = jnp.exp(scores - lse)
            if masked:
                probs = jnp.where(allowed_keys(key_tile, index, length), probs, 0.0)
            d_probs = mm_nt(v_sc[there], d_stack)
            d_scores = (probs * (d_probs - delta)).astype(BF16)
            dm[there, 2 * WIDE :] += mm(probs.astype(BF16), d_stack)
            dm[there, WIDE : 2 * WIDE] += mm(d_scores, q_stack)
            dqt[...] += mm(kt_sc[key_tile], d_scores)

        over_key_tiles(index, length, visit)
        dm[here, :WIDE] = unstack_heads(dqt[...].T) * (1.0 / math.sqrt(HEAD))
        return carry

    lax.fori_loop(0, (length + TILE - 1) // TILE, query_tile, 0)
    gt_ref[...] = jnp.zeros(gt_ref.shape, F32)
    for tile in range(tiles):
        begin = tile * TILE
        total = taps[0:1] * dm[begin : begin + TILE]
        total += taps[1:2] * dm[begin + 1 : begin + 1 + TILE]
        total += taps[2:3] * dm[begin + 2 : begin + 2 + TILE]
        dp_ref[begin : begin + TILE] = total.astype(BF16)
        for tap in range(3):
            behind = wide[begin + 8 - tap : begin + 8 - tap + TILE]
            gt_ref[tap : tap + 1] += jnp.sum(
                dm[begin : begin + TILE] * behind, axis=0, keepdims=True
            )


def attend_back(info, proj, taps, attended, d_attended, lse):
    slots, rows = proj.shape[:2]
    tiles = rows // TILE
    own = lambda i, info: (i, 0, 0)
    return pl.pallas_call(
        attend_back_kernel,
        grid_spec=pltpu.PrefetchScalarGridSpec(
            num_scalar_prefetch=1,
            grid=(slots,),
            in_specs=[
                pl.BlockSpec((1, rows, 3 * WIDE), own),
                pl.BlockSpec((1, 3, 3 * WIDE), lambda i, info: (info[i, 1], 0, 0)),
                pl.BlockSpec((1, rows, WIDE), own),
                pl.BlockSpec((1, rows, WIDE), own),
                pl.BlockSpec((1, tiles, 2 * TILE), own),
            ],
            out_specs=[
                pl.BlockSpec((1, rows, 3 * WIDE), own),
                pl.BlockSpec((1, 8, 3 * WIDE), own),
            ],
            scratch_shapes=[
                pltpu.VMEM((rows + 8, 3 * WIDE), F32),
                pltpu.VMEM((rows, WIDE), BF16),
                pltpu.VMEM((rows, WIDE), BF16),
                pltpu.VMEM((rows, WIDE), BF16),
                pltpu.VMEM((tiles, WIDE, TILE), BF16),
                pltpu.VMEM((rows + 8, 3 * WIDE), F32),
                pltpu.VMEM((WIDE, 2 * TILE), F32),
            ],
        ),
        out_shape=[
            jax.ShapeDtypeStruct((slots, rows, 3 * WIDE), BF16),
            jax.ShapeDtypeStruct((slots, 8, 3 * WIDE), F32),
        ],
        compiler_params=params(48),
        name="attend_back",
    )(info, proj, taps, attended, d_attended, lse)


def dense_kernel(
    x_ref, att_ref, cot_ref, weight_ref, gain_ref, wo_ref, wu_ref, wd_ref,
    out_ref, dh_ref, datt_ref, n2_ref, sq_ref, du_ref, da_ref, cz_ref, gain_grad_ref, stats_ref,
    act_sc, att_sc,
):
    rows, width = x_ref.shape[1:]
    hidden_units = wu_ref.shape[1]
    step = width
    for pair in range(PAIRS):
        att_sc[:, pair * WIDE : (pair + 1) * WIDE] = att_ref[pair]
    weight = weight_ref[0]
    gain = gain_ref[...].astype(F32)
    branch = mm(att_sc[...], wo_ref[...])
    hidden = x_ref[0].astype(F32) + branch
    factor = lax.rsqrt(jnp.mean(hidden * hidden, axis=-1, keepdims=True) + 1e-06)
    normed = (hidden * factor * gain).astype(BF16)
    n2_ref[0] = normed
    total = jnp.zeros((rows, width), F32)
    for begin in range(0, hidden_units, step):
        cols = slice(begin, begin + step)
        active = jnp.maximum(mm(normed, wu_ref[:, cols]), 0.0)
        act_sc[:, cols] = active
        squared = (active * active).astype(BF16)
        sq_ref[0, :, cols] = squared
        total += mm(squared, wd_ref[cols])
    full = hidden + total
    out_ref[0] = full.astype(BF16)

    def masked(values):
        per_row = jnp.sum(values * values, axis=-1, keepdims=True)
        return jnp.sum(weight * per_row, axis=0, keepdims=True)

    @pl.when(pl.program_id(0) == 0)
    def _():
        stats_ref[...] = jnp.zeros(stats_ref.shape, F32)
        gain_grad_ref[...] = jnp.zeros(gain_grad_ref.shape, F32)

    parts = [masked(full), masked(branch), masked(total), jnp.sum(weight, axis=0, keepdims=True)]
    for place, part in enumerate(parts):
        stats_ref[place : place + 1] += jnp.broadcast_to(part, (1, WIDE))
    cotangent = (cot_ref[0].astype(F32) * weight).astype(BF16)
    cz_ref[0] = cotangent
    d_normed = jnp.zeros((rows, width), F32)
    for begin in range(0, hidden_units, step):
        cols = slice(begin, begin + step)
        d_squared = mm_nt(cotangent, wd_ref[cols])
        d_up = (2.0 * act_sc[:, cols] * d_squared).astype(BF16)
        du_ref[0, :, cols] = d_up
        d_normed += mm_nt(d_up, wu_ref[:, cols])
    weighted = d_normed * gain
    inner = jnp.mean(weighted * hidden, axis=-1, keepdims=True)
    d_hidden = cotangent.astype(F32) + factor * weighted - hidden * (factor * factor * factor) * inner
    gain_grad_ref[...] += jnp.sum(d_normed * hidden * factor, axis=0, keepdims=True)
    dh_ref[0] = d_hidden
    d_attn = d_hidden.astype(BF16)
    da_ref[0] = d_attn
    d_att = mm_nt(d_attn, wo_ref[...]).astype(BF16)
    for pair in range(PAIRS):
        datt_ref[pair] = d_att[:, pair * WIDE : (pair + 1) * WIDE]


def dense_send_kernel(
    x_ref, units_ref, cot_ref, weight_ref, gain_ref, wo_ref, wu_ref, wd_ref,
    out_ref, dh_ref, inbox, att_ref, n2_ref, sq_ref, du_ref, da_ref, cz_ref, gain_grad_ref, stats_ref,
    act_sc, att_sc, att_in, d_blocks, in_s, in_r, out_s, out_r,
):
    group = pl.program_id(0)
    in_sems, out_sems = (in_s, in_r), (out_s, out_r)
    slots = units_ref.shape[0]

    @pl.when(group == 0)
    def _():
        meet_group()
        for slot in range(slots):
            send_blocks(units_ref, att_in, in_sems, slot)

    for slot in range(slots):
        first = slot * GROUP // PAIRS
        pl.when(group == first)(lambda slot=slot: wait_blocks(units_ref, att_in, in_sems, slot))
    here = pl.ds(group * PAIRS, PAIRS)
    att_ref[...] = att_in[here]
    dense_kernel(
        x_ref, att_in.at[here], cot_ref, weight_ref, gain_ref, wo_ref, wu_ref, wd_ref,
        out_ref, dh_ref, d_blocks.at[here], n2_ref, sq_ref, du_ref, da_ref, cz_ref, gain_grad_ref,
        stats_ref, act_sc, att_sc,
    )
    for pair in range(PAIRS):
        send_unit(d_blocks, inbox, out_sems, group * PAIRS + pair)
    pl.when(group == pl.num_programs(0) - 1)(lambda: wait_units(d_blocks, inbox, out_sems))


def dense_send(x, units, grad_output, weight, gain, w_out, w_up, w_down):
    groups, rows, width = x.shape
    hidden_units = w_up.shape[1]
    slots = groups * PAIRS // GROUP
    per_group = lambda s: (s, 0, 0)
    fixed = lambda s: (0, 0)
    once = pl.Buffered(1)
    anywhere = pl.BlockSpec(memory_space=pl.ANY)
    row_block = pl.BlockSpec((1, rows, width), per_group)
    wide_block = pl.BlockSpec((1, rows, hidden_units), per_group)
    low = jax.ShapeDtypeStruct(x.shape, BF16)
    wide_low = jax.ShapeDtypeStruct((groups, rows, hidden_units), BF16)
    unit_rows = (groups * PAIRS, rows, WIDE)
    return pl.pallas_call(
        dense_send_kernel,
        grid=(groups,),
        in_specs=[
            row_block,
            anywhere,
            row_block,
            pl.BlockSpec((1, rows, 1), per_group),
            pl.BlockSpec((1, width), fixed),
            pl.BlockSpec(w_out.shape, fixed, pipeline_mode=once),
            pl.BlockSpec(w_up.shape, fixed, pipeline_mode=once),
            pl.BlockSpec(w_down.shape, fixed, pipeline_mode=once),
        ],
        out_specs=[
            row_block,
            row_block,
            anywhere,
            pl.BlockSpec((PAIRS, rows, WIDE), per_group),
            row_block,
            wide_block,
            wide_block,
            row_block,
            row_block,
            pl.BlockSpec((1, width), fixed),
            pl.BlockSpec((8, WIDE), fixed),
        ],
        out_shape=[
            low,
            jax.ShapeDtypeStruct(x.shape, F32),
            jax.ShapeDtypeStruct((slots, GROUP, rows, WIDE), BF16),
            jax.ShapeDtypeStruct(unit_rows, BF16),
            low,
            wide_low,
            wide_low,
            low,
            low,
            jax.ShapeDtypeStruct((1, width), F32),
            jax.ShapeDtypeStruct((8, WIDE), F32),
        ],
        scratch_shapes=[
            pltpu.VMEM((rows, hidden_units), F32),
            pltpu.VMEM((rows, width), BF16),
            pltpu.VMEM(unit_rows, BF16),
            pltpu.VMEM(unit_rows, BF16),
            DMA((slots, GROUP)),
            DMA((slots, GROUP)),
            DMA((groups * PAIRS,)),
            DMA((slots, GROUP)),
        ],
        compiler_params=group_params(2, 58),
        name="dense_send",
    )(x, units, grad_output, weight, gain.reshape(1, width), w_out, w_up, w_down)


def dense(x, attended, grad_output, weight, gain, w_out, w_up, w_down):
    groups, rows, width = x.shape
    hidden_units = w_up.shape[1]
    per_group = lambda s: (s, 0, 0)
    fixed = lambda s: (0, 0)
    once = pl.Buffered(1)
    row_block = pl.BlockSpec((1, rows, width), per_group)
    wide_block = pl.BlockSpec((1, rows, hidden_units), per_group)
    unit_block = pl.BlockSpec((PAIRS, rows, WIDE), per_group)
    low = jax.ShapeDtypeStruct(x.shape, BF16)
    wide_low = jax.ShapeDtypeStruct((groups, rows, hidden_units), BF16)
    return pl.pallas_call(
        dense_kernel,
        grid=(groups,),
        in_specs=[
            row_block,
            unit_block,
            row_block,
            pl.BlockSpec((1, rows, 1), per_group),
            pl.BlockSpec((1, width), fixed),
            pl.BlockSpec(w_out.shape, fixed, pipeline_mode=once),
            pl.BlockSpec(w_up.shape, fixed, pipeline_mode=once),
            pl.BlockSpec(w_down.shape, fixed, pipeline_mode=once),
        ],
        out_specs=[
            row_block,
            row_block,
            unit_block,
            row_block,
            wide_block,
            wide_block,
            row_block,
            row_block,
            pl.BlockSpec((1, width), fixed),
            pl.BlockSpec((8, WIDE), fixed),
        ],
        out_shape=[
            low,
            jax.ShapeDtypeStruct(x.shape, F32),
            jax.ShapeDtypeStruct((groups * PAIRS, rows, WIDE), BF16),
            low,
            wide_low,
            wide_low,
            low,
            low,
            jax.ShapeDtypeStruct((1, width), F32),
            jax.ShapeDtypeStruct((8, WIDE), F32),
        ],
        scratch_shapes=[pltpu.VMEM((rows, hidden_units), F32), pltpu.VMEM((rows, width), BF16)],
        compiler_params=params(58),
        name="dense",
    )(x, attended, grad_output, weight, gain.reshape(1, width), w_out, w_up, w_down)


PART = 384


def feed_grads_kernel(sq_ref, cz_ref, n2_ref, du_ref, att_ref, da_ref, out_ref, n2_t):
    half, sub = pl.program_id(0), pl.program_id(1)
    groups, rows, width = n2_ref.shape
    tokens = groups * rows

    @pl.when((half == 0) & (sub == 0))
    def _():
        for group in range(groups):
            n2_t[:, group * rows : (group + 1) * rows] = n2_ref[group].astype(F32).T.astype(BF16)

    down = mm_tn(sq_ref[...].reshape(tokens, PART), cz_ref[...].reshape(tokens, width))
    for place in range(4):
        for side in range(2):
            out_ref[place, pl.ds(sub, 1), side * 96 : side * 96 + 96] = down[
                place * 96 : (place + 1) * 96, side * PART : (side + 1) * PART
            ].astype(BF16)[None]
    up = mm(n2_t[...], du_ref[...].reshape(tokens, PART))
    out_ref[pl.ds(sub, 1), :, 192:384] = up.astype(BF16).reshape(1, 4, 192, PART)

    @pl.when(sub == 0)
    def _():
        for pair in range(PAIRS):
            block = mm_tn(
                att_ref[:, pair].reshape(tokens, WIDE), da_ref[...].reshape(tokens, PART)
            ).astype(BF16)
            for low in range(0, WIDE, 16):
                row = pair * WIDE + low
                batch, inner = row // 192, row % 192
                out_ref[inner // 48, batch, 384 + inner % 48 : 400 + inner % 48] = block[low : low + 16]


def feed_grads(squared, cotangent, normed2, d_up, attended, d_attn):
    groups, rows, width = normed2.shape
    whole = lambda h, b: (0, 0, 0)
    return pl.pallas_call(
        feed_grads_kernel,
        grid=(2, 4),
        in_specs=[
            pl.BlockSpec((groups, rows, PART), lambda h, b: (0, 0, 2 * b + h)),
            pl.BlockSpec((groups, rows, width), whole, pipeline_mode=pl.Buffered(1)),
            pl.BlockSpec((groups, rows, width), whole, pipeline_mode=pl.Buffered(1)),
            pl.BlockSpec((groups, rows, PART), lambda h, b: (0, 0, 4 * h + b)),
            pl.BlockSpec(
                (groups, PAIRS, rows, WIDE), lambda h, b: (0, 0, 0, 0), pipeline_mode=pl.Buffered(1)
            ),
            pl.BlockSpec((groups, rows, PART), lambda h, b: (0, 0, h)),
        ],
        out_specs=pl.BlockSpec((4, 4, 432, PART), lambda h, b: (h, 0, 0, 0)),
        out_shape=jax.ShapeDtypeStruct((8, 4, 432, PART), BF16),
        scratch_shapes=[pltpu.VMEM((width, groups * rows), BF16)],
        compiler_params=params(58),
        name="feed_grads",
    )(squared, cotangent, normed2, d_up, attended.reshape(groups, PAIRS, rows, WIDE), d_attn)


def feed_grads_send_kernel(
    sq_ref, cz_ref, n2_ref, du_ref, att_ref, da_ref, sum_ref,
    n2_t, pieces, core_in, down_s, down_r, up_s, up_r, out_s, out_r,
):
    half, sub = pl.program_id(0), pl.program_id(1)
    me = lax.axis_index("seq")
    core = lax.rem(me, 2)
    other = 1 - core

    @pl.when((half == 0) & (sub == 0))
    def _():
        barrier = pltpu.get_barrier_semaphore()
        pl.semaphore_signal(barrier, inc=1, device_id={"seq": me ^ 1}, device_id_type=MESH)
        pl.semaphore_wait(barrier, 1)

    feed_grads_kernel(
        sq_ref, cz_ref, n2_ref, du_ref, att_ref, da_ref, pieces.at[pl.ds(half * 4, 4)], n2_t
    )

    def down(part, batch, side):
        chip = part * 2 + side
        return remote(
            pieces.at[chip * 2 + other, batch, 0:192],
            core_in.at[chip, batch, 0:192],
            (down_s.at[part, batch, side], down_r.at[part, batch, side]),
            "seq",
            me ^ 1,
        )

    def up(chip):
        return remote(
            pieces.at[chip * 2 + other, :, 192:384],
            core_in.at[chip, :, 192:384],
            (up_s.at[chip], up_r.at[chip]),
            "seq",
            me ^ 1,
        )

    def out(chip):
        return remote(
            pieces.at[chip * 2 + other, :, 384:432],
            core_in.at[chip, :, 384:432],
            (out_s.at[chip], out_r.at[chip]),
            "seq",
            me ^ 1,
        )

    for side in range(2):
        down(half, sub, side).start()

    @pl.when(sub == 0)
    def _():
        for side in range(2):
            out(half * 2 + side).start()

    @pl.when(lax.rem(sub, 2) == other)
    def _():
        up(half * 2 + sub // 2).start()

    @pl.when((half == 1) & (sub == 3))
    def _():
        for part in range(2):
            for side in range(2):
                chip = part * 2 + side
                for batch in range(4):
                    down(part, batch, side).wait()
                up(chip).wait()
                out(chip).wait()
                for batch in range(4):
                    both = pieces[chip * 2 + core, batch].astype(F32) + core_in[chip, batch].astype(F32)
                    sum_ref[chip, batch] = both.astype(BF16)


def feed_grads_send(squared, cotangent, normed2, d_up, attended, d_attn):
    groups, rows, width = normed2.shape
    whole = lambda h, b: (0, 0, 0)
    once = pl.Buffered(1)
    quarter = (4, 4, 432, PART)
    return pl.pallas_call(
        feed_grads_send_kernel,
        grid=(2, 4),
        in_specs=[
            pl.BlockSpec((groups, rows, PART), lambda h, b: (0, 0, 2 * b + h)),
            pl.BlockSpec((groups, rows, width), whole, pipeline_mode=once),
            pl.BlockSpec((groups, rows, width), whole, pipeline_mode=once),
            pl.BlockSpec((groups, rows, PART), lambda h, b: (0, 0, 4 * h + b)),
            pl.BlockSpec((groups, PAIRS, rows, WIDE), lambda h, b: (0, 0, 0, 0), pipeline_mode=once),
            pl.BlockSpec((groups, rows, PART), lambda h, b: (0, 0, h)),
        ],
        out_specs=pl.BlockSpec(quarter, lambda h, b: (0, 0, 0, 0), pipeline_mode=once),
        out_shape=jax.ShapeDtypeStruct(quarter, BF16),
        scratch_shapes=[
            pltpu.VMEM((width, groups * rows), BF16),
            pltpu.VMEM((8, 4, 432, PART), BF16),
            pltpu.VMEM(quarter, BF16),
            DMA((2, 4, 2)),
            DMA((2, 4, 2)),
            DMA((4,)),
            DMA((4,)),
            DMA((4,)),
            DMA((4,)),
        ],
        compiler_params=group_params(3, 58),
        name="feed_grads_send",
    )(squared, cotangent, normed2, d_up, attended.reshape(groups, PAIRS, rows, WIDE), d_attn)


def input_grads_kernel(
    dp_ref, n1_ref, x_ref, dh_ref, w_ref, gain_ref, out_ref, gx_ref, gain_grad_ref, n1_t, total, w_sc
):
    pair = pl.program_id(0)
    groups, rows, width = n1_ref.shape
    tokens = groups * rows

    @pl.when(pair == 0)
    def _():
        for group in range(groups):
            n1_t[:, group * rows : (group + 1) * rows] = n1_ref[group].astype(F32).T.astype(BF16)
        total[...] = jnp.zeros(total.shape, F32)

    d_proj = dp_ref[...].reshape(tokens, 3 * WIDE)
    grad = mm(n1_t[...], d_proj).astype(BF16)
    for batch in range(4):
        for chip in range(4):
            begin = batch * 192 + chip * 48
            out_ref[0, 0, chip, batch] = grad[begin : begin + 48]
    for part in range(3):
        cols = pl.ds(pl.multiple_of(part * width + pair * WIDE, WIDE), WIDE)
        w_sc[:, part * WIDE : (part + 1) * WIDE] = w_ref[:, cols]
    total[...] += mm_nt(d_proj, w_sc[...])

    @pl.when(pair == PAIRS - 1)
    def _():
        gain = gain_ref[...].astype(F32)
        gain_sum = jnp.zeros((1, width), F32)
        for group in range(groups):
            x = x_ref[group].astype(F32)
            d_normed = total[group * rows : (group + 1) * rows]
            factor = lax.rsqrt(jnp.mean(x * x, axis=-1, keepdims=True) + 1e-06)
            weighted = d_normed * gain
            inner = jnp.mean(weighted * x, axis=-1, keepdims=True)
            gx_ref[group] = (
                dh_ref[group] + factor * weighted - x * (factor * factor * factor) * inner
            )
            gain_sum += jnp.sum(d_normed * x * factor, axis=0, keepdims=True)
        gain_grad_ref[...] = gain_sum


def input_grads(d_proj, normed1, x, d_hidden, w_qkv, gain):
    groups, rows, width = x.shape
    whole = lambda p: (0, 0, 0)
    once = pl.Buffered(1)
    tokens = pl.BlockSpec((groups, rows, width), whole, pipeline_mode=once)
    return pl.pallas_call(
        input_grads_kernel,
        grid=(PAIRS,),
        in_specs=[
            pl.BlockSpec((groups, 1, rows, 3 * WIDE), lambda p: (0, p, 0, 0)),
            tokens,
            tokens,
            tokens,
            pl.BlockSpec(w_qkv.shape, lambda p: (0, 0), pipeline_mode=once),
            pl.BlockSpec((1, width), lambda p: (0, 0)),
        ],
        out_specs=[
            pl.BlockSpec((1, 1, 4, 4, 48, PART), lambda p: (p % 3, p // 3, 0, 0, 0, 0)),
            tokens,
            pl.BlockSpec((1, width), lambda p: (0, 0)),
        ],
        out_shape=[
            jax.ShapeDtypeStruct((3, 2, 4, 4, 48, PART), BF16),
            jax.ShapeDtypeStruct(x.shape, F32),
            jax.ShapeDtypeStruct((1, width), F32),
        ],
        scratch_shapes=[
            pltpu.VMEM((width, groups * rows), BF16),
            pltpu.VMEM((groups * rows, width), F32),
            pltpu.VMEM((width, 3 * WIDE), BF16),
        ],
        compiler_params=params(58),
        name="input_grads",
    )(d_proj.reshape(groups, PAIRS, rows, 3 * WIDE), normed1, x, d_hidden, w_qkv, gain.reshape(1, width))


def finish_kernel(
    units_ref, n1_ref, x_ref, dh_ref, w_ref, gain_ref, feed_ref, small_ref,
    gx_ref, qkv_out, feed_out, small_out,
    dp_in, n1_v, n1_t, x_v, dh_v, w_v, feed_v, dn, grads, pieces,
    core_in, here, chip_in, mine, z_in, qkv_all, feed_mine, feed_in, feed_all,
    row_own, row_in, row_sum, col_in,
    load_s, dp_s, dp_r, core_s, core_r, chip_s, chip_r, z_s, z_r, qkv_s, qkv_r, fz_s, fz_r, fa_s, fa_r,
    row_s, row_r, col_s, col_r,
):
    me = lax.axis_index("seq")
    z = lax.axis_index("batch")
    core, chip = lax.rem(me, 2), me // 2
    groups, block, width = n1_v.shape
    tokens = groups * block
    middle = tokens // 2
    chunks = pieces.shape[0]
    slots = units_ref.shape[0]
    rows = feed_in.shape[2]
    barrier = pltpu.get_barrier_semaphore()
    for bit in range(1, 8):
        pl.semaphore_signal(barrier, inc=1, device_id={"seq": me ^ bit}, device_id_type=MESH)
    for bit in range(1, 4):
        pl.semaphore_signal(barrier, inc=1, device_id={"batch": z ^ bit}, device_id_type=MESH)
    pl.semaphore_wait(barrier, 10)

    def send(source, target, sems, axis, peer):
        copy = remote(source, target, sems, axis, peer)
        copy.start()
        return copy

    def spread(ref, s, r):
        return [
            send(ref.at[me], ref.at[me], (s.at[step], r.at[step]), "seq", me ^ max(2 * step, 1))
            for step in range(4)
        ]

    def relay(ref, first, s, r):
        more = []
        for step in range(1, 4):
            first[step].wait()
            slot = me ^ (2 * step)
            more.append(
                send(ref.at[slot], ref.at[slot], (s.at[3 + step], r.at[3 + step]), "seq", me ^ 1)
            )
        return [first[0]] + more

    for slot in range(slots):
        send_blocks(units_ref, dp_in, (dp_s, dp_r), slot)
    loads = [
        pltpu.make_async_copy(source, target, load_s.at[place])
        for place, (source, target) in enumerate(
            [(feed_ref, feed_v), (n1_ref, n1_v), (w_ref, w_v), (x_ref, x_v), (dh_ref, dh_v)]
        )
    ]
    for copy in loads:
        copy.start()

    loads[0].wait()
    for batch in range(4):
        both = feed_v[0, batch].astype(F32)
        for q in range(1, 4):
            both = both + feed_v[q, batch].astype(F32)
        feed_mine[batch] = both.astype(BF16)
    feed_z = [
        [
            send(
                feed_mine.at[z ^ bit, c * rows : (c + 1) * rows],
                feed_in.at[c, bit - 1],
                (fz_s.at[c, bit - 1], fz_r.at[c, bit - 1]),
                "batch",
                z ^ bit,
            )
            for bit in range(1, 4)
        ]
        for c in range(chunks)
    ]
    loads[1].wait()
    for group in range(groups):
        n1_t[:, group * block : (group + 1) * block] = n1_v[group].astype(F32).T.astype(BF16)
    for copy in loads[2:]:
        copy.wait()
    gain = gain_ref[...].astype(F32)

    def unit_rows(pair, first):
        return jnp.concatenate(
            [dp_in[(first + more) * PAIRS + pair] for more in range(groups // 2)], axis=0
        )

    def pair_weights(pair):
        return jnp.concatenate(
            [
                w_v[:, part * width + pair * WIDE : part * width + (pair + 1) * WIDE]
                for part in range(3)
            ],
            axis=1,
        )

    def input_half(first):
        gain_sum = jnp.zeros((1, width), F32)
        for more in range(groups // 2):
            group = first + more
            x = x_v[group].astype(F32)
            d_normed = dn[group * block : (group + 1) * block]
            factor = lax.rsqrt(jnp.mean(x * x, axis=-1, keepdims=True) + 1e-06)
            weighted = d_normed * gain
            inner = jnp.mean(weighted * x, axis=-1, keepdims=True)
            dh_v[group] += factor * weighted - x * (factor * factor * factor) * inner
            gain_sum += jnp.sum(d_normed * x * factor, axis=0, keepdims=True)
        return gain_sum

    for slot in range(slots):
        if (slot * GROUP) // PAIRS < groups // 2:
            wait_blocks(units_ref, dp_in, (dp_s, dp_r), slot)
    for pair in range(PAIRS):
        d_rows = unit_rows(pair, 0)
        grads[pair] = mm(n1_t[:, :middle], d_rows)
        part = mm_nt(d_rows, pair_weights(pair))
        if pair == 0:
            dn[:middle] = part
        else:
            dn[:middle] += part
    gain_sum = input_half(0)
    for slot in range(slots):
        if (slot * GROUP) // PAIRS >= groups // 2:
            wait_blocks(units_ref, dp_in, (dp_s, dp_r), slot)

    feed_first = []
    for c in range(chunks):
        for copy in feed_z[c]:
            copy.wait()
        both = feed_mine[z, c * rows : (c + 1) * rows].astype(F32)
        for bit in range(3):
            both = both + feed_in[c, bit].astype(F32)
        feed_all[c, pl.ds(me, 1)] = both.astype(BF16)[None]
        feed_first.append(spread(feed_all.at[c], fa_s.at[c], fa_r.at[c]))

    to_core, to_chip = [], []

    def pass_on(c):
        to_core[c].wait()
        for q in range(4):
            both = pieces[c, core, q].astype(F32) + core_in[c, q].astype(F32)
            here[c, q] = both.astype(BF16)
        to_chip.append(
            [
                send(
                    here.at[c, chip ^ bit],
                    chip_in.at[c, bit - 1],
                    (chip_s.at[c, bit - 1], chip_r.at[c, bit - 1]),
                    "seq",
                    me ^ (2 * bit),
                )
                for bit in range(1, 4)
            ]
        )

    for c in range(chunks):
        for side in range(2):
            pair = side * chunks + c
            grad = (grads[pair] + mm(n1_t[:, middle:], unit_rows(pair, groups // 2))).astype(BF16)
            for batch in range(4):
                for q in range(4):
                    begin = batch * 192 + q * 48
                    pieces[c, side, q, batch] = grad[begin : begin + 48]
        to_core.append(
            send(
                pieces.at[c, 1 - core], core_in.at[c], (core_s.at[c], core_r.at[c]), "seq", me ^ 1
            )
        )
        if c > 0:
            pass_on(c - 1)
    for pair in range(PAIRS):
        part = mm_nt(unit_rows(pair, groups // 2), pair_weights(pair))
        if pair == 0:
            dn[middle:] = part
        else:
            dn[middle:] += part
        if pair == 0:
            pass_on(chunks - 1)
    gain_sum = gain_sum + input_half(groups // 2)
    gx_copy = pltpu.make_async_copy(dh_v, gx_ref, load_s.at[len(loads)])
    gx_copy.start()
    row_own[...] = small_ref[...]
    row_own[9:10] = gain_sum
    row_in[pl.ds(me, 1)] = row_own[...][None]
    rows_out = [
        send(row_own, row_in.at[me], (row_s.at[bit - 1], row_r.at[bit - 1]), "seq", me ^ bit)
        for bit in range(1, 8)
    ]
    to_z = []
    for c in range(chunks):
        for copy in to_chip[c]:
            copy.wait()
        both = here[c, chip].astype(F32)
        for bit in range(3):
            both = both + chip_in[c, bit].astype(F32)
        mine[c] = both.astype(BF16)
        to_z.append(
            [
                send(
                    mine.at[c, z ^ bit],
                    z_in.at[c, bit - 1],
                    (z_s.at[c, bit - 1], z_r.at[c, bit - 1]),
                    "batch",
                    z ^ bit,
                )
                for bit in range(1, 4)
            ]
        )
    for copy in rows_out:
        copy.wait()
    total = row_in[0]
    for place in range(1, 8):
        total = total + row_in[place]
    row_sum[...] = total
    col_in[pl.ds(z, 1)] = total[None]
    cols_out = [
        send(row_sum, col_in.at[z], (col_s.at[bit - 1], col_r.at[bit - 1]), "batch", z ^ bit)
        for bit in range(1, 4)
    ]
    last = []
    for c in range(chunks):
        last += relay(feed_all.at[c], feed_first[c], fa_s.at[c], fa_r.at[c])
    qkv_first = []
    for c in range(chunks):
        for copy in to_z[c]:
            copy.wait()
        both = mine[c, z].astype(F32)
        for bit in range(3):
            both = both + z_in[c, bit].astype(F32)
        qkv_all[c, pl.ds(me, 1)] = both.astype(BF16)[None]
        qkv_first.append(spread(qkv_all.at[c], qkv_s.at[c], qkv_r.at[c]))
    for c in range(chunks):
        last += relay(qkv_all.at[c], qkv_first[c], qkv_s.at[c], qkv_r.at[c])
    for copy in cols_out:
        copy.wait()
    small_out[...] = ((col_in[0] + col_in[1]) + col_in[2]) + col_in[3]
    for copy in last:
        copy.wait()
    qkv_out[...] = qkv_all[...]
    feed_out[...] = feed_all[...]
    gx_copy.wait()


def finish(units, normed1, x, d_hidden, w_qkv, gain, feed, small):
    groups, block, width = x.shape
    chunks, rows, feed_rows = 3, 48, 144
    tokens = groups * block
    slots = units.shape[0]
    vmem = pl.BlockSpec(memory_space=pltpu.VMEM)
    anywhere = pl.BlockSpec(memory_space=pl.ANY)
    pairs = [DMA((slots, GROUP)), DMA((slots, GROUP))]
    for shape in [(), (3,), (3,), (7,), (3,), (7,)]:
        pairs += [DMA((chunks,) + shape), DMA((chunks,) + shape)]
    low = lambda *shape: pltpu.VMEM(shape, BF16)
    return pl.pallas_call(
        finish_kernel,
        in_specs=[anywhere] * 5 + [vmem, anywhere, vmem],
        out_specs=[anywhere, vmem, vmem, vmem],
        out_shape=[
            jax.ShapeDtypeStruct(x.shape, F32),
            jax.ShapeDtypeStruct((chunks, 8, rows, PART), BF16),
            jax.ShapeDtypeStruct((chunks, 8, feed_rows, PART), BF16),
            jax.ShapeDtypeStruct(small.shape, F32),
        ],
        scratch_shapes=[
            low(groups * PAIRS, block, 3 * WIDE),
            low(groups, block, width),
            low(width, tokens),
            low(groups, block, width),
            pltpu.VMEM((groups, block, width), F32),
            low(*w_qkv.shape),
            low(4, 4, chunks * feed_rows, PART),
            pltpu.VMEM((tokens, width), F32),
            pltpu.VMEM((PAIRS, width, 3 * WIDE), F32),
            low(chunks, 2, 4, 4, rows, PART),
            low(chunks, 4, 4, rows, PART),
            low(chunks, 4, 4, rows, PART),
            low(chunks, 3, 4, rows, PART),
            low(chunks, 4, rows, PART),
            low(chunks, 3, rows, PART),
            low(chunks, 8, rows, PART),
            low(4, chunks * feed_rows, PART),
            low(chunks, 3, feed_rows, PART),
            low(chunks, 8, feed_rows, PART),
            pltpu.VMEM(small.shape, F32),
            pltpu.VMEM((8,) + small.shape, F32),
            pltpu.VMEM(small.shape, F32),
            pltpu.VMEM((4,) + small.shape, F32),
            DMA((6,)),
        ]
        + pairs
        + [DMA((7,)), DMA((7,)), DMA((3,)), DMA((3,))],
        compiler_params=group_params(0, 60),
        name="finish",
    )(units, normed1, x, d_hidden, w_qkv, gain.reshape(1, width), feed, small)


def unpack_kernel(feed_ref, qkv_ref, down_ref, up_ref, out_ref, grad_ref):
    down_ref[:, :PART] = feed_ref[0, 0, :96].astype(F32)
    down_ref[:48, PART:] = feed_ref[0, 0, 96:].astype(F32)
    down_ref[48:, PART:] = feed_ref[1, 0, :48].astype(F32)
    up_ref[:96] = feed_ref[1, 0, 48:].astype(F32)
    up_ref[96:] = feed_ref[2, 0, :96].astype(F32)
    out_ref[...] = feed_ref[2, 0, 96:].astype(F32)
    place = pl.program_id(0)

    def put(core):
        for c in range(3):
            for part in range(3):
                begin = part * PAIRS * WIDE + (core * 3 + c) * WIDE
                grad_ref[:, begin : begin + WIDE] = qkv_ref[
                    c, 0, :, part * WIDE : (part + 1) * WIDE
                ].astype(F32)

    for core in range(2):
        pl.when(place % 2 == core)(functools.partial(put, core))


def unpack(feed, qkv):
    return pl.pallas_call(
        unpack_kernel,
        grid=(8,),
        in_specs=[
            pl.BlockSpec((3, 1, 144, PART), lambda r: (0, r, 0, 0)),
            pl.BlockSpec((3, 1, 48, PART), lambda r: (0, r, 0, 0)),
        ],
        out_specs=[
            pl.BlockSpec((96, 2 * PART), lambda r: (r, 0)),
            pl.BlockSpec((192, PART), lambda r: (0, r)),
            pl.BlockSpec((48, PART), lambda r: (r % 4, r // 4)),
            pl.BlockSpec((48, 3 * PAIRS * WIDE), lambda r: (r // 2, 0)),
        ],
        out_shape=[
            jax.ShapeDtypeStruct((768, 2 * PART), F32),
            jax.ShapeDtypeStruct((192, 8 * PART), F32),
            jax.ShapeDtypeStruct((192, 2 * PART), F32),
            jax.ShapeDtypeStruct((192, 3 * PAIRS * WIDE), F32),
        ],
        compiler_params=params(32),
        name="unpack",
    )(feed, qkv)


def exchange(blocks):
    return lax.all_to_all(blocks, "seq", 0, 0, tiled=True)


def plain_gradients(feed, qkv):
    down = feed[:, :, :192].reshape(8, 4, 2, 96, PART).transpose(1, 0, 3, 2, 4)
    up = feed[:, :, 192:384].transpose(1, 2, 0, 3)
    out = feed[:, :, 384:].reshape(2, 4, 4, 48, PART).transpose(2, 1, 3, 0, 4)
    grad = qkv.reshape(3, 2, 4, 4, 48, 3, WIDE).transpose(3, 2, 4, 5, 1, 0, 6)
    return (
        down.reshape(3072, 768),
        up.reshape(768, 3072),
        out.reshape(768, 768),
        grad.reshape(768, 2304),
    )


def shards(
    stream_in,
    lengths,
    token_mask,
    norm1_gain,
    w_qkv,
    conv_taps,
    w_out,
    norm2_gain,
    w_up,
    w_down,
    grad_output,
):
    groups, block_len, width = stream_in.shape
    count = lax.axis_size("seq")
    batches = lax.axis_size("batch")
    place = lax.axis_index("seq")
    units = groups * PAIRS
    slots = -(-units // count)
    spare = slots * count - units
    offset = place * block_len
    taps = conv_taps.astype(F32).reshape(3, 3, PAIRS, WIDE).transpose(2, 0, 1, 3)
    taps = taps.reshape(PAIRS, 3, 3 * WIDE)

    fitted = count == GROUP and batches == 4 and units % GROUP == 0

    def to_heads(blocks):
        blocks = jnp.pad(blocks, ((0, spare), (0, 0), (0, 0)))
        blocks = blocks.reshape((slots, count) + blocks.shape[1:])
        return jnp.stack([exchange(blocks[slot]) for slot in range(slots)])

    def to_tokens(rows):
        rows = rows.reshape(slots, count, block_len, rows.shape[2])
        return jnp.concatenate([exchange(rows[slot]) for slot in range(slots)])[:units]

    unit = jnp.arange(slots) * count + place
    sequence = jnp.minimum(unit // PAIRS, groups - 1)
    info = jnp.stack([jnp.where(unit < units, lengths[sequence], 0), unit % PAIRS], axis=1)
    info = info.astype(jnp.int32)

    if fitted:
        normed1, proj = project_send(stream_in, norm1_gain, w_qkv)
    else:
        normed1, proj = project(stream_in, norm1_gain, w_qkv)
        proj = to_heads(proj)
    proj = proj.reshape(slots, count * block_len, 3 * WIDE)
    unit_out, unit_lse = attend(info, proj, taps)

    positions = offset + jnp.arange(block_len, dtype=jnp.int32)
    inside = (positions[None, :] < lengths[:, None]).astype(F32)
    stat_weight = (token_mask.astype(F32) * inside)[..., None]
    rest = (grad_output, stat_weight, norm2_gain, w_out, w_up, w_down)
    if fitted:
        blocks = unit_out.reshape(slots, count, block_len, WIDE)
        stream_out, d_hidden, d_units, attended, *saved = dense_send(stream_in, blocks, *rest)
    else:
        attended = to_tokens(unit_out)
        stream_out, d_hidden, d_units, *saved = dense(stream_in, attended, *rest)
        d_units = to_heads(d_units)
    normed2, squared, d_up, d_attn, cotangent, grad_norm2, local_stats = saved
    d_units = d_units.reshape(slots, count * block_len, WIDE)
    saved = (squared, cotangent, normed2, d_up, attended, d_attn)
    if fitted:
        feed = feed_grads_send(*saved)
        same_core = [[core + 2 * chip for chip in range(4)] for core in range(2)]
        feed = lax.all_to_all(feed, "seq", 0, 0, tiled=True, axis_index_groups=same_core)
    else:
        feed = feed_grads(*saved)

    back, parts = attend_back(info, proj, taps, unit_out, d_units, unit_lse)
    unit_taps = jnp.zeros((PAIRS, 3, 3 * WIDE), F32)
    for slot in range(slots):
        chosen = jnp.arange(PAIRS)[:, None, None] == info[slot, 1]
        unit_taps = unit_taps + jnp.where(chosen, parts[slot, None, :3], 0.0)
    grad_taps = unit_taps.reshape(PAIRS, 3, 3, WIDE).transpose(1, 2, 0, 3).reshape(9, width)
    stats_row = jnp.pad(local_stats[:4, 0], (0, width - 4)).reshape(1, width)

    def small_rows(grad_norm1):
        zeros = jnp.zeros((4, width), F32)
        return jnp.concatenate([grad_taps, grad_norm1, grad_norm2, stats_row, zeros], axis=0)

    if fitted:
        blocks = back.reshape(slots, count, block_len, 3 * WIDE)
        small = small_rows(jnp.zeros((1, width), F32))
        grad_input, qkv, feed, small = finish(
            blocks, normed1, stream_in, d_hidden, w_qkv, norm1_gain, feed, small
        )
        total_down, total_up, total_wout, total_qkv = unpack(feed, qkv)
    else:
        pieces, grad_input, grad_norm1 = input_grads(
            to_tokens(back), normed1, stream_in, d_hidden, w_qkv, norm1_gain
        )

        def reduce(gradient):
            share = lax.psum_scatter(gradient, ("batch", "seq"), scatter_dimension=0, tiled=True)
            return lax.all_gather(share, "seq", axis=0, tiled=True).astype(F32)

        total_down, total_up, total_wout, total_qkv = map(reduce, plain_gradients(feed, pieces))
        small = lax.psum(small_rows(grad_norm1), ("seq", "batch"))
    share = width // batches
    begin = lax.axis_index("batch") * share
    block_rms = jnp.sqrt(small[11, :3] / (width * small[11, 3]))
    return (
        stream_out,
        grad_input,
        lax.dynamic_slice_in_dim(small[9], begin, share),
        total_qkv,
        small[:9].reshape(3, 3 * width),
        total_wout,
        lax.dynamic_slice_in_dim(small[10], begin, share),
        total_up,
        total_down,
        block_rms,
    )


def solution(mesh):
    tokens = P("batch", "seq", None)
    return jax.shard_map(
        shards,
        mesh=mesh,
        in_specs=(
            tokens,
            P("batch"),
            P("batch", "seq"),
            P(),
            P(),
            P(),
            P(),
            P(),
            P(),
            P(),
            tokens,
        ),
        out_specs=(
            tokens,
            tokens,
            P("batch"),
            P("batch", None),
            P(),
            P("batch", None),
            P("batch"),
            P("batch", None),
            P("batch", None),
            P(),
        ),
        check_vma=False,
    )
```

```python
import functools
import math

import jax
import jax.numpy as jnp
from jax import lax
from jax.experimental import pallas as pl
from jax.experimental.pallas import tpu as pltpu
from jax.sharding import PartitionSpec as P

HEADS = 12
HEAD = 64
PAIRS = HEADS // 2
WIDE = 2 * HEAD
TILE = 256
ROWS = 512
BACK = 256
STRIP = 32
LIMIT = 62 << 20
NEG = -1e30
F32 = jnp.float32
BF16 = jnp.bfloat16


def mm(left_op, right_op):
    return jnp.dot(left_op, right_op, preferred_element_type=F32)


def mm_nt(left_op, right_op):
    return lax.dot_general(
        left_op, right_op, (((1,), (1,)), ((), ())), preferred_element_type=F32
    )


def mm_tn(left_op, right_op):
    return lax.dot_general(
        left_op, right_op, (((0,), (0,)), ((), ())), preferred_element_type=F32
    )


def params():
    return pltpu.CompilerParams(vmem_limit_bytes=LIMIT)


MESH = pl.DeviceIdType.MESH
GROUP = 8
DMA = pltpu.SemaphoreType.DMA


def remote(source, target, sems, axis, peer):
    return pltpu.make_async_remote_copy(
        src_ref=source,
        dst_ref=target,
        send_sem=sems[0],
        recv_sem=sems[1],
        device_id={axis: peer},
        device_id_type=MESH,
    )


def meet_group():
    me = lax.axis_index("seq")
    barrier = pltpu.get_barrier_semaphore()
    for bit in range(1, GROUP):
        pl.semaphore_signal(barrier, inc=1, device_id={"seq": me ^ bit}, device_id_type=MESH)
    pl.semaphore_wait(barrier, GROUP - 1)


def unit_copy(blocks, inbox, sems, unit):
    me = lax.axis_index("seq")
    owner, slot = lax.rem(unit, GROUP), unit // GROUP
    return owner, remote(
        blocks.at[unit],
        inbox.at[slot, me],
        (sems[0].at[unit], sems[1].at[slot, me ^ owner]),
        "seq",
        owner,
    )


def send_unit(blocks, inbox, sems, unit):
    me = lax.axis_index("seq")
    owner, copy = unit_copy(blocks, inbox, sems, unit)

    @pl.when(owner != me)
    def _():
        copy.start()

    @pl.when(owner == me)
    def _():
        slot = unit // GROUP
        pltpu.make_async_copy(blocks.at[unit], inbox.at[slot, me], sems[1].at[slot, 0]).start()


def wait_unit(blocks, inbox, sems, slot):
    me = lax.axis_index("seq")
    unit = slot * GROUP + me
    pltpu.make_async_copy(blocks.at[unit], inbox.at[slot, me], sems[1].at[slot, 0]).wait()
    for bit in range(1, GROUP):
        remote(
            blocks.at[unit],
            inbox.at[slot, me ^ bit],
            (sems[0].at[unit], sems[1].at[slot, bit]),
            "seq",
            me ^ bit,
        ).wait_recv()


def wait_sent(blocks, inbox, sems):
    me = lax.axis_index("seq")

    def one(unit, carry):
        owner, copy = unit_copy(blocks, inbox, sems, unit)
        pl.when(owner != me)(copy.wait_send)
        return carry

    lax.fori_loop(0, blocks.shape[0], one, 0)


def wait_units(blocks, inbox, sems):
    for slot in range(blocks.shape[0] // GROUP):
        wait_unit(blocks, inbox, sems, slot)
    wait_sent(blocks, inbox, sems)


def block_copies(units, inbox, sems, slot):
    me = lax.axis_index("seq")
    return [
        remote(
            units.at[slot, me ^ bit],
            inbox.at[slot * GROUP + me],
            (sems[0].at[slot, bit], sems[1].at[slot, bit]),
            "seq",
            me ^ bit,
        )
        for bit in range(1, GROUP)
    ]


def own_block(units, inbox, sems, slot):
    me = lax.axis_index("seq")
    return pltpu.make_async_copy(
        units.at[slot, me], inbox.at[slot * GROUP + me], sems[1].at[slot, 0]
    )


def send_blocks(units, inbox, sems, slot):
    own_block(units, inbox, sems, slot).start()
    for copy in block_copies(units, inbox, sems, slot):
        copy.start()


def wait_blocks(units, inbox, sems, slot):
    own_block(units, inbox, sems, slot).wait()
    for copy in block_copies(units, inbox, sems, slot):
        copy.wait()


def group_params(number):
    return pltpu.CompilerParams(
        collective_id=number, has_side_effects=True, vmem_limit_bytes=LIMIT
    )


def gain_row(gain_ref):
    return gain_ref[...].astype(F32).reshape(1, gain_ref.shape[0])


def project_kernel(x_ref, gain_ref, w_ref, n_ref, p_ref):
    x = x_ref[0].astype(F32)
    factor = lax.rsqrt(jnp.mean(x * x, axis=-1, keepdims=True) + 1e-06)
    normed = (x * factor * gain_row(gain_ref)).astype(BF16)
    n_ref[0] = normed
    width = x.shape[1]
    for part in range(3):
        cols = mm(normed, w_ref[:, part * width : (part + 1) * width])
        for pair in range(PAIRS):
            p_ref[pair, :, part * WIDE : (part + 1) * WIDE] = cols[
                :, pair * WIDE : (pair + 1) * WIDE
            ].astype(BF16)


def project(x, gain, w_qkv):
    groups, rows, width = x.shape
    return pl.pallas_call(
        project_kernel,
        grid=(groups,),
        in_specs=[
            pl.BlockSpec((1, rows, width), lambda s: (s, 0, 0)),
            pl.BlockSpec((width,), lambda s: (0,)),
            pl.BlockSpec(w_qkv.shape, lambda s: (0, 0)),
        ],
        out_specs=[
            pl.BlockSpec((1, rows, width), lambda s: (s, 0, 0)),
            pl.BlockSpec((PAIRS, rows, 3 * WIDE), lambda s: (s, 0, 0)),
        ],
        out_shape=[
            jax.ShapeDtypeStruct(x.shape, BF16),
            jax.ShapeDtypeStruct((groups * PAIRS, rows, 3 * WIDE), BF16),
        ],
        compiler_params=params(),
        name="project",
    )(x, gain, w_qkv)


def stack_heads(rows):
    lane = lax.broadcasted_iota(jnp.int32, rows.shape, 1)
    zero = jnp.zeros_like(rows)
    first = jnp.where(lane < HEAD, rows, zero)
    second = jnp.where(lane < HEAD, zero, rows)
    return jnp.concatenate([first, second], axis=0)


def unstack_heads(rows):
    half = rows.shape[0] // 2
    lane = lax.broadcasted_iota(jnp.int32, (half, rows.shape[1]), 1)
    return jnp.where(lane < HEAD, rows[:half], rows[half:])


def step_rows(index, size):
    return pl.ds(pl.multiple_of(index * size, size), size)


def own_unit(lengths, groups, count, slot):
    unit = slot * count + lax.axis_index("seq")
    length = lengths[jnp.minimum(unit // PAIRS, groups - 1)]
    return jnp.where(unit < groups * PAIRS, length, 0), lax.rem(unit, PAIRS)


def pair_taps(taps_ref, taps_sc, pair):
    width = taps_ref.shape[1] // 3
    for part in range(3):
        cols = pl.ds(pl.multiple_of(part * width + pair * WIDE, WIDE), WIDE)
        taps_sc[0:3, part * WIDE : (part + 1) * WIDE] = taps_ref[:, cols].astype(F32)


def convolve(wide_ref, taps_ref, tile, cols):
    begin = 8 + tile * TILE
    total = taps_ref[0:1, cols] * wide_ref[begin : begin + TILE, cols]
    total += taps_ref[1:2, cols] * wide_ref[begin - 1 : begin - 1 + TILE, cols]
    total += taps_ref[2:3, cols] * wide_ref[begin - 2 : begin - 2 + TILE, cols]
    return total.astype(BF16)


Q_COLS, K_COLS, V_COLS = (slice(part * WIDE, (part + 1) * WIDE) for part in range(3))


def key_limits(index, length, size):
    lane = lax.broadcasted_iota(jnp.int32, (STRIP, 2 * size), 1)
    return jnp.minimum(index * size + (lane & (size - 1)) + 1, length)


def over_key_steps(index, length, size, visit, carry):
    full = jnp.minimum(index * size, length) // size
    last = (jnp.minimum((index + 1) * size, length) + size - 1) // size
    carry = lax.fori_loop(0, full, lambda step, c: visit(step, False, c), carry)
    return lax.fori_loop(full, last, lambda step, c: visit(step, True, c), carry)


def attend_kernel(
    groups, count, lengths, p_ref, taps_ref, o_ref, lse_ref, taps, wide, q_sc, k_sc, vt_sc, acc, s_sc, e_sc
):
    length, pair = own_unit(lengths, groups, count, pl.program_id(0))
    wide[0:8] = jnp.zeros((8, wide.shape[1]), F32)
    wide[8:] = p_ref[0].astype(F32)
    attend_unit(
        length, pair, False, taps_ref, o_ref.at[0], lse_ref.at[0], taps, wide, q_sc, k_sc, vt_sc, acc, s_sc, e_sc
    )


def attend_unit(
    length, pair, whole, taps_ref, o_ref, lse_ref, taps, wide, q_sc, k_sc, vt_sc, acc, s_sc, e_sc
):
    tiles = q_sc.shape[0] // TILE
    per_step = ROWS // TILE
    pair_taps(taps_ref, taps, pair)
    vt_sc[:, WIDE:] = jnp.ones((vt_sc.shape[0], vt_sc.shape[1] - WIDE, ROWS), BF16)
    for tile in range(tiles):
        rows = slice(tile * TILE, (tile + 1) * TILE)
        q_sc[rows] = convolve(wide, taps, tile, Q_COLS) * (1.0 / math.sqrt(HEAD))

        def keys_values():
            k_sc[rows] = convolve(wide, taps, tile, K_COLS)
            cols = slice(tile % per_step * TILE, (tile % per_step + 1) * TILE)
            values = convolve(wide, taps, tile, V_COLS)
            vt_sc[tile // per_step, :WIDE, cols] = values.astype(F32).T.astype(BF16)

        if whole:
            keys_values()
        else:
            pl.when(tile // per_step * ROWS < length)(keys_values)

    k_row = lax.broadcasted_iota(jnp.int32, (STRIP, 2 * ROWS), 0)

    def query_step(index, carry):
        q_stack = stack_heads(q_sc[step_rows(index, ROWS)])
        limit = key_limits(index, length, ROWS)
        acc[...] = jnp.zeros(acc.shape, F32)

        def visit(step, masked, old):
            s_sc[...] = mm_nt(k_sc[step_rows(step, ROWS)], q_stack)
            top = jnp.full((8, 2 * ROWS), NEG, F32)
            for begin in range(0, ROWS, STRIP):
                scores = s_sc[begin : begin + STRIP]
                if masked:
                    scores = jnp.where(k_row < limit - (step * ROWS + begin), scores, NEG)
                    s_sc[begin : begin + STRIP] = scores
                for low in range(0, STRIP, 8):
                    top = jnp.maximum(top, scores[low : low + 8])
            new = jnp.maximum(old, jnp.max(top, axis=0, keepdims=True))
            for begin in range(0, ROWS, STRIP):
                e_sc[begin : begin + STRIP] = jnp.exp(s_sc[begin : begin + STRIP] - new).astype(BF16)
            acc[...] = acc[...] * jnp.exp(old - new) + mm(vt_sc[step], e_sc[...])
            return new

        top = jnp.full((1, 2 * ROWS), NEG, F32)
        if whole:
            top = lax.fori_loop(0, index + 1, lambda step, c: visit(step, True, c), top)
        else:
            top = over_key_steps(index, length, ROWS, visit, top)
        total = acc[WIDE : WIDE + 1]
        out = (acc[:WIDE] / total).T
        o_ref[step_rows(index, ROWS)] = unstack_heads(out).astype(BF16)
        lse_ref[pl.ds(index, 1)] = top + jnp.log(total)
        return carry

    lax.fori_loop(0, q_sc.shape[0] // ROWS, query_step, 0)


def attend(lengths, proj, taps, count):
    slots, rows = proj.shape[:2]
    steps = rows // ROWS
    own = lambda i, lengths: (i, 0, 0)
    return pl.pallas_call(
        functools.partial(attend_kernel, lengths.shape[0], count),
        grid_spec=pltpu.PrefetchScalarGridSpec(
            num_scalar_prefetch=1,
            grid=(slots,),
            in_specs=[
                pl.BlockSpec((1, rows, 3 * WIDE), own),
                pl.BlockSpec(taps.shape, lambda i, lengths: (0, 0)),
            ],
            out_specs=[
                pl.BlockSpec((1, rows, WIDE), own),
                pl.BlockSpec((1, steps, 2 * ROWS), own),
            ],
            scratch_shapes=[
                pltpu.VMEM((8, 3 * WIDE), F32),
                pltpu.VMEM((rows + 8, 3 * WIDE), F32),
                pltpu.VMEM((rows, WIDE), BF16),
                pltpu.VMEM((rows, WIDE), BF16),
                pltpu.VMEM((steps, WIDE + 16, ROWS), BF16),
                pltpu.VMEM((WIDE + 16, 2 * ROWS), F32),
                pltpu.VMEM((ROWS, 2 * ROWS), F32),
                pltpu.VMEM((ROWS, 2 * ROWS), BF16),
            ],
        ),
        out_shape=[
            jax.ShapeDtypeStruct((slots, rows, WIDE), BF16),
            jax.ShapeDtypeStruct((slots, steps, 2 * ROWS), F32),
        ],
        compiler_params=params(),
        name="attend",
    )(lengths, proj, taps)


def front_kernel(
    lengths, x_ref, gain_ref, w_ref, taps_ref, n1_out, proj_out, units_out, att_out, lse_ref,
    x_v, w_v, n1_v, blocks, proj, units, att, taps, wide, q_sc, k_sc, vt_sc, acc, s_sc, e_sc,
    load_s, send_s, send_r, out_s, out_r,
):
    groups = x_v.shape[0]
    slots = proj.shape[0]
    block = x_v.shape[1]
    sems, out_sems = (send_s, send_r), (out_s, out_r)
    loads = [pltpu.make_async_copy(w_ref, w_v, load_s.at[0]), pltpu.make_async_copy(x_ref, x_v, load_s.at[1])]
    for copy in loads:
        copy.start()
    meet_group()
    for copy in loads:
        copy.wait()

    def sequence(group, carry):
        here = pl.ds(group, 1)
        project_kernel(
            x_v.at[here], gain_ref, w_v, n1_v.at[here], blocks.at[pl.ds(group * PAIRS, PAIRS)]
        )
        for pair in range(PAIRS):
            send_unit(blocks, proj, sems, group * PAIRS + pair)
        return carry

    lax.fori_loop(0, groups, sequence, 0)
    stores = [pltpu.make_async_copy(n1_v, n1_out, load_s.at[2])]
    stores[0].start()

    def one_slot(slot, carry):
        wait_unit(blocks, proj, sems, slot)
        length, pair = own_unit(lengths, groups, GROUP, slot)
        wide[0:8] = jnp.zeros((8, wide.shape[1]), F32)
        for place in range(GROUP):
            wide[8 + place * block : 8 + (place + 1) * block] = proj[slot, place].astype(F32)
        attend_unit(
            length, pair, True, taps_ref, units.at[slot], lse_ref.at[slot],
            taps, wide, q_sc, k_sc, vt_sc, acc, s_sc, e_sc,
        )
        send_rows(units, att, out_sems, slot, block)
        return carry

    lax.fori_loop(0, slots, one_slot, 0)
    stores.append(pltpu.make_async_copy(proj, proj_out, load_s.at[3]))
    stores.append(pltpu.make_async_copy(units, units_out, load_s.at[4]))
    for copy in stores[1:]:
        copy.start()
    for slot in range(slots):
        wait_rows(units, att, out_sems, slot, block)
    stores.append(pltpu.make_async_copy(att, att_out, load_s.at[5]))
    stores[-1].start()
    wait_sent(blocks, proj, sems)
    for copy in stores:
        copy.wait()


def row_copies(units, inbox, sems, slot, block):
    me = lax.axis_index("seq")
    return [
        remote(
            units.at[slot, pl.ds(pl.multiple_of((me ^ bit) * block, block), block)],
            inbox.at[slot * GROUP + me],
            (sems[0].at[slot, bit], sems[1].at[slot, bit]),
            "seq",
            me ^ bit,
        )
        for bit in range(1, GROUP)
    ]


def own_rows(units, inbox, sems, slot, block):
    me = lax.axis_index("seq")
    return pltpu.make_async_copy(
        units.at[slot, pl.ds(pl.multiple_of(me * block, block), block)],
        inbox.at[slot * GROUP + me],
        sems[1].at[slot, 0],
    )


def send_rows(units, inbox, sems, slot, block):
    own_rows(units, inbox, sems, slot, block).start()
    for copy in row_copies(units, inbox, sems, slot, block):
        copy.start()


def wait_rows(units, inbox, sems, slot, block):
    own_rows(units, inbox, sems, slot, block).wait()
    for copy in row_copies(units, inbox, sems, slot, block):
        copy.wait()


def front(x, gain, w_qkv, taps, lengths):
    groups, block, width = x.shape
    units = groups * PAIRS
    slots = units // GROUP
    rows = GROUP * block
    steps = rows // ROWS
    anywhere = pl.BlockSpec(memory_space=pl.ANY)
    vmem = pl.BlockSpec(memory_space=pltpu.VMEM)
    low = lambda *shape: pltpu.VMEM(shape, BF16)
    return pl.pallas_call(
        front_kernel,
        in_specs=[pl.BlockSpec(memory_space=pltpu.SMEM), anywhere, vmem, anywhere, vmem],
        out_specs=[anywhere] * 4 + [vmem],
        out_shape=[
            jax.ShapeDtypeStruct(x.shape, BF16),
            jax.ShapeDtypeStruct((slots, GROUP, block, 3 * WIDE), BF16),
            jax.ShapeDtypeStruct((slots, rows, WIDE), BF16),
            jax.ShapeDtypeStruct((units, block, WIDE), BF16),
            jax.ShapeDtypeStruct((slots, steps, 2 * ROWS), F32),
        ],
        scratch_shapes=[
            low(*x.shape),
            low(*w_qkv.shape),
            low(*x.shape),
            low(units, block, 3 * WIDE),
            low(slots, GROUP, block, 3 * WIDE),
            low(slots, rows, WIDE),
            low(units, block, WIDE),
            pltpu.VMEM((8, 3 * WIDE), F32),
            pltpu.VMEM((rows + 8, 3 * WIDE), F32),
            low(rows, WIDE),
            low(rows, WIDE),
            low(steps, WIDE + 16, ROWS),
            pltpu.VMEM((WIDE + 16, 2 * ROWS), F32),
            pltpu.VMEM((ROWS, 2 * ROWS), F32),
            low(ROWS, 2 * ROWS),
            DMA((6,)),
            DMA((units,)),
            DMA((slots, GROUP)),
            DMA((slots, GROUP)),
            DMA((slots, GROUP)),
        ],
        compiler_params=group_params(1),
        name="front",
    )(lengths, x, gain, w_qkv, taps)


def attend_back_kernel(
    groups, count, lengths, p_ref, taps_ref, o_ref, do_ref, lse_ref, dp_ref, gt_ref,
    taps, wide, q_sc, k_sc, v_sc, kt_sc, dm, dqt, s_sc, d_sc, e_sc, f_sc,
):
    p_ref, o_ref, do_ref, lse_ref = p_ref.at[0], o_ref.at[0], do_ref.at[0], lse_ref.at[0]
    dp_ref = dp_ref.at[0]
    length, pair = own_unit(lengths, groups, count, pl.program_id(0))
    tiles = p_ref.shape[0] // TILE
    per_step = BACK // TILE
    pair_taps(taps_ref, taps, pair)
    wide[0:8] = jnp.zeros((8, wide.shape[1]), F32)
    wide[8:] = p_ref[...].astype(F32)
    dm[...] = jnp.zeros(dm.shape, F32)
    for tile in range(tiles):
        rows = slice(tile * TILE, (tile + 1) * TILE)

        @pl.when(tile // per_step * BACK < length)
        def _():
            q_sc[rows] = convolve(wide, taps, tile, Q_COLS) * (1.0 / math.sqrt(HEAD))
            keys = convolve(wide, taps, tile, K_COLS)
            k_sc[rows] = keys
            v_sc[rows] = convolve(wide, taps, tile, V_COLS)
            cols = slice(tile % per_step * TILE, (tile % per_step + 1) * TILE)
            kt_sc[tile // per_step, :, cols] = keys.astype(F32).T.astype(BF16)

    lane = lax.broadcasted_iota(jnp.int32, (8, WIDE), 1)
    row = lax.broadcasted_iota(jnp.int32, (8, WIDE), 0)
    picks = jnp.where((lane < HEAD) == (row == 0), 1.0, 0.0).astype(BF16)
    k_row = lax.broadcasted_iota(jnp.int32, (STRIP, 2 * BACK), 0)

    def query_step(index, carry):
        here = step_rows(index, BACK)
        q_stack = stack_heads(q_sc[here])
        d_rows = do_ref[here]
        d_stack = stack_heads(d_rows)
        product = d_rows.astype(F32) * o_ref[here].astype(F32)
        upper = product.astype(BF16)
        lower = (product - upper.astype(F32)).astype(BF16)
        sums = mm_nt(picks, upper) + mm_nt(picks, lower)
        delta = jnp.concatenate([sums[0:1], sums[1:2]], axis=1)
        line, begin = pl.ds(index * BACK // ROWS, 1), lax.rem(index * BACK, ROWS)
        lse = jnp.concatenate(
            [
                lse_ref[line, pl.ds(pl.multiple_of(head * ROWS + begin, BACK), BACK)]
                for head in range(2)
            ],
            axis=1,
        )
        limit = key_limits(index, length, BACK)
        dqt[...] = jnp.zeros(dqt.shape, F32)

        def visit(step, masked, carry):
            there = step_rows(step, BACK)
            s_sc[...] = mm_nt(k_sc[there], q_stack)
            d_sc[...] = mm_nt(v_sc[there], d_stack)
            for begin in range(0, BACK, STRIP):
                strip = slice(begin, begin + STRIP)
                probs = jnp.exp(s_sc[strip] - lse)
                if masked:
                    probs = jnp.where(k_row < limit - (step * BACK + begin), probs, 0.0)
                e_sc[strip] = probs.astype(BF16)
                f_sc[strip] = (probs * (d_sc[strip] - delta)).astype(BF16)
            dm[there, V_COLS] += mm(e_sc[...], d_stack)
            dm[there, K_COLS] += mm(f_sc[...], q_stack)
            dqt[...] += mm(kt_sc[step], f_sc[...])
            return carry

        over_key_steps(index, length, BACK, visit, 0)
        dm[here, Q_COLS] = unstack_heads(dqt[...].T) * (1.0 / math.sqrt(HEAD))
        return carry

    lax.fori_loop(0, (length + BACK - 1) // BACK, query_step, 0)

    @pl.when(pl.program_id(0) == 0)
    def _():
        gt_ref[...] = jnp.zeros(gt_ref.shape, F32)

    sums = [jnp.zeros((1, 3 * WIDE), F32) for _ in range(3)]
    for tile in range(tiles):
        begin = tile * TILE
        total = taps[0:1] * dm[begin : begin + TILE]
        total += taps[1:2] * dm[begin + 1 : begin + 1 + TILE]
        total += taps[2:3] * dm[begin + 2 : begin + 2 + TILE]
        dp_ref[begin : begin + TILE] = total.astype(BF16)
        for tap in range(3):
            behind = wide[begin + 8 - tap : begin + 8 - tap + TILE]
            sums[tap] += jnp.sum(dm[begin : begin + TILE] * behind, axis=0, keepdims=True)
    width = gt_ref.shape[1] // 3
    for tap in range(3):
        for part in range(3):
            cols = pl.ds(pl.multiple_of(part * width + pair * WIDE, WIDE), WIDE)
            gt_ref[tap : tap + 1, cols] += sums[tap][:, part * WIDE : (part + 1) * WIDE]


def attend_back(lengths, proj, taps, attended, d_attended, lse, count):
    slots, rows = proj.shape[:2]
    steps = rows // BACK
    own = lambda i, lengths: (i, 0, 0)
    whole = lambda i, lengths: (0, 0)
    return pl.pallas_call(
        functools.partial(attend_back_kernel, lengths.shape[0], count),
        grid_spec=pltpu.PrefetchScalarGridSpec(
            num_scalar_prefetch=1,
            grid=(slots,),
            in_specs=[
                pl.BlockSpec((1, rows, 3 * WIDE), own),
                pl.BlockSpec(taps.shape, whole),
                pl.BlockSpec((1, rows, WIDE), own),
                pl.BlockSpec((1, rows, WIDE), own),
                pl.BlockSpec((1,) + lse.shape[1:], own),
            ],
            out_specs=[
                pl.BlockSpec((1, rows, 3 * WIDE), own),
                pl.BlockSpec((8, taps.shape[1]), whole),
            ],
            scratch_shapes=[
                pltpu.VMEM((8, 3 * WIDE), F32),
                pltpu.VMEM((rows + 8, 3 * WIDE), F32),
                pltpu.VMEM((rows, WIDE), BF16),
                pltpu.VMEM((rows, WIDE), BF16),
                pltpu.VMEM((rows, WIDE), BF16),
                pltpu.VMEM((steps, WIDE, BACK), BF16),
                pltpu.VMEM((rows + 8, 3 * WIDE), F32),
                pltpu.VMEM((WIDE, 2 * BACK), F32),
                pltpu.VMEM((BACK, 2 * BACK), F32),
                pltpu.VMEM((BACK, 2 * BACK), F32),
                pltpu.VMEM((BACK, 2 * BACK), BF16),
                pltpu.VMEM((BACK, 2 * BACK), BF16),
            ],
        ),
        out_shape=[
            jax.ShapeDtypeStruct((slots, rows, 3 * WIDE), BF16),
            jax.ShapeDtypeStruct((8, taps.shape[1]), F32),
        ],
        compiler_params=params(),
        name="attend_back",
    )(lengths, proj, taps, attended, d_attended, lse)


def dense_kernel(
    x_ref, att_ref, cot_ref, mask_ref, lengths, gain_ref, wo_ref, wu_ref, wd_ref,
    out_ref, dh_ref, datt_ref, n2_ref, sq_ref, du_ref, da_ref, cz_ref, gain_grad_ref, stats_ref,
    act_sc, att_sc,
):
    rows, width = x_ref.shape[1:]
    hidden_units = wu_ref.shape[1]
    step = width
    for pair in range(PAIRS):
        att_sc[:, pair * WIDE : (pair + 1) * WIDE] = att_ref[pair]
    group = pl.program_id(0)
    spot = lax.axis_index("seq") * rows + lax.broadcasted_iota(jnp.int32, (1, rows), 1)
    counts = jnp.where(spot < lengths[group], mask_ref[pl.ds(group, 1)].astype(F32), 0.0)
    weight = jnp.broadcast_to(counts, (WIDE, rows)).T[:, :1]
    gain = gain_row(gain_ref)
    branch = mm(att_sc[...], wo_ref[...])
    hidden = x_ref[0].astype(F32) + branch
    factor = lax.rsqrt(jnp.mean(hidden * hidden, axis=-1, keepdims=True) + 1e-06)
    normed = (hidden * factor * gain).astype(BF16)
    n2_ref[0] = normed
    total = jnp.zeros((rows, width), F32)
    for begin in range(0, hidden_units, step):
        cols = slice(begin, begin + step)
        active = jnp.maximum(mm(normed, wu_ref[:, cols]), 0.0)
        act_sc[:, cols] = active
        squared = (active * active).astype(BF16)
        sq_ref[0, :, cols] = squared
        total += mm(squared, wd_ref[cols])
    full = hidden + total
    out_ref[0] = full.astype(BF16)

    def masked(values):
        per_row = jnp.sum(values * values, axis=-1, keepdims=True)
        return jnp.sum(weight * per_row, axis=0, keepdims=True)

    @pl.when(pl.program_id(0) == 0)
    def _():
        stats_ref[...] = jnp.zeros(stats_ref.shape, F32)
        gain_grad_ref[...] = jnp.zeros(gain_grad_ref.shape, F32)

    parts = [masked(full), masked(branch), masked(total), jnp.sum(weight, axis=0, keepdims=True)]
    for place, part in enumerate(parts):
        stats_ref[place : place + 1] += jnp.broadcast_to(part, (1, WIDE))
    cotangent = (cot_ref[0].astype(F32) * weight).astype(BF16)
    cz_ref[0] = cotangent
    d_normed = jnp.zeros((rows, width), F32)
    for begin in range(0, hidden_units, step):
        cols = slice(begin, begin + step)
        d_squared = mm_nt(cotangent, wd_ref[cols])
        d_up = (2.0 * act_sc[:, cols] * d_squared).astype(BF16)
        du_ref[0, :, cols] = d_up
        d_normed += mm_nt(d_up, wu_ref[:, cols])
    weighted = d_normed * gain
    inner = jnp.mean(weighted * hidden, axis=-1, keepdims=True)
    d_hidden = cotangent.astype(F32) + factor * weighted - hidden * (factor * factor * factor) * inner
    gain_grad_ref[...] += jnp.sum(d_normed * hidden * factor, axis=0, keepdims=True)
    dh_ref[0] = d_hidden
    d_attn = d_hidden.astype(BF16)
    da_ref[0] = d_attn
    d_att = mm_nt(d_attn, wo_ref[...]).astype(BF16)
    for pair in range(PAIRS):
        datt_ref[pair] = d_att[:, pair * WIDE : (pair + 1) * WIDE]


def dense_send_kernel(
    x_ref, att_ref, cot_ref, mask_ref, lengths, gain_ref, wo_ref, wu_ref, wd_ref,
    out_ref, dh_ref, inbox, n2_ref, sq_ref, du_ref, da_ref, cz_ref, gain_grad_ref, stats_ref,
    act_sc, att_sc, d_blocks, out_s, out_r,
):
    group = pl.program_id(0)
    out_sems = (out_s, out_r)
    pl.when(group == 0)(meet_group)
    here = pl.ds(group * PAIRS, PAIRS)
    dense_kernel(
        x_ref, att_ref, cot_ref, mask_ref, lengths, gain_ref, wo_ref, wu_ref, wd_ref,
        out_ref, dh_ref, d_blocks.at[here], n2_ref, sq_ref, du_ref, da_ref, cz_ref, gain_grad_ref,
        stats_ref, act_sc, att_sc,
    )
    for pair in range(PAIRS):
        send_unit(d_blocks, inbox, out_sems, group * PAIRS + pair)
    pl.when(group == pl.num_programs(0) - 1)(lambda: wait_units(d_blocks, inbox, out_sems))


def dense_send(x, attended, grad_output, token_mask, lengths, gain, w_out, w_up, w_down):
    groups, rows, width = x.shape
    hidden_units = w_up.shape[1]
    slots = groups * PAIRS // GROUP
    per_group = lambda s: (s, 0, 0)
    fixed = lambda s: (0, 0)
    once = pl.Buffered(1)
    anywhere = pl.BlockSpec(memory_space=pl.ANY)
    row_block = pl.BlockSpec((1, rows, width), per_group)
    wide_block = pl.BlockSpec((1, rows, hidden_units), per_group)
    low = jax.ShapeDtypeStruct(x.shape, BF16)
    wide_low = jax.ShapeDtypeStruct((groups, rows, hidden_units), BF16)
    unit_rows = (groups * PAIRS, rows, WIDE)
    return pl.pallas_call(
        dense_send_kernel,
        grid=(groups,),
        in_specs=[
            row_block,
            pl.BlockSpec((PAIRS, rows, WIDE), per_group),
            row_block,
            pl.BlockSpec(token_mask.shape, fixed),
            pl.BlockSpec(memory_space=pltpu.SMEM),
            pl.BlockSpec((width,), lambda s: (0,)),
            pl.BlockSpec(w_out.shape, fixed, pipeline_mode=once),
            pl.BlockSpec(w_up.shape, fixed, pipeline_mode=once),
            pl.BlockSpec(w_down.shape, fixed, pipeline_mode=once),
        ],
        out_specs=[
            row_block,
            row_block,
            anywhere,
            row_block,
            wide_block,
            wide_block,
            row_block,
            row_block,
            pl.BlockSpec((1, width), fixed),
            pl.BlockSpec((8, WIDE), fixed),
        ],
        out_shape=[
            low,
            jax.ShapeDtypeStruct(x.shape, F32),
            jax.ShapeDtypeStruct((slots, GROUP, rows, WIDE), BF16),
            low,
            wide_low,
            wide_low,
            low,
            low,
            jax.ShapeDtypeStruct((1, width), F32),
            jax.ShapeDtypeStruct((8, WIDE), F32),
        ],
        scratch_shapes=[
            pltpu.VMEM((rows, hidden_units), F32),
            pltpu.VMEM((rows, width), BF16),
            pltpu.VMEM(unit_rows, BF16),
            DMA((groups * PAIRS,)),
            DMA((slots, GROUP)),
        ],
        compiler_params=group_params(2),
        name="dense_send",
    )(x, attended, grad_output, token_mask, lengths, gain, w_out, w_up, w_down)


def dense(x, attended, grad_output, token_mask, lengths, gain, w_out, w_up, w_down):
    groups, rows, width = x.shape
    hidden_units = w_up.shape[1]
    per_group = lambda s: (s, 0, 0)
    fixed = lambda s: (0, 0)
    once = pl.Buffered(1)
    row_block = pl.BlockSpec((1, rows, width), per_group)
    wide_block = pl.BlockSpec((1, rows, hidden_units), per_group)
    unit_block = pl.BlockSpec((PAIRS, rows, WIDE), per_group)
    low = jax.ShapeDtypeStruct(x.shape, BF16)
    wide_low = jax.ShapeDtypeStruct((groups, rows, hidden_units), BF16)
    return pl.pallas_call(
        dense_kernel,
        grid=(groups,),
        in_specs=[
            row_block,
            unit_block,
            row_block,
            pl.BlockSpec(token_mask.shape, fixed),
            pl.BlockSpec(memory_space=pltpu.SMEM),
            pl.BlockSpec((width,), lambda s: (0,)),
            pl.BlockSpec(w_out.shape, fixed, pipeline_mode=once),
            pl.BlockSpec(w_up.shape, fixed, pipeline_mode=once),
            pl.BlockSpec(w_down.shape, fixed, pipeline_mode=once),
        ],
        out_specs=[
            row_block,
            row_block,
            unit_block,
            row_block,
            wide_block,
            wide_block,
            row_block,
            row_block,
            pl.BlockSpec((1, width), fixed),
            pl.BlockSpec((8, WIDE), fixed),
        ],
        out_shape=[
            low,
            jax.ShapeDtypeStruct(x.shape, F32),
            jax.ShapeDtypeStruct((groups * PAIRS, rows, WIDE), BF16),
            low,
            wide_low,
            wide_low,
            low,
            low,
            jax.ShapeDtypeStruct((1, width), F32),
            jax.ShapeDtypeStruct((8, WIDE), F32),
        ],
        scratch_shapes=[pltpu.VMEM((rows, hidden_units), F32), pltpu.VMEM((rows, width), BF16)],
        compiler_params=params(),
        name="dense",
    )(x, attended, grad_output, token_mask, lengths, gain, w_out, w_up, w_down)


PART = 384


def feed_grads_kernel(sq_ref, cz_ref, n2_ref, du_ref, att_ref, da_ref, out_ref, n2_t):
    half, sub = pl.program_id(0), pl.program_id(1)
    groups, rows, width = n2_ref.shape
    tokens = groups * rows

    @pl.when((half == 0) & (sub == 0))
    def _():
        for group in range(groups):
            n2_t[:, group * rows : (group + 1) * rows] = n2_ref[group].astype(F32).T.astype(BF16)

    down = mm_tn(sq_ref[...].reshape(tokens, PART), cz_ref[...].reshape(tokens, width))
    for place in range(4):
        for side in range(2):
            out_ref[place, pl.ds(sub, 1), side * 96 : side * 96 + 96] = down[
                place * 96 : (place + 1) * 96, side * PART : (side + 1) * PART
            ].astype(BF16)[None]
    up = mm(n2_t[...], du_ref[...].reshape(tokens, PART))
    out_ref[pl.ds(sub, 1), :, 192:384] = up.astype(BF16).reshape(1, 4, 192, PART)

    @pl.when(sub == 0)
    def _():
        for pair in range(PAIRS):
            block = mm_tn(
                att_ref[:, pair].reshape(tokens, WIDE), da_ref[...].reshape(tokens, PART)
            ).astype(BF16)
            for low in range(0, WIDE, 16):
                row = pair * WIDE + low
                batch, inner = row // 192, row % 192
                out_ref[inner // 48, batch, 384 + inner % 48 : 400 + inner % 48] = block[low : low + 16]


def feed_grads(squared, cotangent, normed2, d_up, attended, d_attn):
    groups, rows, width = normed2.shape
    whole = lambda h, b: (0, 0, 0)
    return pl.pallas_call(
        feed_grads_kernel,
        grid=(2, 4),
        in_specs=[
            pl.BlockSpec((groups, rows, PART), lambda h, b: (0, 0, 2 * b + h)),
            pl.BlockSpec((groups, rows, width), whole, pipeline_mode=pl.Buffered(1)),
            pl.BlockSpec((groups, rows, width), whole, pipeline_mode=pl.Buffered(1)),
            pl.BlockSpec((groups, rows, PART), lambda h, b: (0, 0, 4 * h + b)),
            pl.BlockSpec(
                (groups, PAIRS, rows, WIDE), lambda h, b: (0, 0, 0, 0), pipeline_mode=pl.Buffered(1)
            ),
            pl.BlockSpec((groups, rows, PART), lambda h, b: (0, 0, h)),
        ],
        out_specs=pl.BlockSpec((4, 4, 432, PART), lambda h, b: (h, 0, 0, 0)),
        out_shape=jax.ShapeDtypeStruct((8, 4, 432, PART), BF16),
        scratch_shapes=[pltpu.VMEM((width, groups * rows), BF16)],
        compiler_params=params(),
        name="feed_grads",
    )(squared, cotangent, normed2, d_up, attended.reshape(groups, PAIRS, rows, WIDE), d_attn)


def feed_grads_send_kernel(
    sq_ref, cz_ref, n2_ref, du_ref, att_ref, da_ref, sum_ref,
    n2_t, pieces, core_in, down_s, down_r, up_s, up_r, out_s, out_r,
):
    half, sub = pl.program_id(0), pl.program_id(1)
    me = lax.axis_index("seq")
    core = lax.rem(me, 2)
    other = 1 - core

    @pl.when((half == 0) & (sub == 0))
    def _():
        barrier = pltpu.get_barrier_semaphore()
        pl.semaphore_signal(barrier, inc=1, device_id={"seq": me ^ 1}, device_id_type=MESH)
        pl.semaphore_wait(barrier, 1)

    feed_grads_kernel(
        sq_ref, cz_ref, n2_ref, du_ref, att_ref, da_ref, pieces.at[pl.ds(half * 4, 4)], n2_t
    )

    def down(part, batch, side):
        chip = part * 2 + side
        return remote(
            pieces.at[chip * 2 + other, batch, 0:192],
            core_in.at[chip, batch, 0:192],
            (down_s.at[part, batch, side], down_r.at[part, batch, side]),
            "seq",
            me ^ 1,
        )

    def up(chip):
        return remote(
            pieces.at[chip * 2 + other, :, 192:384],
            core_in.at[chip, :, 192:384],
            (up_s.at[chip], up_r.at[chip]),
            "seq",
            me ^ 1,
        )

    def out(chip):
        return remote(
            pieces.at[chip * 2 + other, :, 384:432],
            core_in.at[chip, :, 384:432],
            (out_s.at[chip], out_r.at[chip]),
            "seq",
            me ^ 1,
        )

    for side in range(2):
        down(half, sub, side).start()

    @pl.when(sub == 0)
    def _():
        for side in range(2):
            out(half * 2 + side).start()

    @pl.when(lax.rem(sub, 2) == other)
    def _():
        up(half * 2 + sub // 2).start()

    @pl.when((half == 1) & (sub == 3))
    def _():
        for part in range(2):
            for side in range(2):
                chip = part * 2 + side
                for batch in range(4):
                    down(part, batch, side).wait()
                up(chip).wait()
                out(chip).wait()
                for batch in range(4):
                    both = pieces[chip * 2 + core, batch].astype(F32) + core_in[chip, batch].astype(F32)
                    sum_ref[chip, batch] = both.astype(BF16)


def feed_grads_send(squared, cotangent, normed2, d_up, attended, d_attn):
    groups, rows, width = normed2.shape
    whole = lambda h, b: (0, 0, 0)
    once = pl.Buffered(1)
    quarter = (4, 4, 432, PART)
    return pl.pallas_call(
        feed_grads_send_kernel,
        grid=(2, 4),
        in_specs=[
            pl.BlockSpec((groups, rows, PART), lambda h, b: (0, 0, 2 * b + h)),
            pl.BlockSpec((groups, rows, width), whole, pipeline_mode=once),
            pl.BlockSpec((groups, rows, width), whole, pipeline_mode=once),
            pl.BlockSpec((groups, rows, PART), lambda h, b: (0, 0, 4 * h + b)),
            pl.BlockSpec((groups, PAIRS, rows, WIDE), lambda h, b: (0, 0, 0, 0), pipeline_mode=once),
            pl.BlockSpec((groups, rows, PART), lambda h, b: (0, 0, h)),
        ],
        out_specs=pl.BlockSpec(quarter, lambda h, b: (0, 0, 0, 0), pipeline_mode=once),
        out_shape=jax.ShapeDtypeStruct(quarter, BF16),
        scratch_shapes=[
            pltpu.VMEM((width, groups * rows), BF16),
            pltpu.VMEM((8, 4, 432, PART), BF16),
            pltpu.VMEM(quarter, BF16),
            DMA((2, 4, 2)),
            DMA((2, 4, 2)),
            DMA((4,)),
            DMA((4,)),
            DMA((4,)),
            DMA((4,)),
        ],
        compiler_params=group_params(3),
        name="feed_grads_send",
    )(squared, cotangent, normed2, d_up, attended.reshape(groups, PAIRS, rows, WIDE), d_attn)


def input_grads_kernel(
    dp_ref, n1_ref, x_ref, dh_ref, w_ref, gain_ref, out_ref, gx_ref, gain_grad_ref, n1_t, total, w_sc
):
    pair = pl.program_id(0)
    groups, rows, width = n1_ref.shape
    tokens = groups * rows

    @pl.when(pair == 0)
    def _():
        for group in range(groups):
            n1_t[:, group * rows : (group + 1) * rows] = n1_ref[group].astype(F32).T.astype(BF16)
        total[...] = jnp.zeros(total.shape, F32)

    d_proj = dp_ref[...].reshape(tokens, 3 * WIDE)
    grad = mm(n1_t[...], d_proj).astype(BF16)
    for batch in range(4):
        for chip in range(4):
            begin = batch * 192 + chip * 48
            out_ref[0, 0, chip, batch] = grad[begin : begin + 48]
    for part in range(3):
        cols = pl.ds(pl.multiple_of(part * width + pair * WIDE, WIDE), WIDE)
        w_sc[:, part * WIDE : (part + 1) * WIDE] = w_ref[:, cols]
    total[...] += mm_nt(d_proj, w_sc[...])

    @pl.when(pair == PAIRS - 1)
    def _():
        gain = gain_row(gain_ref)
        gain_sum = jnp.zeros((1, width), F32)
        for group in range(groups):
            x = x_ref[group].astype(F32)
            d_normed = total[group * rows : (group + 1) * rows]
            factor = lax.rsqrt(jnp.mean(x * x, axis=-1, keepdims=True) + 1e-06)
            weighted = d_normed * gain
            inner = jnp.mean(weighted * x, axis=-1, keepdims=True)
            gx_ref[group] = (
                dh_ref[group] + factor * weighted - x * (factor * factor * factor) * inner
            )
            gain_sum += jnp.sum(d_normed * x * factor, axis=0, keepdims=True)
        gain_grad_ref[...] = gain_sum


def input_grads(d_proj, normed1, x, d_hidden, w_qkv, gain):
    groups, rows, width = x.shape
    whole = lambda p: (0, 0, 0)
    once = pl.Buffered(1)
    tokens = pl.BlockSpec((groups, rows, width), whole, pipeline_mode=once)
    return pl.pallas_call(
        input_grads_kernel,
        grid=(PAIRS,),
        in_specs=[
            pl.BlockSpec((groups, 1, rows, 3 * WIDE), lambda p: (0, p, 0, 0)),
            tokens,
            tokens,
            tokens,
            pl.BlockSpec(w_qkv.shape, lambda p: (0, 0), pipeline_mode=once),
            pl.BlockSpec((width,), lambda p: (0,)),
        ],
        out_specs=[
            pl.BlockSpec((1, 1, 4, 4, 48, PART), lambda p: (p % 3, p // 3, 0, 0, 0, 0)),
            tokens,
            pl.BlockSpec((1, width), lambda p: (0, 0)),
        ],
        out_shape=[
            jax.ShapeDtypeStruct((3, 2, 4, 4, 48, PART), BF16),
            jax.ShapeDtypeStruct(x.shape, F32),
            jax.ShapeDtypeStruct((1, width), F32),
        ],
        scratch_shapes=[
            pltpu.VMEM((width, groups * rows), BF16),
            pltpu.VMEM((groups * rows, width), F32),
            pltpu.VMEM((width, 3 * WIDE), BF16),
        ],
        compiler_params=params(),
        name="input_grads",
    )(d_proj.reshape(groups, PAIRS, rows, 3 * WIDE), normed1, x, d_hidden, w_qkv, gain)


def finish_kernel(
    units_ref, n1_ref, x_ref, dh_ref, w_ref, gain_ref, feed_ref, gt_ref, gain2_ref, stats_ref,
    gx_ref, qkv_out, feed_out, small_out,
    dp_in, n1_v, n1_t, x_v, dh_v, w_v, feed_v, dn, grads, pieces,
    core_in, here, chip_in, mine, z_in, qkv_all, feed_mine, feed_in, feed_all,
    row_own, row_in, row_sum, col_in,
    load_s, dp_s, dp_r, core_s, core_r, chip_s, chip_r, z_s, z_r, qkv_s, qkv_r, fz_s, fz_r, fa_s, fa_r,
    row_s, row_r, col_s, col_r,
):
    me = lax.axis_index("seq")
    z = lax.axis_index("batch")
    core, chip = lax.rem(me, 2), me // 2
    groups, block, width = n1_v.shape
    tokens = groups * block
    middle = tokens // 2
    chunks = pieces.shape[0]
    slots = units_ref.shape[0]
    rows = feed_in.shape[2]
    barrier = pltpu.get_barrier_semaphore()
    for bit in range(1, 8):
        pl.semaphore_signal(barrier, inc=1, device_id={"seq": me ^ bit}, device_id_type=MESH)
    for bit in range(1, 4):
        pl.semaphore_signal(barrier, inc=1, device_id={"batch": z ^ bit}, device_id_type=MESH)
    pl.semaphore_wait(barrier, 10)

    def send(source, target, sems, axis, peer):
        copy = remote(source, target, sems, axis, peer)
        copy.start()
        return copy

    def spread(ref, s, r):
        return [
            send(ref.at[me], ref.at[me], (s.at[step], r.at[step]), "seq", me ^ max(2 * step, 1))
            for step in range(4)
        ]

    def relay(ref, first, s, r):
        more = []
        for step in range(1, 4):
            first[step].wait()
            slot = me ^ (2 * step)
            more.append(
                send(ref.at[slot], ref.at[slot], (s.at[3 + step], r.at[3 + step]), "seq", me ^ 1)
            )
        return [first[0]] + more

    for slot in range(slots):
        send_blocks(units_ref, dp_in, (dp_s, dp_r), slot)
    loads = [
        pltpu.make_async_copy(source, target, load_s.at[place])
        for place, (source, target) in enumerate(
            [(feed_ref, feed_v), (n1_ref, n1_v), (w_ref, w_v), (x_ref, x_v), (dh_ref, dh_v)]
        )
    ]
    for copy in loads:
        copy.start()

    loads[0].wait()
    for batch in range(4):
        both = feed_v[0, batch].astype(F32)
        for q in range(1, 4):
            both = both + feed_v[q, batch].astype(F32)
        feed_mine[batch] = both.astype(BF16)
    feed_z = [
        [
            send(
                feed_mine.at[z ^ bit, c * rows : (c + 1) * rows],
                feed_in.at[c, bit - 1],
                (fz_s.at[c, bit - 1], fz_r.at[c, bit - 1]),
                "batch",
                z ^ bit,
            )
            for bit in range(1, 4)
        ]
        for c in range(chunks)
    ]
    loads[1].wait()
    for group in range(groups):
        n1_t[:, group * block : (group + 1) * block] = n1_v[group].astype(F32).T.astype(BF16)
    for copy in loads[2:]:
        copy.wait()
    gain = gain_row(gain_ref)

    def unit_rows(pair, first):
        return jnp.concatenate(
            [dp_in[(first + more) * PAIRS + pair] for more in range(groups // 2)], axis=0
        )

    def pair_weights(pair):
        return jnp.concatenate(
            [
                w_v[:, pl.ds(pl.multiple_of(part * width + pair * WIDE, WIDE), WIDE)]
                for part in range(3)
            ],
            axis=1,
        )

    def input_half(first):
        gain_sum = jnp.zeros((1, width), F32)
        for more in range(groups // 2):
            group = first + more
            x = x_v[group].astype(F32)
            d_normed = dn[group * block : (group + 1) * block]
            factor = lax.rsqrt(jnp.mean(x * x, axis=-1, keepdims=True) + 1e-06)
            weighted = d_normed * gain
            inner = jnp.mean(weighted * x, axis=-1, keepdims=True)
            dh_v[group] += factor * weighted - x * (factor * factor * factor) * inner
            gain_sum += jnp.sum(d_normed * x * factor, axis=0, keepdims=True)
        return gain_sum

    for slot in range(slots):
        if (slot * GROUP) // PAIRS < groups // 2:
            wait_blocks(units_ref, dp_in, (dp_s, dp_r), slot)
    dn[...] = jnp.zeros(dn.shape, F32)

    def first_half(pair, carry):
        d_rows = unit_rows(pair, 0)
        grads[pair] = mm(n1_t[:, :middle], d_rows)
        dn[:middle] += mm_nt(d_rows, pair_weights(pair))
        return carry

    lax.fori_loop(0, PAIRS, first_half, 0)
    gain_sum = input_half(0)
    for slot in range(slots):
        if (slot * GROUP) // PAIRS >= groups // 2:
            wait_blocks(units_ref, dp_in, (dp_s, dp_r), slot)

    feed_first = []
    for c in range(chunks):
        for copy in feed_z[c]:
            copy.wait()
        both = feed_mine[z, c * rows : (c + 1) * rows].astype(F32)
        for bit in range(3):
            both = both + feed_in[c, bit].astype(F32)
        feed_all[c, pl.ds(me, 1)] = both.astype(BF16)[None]
        feed_first.append(spread(feed_all.at[c], fa_s.at[c], fa_r.at[c]))

    to_core, to_chip = [], []

    def pass_on(c):
        to_core[c].wait()
        for q in range(4):
            both = pieces[c, core, q].astype(F32) + core_in[c, q].astype(F32)
            here[c, q] = both.astype(BF16)
        to_chip.append(
            [
                send(
                    here.at[c, chip ^ bit],
                    chip_in.at[c, bit - 1],
                    (chip_s.at[c, bit - 1], chip_r.at[c, bit - 1]),
                    "seq",
                    me ^ (2 * bit),
                )
                for bit in range(1, 4)
            ]
        )

    for c in range(chunks):

        def second_half(side, carry, c=c):
            pair = side * chunks + c
            grad = (grads[pair] + mm(n1_t[:, middle:], unit_rows(pair, groups // 2))).astype(BF16)
            for batch in range(4):
                for q in range(4):
                    begin = batch * 192 + q * 48
                    pieces[c, side, q, batch] = grad[begin : begin + 48]
            return carry

        lax.fori_loop(0, 2, second_half, 0)
        to_core.append(
            send(
                pieces.at[c, 1 - core], core_in.at[c], (core_s.at[c], core_r.at[c]), "seq", me ^ 1
            )
        )
        if c > 0:
            pass_on(c - 1)

    def second_rows(pair, carry):
        dn[middle:] += mm_nt(unit_rows(pair, groups // 2), pair_weights(pair))
        return carry

    lax.fori_loop(0, 2, second_rows, 0)
    pass_on(chunks - 1)
    lax.fori_loop(2, PAIRS, second_rows, 0)
    gain_sum = gain_sum + input_half(groups // 2)
    gx_copy = pltpu.make_async_copy(dh_v, gx_ref, load_s.at[len(loads)])
    gx_copy.start()
    row_own[...] = jnp.zeros(row_own.shape, F32)
    for tap in range(3):
        for part in range(3):
            row = tap * 3 + part
            row_own[row : row + 1] = gt_ref[tap : tap + 1, part * width : (part + 1) * width]
    row_own[9:10] = gain_sum
    row_own[10:11] = gain2_ref[...]
    for place in range(4):
        row_own[11:12, place * WIDE : (place + 1) * WIDE] = stats_ref[place : place + 1]
    row_in[pl.ds(me, 1)] = row_own[...][None]
    rows_out = [
        send(row_own, row_in.at[me], (row_s.at[bit - 1], row_r.at[bit - 1]), "seq", me ^ bit)
        for bit in range(1, 8)
    ]
    to_z = []
    for c in range(chunks):
        for copy in to_chip[c]:
            copy.wait()
        both = here[c, chip].astype(F32)
        for bit in range(3):
            both = both + chip_in[c, bit].astype(F32)
        mine[c] = both.astype(BF16)
        to_z.append(
            [
                send(
                    mine.at[c, z ^ bit],
                    z_in.at[c, bit - 1],
                    (z_s.at[c, bit - 1], z_r.at[c, bit - 1]),
                    "batch",
                    z ^ bit,
                )
                for bit in range(1, 4)
            ]
        )
    for copy in rows_out:
        copy.wait()
    total = row_in[0]
    for place in range(1, 8):
        total = total + row_in[place]
    row_sum[...] = total
    col_in[pl.ds(z, 1)] = total[None]
    cols_out = [
        send(row_sum, col_in.at[z], (col_s.at[bit - 1], col_r.at[bit - 1]), "batch", z ^ bit)
        for bit in range(1, 4)
    ]
    last = []
    for c in range(chunks):
        last += relay(feed_all.at[c], feed_first[c], fa_s.at[c], fa_r.at[c])
    qkv_first = []
    for c in range(chunks):
        for copy in to_z[c]:
            copy.wait()
        both = mine[c, z].astype(F32)
        for bit in range(3):
            both = both + z_in[c, bit].astype(F32)
        qkv_all[c, pl.ds(me, 1)] = both.astype(BF16)[None]
        qkv_first.append(spread(qkv_all.at[c], qkv_s.at[c], qkv_r.at[c]))
    for c in range(chunks):
        last += relay(qkv_all.at[c], qkv_first[c], qkv_s.at[c], qkv_r.at[c])
    for copy in cols_out:
        copy.wait()
    small_out[...] = ((col_in[0] + col_in[1]) + col_in[2]) + col_in[3]
    for copy in last:
        copy.wait()
    qkv_out[...] = qkv_all[...]
    feed_out[...] = feed_all[...]
    gx_copy.wait()


def finish(units, normed1, x, d_hidden, w_qkv, gain, feed, grad_taps, grad_norm2, stats):
    groups, block, width = x.shape
    chunks, rows, feed_rows = 3, 48, 144
    small_shape = (16, width)
    tokens = groups * block
    slots = units.shape[0]
    vmem = pl.BlockSpec(memory_space=pltpu.VMEM)
    anywhere = pl.BlockSpec(memory_space=pl.ANY)
    pairs = [DMA((slots, GROUP)), DMA((slots, GROUP))]
    for shape in [(), (3,), (3,), (7,), (3,), (7,)]:
        pairs += [DMA((chunks,) + shape), DMA((chunks,) + shape)]
    low = lambda *shape: pltpu.VMEM(shape, BF16)
    return pl.pallas_call(
        finish_kernel,
        in_specs=[anywhere] * 5 + [vmem, anywhere] + [vmem] * 3,
        out_specs=[anywhere, vmem, vmem, vmem],
        out_shape=[
            jax.ShapeDtypeStruct(x.shape, F32),
            jax.ShapeDtypeStruct((chunks, 8, rows, PART), BF16),
            jax.ShapeDtypeStruct((chunks, 8, feed_rows, PART), BF16),
            jax.ShapeDtypeStruct(small_shape, F32),
        ],
        scratch_shapes=[
            low(groups * PAIRS, block, 3 * WIDE),
            low(groups, block, width),
            low(width, tokens),
            low(groups, block, width),
            pltpu.VMEM((groups, block, width), F32),
            low(*w_qkv.shape),
            low(4, 4, chunks * feed_rows, PART),
            pltpu.VMEM((tokens, width), F32),
            pltpu.VMEM((PAIRS, width, 3 * WIDE), F32),
            low(chunks, 2, 4, 4, rows, PART),
            low(chunks, 4, 4, rows, PART),
            low(chunks, 4, 4, rows, PART),
            low(chunks, 3, 4, rows, PART),
            low(chunks, 4, rows, PART),
            low(chunks, 3, rows, PART),
            low(chunks, 8, rows, PART),
            low(4, chunks * feed_rows, PART),
            low(chunks, 3, feed_rows, PART),
            low(chunks, 8, feed_rows, PART),
            pltpu.VMEM(small_shape, F32),
            pltpu.VMEM((8,) + small_shape, F32),
            pltpu.VMEM(small_shape, F32),
            pltpu.VMEM((4,) + small_shape, F32),
            DMA((6,)),
        ]
        + pairs
        + [DMA((7,)), DMA((7,)), DMA((3,)), DMA((3,))],
        compiler_params=group_params(0),
        name="finish",
    )(units, normed1, x, d_hidden, w_qkv, gain, feed, grad_taps, grad_norm2, stats)


def unpack_kernel(
    feed_ref, qkv_ref, small_ref, down_ref, up_ref, out_ref, grad_ref, taps_ref, gain1_ref, gain2_ref, rms_ref
):
    down_ref[:, :PART] = feed_ref[0, 0, :96].astype(F32)
    down_ref[:48, PART:] = feed_ref[0, 0, 96:].astype(F32)
    down_ref[48:, PART:] = feed_ref[1, 0, :48].astype(F32)
    up_ref[:96] = feed_ref[1, 0, 48:].astype(F32)
    up_ref[96:] = feed_ref[2, 0, :96].astype(F32)
    out_ref[...] = feed_ref[2, 0, 96:].astype(F32)
    place = pl.program_id(0)

    def put(core):
        for c in range(3):
            for part in range(3):
                begin = part * PAIRS * WIDE + (core * 3 + c) * WIDE
                grad_ref[:, begin : begin + WIDE] = qkv_ref[
                    c, 0, :, part * WIDE : (part + 1) * WIDE
                ].astype(F32)

    for core in range(2):
        pl.when(place % 2 == core)(functools.partial(put, core))

    @pl.when(place == 0)
    def _():
        width = small_ref.shape[1]
        for tap in range(3):
            for part in range(3):
                row = tap * 3 + part
                taps_ref[tap : tap + 1, part * width : (part + 1) * width] = small_ref[row : row + 1]
        z = lax.axis_index("batch")
        for row, ref in ((9, gain1_ref), (10, gain2_ref)):
            own = jnp.zeros((1, width // 4), F32)
            for batch in range(4):
                share = small_ref[row : row + 1, batch * width // 4 : (batch + 1) * width // 4]
                own = jnp.where(z == batch, share, own)
            ref[...] = own
        count = small_ref[11:12, 3 * WIDE : 4 * WIDE]
        for place_ in range(3):
            total = small_ref[11:12, place_ * WIDE : (place_ + 1) * WIDE]
            rms_ref[place_ : place_ + 1] = jnp.sqrt(total / (width * count))


def unpack(feed, qkv, small):
    return pl.pallas_call(
        unpack_kernel,
        grid=(8,),
        in_specs=[
            pl.BlockSpec((3, 1, 144, PART), lambda r: (0, r, 0, 0)),
            pl.BlockSpec((3, 1, 48, PART), lambda r: (0, r, 0, 0)),
            pl.BlockSpec(small.shape, lambda r: (0, 0)),
        ],
        out_specs=[
            pl.BlockSpec((96, 2 * PART), lambda r: (r, 0)),
            pl.BlockSpec((192, PART), lambda r: (0, r)),
            pl.BlockSpec((48, PART), lambda r: (r % 4, r // 4)),
            pl.BlockSpec((48, 3 * PAIRS * WIDE), lambda r: (r // 2, 0)),
            pl.BlockSpec((3, 3 * PAIRS * WIDE), lambda r: (0, 0)),
            pl.BlockSpec((1, 192), lambda r: (0, 0)),
            pl.BlockSpec((1, 192), lambda r: (0, 0)),
            pl.BlockSpec((8, WIDE), lambda r: (0, 0)),
        ],
        out_shape=[
            jax.ShapeDtypeStruct((768, 2 * PART), F32),
            jax.ShapeDtypeStruct((192, 8 * PART), F32),
            jax.ShapeDtypeStruct((192, 2 * PART), F32),
            jax.ShapeDtypeStruct((192, 3 * PAIRS * WIDE), F32),
            jax.ShapeDtypeStruct((3, 3 * PAIRS * WIDE), F32),
            jax.ShapeDtypeStruct((1, 192), F32),
            jax.ShapeDtypeStruct((1, 192), F32),
            jax.ShapeDtypeStruct((8, WIDE), F32),
        ],
        compiler_params=params(),
        name="unpack",
    )(feed, qkv, small)


def exchange(blocks):
    return lax.all_to_all(blocks, "seq", 0, 0, tiled=True)


def plain_gradients(feed, qkv):
    down = feed[:, :, :192].reshape(8, 4, 2, 96, PART).transpose(1, 0, 3, 2, 4)
    up = feed[:, :, 192:384].transpose(1, 2, 0, 3)
    out = feed[:, :, 384:].reshape(2, 4, 4, 48, PART).transpose(2, 1, 3, 0, 4)
    grad = qkv.reshape(3, 2, 4, 4, 48, 3, WIDE).transpose(3, 2, 4, 5, 1, 0, 6)
    return (
        down.reshape(3072, 768),
        up.reshape(768, 3072),
        out.reshape(768, 768),
        grad.reshape(768, 2304),
    )


def shards(
    stream_in,
    lengths,
    token_mask,
    norm1_gain,
    w_qkv,
    conv_taps,
    w_out,
    norm2_gain,
    w_up,
    w_down,
    grad_output,
):
    groups, block_len, width = stream_in.shape
    count = lax.axis_size("seq")
    batches = lax.axis_size("batch")
    units = groups * PAIRS
    slots = -(-units // count)
    spare = slots * count - units
    fitted = count == GROUP and batches == 4 and units % GROUP == 0

    def to_heads(blocks):
        blocks = jnp.pad(blocks, ((0, spare), (0, 0), (0, 0)))
        blocks = blocks.reshape((slots, count) + blocks.shape[1:])
        return jnp.stack([exchange(blocks[slot]) for slot in range(slots)])

    def to_tokens(rows):
        rows = rows.reshape(slots, count, block_len, rows.shape[2])
        return jnp.concatenate([exchange(rows[slot]) for slot in range(slots)])[:units]

    rest = (grad_output, token_mask, lengths, norm2_gain, w_out, w_up, w_down)
    if fitted:
        normed1, proj, unit_out, attended, unit_lse = front(
            stream_in, norm1_gain, w_qkv, conv_taps, lengths
        )
        proj = proj.reshape(slots, count * block_len, 3 * WIDE)
        stream_out, d_hidden, d_units, *saved = dense_send(stream_in, attended, *rest)
    else:
        normed1, proj = project(stream_in, norm1_gain, w_qkv)
        proj = to_heads(proj).reshape(slots, count * block_len, 3 * WIDE)
        unit_out, unit_lse = attend(lengths, proj, conv_taps, count)
        attended = to_tokens(unit_out)
        stream_out, d_hidden, d_units, *saved = dense(stream_in, attended, *rest)
        d_units = to_heads(d_units)
    normed2, squared, d_up, d_attn, cotangent, grad_norm2, stats = saved
    d_units = d_units.reshape(slots, count * block_len, WIDE)
    saved = (squared, cotangent, normed2, d_up, attended, d_attn)
    if fitted:
        feed = feed_grads_send(*saved)
        same_core = [[core + 2 * chip for chip in range(4)] for core in range(2)]
        feed = lax.all_to_all(feed, "seq", 0, 0, tiled=True, axis_index_groups=same_core)
    else:
        feed = feed_grads(*saved)
    back, grad_taps = attend_back(lengths, proj, conv_taps, unit_out, d_units, unit_lse, count)

    if fitted:
        blocks = back.reshape(slots, count, block_len, 3 * WIDE)
        grad_input, qkv, feed, small = finish(
            blocks, normed1, stream_in, d_hidden, w_qkv, norm1_gain, feed, grad_taps, grad_norm2, stats
        )
        down, up, out, grad_qkv, taps, gain1, gain2, rms = unpack(feed, qkv, small)
        gain1, gain2, rms = gain1[0], gain2[0], rms[:3, 0]
    else:
        pieces, grad_input, grad_norm1 = input_grads(
            to_tokens(back), normed1, stream_in, d_hidden, w_qkv, norm1_gain
        )

        def reduce(gradient):
            share = lax.psum_scatter(gradient, ("batch", "seq"), scatter_dimension=0, tiled=True)
            return lax.all_gather(share, "seq", axis=0, tiled=True).astype(F32)

        down, up, out, grad_qkv = map(reduce, plain_gradients(feed, pieces))
        small = (grad_taps[:3], grad_norm1[0], grad_norm2[0], stats[:4, 0])
        taps, gain1, gain2, stats = lax.psum(small, ("seq", "batch"))
        share = width // batches
        begin = lax.axis_index("batch") * share
        gain1, gain2 = (lax.dynamic_slice_in_dim(gain, begin, share) for gain in (gain1, gain2))
        rms = jnp.sqrt(stats[:3] / (width * stats[3]))
    return (stream_out, grad_input, gain1, grad_qkv, taps, out, gain2, up, down, rms)


def solution(mesh):
    tokens = P("batch", "seq", None)
    return jax.shard_map(
        shards,
        mesh=mesh,
        in_specs=(
            tokens,
            P("batch"),
            P("batch", "seq"),
            P(),
            P(),
            P(),
            P(),
            P(),
            P(),
            P(),
            tokens,
        ),
        out_specs=(
            tokens,
            tokens,
            P("batch"),
            P("batch", None),
            P(),
            P("batch", None),
            P("batch"),
            P("batch", None),
            P("batch", None),
            P(),
        ),
        check_vma=False,
    )
```

```python
import functools
import math

import jax
import jax.numpy as jnp
from jax import lax
from jax.experimental import pallas as pl
from jax.experimental.pallas import tpu as pltpu
from jax.sharding import PartitionSpec as P

HEADS = 12
HEAD = 64
PAIRS = HEADS // 2
WIDE = 2 * HEAD
TILE = 256
ROWS = 512
BACK = 256
STRIP = 32
LIMIT = 62 << 20
NEG = -1e30
F32 = jnp.float32
BF16 = jnp.bfloat16


def mm(left_op, right_op):
    return jnp.dot(left_op, right_op, preferred_element_type=F32)


def mm_nt(left_op, right_op):
    return lax.dot_general(
        left_op, right_op, (((1,), (1,)), ((), ())), preferred_element_type=F32
    )


def mm_tn(left_op, right_op):
    return lax.dot_general(
        left_op, right_op, (((0,), (0,)), ((), ())), preferred_element_type=F32
    )


def params():
    return pltpu.CompilerParams(vmem_limit_bytes=LIMIT)


MESH = pl.DeviceIdType.MESH
GROUP = 8
DMA = pltpu.SemaphoreType.DMA


def remote(source, target, sems, axis, peer):
    return pltpu.make_async_remote_copy(
        src_ref=source,
        dst_ref=target,
        send_sem=sems[0],
        recv_sem=sems[1],
        device_id={axis: peer},
        device_id_type=MESH,
    )


def meet_group():
    me = lax.axis_index("seq")
    barrier = pltpu.get_barrier_semaphore()
    for bit in range(1, GROUP):
        pl.semaphore_signal(barrier, inc=1, device_id={"seq": me ^ bit}, device_id_type=MESH)
    pl.semaphore_wait(barrier, GROUP - 1)


def unit_copy(blocks, inbox, sems, unit):
    me = lax.axis_index("seq")
    owner, slot = lax.rem(unit, GROUP), unit // GROUP
    return owner, remote(
        blocks.at[unit],
        inbox.at[slot, me],
        (sems[0].at[unit], sems[1].at[slot, me ^ owner]),
        "seq",
        owner,
    )


def send_unit(blocks, inbox, sems, unit):
    me = lax.axis_index("seq")
    owner, copy = unit_copy(blocks, inbox, sems, unit)

    @pl.when(owner != me)
    def _():
        copy.start()

    @pl.when(owner == me)
    def _():
        slot = unit // GROUP
        pltpu.make_async_copy(blocks.at[unit], inbox.at[slot, me], sems[1].at[slot, 0]).start()


def wait_unit(blocks, inbox, sems, slot):
    me = lax.axis_index("seq")
    unit = slot * GROUP + me
    pltpu.make_async_copy(blocks.at[unit], inbox.at[slot, me], sems[1].at[slot, 0]).wait()
    for bit in range(1, GROUP):
        remote(
            blocks.at[unit],
            inbox.at[slot, me ^ bit],
            (sems[0].at[unit], sems[1].at[slot, bit]),
            "seq",
            me ^ bit,
        ).wait_recv()


def wait_sent(blocks, inbox, sems):
    me = lax.axis_index("seq")

    def one(unit, carry):
        owner, copy = unit_copy(blocks, inbox, sems, unit)
        pl.when(owner != me)(copy.wait_send)
        return carry

    lax.fori_loop(0, blocks.shape[0], one, 0)


def wait_units(blocks, inbox, sems):
    for slot in range(blocks.shape[0] // GROUP):
        wait_unit(blocks, inbox, sems, slot)
    wait_sent(blocks, inbox, sems)


def block_copies(units, inbox, sems, slot):
    me = lax.axis_index("seq")
    return [
        remote(
            units.at[slot, me ^ bit],
            inbox.at[slot * GROUP + me],
            (sems[0].at[slot, bit], sems[1].at[slot, bit]),
            "seq",
            me ^ bit,
        )
        for bit in range(1, GROUP)
    ]


def own_block(units, inbox, sems, slot):
    me = lax.axis_index("seq")
    return pltpu.make_async_copy(
        units.at[slot, me], inbox.at[slot * GROUP + me], sems[1].at[slot, 0]
    )


def send_blocks(units, inbox, sems, slot):
    own_block(units, inbox, sems, slot).start()
    for copy in block_copies(units, inbox, sems, slot):
        copy.start()


def wait_blocks(units, inbox, sems, slot):
    own_block(units, inbox, sems, slot).wait()
    for copy in block_copies(units, inbox, sems, slot):
        copy.wait()


def group_params(number):
    return pltpu.CompilerParams(
        collective_id=number, has_side_effects=True, vmem_limit_bytes=LIMIT
    )


def gain_row(gain_ref):
    return gain_ref[...].astype(F32).reshape(1, gain_ref.shape[0])


def project_kernel(x_ref, gain_ref, w_ref, n_ref, p_ref):
    x = x_ref[0].astype(F32)
    factor = lax.rsqrt(jnp.mean(x * x, axis=-1, keepdims=True) + 1e-06)
    normed = (x * factor * gain_row(gain_ref)).astype(BF16)
    n_ref[0] = normed
    width = x.shape[1]
    for part in range(3):
        cols = mm(normed, w_ref[:, part * width : (part + 1) * width])
        for pair in range(PAIRS):
            p_ref[pair, :, part * WIDE : (part + 1) * WIDE] = cols[
                :, pair * WIDE : (pair + 1) * WIDE
            ].astype(BF16)


def project(x, gain, w_qkv):
    groups, rows, width = x.shape
    return pl.pallas_call(
        project_kernel,
        grid=(groups,),
        in_specs=[
            pl.BlockSpec((1, rows, width), lambda s: (s, 0, 0)),
            pl.BlockSpec((width,), lambda s: (0,)),
            pl.BlockSpec(w_qkv.shape, lambda s: (0, 0)),
        ],
        out_specs=[
            pl.BlockSpec((1, rows, width), lambda s: (s, 0, 0)),
            pl.BlockSpec((PAIRS, rows, 3 * WIDE), lambda s: (s, 0, 0)),
        ],
        out_shape=[
            jax.ShapeDtypeStruct(x.shape, BF16),
            jax.ShapeDtypeStruct((groups * PAIRS, rows, 3 * WIDE), BF16),
        ],
        compiler_params=params(),
        name="project",
    )(x, gain, w_qkv)


def stack_heads(rows):
    lane = lax.broadcasted_iota(jnp.int32, rows.shape, 1)
    zero = jnp.zeros_like(rows)
    first = jnp.where(lane < HEAD, rows, zero)
    second = jnp.where(lane < HEAD, zero, rows)
    return jnp.concatenate([first, second], axis=0)


def unstack_heads(rows):
    half = rows.shape[0] // 2
    lane = lax.broadcasted_iota(jnp.int32, (half, rows.shape[1]), 1)
    return jnp.where(lane < HEAD, rows[:half], rows[half:])


def step_rows(index, size):
    return pl.ds(pl.multiple_of(index * size, size), size)


def own_unit(lengths, groups, count, slot):
    unit = slot * count + lax.axis_index("seq")
    length = lengths[jnp.minimum(unit // PAIRS, groups - 1)]
    return jnp.where(unit < groups * PAIRS, length, 0), lax.rem(unit, PAIRS)


def pair_taps(taps_ref, taps_sc, pair):
    width = taps_ref.shape[1] // 3
    for part in range(3):
        cols = pl.ds(pl.multiple_of(part * width + pair * WIDE, WIDE), WIDE)
        taps_sc[0:3, part * WIDE : (part + 1) * WIDE] = taps_ref[:, cols].astype(F32)


def convolve(wide_ref, taps_ref, tile, cols):
    begin = 8 + tile * TILE
    total = taps_ref[0:1, cols] * wide_ref[begin : begin + TILE, cols]
    total += taps_ref[1:2, cols] * wide_ref[begin - 1 : begin - 1 + TILE, cols]
    total += taps_ref[2:3, cols] * wide_ref[begin - 2 : begin - 2 + TILE, cols]
    return total.astype(BF16)


Q_COLS, K_COLS, V_COLS = (slice(part * WIDE, (part + 1) * WIDE) for part in range(3))


def key_limits(index, length, size):
    lane = lax.broadcasted_iota(jnp.int32, (STRIP, 2 * size), 1)
    return jnp.minimum(index * size + (lane & (size - 1)) + 1, length)


def over_key_steps(index, length, size, visit, carry):
    full = jnp.minimum(index * size, length) // size
    last = (jnp.minimum((index + 1) * size, length) + size - 1) // size
    carry = lax.fori_loop(0, full, lambda step, c: visit(step, False, c), carry)
    return lax.fori_loop(full, last, lambda step, c: visit(step, True, c), carry)


def attend_kernel(
    groups, count, lengths, p_ref, taps_ref, o_ref, lse_ref, taps, wide, q_sc, k_sc, vt_sc, acc, s_sc, e_sc
):
    length, pair = own_unit(lengths, groups, count, pl.program_id(0))
    wide[0:8] = jnp.zeros((8, wide.shape[1]), F32)
    wide[8:] = p_ref[0].astype(F32)
    attend_unit(
        length, pair, False, taps_ref, o_ref.at[0], lse_ref.at[0], taps, wide, q_sc, k_sc, vt_sc, acc, s_sc, e_sc
    )


def attend_unit(
    length, pair, whole, taps_ref, o_ref, lse_ref, taps, wide, q_sc, k_sc, vt_sc, acc, s_sc, e_sc
):
    tiles = q_sc.shape[0] // TILE
    per_step = ROWS // TILE
    pair_taps(taps_ref, taps, pair)
    vt_sc[:, WIDE:] = jnp.ones((vt_sc.shape[0], vt_sc.shape[1] - WIDE, ROWS), BF16)
    for tile in range(tiles):
        rows = slice(tile * TILE, (tile + 1) * TILE)
        q_sc[rows] = convolve(wide, taps, tile, Q_COLS) * (1.0 / math.sqrt(HEAD))

        def keys_values():
            k_sc[rows] = convolve(wide, taps, tile, K_COLS)
            cols = slice(tile % per_step * TILE, (tile % per_step + 1) * TILE)
            values = convolve(wide, taps, tile, V_COLS)
            vt_sc[tile // per_step, :WIDE, cols] = values.astype(F32).T.astype(BF16)

        if whole:
            keys_values()
        else:
            pl.when(tile // per_step * ROWS < length)(keys_values)

    k_row = lax.broadcasted_iota(jnp.int32, (STRIP, 2 * ROWS), 0)

    def query_step(index, carry):
        q_stack = stack_heads(q_sc[step_rows(index, ROWS)])
        limit = key_limits(index, length, ROWS)
        acc[...] = jnp.zeros(acc.shape, F32)

        def visit(step, mask, old):
            s_sc[...] = mm_nt(k_sc[step_rows(step, ROWS)], q_stack)

            def strip_of(begin):
                scores = s_sc[begin : begin + STRIP]
                if mask == "none":
                    return scores
                if mask == "length":
                    keep = k_row[:, :WIDE] < length - (step * ROWS + begin)
                    keep = jnp.concatenate([keep] * (2 * ROWS // WIDE), axis=1)
                else:
                    keep = k_row < limit - (step * ROWS + begin)
                return jnp.where(keep, scores, NEG)

            top = jnp.full((8, 2 * ROWS), NEG, F32)
            for begin in range(0, ROWS, STRIP):
                scores = strip_of(begin)
                for low in range(0, STRIP, 8):
                    top = jnp.maximum(top, scores[low : low + 8])
            new = jnp.maximum(old, jnp.max(top, axis=0, keepdims=True))
            for begin in range(0, ROWS, STRIP):
                e_sc[begin : begin + STRIP] = jnp.exp(strip_of(begin) - new).astype(BF16)
            acc[...] = acc[...] * jnp.exp(old - new) + mm(vt_sc[step], e_sc[...])
            return new

        top = jnp.full((1, 2 * ROWS), NEG, F32)
        if whole:
            top = lax.fori_loop(0, index, lambda step, c: visit(step, "length", c), top)
            top = visit(index, "both", top)
        else:

            def either(step, masked, top):
                return visit(step, "both" if masked else "none", top)

            top = over_key_steps(index, length, ROWS, either, top)
        total = acc[WIDE : WIDE + 1]
        out = (acc[:WIDE] / total).T
        o_ref[step_rows(index, ROWS)] = unstack_heads(out).astype(BF16)
        lse_ref[pl.ds(index, 1)] = top + jnp.log(total)
        return carry

    lax.fori_loop(0, q_sc.shape[0] // ROWS, query_step, 0)


def attend(lengths, proj, taps, count):
    slots, rows = proj.shape[:2]
    steps = rows // ROWS
    own = lambda i, lengths: (i, 0, 0)
    return pl.pallas_call(
        functools.partial(attend_kernel, lengths.shape[0], count),
        grid_spec=pltpu.PrefetchScalarGridSpec(
            num_scalar_prefetch=1,
            grid=(slots,),
            in_specs=[
                pl.BlockSpec((1, rows, 3 * WIDE), own),
                pl.BlockSpec(taps.shape, lambda i, lengths: (0, 0)),
            ],
            out_specs=[
                pl.BlockSpec((1, rows, WIDE), own),
                pl.BlockSpec((1, steps, 2 * ROWS), own),
            ],
            scratch_shapes=[
                pltpu.VMEM((8, 3 * WIDE), F32),
                pltpu.VMEM((rows + 8, 3 * WIDE), F32),
                pltpu.VMEM((rows, WIDE), BF16),
                pltpu.VMEM((rows, WIDE), BF16),
                pltpu.VMEM((steps, WIDE + 16, ROWS), BF16),
                pltpu.VMEM((WIDE + 16, 2 * ROWS), F32),
                pltpu.VMEM((ROWS, 2 * ROWS), F32),
                pltpu.VMEM((ROWS, 2 * ROWS), BF16),
            ],
        ),
        out_shape=[
            jax.ShapeDtypeStruct((slots, rows, WIDE), BF16),
            jax.ShapeDtypeStruct((slots, steps, 2 * ROWS), F32),
        ],
        compiler_params=params(),
        name="attend",
    )(lengths, proj, taps)


def front_kernel(
    lengths, x_ref, gain_ref, w_ref, taps_ref, n1_out, proj_out, units_out, att_out, lse_ref,
    x_v, w_v, n1_v, blocks, proj, units, att, taps, wide, q_sc, k_sc, vt_sc, acc, s_sc, e_sc,
    load_s, send_s, send_r, out_s, out_r,
):
    groups = x_v.shape[0]
    slots = proj.shape[0]
    block = x_v.shape[1]
    sems, out_sems = (send_s, send_r), (out_s, out_r)
    loads = [pltpu.make_async_copy(w_ref, w_v, load_s.at[0]), pltpu.make_async_copy(x_ref, x_v, load_s.at[1])]
    for copy in loads:
        copy.start()
    meet_group()
    for copy in loads:
        copy.wait()

    def sequence(group, carry):
        here = pl.ds(group, 1)
        project_kernel(
            x_v.at[here], gain_ref, w_v, n1_v.at[here], blocks.at[pl.ds(group * PAIRS, PAIRS)]
        )
        for pair in range(PAIRS):
            send_unit(blocks, proj, sems, group * PAIRS + pair)
        return carry

    lax.fori_loop(0, groups, sequence, 0)
    stores = [pltpu.make_async_copy(n1_v, n1_out, load_s.at[2])]
    stores[0].start()

    def one_slot(slot, carry):
        wait_unit(blocks, proj, sems, slot)
        length, pair = own_unit(lengths, groups, GROUP, slot)
        wide[0:8] = jnp.zeros((8, wide.shape[1]), F32)
        for place in range(GROUP):
            wide[8 + place * block : 8 + (place + 1) * block] = proj[slot, place].astype(F32)
        attend_unit(
            length, pair, True, taps_ref, units.at[slot], lse_ref.at[slot],
            taps, wide, q_sc, k_sc, vt_sc, acc, s_sc, e_sc,
        )
        send_rows(units, att, out_sems, slot, block)
        return carry

    lax.fori_loop(0, slots, one_slot, 0)
    stores.append(pltpu.make_async_copy(proj, proj_out, load_s.at[3]))
    stores.append(pltpu.make_async_copy(units, units_out, load_s.at[4]))
    for copy in stores[1:]:
        copy.start()
    for slot in range(slots):
        wait_rows(units, att, out_sems, slot, block)
    stores.append(pltpu.make_async_copy(att, att_out, load_s.at[5]))
    stores[-1].start()
    wait_sent(blocks, proj, sems)
    for copy in stores:
        copy.wait()


def row_copies(units, inbox, sems, slot, block):
    me = lax.axis_index("seq")
    return [
        remote(
            units.at[slot, pl.ds(pl.multiple_of((me ^ bit) * block, block), block)],
            inbox.at[slot * GROUP + me],
            (sems[0].at[slot, bit], sems[1].at[slot, bit]),
            "seq",
            me ^ bit,
        )
        for bit in range(1, GROUP)
    ]


def own_rows(units, inbox, sems, slot, block):
    me = lax.axis_index("seq")
    return pltpu.make_async_copy(
        units.at[slot, pl.ds(pl.multiple_of(me * block, block), block)],
        inbox.at[slot * GROUP + me],
        sems[1].at[slot, 0],
    )


def send_rows(units, inbox, sems, slot, block):
    own_rows(units, inbox, sems, slot, block).start()
    for copy in row_copies(units, inbox, sems, slot, block):
        copy.start()


def wait_rows(units, inbox, sems, slot, block):
    own_rows(units, inbox, sems, slot, block).wait()
    for copy in row_copies(units, inbox, sems, slot, block):
        copy.wait()


def front(x, gain, w_qkv, taps, lengths):
    groups, block, width = x.shape
    units = groups * PAIRS
    slots = units // GROUP
    rows = GROUP * block
    steps = rows // ROWS
    anywhere = pl.BlockSpec(memory_space=pl.ANY)
    vmem = pl.BlockSpec(memory_space=pltpu.VMEM)
    low = lambda *shape: pltpu.VMEM(shape, BF16)
    return pl.pallas_call(
        front_kernel,
        in_specs=[pl.BlockSpec(memory_space=pltpu.SMEM), anywhere, vmem, anywhere, vmem],
        out_specs=[anywhere] * 4 + [vmem],
        out_shape=[
            jax.ShapeDtypeStruct(x.shape, BF16),
            jax.ShapeDtypeStruct((slots, GROUP, block, 3 * WIDE), BF16),
            jax.ShapeDtypeStruct((slots, rows, WIDE), BF16),
            jax.ShapeDtypeStruct((units, block, WIDE), BF16),
            jax.ShapeDtypeStruct((slots, steps, 2 * ROWS), F32),
        ],
        scratch_shapes=[
            low(*x.shape),
            low(*w_qkv.shape),
            low(*x.shape),
            low(units, block, 3 * WIDE),
            low(slots, GROUP, block, 3 * WIDE),
            low(slots, rows, WIDE),
            low(units, block, WIDE),
            pltpu.VMEM((8, 3 * WIDE), F32),
            pltpu.VMEM((rows + 8, 3 * WIDE), F32),
            low(rows, WIDE),
            low(rows, WIDE),
            low(steps, WIDE + 16, ROWS),
            pltpu.VMEM((WIDE + 16, 2 * ROWS), F32),
            pltpu.VMEM((ROWS, 2 * ROWS), F32),
            low(ROWS, 2 * ROWS),
            DMA((6,)),
            DMA((units,)),
            DMA((slots, GROUP)),
            DMA((slots, GROUP)),
            DMA((slots, GROUP)),
        ],
        compiler_params=group_params(1),
        name="front",
    )(lengths, x, gain, w_qkv, taps)


def attend_back_kernel(
    groups, count, lengths, p_ref, taps_ref, o_ref, do_ref, lse_ref, dp_ref, gt_ref,
    taps, wide, q_sc, k_sc, v_sc, kt_sc, dm, dqt, s_sc, d_sc, e_sc, f_sc,
):
    p_ref, o_ref, do_ref, lse_ref = p_ref.at[0], o_ref.at[0], do_ref.at[0], lse_ref.at[0]
    dp_ref = dp_ref.at[0]
    length, pair = own_unit(lengths, groups, count, pl.program_id(0))
    tiles = p_ref.shape[0] // TILE
    per_step = BACK // TILE
    pair_taps(taps_ref, taps, pair)
    wide[0:8] = jnp.zeros((8, wide.shape[1]), F32)
    wide[8:] = p_ref[...].astype(F32)
    dm[...] = jnp.zeros(dm.shape, F32)
    for tile in range(tiles):
        rows = slice(tile * TILE, (tile + 1) * TILE)

        @pl.when(tile // per_step * BACK < length)
        def _():
            q_sc[rows] = convolve(wide, taps, tile, Q_COLS) * (1.0 / math.sqrt(HEAD))
            keys = convolve(wide, taps, tile, K_COLS)
            k_sc[rows] = keys
            v_sc[rows] = convolve(wide, taps, tile, V_COLS)
            cols = slice(tile % per_step * TILE, (tile % per_step + 1) * TILE)
            kt_sc[tile // per_step, :, cols] = keys.astype(F32).T.astype(BF16)

    lane = lax.broadcasted_iota(jnp.int32, (8, WIDE), 1)
    row = lax.broadcasted_iota(jnp.int32, (8, WIDE), 0)
    picks = jnp.where((lane < HEAD) == (row == 0), 1.0, 0.0).astype(BF16)
    k_row = lax.broadcasted_iota(jnp.int32, (STRIP, 2 * BACK), 0)

    def query_step(index, carry):
        here = step_rows(index, BACK)
        q_stack = stack_heads(q_sc[here])
        d_rows = do_ref[here]
        d_stack = stack_heads(d_rows)
        product = d_rows.astype(F32) * o_ref[here].astype(F32)
        upper = product.astype(BF16)
        lower = (product - upper.astype(F32)).astype(BF16)
        sums = mm_nt(picks, upper) + mm_nt(picks, lower)
        delta = jnp.concatenate([sums[0:1], sums[1:2]], axis=1)
        line, begin = pl.ds(index * BACK // ROWS, 1), lax.rem(index * BACK, ROWS)
        lse = jnp.concatenate(
            [
                lse_ref[line, pl.ds(pl.multiple_of(head * ROWS + begin, BACK), BACK)]
                for head in range(2)
            ],
            axis=1,
        )
        limit = key_limits(index, length, BACK)
        dqt[...] = jnp.zeros(dqt.shape, F32)

        def visit(step, masked, carry):
            there = step_rows(step, BACK)
            s_sc[...] = mm_nt(k_sc[there], q_stack)
            d_sc[...] = mm_nt(v_sc[there], d_stack)
            for begin in range(0, BACK, STRIP):
                strip = slice(begin, begin + STRIP)
                probs = jnp.exp(s_sc[strip] - lse)
                if masked:
                    probs = jnp.where(k_row < limit - (step * BACK + begin), probs, 0.0)
                e_sc[strip] = probs.astype(BF16)
                f_sc[strip] = (probs * (d_sc[strip] - delta)).astype(BF16)
            dm[there, V_COLS] += mm(e_sc[...], d_stack)
            dm[there, K_COLS] += mm(f_sc[...], q_stack)
            dqt[...] += mm(kt_sc[step], f_sc[...])
            return carry

        over_key_steps(index, length, BACK, visit, 0)
        dm[here, Q_COLS] = unstack_heads(dqt[...].T) * (1.0 / math.sqrt(HEAD))
        return carry

    lax.fori_loop(0, (length + BACK - 1) // BACK, query_step, 0)

    @pl.when(pl.program_id(0) == 0)
    def _():
        gt_ref[...] = jnp.zeros(gt_ref.shape, F32)

    sums = [jnp.zeros((1, 3 * WIDE), F32) for _ in range(3)]
    for tile in range(tiles):
        begin = tile * TILE
        total = taps[0:1] * dm[begin : begin + TILE]
        total += taps[1:2] * dm[begin + 1 : begin + 1 + TILE]
        total += taps[2:3] * dm[begin + 2 : begin + 2 + TILE]
        dp_ref[begin : begin + TILE] = total.astype(BF16)
        for tap in range(3):
            behind = wide[begin + 8 - tap : begin + 8 - tap + TILE]
            sums[tap] += jnp.sum(dm[begin : begin + TILE] * behind, axis=0, keepdims=True)
    width = gt_ref.shape[1] // 3
    for tap in range(3):
        for part in range(3):
            cols = pl.ds(pl.multiple_of(part * width + pair * WIDE, WIDE), WIDE)
            gt_ref[tap : tap + 1, cols] += sums[tap][:, part * WIDE : (part + 1) * WIDE]


def attend_back(lengths, proj, taps, attended, d_attended, lse, count):
    slots, rows = proj.shape[:2]
    steps = rows // BACK
    own = lambda i, lengths: (i, 0, 0)
    whole = lambda i, lengths: (0, 0)
    return pl.pallas_call(
        functools.partial(attend_back_kernel, lengths.shape[0], count),
        grid_spec=pltpu.PrefetchScalarGridSpec(
            num_scalar_prefetch=1,
            grid=(slots,),
            in_specs=[
                pl.BlockSpec((1, rows, 3 * WIDE), own),
                pl.BlockSpec(taps.shape, whole),
                pl.BlockSpec((1, rows, WIDE), own),
                pl.BlockSpec((1, rows, WIDE), own),
                pl.BlockSpec((1,) + lse.shape[1:], own),
            ],
            out_specs=[
                pl.BlockSpec((1, rows, 3 * WIDE), own),
                pl.BlockSpec((8, taps.shape[1]), whole),
            ],
            scratch_shapes=[
                pltpu.VMEM((8, 3 * WIDE), F32),
                pltpu.VMEM((rows + 8, 3 * WIDE), F32),
                pltpu.VMEM((rows, WIDE), BF16),
                pltpu.VMEM((rows, WIDE), BF16),
                pltpu.VMEM((rows, WIDE), BF16),
                pltpu.VMEM((steps, WIDE, BACK), BF16),
                pltpu.VMEM((rows + 8, 3 * WIDE), F32),
                pltpu.VMEM((WIDE, 2 * BACK), F32),
                pltpu.VMEM((BACK, 2 * BACK), F32),
                pltpu.VMEM((BACK, 2 * BACK), F32),
                pltpu.VMEM((BACK, 2 * BACK), BF16),
                pltpu.VMEM((BACK, 2 * BACK), BF16),
            ],
        ),
        out_shape=[
            jax.ShapeDtypeStruct((slots, rows, 3 * WIDE), BF16),
            jax.ShapeDtypeStruct((8, taps.shape[1]), F32),
        ],
        compiler_params=params(),
        name="attend_back",
    )(lengths, proj, taps, attended, d_attended, lse)


def dense_kernel(
    x_ref, att_ref, cot_ref, mask_ref, lengths, gain_ref, wo_ref, wu_ref, wd_ref,
    out_ref, dh_ref, datt_ref, n2_ref, sq_ref, du_ref, da_ref, cz_ref, gain_grad_ref, stats_ref,
    act_sc, att_sc,
):
    rows, width = x_ref.shape[1:]
    hidden_units = wu_ref.shape[1]
    step = width
    for pair in range(PAIRS):
        att_sc[:, pair * WIDE : (pair + 1) * WIDE] = att_ref[pair]
    group = pl.program_id(0)
    spot = lax.axis_index("seq") * rows + lax.broadcasted_iota(jnp.int32, (1, rows), 1)
    counts = jnp.where(spot < lengths[group], mask_ref[pl.ds(group, 1)].astype(F32), 0.0)
    weight = jnp.broadcast_to(counts, (WIDE, rows)).T[:, :1]
    gain = gain_row(gain_ref)
    branch = mm(att_sc[...], wo_ref[...])
    hidden = x_ref[0].astype(F32) + branch
    factor = lax.rsqrt(jnp.mean(hidden * hidden, axis=-1, keepdims=True) + 1e-06)
    normed = (hidden * factor * gain).astype(BF16)
    n2_ref[0] = normed
    total = jnp.zeros((rows, width), F32)
    for begin in range(0, hidden_units, step):
        cols = slice(begin, begin + step)
        active = jnp.maximum(mm(normed, wu_ref[:, cols]), 0.0)
        act_sc[:, cols] = active
        squared = (active * active).astype(BF16)
        sq_ref[0, :, cols] = squared
        total += mm(squared, wd_ref[cols])
    full = hidden + total
    out_ref[0] = full.astype(BF16)

    def masked(values):
        per_row = jnp.sum(values * values, axis=-1, keepdims=True)
        return jnp.sum(weight * per_row, axis=0, keepdims=True)

    @pl.when(pl.program_id(0) == 0)
    def _():
        stats_ref[...] = jnp.zeros(stats_ref.shape, F32)
        gain_grad_ref[...] = jnp.zeros(gain_grad_ref.shape, F32)

    parts = [masked(full), masked(branch), masked(total), jnp.sum(weight, axis=0, keepdims=True)]
    for place, part in enumerate(parts):
        stats_ref[place : place + 1] += jnp.broadcast_to(part, (1, WIDE))
    cotangent = (cot_ref[0].astype(F32) * weight).astype(BF16)
    cz_ref[0] = cotangent
    d_normed = jnp.zeros((rows, width), F32)
    for begin in range(0, hidden_units, step):
        cols = slice(begin, begin + step)
        d_squared = mm_nt(cotangent, wd_ref[cols])
        d_up = (2.0 * act_sc[:, cols] * d_squared).astype(BF16)
        du_ref[0, :, cols] = d_up
        d_normed += mm_nt(d_up, wu_ref[:, cols])
    weighted = d_normed * gain
    inner = jnp.mean(weighted * hidden, axis=-1, keepdims=True)
    d_hidden = cotangent.astype(F32) + factor * weighted - hidden * (factor * factor * factor) * inner
    gain_grad_ref[...] += jnp.sum(d_normed * hidden * factor, axis=0, keepdims=True)
    dh_ref[0] = d_hidden
    d_attn = d_hidden.astype(BF16)
    da_ref[0] = d_attn
    d_att = mm_nt(d_attn, wo_ref[...]).astype(BF16)
    for pair in range(PAIRS):
        datt_ref[pair] = d_att[:, pair * WIDE : (pair + 1) * WIDE]


def dense_send_kernel(
    x_ref, att_ref, cot_ref, mask_ref, lengths, gain_ref, wo_ref, wu_ref, wd_ref,
    out_ref, dh_ref, inbox, n2_ref, sq_ref, du_ref, da_ref, cz_ref, gain_grad_ref, stats_ref,
    act_sc, att_sc, d_blocks, out_s, out_r,
):
    group = pl.program_id(0)
    out_sems = (out_s, out_r)
    pl.when(group == 0)(meet_group)
    here = pl.ds(group * PAIRS, PAIRS)
    dense_kernel(
        x_ref, att_ref, cot_ref, mask_ref, lengths, gain_ref, wo_ref, wu_ref, wd_ref,
        out_ref, dh_ref, d_blocks.at[here], n2_ref, sq_ref, du_ref, da_ref, cz_ref, gain_grad_ref,
        stats_ref, act_sc, att_sc,
    )
    for pair in range(PAIRS):
        send_unit(d_blocks, inbox, out_sems, group * PAIRS + pair)
    pl.when(group == pl.num_programs(0) - 1)(lambda: wait_units(d_blocks, inbox, out_sems))


def dense_send(x, attended, grad_output, token_mask, lengths, gain, w_out, w_up, w_down):
    groups, rows, width = x.shape
    hidden_units = w_up.shape[1]
    slots = groups * PAIRS // GROUP
    per_group = lambda s: (s, 0, 0)
    fixed = lambda s: (0, 0)
    once = pl.Buffered(1)
    anywhere = pl.BlockSpec(memory_space=pl.ANY)
    row_block = pl.BlockSpec((1, rows, width), per_group)
    wide_block = pl.BlockSpec((1, rows, hidden_units), per_group)
    low = jax.ShapeDtypeStruct(x.shape, BF16)
    wide_low = jax.ShapeDtypeStruct((groups, rows, hidden_units), BF16)
    unit_rows = (groups * PAIRS, rows, WIDE)
    return pl.pallas_call(
        dense_send_kernel,
        grid=(groups,),
        in_specs=[
            row_block,
            pl.BlockSpec((PAIRS, rows, WIDE), per_group),
            row_block,
            pl.BlockSpec(token_mask.shape, fixed),
            pl.BlockSpec(memory_space=pltpu.SMEM),
            pl.BlockSpec((width,), lambda s: (0,)),
            pl.BlockSpec(w_out.shape, fixed, pipeline_mode=once),
            pl.BlockSpec(w_up.shape, fixed, pipeline_mode=once),
            pl.BlockSpec(w_down.shape, fixed, pipeline_mode=once),
        ],
        out_specs=[
            row_block,
            row_block,
            anywhere,
            row_block,
            wide_block,
            wide_block,
            row_block,
            row_block,
            pl.BlockSpec((1, width), fixed),
            pl.BlockSpec((8, WIDE), fixed),
        ],
        out_shape=[
            low,
            jax.ShapeDtypeStruct(x.shape, F32),
            jax.ShapeDtypeStruct((slots, GROUP, rows, WIDE), BF16),
            low,
            wide_low,
            wide_low,
            low,
            low,
            jax.ShapeDtypeStruct((1, width), F32),
            jax.ShapeDtypeStruct((8, WIDE), F32),
        ],
        scratch_shapes=[
            pltpu.VMEM((rows, hidden_units), F32),
            pltpu.VMEM((rows, width), BF16),
            pltpu.VMEM(unit_rows, BF16),
            DMA((groups * PAIRS,)),
            DMA((slots, GROUP)),
        ],
        compiler_params=group_params(2),
        name="dense_send",
    )(x, attended, grad_output, token_mask, lengths, gain, w_out, w_up, w_down)


def dense(x, attended, grad_output, token_mask, lengths, gain, w_out, w_up, w_down):
    groups, rows, width = x.shape
    hidden_units = w_up.shape[1]
    per_group = lambda s: (s, 0, 0)
    fixed = lambda s: (0, 0)
    once = pl.Buffered(1)
    row_block = pl.BlockSpec((1, rows, width), per_group)
    wide_block = pl.BlockSpec((1, rows, hidden_units), per_group)
    unit_block = pl.BlockSpec((PAIRS, rows, WIDE), per_group)
    low = jax.ShapeDtypeStruct(x.shape, BF16)
    wide_low = jax.ShapeDtypeStruct((groups, rows, hidden_units), BF16)
    return pl.pallas_call(
        dense_kernel,
        grid=(groups,),
        in_specs=[
            row_block,
            unit_block,
            row_block,
            pl.BlockSpec(token_mask.shape, fixed),
            pl.BlockSpec(memory_space=pltpu.SMEM),
            pl.BlockSpec((width,), lambda s: (0,)),
            pl.BlockSpec(w_out.shape, fixed, pipeline_mode=once),
            pl.BlockSpec(w_up.shape, fixed, pipeline_mode=once),
            pl.BlockSpec(w_down.shape, fixed, pipeline_mode=once),
        ],
        out_specs=[
            row_block,
            row_block,
            unit_block,
            row_block,
            wide_block,
            wide_block,
            row_block,
            row_block,
            pl.BlockSpec((1, width), fixed),
            pl.BlockSpec((8, WIDE), fixed),
        ],
        out_shape=[
            low,
            jax.ShapeDtypeStruct(x.shape, F32),
            jax.ShapeDtypeStruct((groups * PAIRS, rows, WIDE), BF16),
            low,
            wide_low,
            wide_low,
            low,
            low,
            jax.ShapeDtypeStruct((1, width), F32),
            jax.ShapeDtypeStruct((8, WIDE), F32),
        ],
        scratch_shapes=[pltpu.VMEM((rows, hidden_units), F32), pltpu.VMEM((rows, width), BF16)],
        compiler_params=params(),
        name="dense",
    )(x, attended, grad_output, token_mask, lengths, gain, w_out, w_up, w_down)


PART = 384
BY_CHIP = 288


def feed_grads_kernel(sq_ref, cz_ref, n2_ref, du_ref, att_ref, da_ref, out_ref, n2_t):
    half, sub = pl.program_id(0), pl.program_id(1)
    groups, rows, width = n2_ref.shape
    tokens = groups * rows

    @pl.when((half == 0) & (sub == 0))
    def _():
        for group in range(groups):
            n2_t[:, group * rows : (group + 1) * rows] = n2_ref[group].astype(F32).T.astype(BF16)

    down = mm_tn(sq_ref[...].reshape(tokens, PART), cz_ref[...].reshape(tokens, width))
    for place in range(4):
        for side in range(2):
            out_ref[place, pl.ds(sub, 1), side * 96 : side * 96 + 96] = down[
                place * 96 : (place + 1) * 96, side * PART : (side + 1) * PART
            ].astype(BF16)[None]
    up = mm(n2_t[...], du_ref[...].reshape(tokens, PART))
    out_ref[pl.ds(sub, 1), :, 192:384] = up.astype(BF16).reshape(1, 4, 192, PART)

    @pl.when(sub == 0)
    def _():
        att = jnp.concatenate(
            [att_ref[:, pair].reshape(tokens, WIDE) for pair in range(PAIRS)], axis=1
        )
        out = mm_tn(att, da_ref[...].reshape(tokens, PART)).astype(BF16)
        for batch in range(4):
            for q in range(4):
                begin = batch * 192 + q * 48
                out_ref[q, batch, 384:432] = out[begin : begin + 48]


def feed_grads(squared, cotangent, normed2, d_up, attended, d_attn):
    groups, rows, width = normed2.shape
    whole = lambda h, b: (0, 0, 0)
    return pl.pallas_call(
        feed_grads_kernel,
        grid=(2, 4),
        in_specs=[
            pl.BlockSpec((groups, rows, PART), lambda h, b: (0, 0, 2 * b + h)),
            pl.BlockSpec((groups, rows, width), whole, pipeline_mode=pl.Buffered(1)),
            pl.BlockSpec((groups, rows, width), whole, pipeline_mode=pl.Buffered(1)),
            pl.BlockSpec((groups, rows, PART), lambda h, b: (0, 0, 4 * h + b)),
            pl.BlockSpec(
                (groups, PAIRS, rows, WIDE), lambda h, b: (0, 0, 0, 0), pipeline_mode=pl.Buffered(1)
            ),
            pl.BlockSpec((groups, rows, PART), lambda h, b: (0, 0, h)),
        ],
        out_specs=pl.BlockSpec((4, 4, 432, PART), lambda h, b: (h, 0, 0, 0)),
        out_shape=jax.ShapeDtypeStruct((8, 4, 432, PART), BF16),
        scratch_shapes=[pltpu.VMEM((width, groups * rows), BF16)],
        compiler_params=params(),
        name="feed_grads",
    )(squared, cotangent, normed2, d_up, attended.reshape(groups, PAIRS, rows, WIDE), d_attn)


def feed_grads_send_kernel(
    sq_ref, cz_ref, n2_ref, du_ref, att_ref, da_ref, chip_ref, z_ref,
    n2_t, pieces, core_in, down_s, down_r, up_s, up_r, out_s, out_r,
):
    half, sub = pl.program_id(0), pl.program_id(1)
    me = lax.axis_index("seq")
    core = lax.rem(me, 2)
    other = 1 - core

    @pl.when((half == 0) & (sub == 0))
    def _():
        barrier = pltpu.get_barrier_semaphore()
        pl.semaphore_signal(barrier, inc=1, device_id={"seq": me ^ 1}, device_id_type=MESH)
        pl.semaphore_wait(barrier, 1)

    feed_grads_kernel(
        sq_ref, cz_ref, n2_ref, du_ref, att_ref, da_ref, pieces.at[pl.ds(half * 4, 4)], n2_t
    )

    def down(part, batch, side):
        chip = part * 2 + side
        return remote(
            pieces.at[chip * 2 + other, batch, 0:192],
            core_in.at[chip, batch, 0:192],
            (down_s.at[part, batch, side], down_r.at[part, batch, side]),
            "seq",
            me ^ 1,
        )

    def up(chip):
        return remote(
            pieces.at[chip * 2 + other, :, 192:384],
            core_in.at[chip, :, 192:384],
            (up_s.at[chip], up_r.at[chip]),
            "seq",
            me ^ 1,
        )

    def out(chip):
        return remote(
            pieces.at[chip * 2 + other, :, 384:432],
            core_in.at[chip, :, 384:432],
            (out_s.at[chip], out_r.at[chip]),
            "seq",
            me ^ 1,
        )

    for side in range(2):
        down(half, sub, side).start()

    @pl.when(sub == 0)
    def _():
        for side in range(2):
            out(half * 2 + side).start()

    @pl.when(lax.rem(sub, 2) == other)
    def _():
        up(half * 2 + sub // 2).start()

    @pl.when((half == 1) & (sub == 3))
    def _():
        for part in range(2):
            for side in range(2):
                chip = part * 2 + side
                for batch in range(4):
                    down(part, batch, side).wait()
                up(chip).wait()
                out(chip).wait()
                for batch in range(4):
                    both = pieces[chip * 2 + core, batch].astype(F32) + core_in[chip, batch].astype(F32)
                    chip_ref[chip, batch] = both[:BY_CHIP].astype(BF16)
                    z_ref[batch, chip] = both[BY_CHIP:].astype(BF16)


def feed_grads_send(squared, cotangent, normed2, d_up, attended, d_attn):
    groups, rows, width = normed2.shape
    whole = lambda h, b: (0, 0, 0)
    once = pl.Buffered(1)
    quarter = (4, 4, 432, PART)
    return pl.pallas_call(
        feed_grads_send_kernel,
        grid=(2, 4),
        in_specs=[
            pl.BlockSpec((groups, rows, PART), lambda h, b: (0, 0, 2 * b + h)),
            pl.BlockSpec((groups, rows, width), whole, pipeline_mode=once),
            pl.BlockSpec((groups, rows, width), whole, pipeline_mode=once),
            pl.BlockSpec((groups, rows, PART), lambda h, b: (0, 0, 4 * h + b)),
            pl.BlockSpec((groups, PAIRS, rows, WIDE), lambda h, b: (0, 0, 0, 0), pipeline_mode=once),
            pl.BlockSpec((groups, rows, PART), lambda h, b: (0, 0, h)),
        ],
        out_specs=[
            pl.BlockSpec((4, 4, BY_CHIP, PART), lambda h, b: (0, 0, 0, 0), pipeline_mode=once),
            pl.BlockSpec((4, 4, 432 - BY_CHIP, PART), lambda h, b: (0, 0, 0, 0), pipeline_mode=once),
        ],
        out_shape=[
            jax.ShapeDtypeStruct((4, 4, BY_CHIP, PART), BF16),
            jax.ShapeDtypeStruct((4, 4, 432 - BY_CHIP, PART), BF16),
        ],
        scratch_shapes=[
            pltpu.VMEM((width, groups * rows), BF16),
            pltpu.VMEM((8, 4, 432, PART), BF16),
            pltpu.VMEM(quarter, BF16),
            DMA((2, 4, 2)),
            DMA((2, 4, 2)),
            DMA((4,)),
            DMA((4,)),
            DMA((4,)),
            DMA((4,)),
        ],
        compiler_params=group_params(3),
        name="feed_grads_send",
    )(squared, cotangent, normed2, d_up, attended.reshape(groups, PAIRS, rows, WIDE), d_attn)


def input_grads_kernel(
    dp_ref, n1_ref, x_ref, dh_ref, w_ref, gain_ref, out_ref, gx_ref, gain_grad_ref, n1_t, total, w_sc
):
    pair = pl.program_id(0)
    groups, rows, width = n1_ref.shape
    tokens = groups * rows

    @pl.when(pair == 0)
    def _():
        for group in range(groups):
            n1_t[:, group * rows : (group + 1) * rows] = n1_ref[group].astype(F32).T.astype(BF16)
        total[...] = jnp.zeros(total.shape, F32)

    d_proj = dp_ref[...].reshape(tokens, 3 * WIDE)
    grad = mm(n1_t[...], d_proj).astype(BF16)
    for batch in range(4):
        for chip in range(4):
            begin = batch * 192 + chip * 48
            out_ref[0, 0, chip, batch] = grad[begin : begin + 48]
    for part in range(3):
        cols = pl.ds(pl.multiple_of(part * width + pair * WIDE, WIDE), WIDE)
        w_sc[:, part * WIDE : (part + 1) * WIDE] = w_ref[:, cols]
    total[...] += mm_nt(d_proj, w_sc[...])

    @pl.when(pair == PAIRS - 1)
    def _():
        gain = gain_row(gain_ref)
        gain_sum = jnp.zeros((1, width), F32)
        for group in range(groups):
            x = x_ref[group].astype(F32)
            d_normed = total[group * rows : (group + 1) * rows]
            factor = lax.rsqrt(jnp.mean(x * x, axis=-1, keepdims=True) + 1e-06)
            weighted = d_normed * gain
            inner = jnp.mean(weighted * x, axis=-1, keepdims=True)
            gx_ref[group] = (
                dh_ref[group] + factor * weighted - x * (factor * factor * factor) * inner
            )
            gain_sum += jnp.sum(d_normed * x * factor, axis=0, keepdims=True)
        gain_grad_ref[...] = gain_sum


def input_grads(d_proj, normed1, x, d_hidden, w_qkv, gain):
    groups, rows, width = x.shape
    whole = lambda p: (0, 0, 0)
    once = pl.Buffered(1)
    tokens = pl.BlockSpec((groups, rows, width), whole, pipeline_mode=once)
    return pl.pallas_call(
        input_grads_kernel,
        grid=(PAIRS,),
        in_specs=[
            pl.BlockSpec((groups, 1, rows, 3 * WIDE), lambda p: (0, p, 0, 0)),
            tokens,
            tokens,
            tokens,
            pl.BlockSpec(w_qkv.shape, lambda p: (0, 0), pipeline_mode=once),
            pl.BlockSpec((width,), lambda p: (0,)),
        ],
        out_specs=[
            pl.BlockSpec((1, 1, 4, 4, 48, PART), lambda p: (p % 3, p // 3, 0, 0, 0, 0)),
            tokens,
            pl.BlockSpec((1, width), lambda p: (0, 0)),
        ],
        out_shape=[
            jax.ShapeDtypeStruct((3, 2, 4, 4, 48, PART), BF16),
            jax.ShapeDtypeStruct(x.shape, F32),
            jax.ShapeDtypeStruct((1, width), F32),
        ],
        scratch_shapes=[
            pltpu.VMEM((width, groups * rows), BF16),
            pltpu.VMEM((groups * rows, width), F32),
            pltpu.VMEM((width, 3 * WIDE), BF16),
        ],
        compiler_params=params(),
        name="input_grads",
    )(d_proj.reshape(groups, PAIRS, rows, 3 * WIDE), normed1, x, d_hidden, w_qkv, gain)


def finish_kernel(
    units_ref, n1_ref, x_ref, dh_ref, w_ref, gain_ref, feed_ref, far_ref, gt_ref, gain2_ref, stats_ref,
    gx_ref, qkv_out, feed_out, small_out,
    dp_in, n1_v, n1_t, x_v, dh_v, w_v, feed_v, far_v, far_mine, far_in, dn, grads, pieces,
    core_in, here, chip_in, mine, z_in, qkv_all, feed_mine, feed_in, feed_all,
    row_own, row_in, row_sum, col_in,
    load_s, far_s, far_r, dp_s, dp_r, core_s, core_r, chip_s, chip_r, z_s, z_r, qkv_s, qkv_r, fz_s, fz_r, fa_s, fa_r,
    row_s, row_r, col_s, col_r,
):
    me = lax.axis_index("seq")
    z = lax.axis_index("batch")
    core, chip = lax.rem(me, 2), me // 2
    groups, block, width = n1_v.shape
    tokens = groups * block
    middle = tokens // 2
    chunks = pieces.shape[0]
    slots = units_ref.shape[0]
    rows = feed_in.shape[2]
    barrier = pltpu.get_barrier_semaphore()
    for bit in range(1, 8):
        pl.semaphore_signal(barrier, inc=1, device_id={"seq": me ^ bit}, device_id_type=MESH)
    for bit in range(1, 4):
        pl.semaphore_signal(barrier, inc=1, device_id={"batch": z ^ bit}, device_id_type=MESH)
    pl.semaphore_wait(barrier, 10)

    def send(source, target, sems, axis, peer):
        copy = remote(source, target, sems, axis, peer)
        copy.start()
        return copy

    across, along = me ^ 2, me ^ 4

    def spread(ref, s, r):
        return [
            send(ref.at[me], ref.at[me], (s.at[step], r.at[step]), "seq", peer)
            for step, peer in enumerate((me ^ 1, across, along))
        ]

    def relay(ref, first, s, r):
        rows = ref.shape[1]
        cut = (rows // 2 + 15) // 16 * 16
        first[1].wait()
        first[2].wait()
        upper, lower = pl.ds(0, cut), pl.ds(cut, rows - cut)
        on = [
            send(ref.at[across, upper], ref.at[across, upper], (s.at[3], r.at[3]), "seq", along),
            send(ref.at[along, lower], ref.at[along, lower], (s.at[4], r.at[4]), "seq", across),
        ]
        more = [
            send(ref.at[slot], ref.at[slot], (s.at[5 + step], r.at[5 + step]), "seq", me ^ 1)
            for step, slot in enumerate((across, along))
        ]
        return [first[0]] + more, on

    def finish_relay(ref, on, s, r):
        for copy in on:
            copy.wait()
        slot = me ^ 6
        return [send(ref.at[slot], ref.at[slot], (s.at[7], r.at[7]), "seq", me ^ 1)]

    for slot in range(slots):
        send_blocks(units_ref, dp_in, (dp_s, dp_r), slot)
    loads = [
        pltpu.make_async_copy(source, target, load_s.at[place])
        for place, (source, target) in enumerate(
            [
                (feed_ref, feed_v),
                (far_ref.at[z], far_v.at[0]),
                (n1_ref, n1_v),
                (w_ref, w_v),
                (x_ref, x_v),
                (dh_ref, dh_v),
            ]
        )
    ]
    for copy in loads:
        copy.start()
    far_z = [
        send(far_ref.at[z ^ bit], far_v.at[bit], (far_s.at[2 + bit], far_r.at[2 + bit]), "batch", z ^ bit)
        for bit in range(1, 4)
    ]

    loads[0].wait()
    for batch in range(4):
        both = feed_v[0, batch].astype(F32)
        for q in range(1, 4):
            both = both + feed_v[q, batch].astype(F32)
        feed_mine[batch] = both.astype(BF16)
    near = feed_mine.shape[1] // rows
    feed_z = [
        [
            send(
                feed_mine.at[z ^ bit, c * rows : (c + 1) * rows],
                feed_in.at[c, bit - 1],
                (fz_s.at[c, bit - 1], fz_r.at[c, bit - 1]),
                "batch",
                z ^ bit,
            )
            for bit in range(1, 4)
        ]
        for c in range(near)
    ]
    loads[2].wait()
    for group in range(groups):
        n1_t[:, group * block : (group + 1) * block] = n1_v[group].astype(F32).T.astype(BF16)
    for copy in loads[3:]:
        copy.wait()
    gain = gain_row(gain_ref)

    def unit_rows(pair, first):
        return jnp.concatenate(
            [dp_in[(first + more) * PAIRS + pair] for more in range(groups // 2)], axis=0
        )

    def pair_weights(pair):
        return jnp.concatenate(
            [
                w_v[:, pl.ds(pl.multiple_of(part * width + pair * WIDE, WIDE), WIDE)]
                for part in range(3)
            ],
            axis=1,
        )

    def input_half(first):
        gain_sum = jnp.zeros((1, width), F32)
        for more in range(groups // 2):
            group = first + more
            x = x_v[group].astype(F32)
            d_normed = dn[group * block : (group + 1) * block]
            factor = lax.rsqrt(jnp.mean(x * x, axis=-1, keepdims=True) + 1e-06)
            weighted = d_normed * gain
            inner = jnp.mean(weighted * x, axis=-1, keepdims=True)
            dh_v[group] += factor * weighted - x * (factor * factor * factor) * inner
            gain_sum += jnp.sum(d_normed * x * factor, axis=0, keepdims=True)
        return gain_sum

    for slot in range(slots):
        if (slot * GROUP) // PAIRS < groups // 2:
            wait_blocks(units_ref, dp_in, (dp_s, dp_r), slot)
    dn[...] = jnp.zeros(dn.shape, F32)

    def first_half(pair, carry):
        d_rows = unit_rows(pair, 0)
        grads[pair] = mm(n1_t[:, :middle], d_rows)
        dn[:middle] += mm_nt(d_rows, pair_weights(pair))
        return carry

    lax.fori_loop(0, PAIRS, first_half, 0)
    gain_sum = input_half(0)
    loads[1].wait()
    for copy in far_z:
        copy.wait()
    for q in range(4):
        both = far_v[0, q].astype(F32)
        for place in range(1, 4):
            both = both + far_v[place, q].astype(F32)
        far_mine[q] = both.astype(BF16)
    far_chips = [
        send(
            far_mine.at[chip ^ bit],
            far_in.at[bit - 1],
            (far_s.at[bit - 1], far_r.at[bit - 1]),
            "seq",
            me ^ (2 * bit),
        )
        for bit in range(1, 4)
    ]
    for slot in range(slots):
        if (slot * GROUP) // PAIRS >= groups // 2:
            wait_blocks(units_ref, dp_in, (dp_s, dp_r), slot)

    feed_first = []

    def spread_feed(c):
        for copy in feed_z[c] if c < near else far_chips:
            copy.wait()
        if c < near:
            both = feed_mine[z, c * rows : (c + 1) * rows].astype(F32)
            for bit in range(3):
                both = both + feed_in[c, bit].astype(F32)
        else:
            both = far_mine[chip].astype(F32)
            for bit in range(3):
                both = both + far_in[bit].astype(F32)
        feed_all[c, pl.ds(me, 1)] = both.astype(BF16)[None]
        feed_first.append(spread(feed_all.at[c], fa_s.at[c], fa_r.at[c]))

    spread_feed(0)
    to_core, to_chip = [], []

    def pass_on(c):
        to_core[c].wait()
        for q in range(4):
            both = pieces[c, core, q].astype(F32) + core_in[c, q].astype(F32)
            here[c, q] = both.astype(BF16)
        to_chip.append(
            [
                send(
                    here.at[c, q, half],
                    chip_in.at[c, place],
                    (chip_s.at[c, place], chip_r.at[c, place]),
                    "seq",
                    peer,
                )
                for place, (q, half, peer) in enumerate(
                    (
                        (chip ^ 1, first_two, across),
                        (chip ^ 3, first_two, across),
                        (chip ^ 2, last_two, along),
                        (chip ^ 3, last_two, along),
                    )
                )
            ]
        )

    first_two, last_two = pl.ds(0, 2), pl.ds(2, 2)

    def pass_again(c):
        for place, (q, half) in enumerate(
            ((chip, first_two), (chip ^ 2, first_two), (chip, last_two), (chip ^ 1, last_two))
        ):
            to_chip[c][place].wait()
            both = here[c, q, half].astype(F32) + chip_in[c, place].astype(F32)
            here[c, q, half] = both.astype(BF16)
        return [
            send(
                here.at[c, q, half],
                chip_in.at[c, place],
                (chip_s.at[c, place], chip_r.at[c, place]),
                "seq",
                peer,
            )
            for place, (q, half, peer) in (
                (4, (chip ^ 2, first_two, along)),
                (5, (chip ^ 1, last_two, across)),
            )
        ]

    for c in range(chunks):

        def second_half(side, carry, c=c):
            pair = side * chunks + c
            grad = (grads[pair] + mm(n1_t[:, middle:], unit_rows(pair, groups // 2))).astype(BF16)
            for batch in range(4):
                for q in range(4):
                    begin = batch * 192 + q * 48
                    pieces[c, side, q, batch] = grad[begin : begin + 48]
            return carry

        lax.fori_loop(0, 2, second_half, 0)
        to_core.append(
            send(
                pieces.at[c, 1 - core], core_in.at[c], (core_s.at[c], core_r.at[c]), "seq", me ^ 1
            )
        )
        if c > 0:
            pass_on(c - 1)

    def second_rows(pair, carry):
        dn[middle:] += mm_nt(unit_rows(pair, groups // 2), pair_weights(pair))
        return carry

    lax.fori_loop(0, 2, second_rows, 0)
    pass_on(chunks - 1)
    again = [pass_again(0)]
    lax.fori_loop(2, 4, second_rows, 0)
    again.append(pass_again(1))
    lax.fori_loop(4, PAIRS, second_rows, 0)
    again.append(pass_again(2))
    for c in range(1, chunks):
        spread_feed(c)
    gain_sum = gain_sum + input_half(groups // 2)
    gx_copy = pltpu.make_async_copy(dh_v, gx_ref, load_s.at[len(loads)])
    gx_copy.start()
    row_own[...] = jnp.zeros(row_own.shape, F32)
    for tap in range(3):
        for part in range(3):
            row = tap * 3 + part
            row_own[row : row + 1] = gt_ref[tap : tap + 1, part * width : (part + 1) * width]
    row_own[9:10] = gain_sum
    row_own[10:11] = gain2_ref[...]
    for place in range(4):
        row_own[11:12, place * WIDE : (place + 1) * WIDE] = stats_ref[place : place + 1]
    row_in[pl.ds(me, 1)] = row_own[...][None]
    rows_out = [
        send(row_own, row_in.at[me], (row_s.at[bit - 1], row_r.at[bit - 1]), "seq", me ^ bit)
        for bit in range(1, 8)
    ]
    to_z = []
    for c in range(chunks):
        for copy in again[c]:
            copy.wait()
        for half, place in ((first_two, 4), (last_two, 5)):
            both = here[c, chip, half].astype(F32) + chip_in[c, place].astype(F32)
            mine[c, half] = both.astype(BF16)
        to_z.append(
            [
                send(
                    mine.at[c, z ^ bit],
                    z_in.at[c, bit - 1],
                    (z_s.at[c, bit - 1], z_r.at[c, bit - 1]),
                    "batch",
                    z ^ bit,
                )
                for bit in range(1, 4)
            ]
        )
    for copy in rows_out:
        copy.wait()
    total = row_in[0]
    for place in range(1, 8):
        total = total + row_in[place]
    row_sum[...] = total
    col_in[pl.ds(z, 1)] = total[None]
    cols_out = [
        send(row_sum, col_in.at[z], (col_s.at[bit - 1], col_r.at[bit - 1]), "batch", z ^ bit)
        for bit in range(1, 4)
    ]
    last, feed_on, qkv_on = [], [], []
    for c in range(chunks):
        more, on = relay(feed_all.at[c], feed_first[c], fa_s.at[c], fa_r.at[c])
        last += more
        feed_on.append(on)
    qkv_first = []
    for c in range(chunks):
        for copy in to_z[c]:
            copy.wait()
        both = mine[c, z].astype(F32)
        for bit in range(3):
            both = both + z_in[c, bit].astype(F32)
        qkv_all[c, pl.ds(me, 1)] = both.astype(BF16)[None]
        qkv_first.append(spread(qkv_all.at[c], qkv_s.at[c], qkv_r.at[c]))
    for c in range(chunks):
        more, on = relay(qkv_all.at[c], qkv_first[c], qkv_s.at[c], qkv_r.at[c])
        last += more
        qkv_on.append(on)
    for c in range(chunks):
        last += finish_relay(feed_all.at[c], feed_on[c], fa_s.at[c], fa_r.at[c])
    for c in range(chunks):
        last += finish_relay(qkv_all.at[c], qkv_on[c], qkv_s.at[c], qkv_r.at[c])
    for copy in cols_out:
        copy.wait()
    small_out[...] = ((col_in[0] + col_in[1]) + col_in[2]) + col_in[3]
    for copy in last:
        copy.wait()
    qkv_out[...] = qkv_all[...]
    feed_out[...] = feed_all[...]
    gx_copy.wait()


def finish(units, normed1, x, d_hidden, w_qkv, gain, feed, far, grad_taps, grad_norm2, stats):
    groups, block, width = x.shape
    chunks, rows, feed_rows = 3, 48, 144
    small_shape = (16, width)
    tokens = groups * block
    slots = units.shape[0]
    vmem = pl.BlockSpec(memory_space=pltpu.VMEM)
    anywhere = pl.BlockSpec(memory_space=pl.ANY)
    pairs = [DMA((slots, GROUP)), DMA((slots, GROUP))]
    for shape in [(), (6,), (3,), (8,), (3,), (8,)]:
        pairs += [DMA((chunks,) + shape), DMA((chunks,) + shape)]
    low = lambda *shape: pltpu.VMEM(shape, BF16)
    return pl.pallas_call(
        finish_kernel,
        in_specs=[anywhere] * 5 + [vmem, anywhere, anywhere] + [vmem] * 3,
        out_specs=[anywhere, vmem, vmem, vmem],
        out_shape=[
            jax.ShapeDtypeStruct(x.shape, F32),
            jax.ShapeDtypeStruct((chunks, 8, rows, PART), BF16),
            jax.ShapeDtypeStruct((chunks, 8, feed_rows, PART), BF16),
            jax.ShapeDtypeStruct(small_shape, F32),
        ],
        scratch_shapes=[
            low(groups * PAIRS, block, 3 * WIDE),
            low(groups, block, width),
            low(width, tokens),
            low(groups, block, width),
            pltpu.VMEM((groups, block, width), F32),
            low(*w_qkv.shape),
            low(*feed.shape),
            low(*far.shape),
            low(*far.shape[1:]),
            low(3, *far.shape[2:]),
            pltpu.VMEM((tokens, width), F32),
            pltpu.VMEM((PAIRS, width, 3 * WIDE), F32),
            low(chunks, 2, 4, 4, rows, PART),
            low(chunks, 4, 4, rows, PART),
            low(chunks, 4, 4, rows, PART),
            low(chunks, 6, 2, rows, PART),
            low(chunks, 4, rows, PART),
            low(chunks, 3, rows, PART),
            low(chunks, 8, rows, PART),
            low(*feed.shape[1:]),
            low(chunks, 3, feed_rows, PART),
            low(chunks, 8, feed_rows, PART),
            pltpu.VMEM(small_shape, F32),
            pltpu.VMEM((8,) + small_shape, F32),
            pltpu.VMEM(small_shape, F32),
            pltpu.VMEM((4,) + small_shape, F32),
            DMA((7,)),
            DMA((6,)),
            DMA((6,)),
        ]
        + pairs
        + [DMA((7,)), DMA((7,)), DMA((3,)), DMA((3,))],
        compiler_params=group_params(0),
        name="finish",
    )(units, normed1, x, d_hidden, w_qkv, gain, feed, far, grad_taps, grad_norm2, stats)


def unpack_kernel(
    feed_ref, qkv_ref, small_ref, down_ref, up_ref, out_ref, grad_ref, taps_ref, gain1_ref, gain2_ref, rms_ref
):
    for r in range(2):
        rows, cols = slice(r * 96, r * 96 + 96), slice(r * PART, (r + 1) * PART)
        down_ref[rows, :PART] = feed_ref[0, r, :96].astype(F32)
        down_ref[r * 96 : r * 96 + 48, PART:] = feed_ref[0, r, 96:].astype(F32)
        down_ref[r * 96 + 48 : r * 96 + 96, PART:] = feed_ref[1, r, :48].astype(F32)
        up_ref[:96, cols] = feed_ref[1, r, 48:].astype(F32)
        up_ref[96:, cols] = feed_ref[2, r, :96].astype(F32)
        out_ref[r * 48 : r * 48 + 48] = feed_ref[2, r, 96:].astype(F32)
        for c in range(3):
            for part in range(3):
                begin = part * PAIRS * WIDE + (r * 3 + c) * WIDE
                grad_ref[:, begin : begin + WIDE] = qkv_ref[
                    c, r, :, part * WIDE : (part + 1) * WIDE
                ].astype(F32)

    @pl.when(pl.program_id(0) == 0)
    def _():
        width = small_ref.shape[1]
        for tap in range(3):
            for part in range(3):
                row = tap * 3 + part
                taps_ref[tap : tap + 1, part * width : (part + 1) * width] = small_ref[row : row + 1]
        z = lax.axis_index("batch")
        for row, ref in ((9, gain1_ref), (10, gain2_ref)):
            own = jnp.zeros((1, width // 4), F32)
            for batch in range(4):
                share = small_ref[row : row + 1, batch * width // 4 : (batch + 1) * width // 4]
                own = jnp.where(z == batch, share, own)
            ref[...] = own.reshape(ref.shape)
        count = small_ref[11:12, 3 * WIDE : 4 * WIDE]
        lane = lax.broadcasted_iota(jnp.int32, (1, WIDE), 1)
        total = jnp.zeros((1, WIDE), F32)
        for place in range(3):
            total = jnp.where(lane == place, small_ref[11:12, place * WIDE : (place + 1) * WIDE], total)
        rms_ref[...] = jnp.sqrt(total / (width * count)).reshape(rms_ref.shape)


def unpack(feed, qkv, small):
    wide = 3 * PAIRS * WIDE
    return pl.pallas_call(
        unpack_kernel,
        grid=(4,),
        in_specs=[
            pl.BlockSpec((3, 2, 144, PART), lambda i: (0, i, 0, 0)),
            pl.BlockSpec((3, 2, 48, PART), lambda i: (0, i, 0, 0)),
            pl.BlockSpec(small.shape, lambda i: (0, 0)),
        ],
        out_specs=[
            pl.BlockSpec((192, 2 * PART), lambda i: (i, 0)),
            pl.BlockSpec((192, 2 * PART), lambda i: (0, i)),
            pl.BlockSpec((96, PART), lambda i: (i % 2, i // 2)),
            pl.BlockSpec((48, wide), lambda i: (i, 0)),
            pl.BlockSpec((3, wide), lambda i: (0, 0)),
            pl.BlockSpec((192,), lambda i: (0,)),
            pl.BlockSpec((192,), lambda i: (0,)),
            pl.BlockSpec((WIDE,), lambda i: (0,)),
        ],
        out_shape=[
            jax.ShapeDtypeStruct((768, 2 * PART), F32),
            jax.ShapeDtypeStruct((192, 8 * PART), F32),
            jax.ShapeDtypeStruct((192, 2 * PART), F32),
            jax.ShapeDtypeStruct((192, wide), F32),
            jax.ShapeDtypeStruct((3, wide), F32),
            jax.ShapeDtypeStruct((192,), F32),
            jax.ShapeDtypeStruct((192,), F32),
            jax.ShapeDtypeStruct((WIDE,), F32),
        ],
        compiler_params=params(),
        name="unpack",
    )(feed, qkv, small)


def exchange(blocks):
    return lax.all_to_all(blocks, "seq", 0, 0, tiled=True)


def plain_gradients(feed, qkv):
    down = feed[:, :, :192].reshape(8, 4, 2, 96, PART).transpose(1, 0, 3, 2, 4)
    up = feed[:, :, 192:384].transpose(1, 2, 0, 3)
    out = feed[:, :, 384:].reshape(2, 4, 4, 48, PART).transpose(2, 1, 3, 0, 4)
    grad = qkv.reshape(3, 2, 4, 4, 48, 3, WIDE).transpose(3, 2, 4, 5, 1, 0, 6)
    return (
        down.reshape(3072, 768),
        up.reshape(768, 3072),
        out.reshape(768, 768),
        grad.reshape(768, 2304),
    )


def shards(
    stream_in,
    lengths,
    token_mask,
    norm1_gain,
    w_qkv,
    conv_taps,
    w_out,
    norm2_gain,
    w_up,
    w_down,
    grad_output,
):
    groups, block_len, width = stream_in.shape
    count = lax.axis_size("seq")
    batches = lax.axis_size("batch")
    units = groups * PAIRS
    slots = -(-units // count)
    spare = slots * count - units
    fitted = count == GROUP and batches == 4 and units % GROUP == 0

    def to_heads(blocks):
        blocks = jnp.pad(blocks, ((0, spare), (0, 0), (0, 0)))
        blocks = blocks.reshape((slots, count) + blocks.shape[1:])
        return jnp.stack([exchange(blocks[slot]) for slot in range(slots)])

    def to_tokens(rows):
        rows = rows.reshape(slots, count, block_len, rows.shape[2])
        return jnp.concatenate([exchange(rows[slot]) for slot in range(slots)])[:units]

    rest = (grad_output, token_mask, lengths, norm2_gain, w_out, w_up, w_down)
    if fitted:
        normed1, proj, unit_out, attended, unit_lse = front(
            stream_in, norm1_gain, w_qkv, conv_taps, lengths
        )
        proj = proj.reshape(slots, count * block_len, 3 * WIDE)
        stream_out, d_hidden, d_units, *saved = dense_send(stream_in, attended, *rest)
    else:
        normed1, proj = project(stream_in, norm1_gain, w_qkv)
        proj = to_heads(proj).reshape(slots, count * block_len, 3 * WIDE)
        unit_out, unit_lse = attend(lengths, proj, conv_taps, count)
        attended = to_tokens(unit_out)
        stream_out, d_hidden, d_units, *saved = dense(stream_in, attended, *rest)
        d_units = to_heads(d_units)
    normed2, squared, d_up, d_attn, cotangent, grad_norm2, stats = saved
    d_units = d_units.reshape(slots, count * block_len, WIDE)
    saved = (squared, cotangent, normed2, d_up, attended, d_attn)
    if fitted:
        feed, far = feed_grads_send(*saved)
        same_core = [[core + 2 * chip for chip in range(4)] for core in range(2)]
        feed = lax.all_to_all(feed, "seq", 0, 0, tiled=True, axis_index_groups=same_core)
    else:
        feed = feed_grads(*saved)
    back, grad_taps = attend_back(lengths, proj, conv_taps, unit_out, d_units, unit_lse, count)

    if fitted:
        blocks = back.reshape(slots, count, block_len, 3 * WIDE)
        grad_input, qkv, feed, small = finish(
            blocks, normed1, stream_in, d_hidden, w_qkv, norm1_gain, feed, far, grad_taps, grad_norm2, stats
        )
        down, up, out, grad_qkv, taps, gain1, gain2, rms = unpack(feed, qkv, small)
        rms = rms[:3]
    else:
        pieces, grad_input, grad_norm1 = input_grads(
            to_tokens(back), normed1, stream_in, d_hidden, w_qkv, norm1_gain
        )

        def reduce(gradient):
            share = lax.psum_scatter(gradient, ("batch", "seq"), scatter_dimension=0, tiled=True)
            return lax.all_gather(share, "seq", axis=0, tiled=True).astype(F32)

        down, up, out, grad_qkv = map(reduce, plain_gradients(feed, pieces))
        small = (grad_taps[:3], grad_norm1[0], grad_norm2[0], stats[:4, 0])
        taps, gain1, gain2, stats = lax.psum(small, ("seq", "batch"))
        share = width // batches
        begin = lax.axis_index("batch") * share
        gain1, gain2 = (lax.dynamic_slice_in_dim(gain, begin, share) for gain in (gain1, gain2))
        rms = jnp.sqrt(stats[:3] / (width * stats[3]))
    return (stream_out, grad_input, gain1, grad_qkv, taps, out, gain2, up, down, rms)


def solution(mesh):
    tokens = P("batch", "seq", None)
    return jax.shard_map(
        shards,
        mesh=mesh,
        in_specs=(
            tokens,
            P("batch"),
            P("batch", "seq"),
            P(),
            P(),
            P(),
            P(),
            P(),
            P(),
            P(),
            tokens,
        ),
        out_specs=(
            tokens,
            tokens,
            P("batch"),
            P("batch", None),
            P(),
            P("batch", None),
            P("batch"),
            P("batch", None),
            P("batch", None),
            P(),
        ),
        check_vma=False,
    )
```

```python
import functools
import math

import jax
import jax.numpy as jnp
from jax import lax
from jax.experimental import pallas as pl
from jax.experimental.pallas import tpu as pltpu
from jax.sharding import PartitionSpec as P

HEADS = 12
HEAD = 64
PAIRS = HEADS // 2
WIDE = 2 * HEAD
TILE = 256
ROWS = 512
BACK = 256
STRIP = 32
LIMIT = 62 << 20
NEG = -1e30
F32 = jnp.float32
BF16 = jnp.bfloat16


def mm(left_op, right_op):
    return jnp.dot(left_op, right_op, preferred_element_type=F32)


def mm_nt(left_op, right_op):
    return lax.dot_general(
        left_op, right_op, (((1,), (1,)), ((), ())), preferred_element_type=F32
    )


def mm_tn(left_op, right_op):
    return lax.dot_general(
        left_op, right_op, (((0,), (0,)), ((), ())), preferred_element_type=F32
    )


def params():
    return pltpu.CompilerParams(vmem_limit_bytes=LIMIT)


MESH = pl.DeviceIdType.MESH
GROUP = 8
DMA = pltpu.SemaphoreType.DMA


def remote(source, target, sems, axis, peer):
    return pltpu.make_async_remote_copy(
        src_ref=source,
        dst_ref=target,
        send_sem=sems[0],
        recv_sem=sems[1],
        device_id={axis: peer},
        device_id_type=MESH,
    )


def meet_group():
    me = lax.axis_index("seq")
    barrier = pltpu.get_barrier_semaphore()
    for bit in range(1, GROUP):
        pl.semaphore_signal(barrier, inc=1, device_id={"seq": me ^ bit}, device_id_type=MESH)
    pl.semaphore_wait(barrier, GROUP - 1)


def unit_copy(blocks, inbox, sems, unit):
    me = lax.axis_index("seq")
    owner, slot = lax.rem(unit, GROUP), unit // GROUP
    return owner, remote(
        blocks.at[unit],
        inbox.at[slot, me],
        (sems[0].at[unit], sems[1].at[slot, me ^ owner]),
        "seq",
        owner,
    )


def send_unit(blocks, inbox, sems, unit):
    me = lax.axis_index("seq")
    owner, copy = unit_copy(blocks, inbox, sems, unit)

    @pl.when(owner != me)
    def _():
        copy.start()

    @pl.when(owner == me)
    def _():
        slot = unit // GROUP
        pltpu.make_async_copy(blocks.at[unit], inbox.at[slot, me], sems[1].at[slot, 0]).start()


def wait_unit(blocks, inbox, sems, slot):
    me = lax.axis_index("seq")
    unit = slot * GROUP + me
    pltpu.make_async_copy(blocks.at[unit], inbox.at[slot, me], sems[1].at[slot, 0]).wait()
    for bit in range(1, GROUP):
        remote(
            blocks.at[unit],
            inbox.at[slot, me ^ bit],
            (sems[0].at[unit], sems[1].at[slot, bit]),
            "seq",
            me ^ bit,
        ).wait_recv()


def wait_sent(blocks, inbox, sems):
    me = lax.axis_index("seq")

    def one(unit, carry):
        owner, copy = unit_copy(blocks, inbox, sems, unit)
        pl.when(owner != me)(copy.wait_send)
        return carry

    lax.fori_loop(0, blocks.shape[0], one, 0)


def wait_units(blocks, inbox, sems):
    for slot in range(blocks.shape[0] // GROUP):
        wait_unit(blocks, inbox, sems, slot)
    wait_sent(blocks, inbox, sems)


def block_copies(units, inbox, sems, slot):
    me = lax.axis_index("seq")
    return [
        remote(
            units.at[slot, me ^ bit],
            inbox.at[slot * GROUP + me],
            (sems[0].at[slot, bit], sems[1].at[slot, bit]),
            "seq",
            me ^ bit,
        )
        for bit in range(1, GROUP)
    ]


def own_block(units, inbox, sems, slot):
    me = lax.axis_index("seq")
    return pltpu.make_async_copy(
        units.at[slot, me], inbox.at[slot * GROUP + me], sems[1].at[slot, 0]
    )


def send_blocks(units, inbox, sems, slot):
    own_block(units, inbox, sems, slot).start()
    for copy in block_copies(units, inbox, sems, slot):
        copy.start()


def wait_blocks(units, inbox, sems, slot):
    own_block(units, inbox, sems, slot).wait()
    for copy in block_copies(units, inbox, sems, slot):
        copy.wait()


def group_params(number):
    return pltpu.CompilerParams(
        collective_id=number, has_side_effects=True, vmem_limit_bytes=LIMIT
    )


def gain_row(gain_ref):
    return gain_ref[...].astype(F32).reshape(1, gain_ref.shape[0])


def project_kernel(x_ref, gain_ref, w_ref, n_ref, p_ref):
    x = x_ref[0].astype(F32)
    factor = lax.rsqrt(jnp.mean(x * x, axis=-1, keepdims=True) + 1e-06)
    normed = (x * factor * gain_row(gain_ref)).astype(BF16)
    n_ref[0] = normed
    width = x.shape[1]
    for part in range(3):
        cols = mm(normed, w_ref[:, part * width : (part + 1) * width])
        for pair in range(PAIRS):
            p_ref[pair, :, part * WIDE : (part + 1) * WIDE] = cols[
                :, pair * WIDE : (pair + 1) * WIDE
            ].astype(BF16)


def project(x, gain, w_qkv):
    groups, rows, width = x.shape
    return pl.pallas_call(
        project_kernel,
        grid=(groups,),
        in_specs=[
            pl.BlockSpec((1, rows, width), lambda s: (s, 0, 0)),
            pl.BlockSpec((width,), lambda s: (0,)),
            pl.BlockSpec(w_qkv.shape, lambda s: (0, 0)),
        ],
        out_specs=[
            pl.BlockSpec((1, rows, width), lambda s: (s, 0, 0)),
            pl.BlockSpec((PAIRS, rows, 3 * WIDE), lambda s: (s, 0, 0)),
        ],
        out_shape=[
            jax.ShapeDtypeStruct(x.shape, BF16),
            jax.ShapeDtypeStruct((groups * PAIRS, rows, 3 * WIDE), BF16),
        ],
        compiler_params=params(),
        name="project",
    )(x, gain, w_qkv)


def stack_heads(rows):
    lane = lax.broadcasted_iota(jnp.int32, rows.shape, 1)
    zero = jnp.zeros_like(rows)
    first = jnp.where(lane < HEAD, rows, zero)
    second = jnp.where(lane < HEAD, zero, rows)
    return jnp.concatenate([first, second], axis=0)


def unstack_heads(rows):
    half = rows.shape[0] // 2
    lane = lax.broadcasted_iota(jnp.int32, (half, rows.shape[1]), 1)
    return jnp.where(lane < HEAD, rows[:half], rows[half:])


def step_rows(index, size):
    return pl.ds(pl.multiple_of(index * size, size), size)


def own_unit(lengths, groups, count, slot):
    unit = slot * count + lax.axis_index("seq")
    length = lengths[jnp.minimum(unit // PAIRS, groups - 1)]
    return jnp.where(unit < groups * PAIRS, length, 0), lax.rem(unit, PAIRS)


def pair_taps(taps_ref, taps_sc, pair):
    width = taps_ref.shape[1] // 3
    for part in range(3):
        cols = pl.ds(pl.multiple_of(part * width + pair * WIDE, WIDE), WIDE)
        taps_sc[0:3, part * WIDE : (part + 1) * WIDE] = taps_ref[:, cols].astype(F32)


def convolve(wide_ref, taps_ref, tile, cols):
    begin = 8 + tile * TILE
    total = taps_ref[0:1, cols] * wide_ref[begin : begin + TILE, cols]
    total += taps_ref[1:2, cols] * wide_ref[begin - 1 : begin - 1 + TILE, cols]
    total += taps_ref[2:3, cols] * wide_ref[begin - 2 : begin - 2 + TILE, cols]
    return total.astype(BF16)


Q_COLS, K_COLS, V_COLS = (slice(part * WIDE, (part + 1) * WIDE) for part in range(3))


def key_limits(index, length, size):
    lane = lax.broadcasted_iota(jnp.int32, (STRIP, 2 * size), 1)
    return jnp.minimum(index * size + (lane & (size - 1)) + 1, length)


def over_key_steps(index, length, size, visit, carry):
    full = jnp.minimum(index * size, length) // size
    last = (jnp.minimum((index + 1) * size, length) + size - 1) // size
    carry = lax.fori_loop(0, full, lambda step, c: visit(step, False, c), carry)
    return lax.fori_loop(full, last, lambda step, c: visit(step, True, c), carry)


def attend_kernel(
    groups, count, lengths, p_ref, taps_ref, o_ref, lse_ref, taps, wide, q_sc, k_sc, vt_sc, acc, s_sc, e_sc
):
    length, pair = own_unit(lengths, groups, count, pl.program_id(0))
    wide[0:8] = jnp.zeros((8, wide.shape[1]), F32)
    wide[8:] = p_ref[0].astype(F32)
    attend_unit(
        length, pair, False, taps_ref, o_ref.at[0], lse_ref.at[0], taps, wide, q_sc, k_sc, vt_sc, acc, s_sc, e_sc
    )


def attend_unit(
    length, pair, whole, taps_ref, o_ref, lse_ref, taps, wide, q_sc, k_sc, vt_sc, acc, s_sc, e_sc
):
    tiles = q_sc.shape[0] // TILE
    per_step = ROWS // TILE
    pair_taps(taps_ref, taps, pair)
    vt_sc[:, WIDE:] = jnp.ones((vt_sc.shape[0], vt_sc.shape[1] - WIDE, ROWS), BF16)
    for tile in range(tiles):
        rows = slice(tile * TILE, (tile + 1) * TILE)
        q_sc[rows] = convolve(wide, taps, tile, Q_COLS) * (1.0 / math.sqrt(HEAD))

        def keys_values():
            k_sc[rows] = convolve(wide, taps, tile, K_COLS)
            cols = slice(tile % per_step * TILE, (tile % per_step + 1) * TILE)
            values = convolve(wide, taps, tile, V_COLS)
            vt_sc[tile // per_step, :WIDE, cols] = values.astype(F32).T.astype(BF16)

        if whole:
            keys_values()
        else:
            pl.when(tile // per_step * ROWS < length)(keys_values)

    k_row = lax.broadcasted_iota(jnp.int32, (STRIP, 2 * ROWS), 0)

    def query_step(index, carry):
        q_stack = stack_heads(q_sc[step_rows(index, ROWS)])
        limit = key_limits(index, length, ROWS)
        acc[...] = jnp.zeros(acc.shape, F32)

        def visit(step, mask, old):
            s_sc[...] = mm_nt(k_sc[step_rows(step, ROWS)], q_stack)

            def strip_of(begin):
                scores = s_sc[begin : begin + STRIP]
                if mask == "none":
                    return scores
                if mask == "length":
                    keep = k_row[:, :WIDE] < length - (step * ROWS + begin)
                    keep = jnp.concatenate([keep] * (2 * ROWS // WIDE), axis=1)
                else:
                    keep = k_row < limit - (step * ROWS + begin)
                return jnp.where(keep, scores, NEG)

            top = jnp.full((8, 2 * ROWS), NEG, F32)
            for begin in range(0, ROWS, STRIP):
                scores = strip_of(begin)
                for low in range(0, STRIP, 8):
                    top = jnp.maximum(top, scores[low : low + 8])
            new = jnp.maximum(old, jnp.max(top, axis=0, keepdims=True))
            for begin in range(0, ROWS, STRIP):
                e_sc[begin : begin + STRIP] = jnp.exp(strip_of(begin) - new).astype(BF16)
            acc[...] = acc[...] * jnp.exp(old - new) + mm(vt_sc[step], e_sc[...])
            return new

        top = jnp.full((1, 2 * ROWS), NEG, F32)
        if whole:
            top = lax.fori_loop(0, index, lambda step, c: visit(step, "length", c), top)
            top = visit(index, "both", top)
        else:

            def either(step, masked, top):
                return visit(step, "both" if masked else "none", top)

            top = over_key_steps(index, length, ROWS, either, top)
        total = acc[WIDE : WIDE + 1]
        out = (acc[:WIDE] / total).T
        o_ref[step_rows(index, ROWS)] = unstack_heads(out).astype(BF16)
        lse_ref[pl.ds(index, 1)] = top + jnp.log(total)
        return carry

    lax.fori_loop(0, q_sc.shape[0] // ROWS, query_step, 0)


def attend(lengths, proj, taps, count):
    slots, rows = proj.shape[:2]
    steps = rows // ROWS
    own = lambda i, lengths: (i, 0, 0)
    return pl.pallas_call(
        functools.partial(attend_kernel, lengths.shape[0], count),
        grid_spec=pltpu.PrefetchScalarGridSpec(
            num_scalar_prefetch=1,
            grid=(slots,),
            in_specs=[
                pl.BlockSpec((1, rows, 3 * WIDE), own),
                pl.BlockSpec(taps.shape, lambda i, lengths: (0, 0)),
            ],
            out_specs=[
                pl.BlockSpec((1, rows, WIDE), own),
                pl.BlockSpec((1, steps, 2 * ROWS), own),
            ],
            scratch_shapes=[
                pltpu.VMEM((8, 3 * WIDE), F32),
                pltpu.VMEM((rows + 8, 3 * WIDE), F32),
                pltpu.VMEM((rows, WIDE), BF16),
                pltpu.VMEM((rows, WIDE), BF16),
                pltpu.VMEM((steps, WIDE + 16, ROWS), BF16),
                pltpu.VMEM((WIDE + 16, 2 * ROWS), F32),
                pltpu.VMEM((ROWS, 2 * ROWS), F32),
                pltpu.VMEM((ROWS, 2 * ROWS), BF16),
            ],
        ),
        out_shape=[
            jax.ShapeDtypeStruct((slots, rows, WIDE), BF16),
            jax.ShapeDtypeStruct((slots, steps, 2 * ROWS), F32),
        ],
        compiler_params=params(),
        name="attend",
    )(lengths, proj, taps)


def row_copies(units, inbox, sems, slot, block):
    me = lax.axis_index("seq")
    return [
        remote(
            units.at[slot, pl.ds(pl.multiple_of((me ^ bit) * block, block), block)],
            inbox.at[slot * GROUP + me],
            (sems[0].at[slot, bit], sems[1].at[slot, bit]),
            "seq",
            me ^ bit,
        )
        for bit in range(1, GROUP)
    ]


def own_rows(units, inbox, sems, slot, block):
    me = lax.axis_index("seq")
    return pltpu.make_async_copy(
        units.at[slot, pl.ds(pl.multiple_of(me * block, block), block)],
        inbox.at[slot * GROUP + me],
        sems[1].at[slot, 0],
    )


def send_rows(units, inbox, sems, slot, block):
    own_rows(units, inbox, sems, slot, block).start()
    for copy in row_copies(units, inbox, sems, slot, block):
        copy.start()


def wait_rows(units, inbox, sems, slot, block):
    own_rows(units, inbox, sems, slot, block).wait()
    for copy in row_copies(units, inbox, sems, slot, block):
        copy.wait()


def attend_back_kernel(
    groups, count, lengths, p_ref, taps_ref, o_ref, do_ref, lse_ref, dp_ref, gt_ref,
    taps, wide, q_sc, k_sc, v_sc, kt_sc, dm, dqt, s_sc, d_sc, e_sc, f_sc,
):
    p_ref, o_ref, do_ref, lse_ref = p_ref.at[0], o_ref.at[0], do_ref.at[0], lse_ref.at[0]
    dp_ref = dp_ref.at[0]
    length, pair = own_unit(lengths, groups, count, pl.program_id(0))
    tiles = p_ref.shape[0] // TILE
    per_step = BACK // TILE
    pair_taps(taps_ref, taps, pair)
    wide[0:8] = jnp.zeros((8, wide.shape[1]), F32)
    wide[8:] = p_ref[...].astype(F32)
    dm[...] = jnp.zeros(dm.shape, F32)
    for tile in range(tiles):
        rows = slice(tile * TILE, (tile + 1) * TILE)

        @pl.when(tile // per_step * BACK < length)
        def _():
            q_sc[rows] = convolve(wide, taps, tile, Q_COLS) * (1.0 / math.sqrt(HEAD))
            keys = convolve(wide, taps, tile, K_COLS)
            k_sc[rows] = keys
            v_sc[rows] = convolve(wide, taps, tile, V_COLS)
            cols = slice(tile % per_step * TILE, (tile % per_step + 1) * TILE)
            kt_sc[tile // per_step, :, cols] = keys.astype(F32).T.astype(BF16)

    lane = lax.broadcasted_iota(jnp.int32, (8, WIDE), 1)
    row = lax.broadcasted_iota(jnp.int32, (8, WIDE), 0)
    picks = jnp.where((lane < HEAD) == (row == 0), 1.0, 0.0).astype(BF16)
    k_row = lax.broadcasted_iota(jnp.int32, (STRIP, 2 * BACK), 0)

    def query_step(index, carry):
        here = step_rows(index, BACK)
        q_stack = stack_heads(q_sc[here])
        d_rows = do_ref[here]
        d_stack = stack_heads(d_rows)
        product = d_rows.astype(F32) * o_ref[here].astype(F32)
        upper = product.astype(BF16)
        lower = (product - upper.astype(F32)).astype(BF16)
        sums = mm_nt(picks, upper) + mm_nt(picks, lower)
        delta = jnp.concatenate([sums[0:1], sums[1:2]], axis=1)
        line, begin = pl.ds(index * BACK // ROWS, 1), lax.rem(index * BACK, ROWS)
        lse = jnp.concatenate(
            [
                lse_ref[line, pl.ds(pl.multiple_of(head * ROWS + begin, BACK), BACK)]
                for head in range(2)
            ],
            axis=1,
        )
        limit = key_limits(index, length, BACK)
        dqt[...] = jnp.zeros(dqt.shape, F32)

        def visit(step, masked, carry):
            there = step_rows(step, BACK)
            s_sc[...] = mm_nt(k_sc[there], q_stack)
            d_sc[...] = mm_nt(v_sc[there], d_stack)
            for begin in range(0, BACK, STRIP):
                strip = slice(begin, begin + STRIP)
                probs = jnp.exp(s_sc[strip] - lse)
                if masked:
                    probs = jnp.where(k_row < limit - (step * BACK + begin), probs, 0.0)
                e_sc[strip] = probs.astype(BF16)
                f_sc[strip] = (probs * (d_sc[strip] - delta)).astype(BF16)
            dm[there, V_COLS] += mm(e_sc[...], d_stack)
            dm[there, K_COLS] += mm(f_sc[...], q_stack)
            dqt[...] += mm(kt_sc[step], f_sc[...])
            return carry

        over_key_steps(index, length, BACK, visit, 0)
        dm[here, Q_COLS] = unstack_heads(dqt[...].T) * (1.0 / math.sqrt(HEAD))
        return carry

    lax.fori_loop(0, (length + BACK - 1) // BACK, query_step, 0)

    @pl.when(pl.program_id(0) == 0)
    def _():
        gt_ref[...] = jnp.zeros(gt_ref.shape, F32)

    sums = [jnp.zeros((1, 3 * WIDE), F32) for _ in range(3)]
    for tile in range(tiles):
        begin = tile * TILE
        total = taps[0:1] * dm[begin : begin + TILE]
        total += taps[1:2] * dm[begin + 1 : begin + 1 + TILE]
        total += taps[2:3] * dm[begin + 2 : begin + 2 + TILE]
        dp_ref[begin : begin + TILE] = total.astype(BF16)
        for tap in range(3):
            behind = wide[begin + 8 - tap : begin + 8 - tap + TILE]
            sums[tap] += jnp.sum(dm[begin : begin + TILE] * behind, axis=0, keepdims=True)
    width = gt_ref.shape[1] // 3
    for tap in range(3):
        for part in range(3):
            cols = pl.ds(pl.multiple_of(part * width + pair * WIDE, WIDE), WIDE)
            gt_ref[tap : tap + 1, cols] += sums[tap][:, part * WIDE : (part + 1) * WIDE]


def attend_back(lengths, proj, taps, attended, d_attended, lse, count):
    slots, rows = proj.shape[:2]
    steps = rows // BACK
    own = lambda i, lengths: (i, 0, 0)
    whole = lambda i, lengths: (0, 0)
    return pl.pallas_call(
        functools.partial(attend_back_kernel, lengths.shape[0], count),
        grid_spec=pltpu.PrefetchScalarGridSpec(
            num_scalar_prefetch=1,
            grid=(slots,),
            in_specs=[
                pl.BlockSpec((1, rows, 3 * WIDE), own),
                pl.BlockSpec(taps.shape, whole),
                pl.BlockSpec((1, rows, WIDE), own),
                pl.BlockSpec((1, rows, WIDE), own),
                pl.BlockSpec((1,) + lse.shape[1:], own),
            ],
            out_specs=[
                pl.BlockSpec((1, rows, 3 * WIDE), own),
                pl.BlockSpec((8, taps.shape[1]), whole),
            ],
            scratch_shapes=[
                pltpu.VMEM((8, 3 * WIDE), F32),
                pltpu.VMEM((rows + 8, 3 * WIDE), F32),
                pltpu.VMEM((rows, WIDE), BF16),
                pltpu.VMEM((rows, WIDE), BF16),
                pltpu.VMEM((rows, WIDE), BF16),
                pltpu.VMEM((steps, WIDE, BACK), BF16),
                pltpu.VMEM((rows + 8, 3 * WIDE), F32),
                pltpu.VMEM((WIDE, 2 * BACK), F32),
                pltpu.VMEM((BACK, 2 * BACK), F32),
                pltpu.VMEM((BACK, 2 * BACK), F32),
                pltpu.VMEM((BACK, 2 * BACK), BF16),
                pltpu.VMEM((BACK, 2 * BACK), BF16),
            ],
        ),
        out_shape=[
            jax.ShapeDtypeStruct((slots, rows, 3 * WIDE), BF16),
            jax.ShapeDtypeStruct((8, taps.shape[1]), F32),
        ],
        compiler_params=params(),
        name="attend_back",
    )(lengths, proj, taps, attended, d_attended, lse)


def dense_kernel(
    group, x_ref, att_ref, cot_ref, mask_ref, lengths, gain_ref, wo_ref, wu_ref, wd_ref,
    out_ref, dh_ref, datt_ref, n2_ref, sq_ref, du_ref, da_ref, cz_ref, gain_grad_ref, stats_ref,
    act_sc, att_sc,
):
    rows, width = x_ref.shape[1:]
    hidden_units = wu_ref.shape[1]
    step = width
    for pair in range(PAIRS):
        att_sc[:, pair * WIDE : (pair + 1) * WIDE] = att_ref[pair]
    spot = lax.axis_index("seq") * rows + lax.broadcasted_iota(jnp.int32, (1, rows), 1)
    counts = jnp.where(spot < lengths[group], mask_ref[pl.ds(group, 1)].astype(F32), 0.0)
    weight = jnp.broadcast_to(counts, (WIDE, rows)).T[:, :1]
    gain = gain_row(gain_ref)
    branch = mm(att_sc[...], wo_ref[...])
    hidden = x_ref[0].astype(F32) + branch
    factor = lax.rsqrt(jnp.mean(hidden * hidden, axis=-1, keepdims=True) + 1e-06)
    normed = (hidden * factor * gain).astype(BF16)
    n2_ref[0] = normed
    total = jnp.zeros((rows, width), F32)
    for begin in range(0, hidden_units, step):
        cols = slice(begin, begin + step)
        active = jnp.maximum(mm(normed, wu_ref[:, cols]), 0.0)
        act_sc[:, cols] = active
        squared = (active * active).astype(BF16)
        sq_ref[0, :, cols] = squared
        total += mm(squared, wd_ref[cols])
    full = hidden + total
    out_ref[0] = full.astype(BF16)

    def masked(values):
        per_row = jnp.sum(values * values, axis=-1, keepdims=True)
        return jnp.sum(weight * per_row, axis=0, keepdims=True)

    @pl.when(group == 0)
    def _():
        stats_ref[...] = jnp.zeros(stats_ref.shape, F32)
        gain_grad_ref[...] = jnp.zeros(gain_grad_ref.shape, F32)

    parts = [masked(full), masked(branch), masked(total), jnp.sum(weight, axis=0, keepdims=True)]
    for place, part in enumerate(parts):
        stats_ref[place : place + 1] += jnp.broadcast_to(part, (1, WIDE))
    cotangent = (cot_ref[0].astype(F32) * weight).astype(BF16)
    cz_ref[0] = cotangent
    d_normed = jnp.zeros((rows, width), F32)
    for begin in range(0, hidden_units, step):
        cols = slice(begin, begin + step)
        d_squared = mm_nt(cotangent, wd_ref[cols])
        d_up = (2.0 * act_sc[:, cols] * d_squared).astype(BF16)
        du_ref[0, :, cols] = d_up
        d_normed += mm_nt(d_up, wu_ref[:, cols])
    weighted = d_normed * gain
    inner = jnp.mean(weighted * hidden, axis=-1, keepdims=True)
    d_hidden = cotangent.astype(F32) + factor * weighted - hidden * (factor * factor * factor) * inner
    gain_grad_ref[...] += jnp.sum(d_normed * hidden * factor, axis=0, keepdims=True)
    dh_ref[0] = d_hidden
    d_attn = d_hidden.astype(BF16)
    da_ref[0] = d_attn
    d_att = mm_nt(d_attn, wo_ref[...]).astype(BF16)
    for pair in range(PAIRS):
        datt_ref[pair] = d_att[:, pair * WIDE : (pair + 1) * WIDE]


def dense(x, attended, grad_output, token_mask, lengths, gain, w_out, w_up, w_down):
    groups, rows, width = x.shape
    hidden_units = w_up.shape[1]
    per_group = lambda s: (s, 0, 0)
    fixed = lambda s: (0, 0)
    once = pl.Buffered(1)
    row_block = pl.BlockSpec((1, rows, width), per_group)
    wide_block = pl.BlockSpec((1, rows, hidden_units), per_group)
    unit_block = pl.BlockSpec((PAIRS, rows, WIDE), per_group)
    low = jax.ShapeDtypeStruct(x.shape, BF16)
    wide_low = jax.ShapeDtypeStruct((groups, rows, hidden_units), BF16)
    return pl.pallas_call(
        lambda *refs: dense_kernel(pl.program_id(0), *refs),
        grid=(groups,),
        in_specs=[
            row_block,
            unit_block,
            row_block,
            pl.BlockSpec(token_mask.shape, fixed),
            pl.BlockSpec(memory_space=pltpu.SMEM),
            pl.BlockSpec((width,), lambda s: (0,)),
            pl.BlockSpec(w_out.shape, fixed, pipeline_mode=once),
            pl.BlockSpec(w_up.shape, fixed, pipeline_mode=once),
            pl.BlockSpec(w_down.shape, fixed, pipeline_mode=once),
        ],
        out_specs=[
            row_block,
            row_block,
            unit_block,
            row_block,
            wide_block,
            wide_block,
            row_block,
            row_block,
            pl.BlockSpec((1, width), fixed),
            pl.BlockSpec((8, WIDE), fixed),
        ],
        out_shape=[
            low,
            jax.ShapeDtypeStruct(x.shape, F32),
            jax.ShapeDtypeStruct((groups * PAIRS, rows, WIDE), BF16),
            low,
            wide_low,
            wide_low,
            low,
            low,
            jax.ShapeDtypeStruct((1, width), F32),
            jax.ShapeDtypeStruct((8, WIDE), F32),
        ],
        scratch_shapes=[pltpu.VMEM((rows, hidden_units), F32), pltpu.VMEM((rows, width), BF16)],
        compiler_params=params(),
        name="dense",
    )(x, attended, grad_output, token_mask, lengths, gain, w_out, w_up, w_down)


def front_kernel(
    lengths, x_ref, gain_ref, w_ref, taps_ref, cot_ref, mask_ref, gain2_ref, wo_ref, wu_ref, wd_ref,
    n1_out, proj_out, units_out, att_out, lse_ref, inbox, gain_grad_ref, stats_ref,
    out_ref, dh_ref, n2_ref, sq_ref, du_ref, da_ref, cz_ref,
    x_v, w_v, n1_v, blocks, proj, units, att, taps, wide, q_sc, k_sc, vt_sc, acc, s_sc, e_sc,
    cot_v, wo_v, wu_v, wd_v, act_sc, att_sc, d_blocks,
    out_b, dh_b, n2_b, sq_b, du_b, da_b, cz_b,
    load_s, store_s, keep_s, send_s, send_r, att_s, att_r, back_s, back_r,
):
    groups, block = x_v.shape[:2]
    slots = proj.shape[0]
    sems, att_sems, back_sems = (send_s, send_r), (att_s, att_r), (back_s, back_r)
    loads = [
        pltpu.make_async_copy(source, target, load_s.at[place])
        for place, (source, target) in enumerate(
            [
                (w_ref, w_v),
                (x_ref, x_v),
                (wo_ref, wo_v),
                (wu_ref, wu_v),
                (wd_ref, wd_v),
                (cot_ref, cot_v),
            ]
        )
    ]
    keeps = [
        pltpu.make_async_copy(source, target, keep_s.at[place])
        for place, (source, target) in enumerate(
            [(n1_v, n1_out), (proj, proj_out), (units, units_out), (att, att_out)]
        )
    ]
    buffers = (out_b, dh_b, n2_b, sq_b, du_b, da_b, cz_b)
    targets = (out_ref, dh_ref, n2_ref, sq_ref, du_ref, da_ref, cz_ref)

    def stores(group):
        side = lax.rem(group, 2)
        return [
            pltpu.make_async_copy(buffer.at[side], target.at[group], store_s.at[place, side])
            for place, (buffer, target) in enumerate(zip(buffers, targets))
        ]

    for copy in loads:
        copy.start()
    meet_group()
    for copy in loads[:2]:
        copy.wait()

    def sequence(group, carry):
        here = pl.ds(group, 1)
        project_kernel(
            x_v.at[here], gain_ref, w_v, n1_v.at[here], blocks.at[pl.ds(group * PAIRS, PAIRS)]
        )
        for pair in range(PAIRS):
            send_unit(blocks, proj, sems, group * PAIRS + pair)
        return carry

    lax.fori_loop(0, groups, sequence, 0)
    keeps[0].start()

    def one_slot(slot, carry):
        wait_unit(blocks, proj, sems, slot)

        @pl.when(slot == slots - 1)
        def _():
            for done in range(slots - 1):
                send_rows(units, att, att_sems, done, block)

        length, pair = own_unit(lengths, groups, GROUP, slot)
        wide[0:8] = jnp.zeros((8, wide.shape[1]), F32)
        for place in range(GROUP):
            wide[8 + place * block : 8 + (place + 1) * block] = proj[slot, place].astype(F32)
        attend_unit(
            length, pair, True, taps_ref, units.at[slot], lse_ref.at[slot],
            taps, wide, q_sc, k_sc, vt_sc, acc, s_sc, e_sc,
        )
        return carry

    lax.fori_loop(0, slots, one_slot, 0)
    send_rows(units, att, att_sems, slots - 1, block)
    keeps[1].start()
    keeps[2].start()
    for copy in loads[2:]:
        copy.wait()

    def dense_group(group, carry):
        for slot in range(slots):

            @pl.when(group == slot * GROUP // PAIRS)
            def _():
                wait_rows(units, att, att_sems, slot, block)
                if slot == slots - 1:
                    keeps[3].start()

        @pl.when(group >= 2)
        def _():
            for copy in stores(group - 2):
                copy.wait()

        here, side = pl.ds(group, 1), pl.ds(lax.rem(group, 2), 1)
        unit = pl.ds(group * PAIRS, PAIRS)
        dense_kernel(
            group, x_v.at[here], att.at[unit], cot_v.at[here], mask_ref, lengths, gain2_ref,
            wo_v, wu_v, wd_v, out_b.at[side], dh_b.at[side], d_blocks.at[unit], n2_b.at[side],
            sq_b.at[side], du_b.at[side], da_b.at[side], cz_b.at[side], gain_grad_ref, stats_ref,
            act_sc, att_sc,
        )
        for pair in range(PAIRS):
            send_unit(d_blocks, inbox, back_sems, group * PAIRS + pair)
        for copy in stores(group):
            copy.start()
        return carry

    lax.fori_loop(0, groups, dense_group, 0)
    wait_sent(blocks, proj, sems)
    wait_units(d_blocks, inbox, back_sems)
    for group in (groups - 2, groups - 1):
        for copy in stores(group):
            copy.wait()
    for copy in keeps:
        copy.wait()


def front(x, gain, w_qkv, taps, lengths, grad_output, token_mask, gain2, w_out, w_up, w_down):
    groups, block, width = x.shape
    hidden_units = w_up.shape[1]
    units = groups * PAIRS
    slots = units // GROUP
    rows = GROUP * block
    steps = rows // ROWS
    anywhere = pl.BlockSpec(memory_space=pl.ANY)
    vmem = pl.BlockSpec(memory_space=pltpu.VMEM)
    low = lambda *shape: pltpu.VMEM(shape, BF16)
    low_out = lambda *shape: jax.ShapeDtypeStruct(shape, BF16)
    wide_out = (groups, block, hidden_units)
    return pl.pallas_call(
        front_kernel,
        in_specs=[pl.BlockSpec(memory_space=pltpu.SMEM), anywhere, vmem, anywhere, vmem]
        + [anywhere, vmem, vmem, anywhere, anywhere, anywhere],
        out_specs=[anywhere] * 4 + [vmem, anywhere, vmem, vmem] + [anywhere] * 7,
        out_shape=[
            low_out(*x.shape),
            low_out(slots, GROUP, block, 3 * WIDE),
            low_out(slots, rows, WIDE),
            low_out(units, block, WIDE),
            jax.ShapeDtypeStruct((slots, steps, 2 * ROWS), F32),
            low_out(slots, GROUP, block, WIDE),
            jax.ShapeDtypeStruct((1, width), F32),
            jax.ShapeDtypeStruct((8, WIDE), F32),
            low_out(*x.shape),
            jax.ShapeDtypeStruct(x.shape, F32),
            low_out(*x.shape),
            low_out(*wide_out),
            low_out(*wide_out),
            low_out(*x.shape),
            low_out(*x.shape),
        ],
        scratch_shapes=[
            low(*x.shape),
            low(*w_qkv.shape),
            low(*x.shape),
            low(units, block, 3 * WIDE),
            low(slots, GROUP, block, 3 * WIDE),
            low(slots, rows, WIDE),
            low(units, block, WIDE),
            pltpu.VMEM((8, 3 * WIDE), F32),
            pltpu.VMEM((rows + 8, 3 * WIDE), F32),
            low(rows, WIDE),
            low(rows, WIDE),
            low(steps, WIDE + 16, ROWS),
            pltpu.VMEM((WIDE + 16, 2 * ROWS), F32),
            pltpu.VMEM((ROWS, 2 * ROWS), F32),
            low(ROWS, 2 * ROWS),
            low(*x.shape),
            low(*w_out.shape),
            low(*w_up.shape),
            low(*w_down.shape),
            pltpu.VMEM((block, hidden_units), F32),
            low(block, width),
            low(units, block, WIDE),
            low(2, block, width),
            pltpu.VMEM((2, block, width), F32),
            low(2, block, width),
            low(2, block, hidden_units),
            low(2, block, hidden_units),
            low(2, block, width),
            low(2, block, width),
            DMA((6,)),
            DMA((7, 2)),
            DMA((4,)),
            DMA((units,)),
            DMA((slots, GROUP)),
            DMA((slots, GROUP)),
            DMA((slots, GROUP)),
            DMA((units,)),
            DMA((slots, GROUP)),
        ],
        compiler_params=group_params(1),
        name="front",
    )(lengths, x, gain, w_qkv, taps, grad_output, token_mask, gain2, w_out, w_up, w_down)


PART = 384
BY_CHIP = 288


def feed_grads_kernel(sq_ref, cz_ref, n2_ref, du_ref, att_ref, da_ref, out_ref, n2_t):
    half, sub = pl.program_id(0), pl.program_id(1)
    groups, rows, width = n2_ref.shape
    tokens = groups * rows

    @pl.when((half == 0) & (sub == 0))
    def _():
        for group in range(groups):
            n2_t[:, group * rows : (group + 1) * rows] = n2_ref[group].astype(F32).T.astype(BF16)

    down = mm_tn(sq_ref[...].reshape(tokens, PART), cz_ref[...].reshape(tokens, width))
    for place in range(4):
        for side in range(2):
            out_ref[place, pl.ds(sub, 1), side * 96 : side * 96 + 96] = down[
                place * 96 : (place + 1) * 96, side * PART : (side + 1) * PART
            ].astype(BF16)[None]
    up = mm(n2_t[...], du_ref[...].reshape(tokens, PART))
    out_ref[pl.ds(sub, 1), :, 192:384] = up.astype(BF16).reshape(1, 4, 192, PART)

    @pl.when(sub == 0)
    def _():
        att = jnp.concatenate(
            [att_ref[:, pair].reshape(tokens, WIDE) for pair in range(PAIRS)], axis=1
        )
        out = mm_tn(att, da_ref[...].reshape(tokens, PART)).astype(BF16)
        for batch in range(4):
            for q in range(4):
                begin = batch * 192 + q * 48
                out_ref[q, batch, 384:432] = out[begin : begin + 48]


def feed_grads(squared, cotangent, normed2, d_up, attended, d_attn):
    groups, rows, width = normed2.shape
    whole = lambda h, b: (0, 0, 0)
    return pl.pallas_call(
        feed_grads_kernel,
        grid=(2, 4),
        in_specs=[
            pl.BlockSpec((groups, rows, PART), lambda h, b: (0, 0, 2 * b + h)),
            pl.BlockSpec((groups, rows, width), whole, pipeline_mode=pl.Buffered(1)),
            pl.BlockSpec((groups, rows, width), whole, pipeline_mode=pl.Buffered(1)),
            pl.BlockSpec((groups, rows, PART), lambda h, b: (0, 0, 4 * h + b)),
            pl.BlockSpec(
                (groups, PAIRS, rows, WIDE), lambda h, b: (0, 0, 0, 0), pipeline_mode=pl.Buffered(1)
            ),
            pl.BlockSpec((groups, rows, PART), lambda h, b: (0, 0, h)),
        ],
        out_specs=pl.BlockSpec((4, 4, 432, PART), lambda h, b: (h, 0, 0, 0)),
        out_shape=jax.ShapeDtypeStruct((8, 4, 432, PART), BF16),
        scratch_shapes=[pltpu.VMEM((width, groups * rows), BF16)],
        compiler_params=params(),
        name="feed_grads",
    )(squared, cotangent, normed2, d_up, attended.reshape(groups, PAIRS, rows, WIDE), d_attn)


def feed_grads_send_kernel(
    sq_ref, cz_ref, n2_ref, du_ref, att_ref, da_ref, chip_ref, z_ref,
    n2_t, pieces, core_in, down_s, down_r, up_s, up_r, out_s, out_r,
):
    half, sub = pl.program_id(0), pl.program_id(1)
    me = lax.axis_index("seq")
    core = lax.rem(me, 2)
    other = 1 - core

    @pl.when((half == 0) & (sub == 0))
    def _():
        barrier = pltpu.get_barrier_semaphore()
        pl.semaphore_signal(barrier, inc=1, device_id={"seq": me ^ 1}, device_id_type=MESH)
        pl.semaphore_wait(barrier, 1)

    feed_grads_kernel(
        sq_ref, cz_ref, n2_ref, du_ref, att_ref, da_ref, pieces.at[pl.ds(half * 4, 4)], n2_t
    )

    def down(part, batch, side):
        chip = part * 2 + side
        return remote(
            pieces.at[chip * 2 + other, batch, 0:192],
            core_in.at[chip, batch, 0:192],
            (down_s.at[part, batch, side], down_r.at[part, batch, side]),
            "seq",
            me ^ 1,
        )

    def up(chip):
        return remote(
            pieces.at[chip * 2 + other, :, 192:384],
            core_in.at[chip, :, 192:384],
            (up_s.at[chip], up_r.at[chip]),
            "seq",
            me ^ 1,
        )

    def out(chip):
        return remote(
            pieces.at[chip * 2 + other, :, 384:432],
            core_in.at[chip, :, 384:432],
            (out_s.at[chip], out_r.at[chip]),
            "seq",
            me ^ 1,
        )

    for side in range(2):
        down(half, sub, side).start()

    @pl.when(sub == 0)
    def _():
        for side in range(2):
            out(half * 2 + side).start()

    @pl.when(lax.rem(sub, 2) == other)
    def _():
        up(half * 2 + sub // 2).start()

    @pl.when((half == 1) & (sub == 3))
    def _():
        for part in range(2):
            for side in range(2):
                chip = part * 2 + side
                for batch in range(4):
                    down(part, batch, side).wait()
                up(chip).wait()
                out(chip).wait()
                for batch in range(4):
                    both = pieces[chip * 2 + core, batch].astype(F32) + core_in[chip, batch].astype(F32)
                    chip_ref[chip, batch] = both[:BY_CHIP].astype(BF16)
                    z_ref[batch, chip] = both[BY_CHIP:].astype(BF16)


def feed_grads_send(squared, cotangent, normed2, d_up, attended, d_attn):
    groups, rows, width = normed2.shape
    whole = lambda h, b: (0, 0, 0)
    once = pl.Buffered(1)
    quarter = (4, 4, 432, PART)
    return pl.pallas_call(
        feed_grads_send_kernel,
        grid=(2, 4),
        in_specs=[
            pl.BlockSpec((groups, rows, PART), lambda h, b: (0, 0, 2 * b + h)),
            pl.BlockSpec((groups, rows, width), whole, pipeline_mode=once),
            pl.BlockSpec((groups, rows, width), whole, pipeline_mode=once),
            pl.BlockSpec((groups, rows, PART), lambda h, b: (0, 0, 4 * h + b)),
            pl.BlockSpec((groups, PAIRS, rows, WIDE), lambda h, b: (0, 0, 0, 0), pipeline_mode=once),
            pl.BlockSpec((groups, rows, PART), lambda h, b: (0, 0, h)),
        ],
        out_specs=[
            pl.BlockSpec((4, 4, BY_CHIP, PART), lambda h, b: (0, 0, 0, 0), pipeline_mode=once),
            pl.BlockSpec((4, 4, 432 - BY_CHIP, PART), lambda h, b: (0, 0, 0, 0), pipeline_mode=once),
        ],
        out_shape=[
            jax.ShapeDtypeStruct((4, 4, BY_CHIP, PART), BF16),
            jax.ShapeDtypeStruct((4, 4, 432 - BY_CHIP, PART), BF16),
        ],
        scratch_shapes=[
            pltpu.VMEM((width, groups * rows), BF16),
            pltpu.VMEM((8, 4, 432, PART), BF16),
            pltpu.VMEM(quarter, BF16),
            DMA((2, 4, 2)),
            DMA((2, 4, 2)),
            DMA((4,)),
            DMA((4,)),
            DMA((4,)),
            DMA((4,)),
        ],
        compiler_params=group_params(3),
        name="feed_grads_send",
    )(squared, cotangent, normed2, d_up, attended.reshape(groups, PAIRS, rows, WIDE), d_attn)


def input_grads_kernel(
    dp_ref, n1_ref, x_ref, dh_ref, w_ref, gain_ref, out_ref, gx_ref, gain_grad_ref, n1_t, total, w_sc
):
    pair = pl.program_id(0)
    groups, rows, width = n1_ref.shape
    tokens = groups * rows

    @pl.when(pair == 0)
    def _():
        for group in range(groups):
            n1_t[:, group * rows : (group + 1) * rows] = n1_ref[group].astype(F32).T.astype(BF16)
        total[...] = jnp.zeros(total.shape, F32)

    d_proj = dp_ref[...].reshape(tokens, 3 * WIDE)
    grad = mm(n1_t[...], d_proj).astype(BF16)
    for batch in range(4):
        for chip in range(4):
            begin = batch * 192 + chip * 48
            out_ref[0, 0, chip, batch] = grad[begin : begin + 48]
    for part in range(3):
        cols = pl.ds(pl.multiple_of(part * width + pair * WIDE, WIDE), WIDE)
        w_sc[:, part * WIDE : (part + 1) * WIDE] = w_ref[:, cols]
    total[...] += mm_nt(d_proj, w_sc[...])

    @pl.when(pair == PAIRS - 1)
    def _():
        gain = gain_row(gain_ref)
        gain_sum = jnp.zeros((1, width), F32)
        for group in range(groups):
            x = x_ref[group].astype(F32)
            d_normed = total[group * rows : (group + 1) * rows]
            factor = lax.rsqrt(jnp.mean(x * x, axis=-1, keepdims=True) + 1e-06)
            weighted = d_normed * gain
            inner = jnp.mean(weighted * x, axis=-1, keepdims=True)
            gx_ref[group] = (
                dh_ref[group] + factor * weighted - x * (factor * factor * factor) * inner
            )
            gain_sum += jnp.sum(d_normed * x * factor, axis=0, keepdims=True)
        gain_grad_ref[...] = gain_sum


def input_grads(d_proj, normed1, x, d_hidden, w_qkv, gain):
    groups, rows, width = x.shape
    whole = lambda p: (0, 0, 0)
    once = pl.Buffered(1)
    tokens = pl.BlockSpec((groups, rows, width), whole, pipeline_mode=once)
    return pl.pallas_call(
        input_grads_kernel,
        grid=(PAIRS,),
        in_specs=[
            pl.BlockSpec((groups, 1, rows, 3 * WIDE), lambda p: (0, p, 0, 0)),
            tokens,
            tokens,
            tokens,
            pl.BlockSpec(w_qkv.shape, lambda p: (0, 0), pipeline_mode=once),
            pl.BlockSpec((width,), lambda p: (0,)),
        ],
        out_specs=[
            pl.BlockSpec((1, 1, 4, 4, 48, PART), lambda p: (p % 3, p // 3, 0, 0, 0, 0)),
            tokens,
            pl.BlockSpec((1, width), lambda p: (0, 0)),
        ],
        out_shape=[
            jax.ShapeDtypeStruct((3, 2, 4, 4, 48, PART), BF16),
            jax.ShapeDtypeStruct(x.shape, F32),
            jax.ShapeDtypeStruct((1, width), F32),
        ],
        scratch_shapes=[
            pltpu.VMEM((width, groups * rows), BF16),
            pltpu.VMEM((groups * rows, width), F32),
            pltpu.VMEM((width, 3 * WIDE), BF16),
        ],
        compiler_params=params(),
        name="input_grads",
    )(d_proj.reshape(groups, PAIRS, rows, 3 * WIDE), normed1, x, d_hidden, w_qkv, gain)


def finish_kernel(
    units_ref, n1_ref, x_ref, dh_ref, w_ref, gain_ref, feed_ref, far_ref, gt_ref, gain2_ref, stats_ref,
    gx_ref, qkv_out, feed_out, small_out,
    dp_in, n1_v, n1_t, x_v, dh_v, w_v, feed_v, far_v, far_mine, far_in, dn, grads, pieces,
    core_in, here, chip_in, mine, z_in, qkv_all, feed_mine, feed_in, feed_all,
    row_own, row_in, row_sum, col_in,
    load_s, far_s, far_r, dp_s, dp_r, core_s, core_r, chip_s, chip_r, z_s, z_r, qkv_s, qkv_r, fz_s, fz_r, fa_s, fa_r,
    row_s, row_r, col_s, col_r,
):
    me = lax.axis_index("seq")
    z = lax.axis_index("batch")
    core, chip = lax.rem(me, 2), me // 2
    groups, block, width = n1_v.shape
    tokens = groups * block
    middle = tokens // 2
    chunks = pieces.shape[0]
    slots = units_ref.shape[0]
    rows = feed_in.shape[2]
    barrier = pltpu.get_barrier_semaphore()
    for bit in range(1, 8):
        pl.semaphore_signal(barrier, inc=1, device_id={"seq": me ^ bit}, device_id_type=MESH)
    for bit in range(1, 4):
        pl.semaphore_signal(barrier, inc=1, device_id={"batch": z ^ bit}, device_id_type=MESH)
    pl.semaphore_wait(barrier, 10)

    def send(source, target, sems, axis, peer):
        copy = remote(source, target, sems, axis, peer)
        copy.start()
        return copy

    across, along = me ^ 2, me ^ 4

    def spread(ref, s, r):
        return [
            send(ref.at[me], ref.at[me], (s.at[step], r.at[step]), "seq", peer)
            for step, peer in enumerate((me ^ 1, across, along))
        ]

    def relay(ref, first, s, r):
        rows = ref.shape[1]
        cut = (rows // 2 + 15) // 16 * 16
        first[1].wait()
        first[2].wait()
        upper, lower = pl.ds(0, cut), pl.ds(cut, rows - cut)
        on = [
            send(ref.at[across, upper], ref.at[across, upper], (s.at[3], r.at[3]), "seq", along),
            send(ref.at[along, lower], ref.at[along, lower], (s.at[4], r.at[4]), "seq", across),
        ]
        more = [
            send(ref.at[slot], ref.at[slot], (s.at[5 + step], r.at[5 + step]), "seq", me ^ 1)
            for step, slot in enumerate((across, along))
        ]
        return [first[0]] + more, on

    def finish_relay(ref, on, s, r):
        for copy in on:
            copy.wait()
        slot = me ^ 6
        return [send(ref.at[slot], ref.at[slot], (s.at[7], r.at[7]), "seq", me ^ 1)]

    for slot in range(slots):
        send_blocks(units_ref, dp_in, (dp_s, dp_r), slot)
    loads = [
        pltpu.make_async_copy(source, target, load_s.at[place])
        for place, (source, target) in enumerate(
            [
                (feed_ref, feed_v),
                (far_ref.at[z], far_v.at[0]),
                (n1_ref, n1_v),
                (w_ref, w_v),
                (x_ref, x_v),
                (dh_ref, dh_v),
            ]
        )
    ]
    for copy in loads:
        copy.start()
    far_z = [
        send(far_ref.at[z ^ bit], far_v.at[bit], (far_s.at[2 + bit], far_r.at[2 + bit]), "batch", z ^ bit)
        for bit in range(1, 4)
    ]

    loads[0].wait()
    for batch in range(4):
        both = feed_v[0, batch].astype(F32)
        for q in range(1, 4):
            both = both + feed_v[q, batch].astype(F32)
        feed_mine[batch] = both.astype(BF16)
    near = feed_mine.shape[1] // rows
    feed_z = [
        [
            send(
                feed_mine.at[z ^ bit, c * rows : (c + 1) * rows],
                feed_in.at[c, bit - 1],
                (fz_s.at[c, bit - 1], fz_r.at[c, bit - 1]),
                "batch",
                z ^ bit,
            )
            for bit in range(1, 4)
        ]
        for c in range(near)
    ]
    loads[2].wait()
    for group in range(groups):
        n1_t[:, group * block : (group + 1) * block] = n1_v[group].astype(F32).T.astype(BF16)
    for copy in loads[3:]:
        copy.wait()
    gain = gain_row(gain_ref)

    def unit_rows(pair, first):
        return jnp.concatenate(
            [dp_in[(first + more) * PAIRS + pair] for more in range(groups // 2)], axis=0
        )

    def pair_weights(pair):
        return jnp.concatenate(
            [
                w_v[:, pl.ds(pl.multiple_of(part * width + pair * WIDE, WIDE), WIDE)]
                for part in range(3)
            ],
            axis=1,
        )

    def input_half(first):
        gain_sum = jnp.zeros((1, width), F32)
        for more in range(groups // 2):
            group = first + more
            x = x_v[group].astype(F32)
            d_normed = dn[group * block : (group + 1) * block]
            factor = lax.rsqrt(jnp.mean(x * x, axis=-1, keepdims=True) + 1e-06)
            weighted = d_normed * gain
            inner = jnp.mean(weighted * x, axis=-1, keepdims=True)
            dh_v[group] += factor * weighted - x * (factor * factor * factor) * inner
            gain_sum += jnp.sum(d_normed * x * factor, axis=0, keepdims=True)
        return gain_sum

    for slot in range(slots):
        if (slot * GROUP) // PAIRS < groups // 2:
            wait_blocks(units_ref, dp_in, (dp_s, dp_r), slot)
    dn[...] = jnp.zeros(dn.shape, F32)

    def first_half(pair, carry):
        d_rows = unit_rows(pair, 0)
        grads[pair] = mm(n1_t[:, :middle], d_rows)
        dn[:middle] += mm_nt(d_rows, pair_weights(pair))
        return carry

    lax.fori_loop(0, PAIRS, first_half, 0)
    gain_sum = input_half(0)
    loads[1].wait()
    for copy in far_z:
        copy.wait()
    for q in range(4):
        both = far_v[0, q].astype(F32)
        for place in range(1, 4):
            both = both + far_v[place, q].astype(F32)
        far_mine[q] = both.astype(BF16)
    far_chips = [
        send(
            far_mine.at[chip ^ bit],
            far_in.at[bit - 1],
            (far_s.at[bit - 1], far_r.at[bit - 1]),
            "seq",
            me ^ (2 * bit),
        )
        for bit in range(1, 4)
    ]
    for slot in range(slots):
        if (slot * GROUP) // PAIRS >= groups // 2:
            wait_blocks(units_ref, dp_in, (dp_s, dp_r), slot)

    feed_first = []

    def spread_feed(c):
        for copy in feed_z[c] if c < near else far_chips:
            copy.wait()
        if c < near:
            both = feed_mine[z, c * rows : (c + 1) * rows].astype(F32)
            for bit in range(3):
                both = both + feed_in[c, bit].astype(F32)
        else:
            both = far_mine[chip].astype(F32)
            for bit in range(3):
                both = both + far_in[bit].astype(F32)
        feed_all[c, pl.ds(me, 1)] = both.astype(BF16)[None]
        feed_first.append(spread(feed_all.at[c], fa_s.at[c], fa_r.at[c]))

    spread_feed(0)
    to_core, to_chip = [], []

    def pass_on(c):
        to_core[c].wait()
        for q in range(4):
            both = pieces[c, core, q].astype(F32) + core_in[c, q].astype(F32)
            here[c, q] = both.astype(BF16)
        to_chip.append(
            [
                send(
                    here.at[c, q, half],
                    chip_in.at[c, place],
                    (chip_s.at[c, place], chip_r.at[c, place]),
                    "seq",
                    peer,
                )
                for place, (q, half, peer) in enumerate(
                    (
                        (chip ^ 1, first_two, across),
                        (chip ^ 3, first_two, across),
                        (chip ^ 2, last_two, along),
                        (chip ^ 3, last_two, along),
                    )
                )
            ]
        )

    first_two, last_two = pl.ds(0, 2), pl.ds(2, 2)

    def pass_again(c):
        for place, (q, half) in enumerate(
            ((chip, first_two), (chip ^ 2, first_two), (chip, last_two), (chip ^ 1, last_two))
        ):
            to_chip[c][place].wait()
            both = here[c, q, half].astype(F32) + chip_in[c, place].astype(F32)
            here[c, q, half] = both.astype(BF16)
        return [
            send(
                here.at[c, q, half],
                chip_in.at[c, place],
                (chip_s.at[c, place], chip_r.at[c, place]),
                "seq",
                peer,
            )
            for place, (q, half, peer) in (
                (4, (chip ^ 2, first_two, along)),
                (5, (chip ^ 1, last_two, across)),
            )
        ]

    for c in range(chunks):

        def second_half(side, carry, c=c):
            pair = side * chunks + c
            grad = (grads[pair] + mm(n1_t[:, middle:], unit_rows(pair, groups // 2))).astype(BF16)
            for batch in range(4):
                for q in range(4):
                    begin = batch * 192 + q * 48
                    pieces[c, side, q, batch] = grad[begin : begin + 48]
            return carry

        lax.fori_loop(0, 2, second_half, 0)
        to_core.append(
            send(
                pieces.at[c, 1 - core], core_in.at[c], (core_s.at[c], core_r.at[c]), "seq", me ^ 1
            )
        )
        if c > 0:
            pass_on(c - 1)

    def second_rows(pair, carry):
        dn[middle:] += mm_nt(unit_rows(pair, groups // 2), pair_weights(pair))
        return carry

    lax.fori_loop(0, 2, second_rows, 0)
    pass_on(chunks - 1)
    again = [pass_again(0)]
    lax.fori_loop(2, 4, second_rows, 0)
    again.append(pass_again(1))
    lax.fori_loop(4, PAIRS, second_rows, 0)
    again.append(pass_again(2))
    for c in range(1, chunks):
        spread_feed(c)
    gain_sum = gain_sum + input_half(groups // 2)
    gx_copy = pltpu.make_async_copy(dh_v, gx_ref, load_s.at[len(loads)])
    gx_copy.start()
    row_own[...] = jnp.zeros(row_own.shape, F32)
    for tap in range(3):
        for part in range(3):
            row = tap * 3 + part
            row_own[row : row + 1] = gt_ref[tap : tap + 1, part * width : (part + 1) * width]
    row_own[9:10] = gain_sum
    row_own[10:11] = gain2_ref[...]
    for place in range(4):
        row_own[11:12, place * WIDE : (place + 1) * WIDE] = stats_ref[place : place + 1]
    row_in[pl.ds(me, 1)] = row_own[...][None]
    rows_out = [
        send(row_own, row_in.at[me], (row_s.at[bit - 1], row_r.at[bit - 1]), "seq", me ^ bit)
        for bit in range(1, 8)
    ]
    to_z = []
    for c in range(chunks):
        for copy in again[c]:
            copy.wait()
        for half, place in ((first_two, 4), (last_two, 5)):
            both = here[c, chip, half].astype(F32) + chip_in[c, place].astype(F32)
            mine[c, half] = both.astype(BF16)
        to_z.append(
            [
                send(
                    mine.at[c, z ^ bit],
                    z_in.at[c, bit - 1],
                    (z_s.at[c, bit - 1], z_r.at[c, bit - 1]),
                    "batch",
                    z ^ bit,
                )
                for bit in range(1, 4)
            ]
        )
    for copy in rows_out:
        copy.wait()
    total = row_in[0]
    for place in range(1, 8):
        total = total + row_in[place]
    row_sum[...] = total
    col_in[pl.ds(z, 1)] = total[None]
    cols_out = [
        send(row_sum, col_in.at[z], (col_s.at[bit - 1], col_r.at[bit - 1]), "batch", z ^ bit)
        for bit in range(1, 4)
    ]
    last, feed_on, qkv_on = [], [], []
    for c in range(chunks):
        more, on = relay(feed_all.at[c], feed_first[c], fa_s.at[c], fa_r.at[c])
        last += more
        feed_on.append(on)
    qkv_first = []
    for c in range(chunks):
        for copy in to_z[c]:
            copy.wait()
        both = mine[c, z].astype(F32)
        for bit in range(3):
            both = both + z_in[c, bit].astype(F32)
        qkv_all[c, pl.ds(me, 1)] = both.astype(BF16)[None]
        qkv_first.append(spread(qkv_all.at[c], qkv_s.at[c], qkv_r.at[c]))
    for c in range(chunks):
        more, on = relay(qkv_all.at[c], qkv_first[c], qkv_s.at[c], qkv_r.at[c])
        last += more
        qkv_on.append(on)
    for c in range(chunks):
        last += finish_relay(feed_all.at[c], feed_on[c], fa_s.at[c], fa_r.at[c])
    for c in range(chunks):
        last += finish_relay(qkv_all.at[c], qkv_on[c], qkv_s.at[c], qkv_r.at[c])
    for copy in cols_out:
        copy.wait()
    small_out[...] = ((col_in[0] + col_in[1]) + col_in[2]) + col_in[3]
    for copy in last:
        copy.wait()
    qkv_out[...] = qkv_all[...]
    feed_out[...] = feed_all[...]
    gx_copy.wait()


def finish(units, normed1, x, d_hidden, w_qkv, gain, feed, far, grad_taps, grad_norm2, stats):
    groups, block, width = x.shape
    chunks, rows, feed_rows = 3, 48, 144
    small_shape = (16, width)
    tokens = groups * block
    slots = units.shape[0]
    vmem = pl.BlockSpec(memory_space=pltpu.VMEM)
    anywhere = pl.BlockSpec(memory_space=pl.ANY)
    pairs = [DMA((slots, GROUP)), DMA((slots, GROUP))]
    for shape in [(), (6,), (3,), (8,), (3,), (8,)]:
        pairs += [DMA((chunks,) + shape), DMA((chunks,) + shape)]
    low = lambda *shape: pltpu.VMEM(shape, BF16)
    return pl.pallas_call(
        finish_kernel,
        in_specs=[anywhere] * 5 + [vmem, anywhere, anywhere] + [vmem] * 3,
        out_specs=[anywhere, vmem, vmem, vmem],
        out_shape=[
            jax.ShapeDtypeStruct(x.shape, F32),
            jax.ShapeDtypeStruct((chunks, 8, rows, PART), BF16),
            jax.ShapeDtypeStruct((chunks, 8, feed_rows, PART), BF16),
            jax.ShapeDtypeStruct(small_shape, F32),
        ],
        scratch_shapes=[
            low(groups * PAIRS, block, 3 * WIDE),
            low(groups, block, width),
            low(width, tokens),
            low(groups, block, width),
            pltpu.VMEM((groups, block, width), F32),
            low(*w_qkv.shape),
            low(*feed.shape),
            low(*far.shape),
            low(*far.shape[1:]),
            low(3, *far.shape[2:]),
            pltpu.VMEM((tokens, width), F32),
            pltpu.VMEM((PAIRS, width, 3 * WIDE), F32),
            low(chunks, 2, 4, 4, rows, PART),
            low(chunks, 4, 4, rows, PART),
            low(chunks, 4, 4, rows, PART),
            low(chunks, 6, 2, rows, PART),
            low(chunks, 4, rows, PART),
            low(chunks, 3, rows, PART),
            low(chunks, 8, rows, PART),
            low(*feed.shape[1:]),
            low(chunks, 3, feed_rows, PART),
            low(chunks, 8, feed_rows, PART),
            pltpu.VMEM(small_shape, F32),
            pltpu.VMEM((8,) + small_shape, F32),
            pltpu.VMEM(small_shape, F32),
            pltpu.VMEM((4,) + small_shape, F32),
            DMA((7,)),
            DMA((6,)),
            DMA((6,)),
        ]
        + pairs
        + [DMA((7,)), DMA((7,)), DMA((3,)), DMA((3,))],
        compiler_params=group_params(0),
        name="finish",
    )(units, normed1, x, d_hidden, w_qkv, gain, feed, far, grad_taps, grad_norm2, stats)


def unpack_kernel(
    feed_ref, qkv_ref, small_ref, down_ref, up_ref, out_ref, grad_ref, taps_ref, gain1_ref, gain2_ref, rms_ref
):
    for r in range(2):
        rows, cols = slice(r * 96, r * 96 + 96), slice(r * PART, (r + 1) * PART)
        down_ref[rows, :PART] = feed_ref[0, r, :96].astype(F32)
        down_ref[r * 96 : r * 96 + 48, PART:] = feed_ref[0, r, 96:].astype(F32)
        down_ref[r * 96 + 48 : r * 96 + 96, PART:] = feed_ref[1, r, :48].astype(F32)
        up_ref[:96, cols] = feed_ref[1, r, 48:].astype(F32)
        up_ref[96:, cols] = feed_ref[2, r, :96].astype(F32)
        out_ref[r * 48 : r * 48 + 48] = feed_ref[2, r, 96:].astype(F32)
        for c in range(3):
            for part in range(3):
                begin = part * PAIRS * WIDE + (r * 3 + c) * WIDE
                grad_ref[:, begin : begin + WIDE] = qkv_ref[
                    c, r, :, part * WIDE : (part + 1) * WIDE
                ].astype(F32)

    @pl.when(pl.program_id(0) == 0)
    def _():
        width = small_ref.shape[1]
        for tap in range(3):
            for part in range(3):
                row = tap * 3 + part
                taps_ref[tap : tap + 1, part * width : (part + 1) * width] = small_ref[row : row + 1]
        z = lax.axis_index("batch")
        for row, ref in ((9, gain1_ref), (10, gain2_ref)):
            own = jnp.zeros((1, width // 4), F32)
            for batch in range(4):
                share = small_ref[row : row + 1, batch * width // 4 : (batch + 1) * width // 4]
                own = jnp.where(z == batch, share, own)
            ref[...] = own.reshape(ref.shape)
        count = small_ref[11:12, 3 * WIDE : 4 * WIDE]
        lane = lax.broadcasted_iota(jnp.int32, (1, WIDE), 1)
        total = jnp.zeros((1, WIDE), F32)
        for place in range(3):
            total = jnp.where(lane == place, small_ref[11:12, place * WIDE : (place + 1) * WIDE], total)
        rms_ref[...] = jnp.sqrt(total / (width * count)).reshape(rms_ref.shape)


def unpack(feed, qkv, small):
    wide = 3 * PAIRS * WIDE
    return pl.pallas_call(
        unpack_kernel,
        grid=(4,),
        in_specs=[
            pl.BlockSpec((3, 2, 144, PART), lambda i: (0, i, 0, 0)),
            pl.BlockSpec((3, 2, 48, PART), lambda i: (0, i, 0, 0)),
            pl.BlockSpec(small.shape, lambda i: (0, 0)),
        ],
        out_specs=[
            pl.BlockSpec((192, 2 * PART), lambda i: (i, 0)),
            pl.BlockSpec((192, 2 * PART), lambda i: (0, i)),
            pl.BlockSpec((96, PART), lambda i: (i % 2, i // 2)),
            pl.BlockSpec((48, wide), lambda i: (i, 0)),
            pl.BlockSpec((3, wide), lambda i: (0, 0)),
            pl.BlockSpec((192,), lambda i: (0,)),
            pl.BlockSpec((192,), lambda i: (0,)),
            pl.BlockSpec((WIDE,), lambda i: (0,)),
        ],
        out_shape=[
            jax.ShapeDtypeStruct((768, 2 * PART), F32),
            jax.ShapeDtypeStruct((192, 8 * PART), F32),
            jax.ShapeDtypeStruct((192, 2 * PART), F32),
            jax.ShapeDtypeStruct((192, wide), F32),
            jax.ShapeDtypeStruct((3, wide), F32),
            jax.ShapeDtypeStruct((192,), F32),
            jax.ShapeDtypeStruct((192,), F32),
            jax.ShapeDtypeStruct((WIDE,), F32),
        ],
        compiler_params=params(),
        name="unpack",
    )(feed, qkv, small)


def exchange(blocks):
    return lax.all_to_all(blocks, "seq", 0, 0, tiled=True)


def plain_gradients(feed, qkv):
    down = feed[:, :, :192].reshape(8, 4, 2, 96, PART).transpose(1, 0, 3, 2, 4)
    up = feed[:, :, 192:384].transpose(1, 2, 0, 3)
    out = feed[:, :, 384:].reshape(2, 4, 4, 48, PART).transpose(2, 1, 3, 0, 4)
    grad = qkv.reshape(3, 2, 4, 4, 48, 3, WIDE).transpose(3, 2, 4, 5, 1, 0, 6)
    return (
        down.reshape(3072, 768),
        up.reshape(768, 3072),
        out.reshape(768, 768),
        grad.reshape(768, 2304),
    )


def shards(
    stream_in,
    lengths,
    token_mask,
    norm1_gain,
    w_qkv,
    conv_taps,
    w_out,
    norm2_gain,
    w_up,
    w_down,
    grad_output,
):
    groups, block_len, width = stream_in.shape
    count = lax.axis_size("seq")
    batches = lax.axis_size("batch")
    units = groups * PAIRS
    slots = -(-units // count)
    spare = slots * count - units
    fitted = count == GROUP and batches == 4 and units % GROUP == 0

    def to_heads(blocks):
        blocks = jnp.pad(blocks, ((0, spare), (0, 0), (0, 0)))
        blocks = blocks.reshape((slots, count) + blocks.shape[1:])
        return jnp.stack([exchange(blocks[slot]) for slot in range(slots)])

    def to_tokens(rows):
        rows = rows.reshape(slots, count, block_len, rows.shape[2])
        return jnp.concatenate([exchange(rows[slot]) for slot in range(slots)])[:units]

    rest = (token_mask, norm2_gain, w_out, w_up, w_down)
    if fitted:
        normed1, proj, unit_out, attended, unit_lse, d_units, grad_norm2, stats, *saved = front(
            stream_in, norm1_gain, w_qkv, conv_taps, lengths, grad_output, *rest
        )
        stream_out, d_hidden, normed2, squared, d_up, d_attn, cotangent = saved
        proj = proj.reshape(slots, count * block_len, 3 * WIDE)
    else:
        normed1, proj = project(stream_in, norm1_gain, w_qkv)
        proj = to_heads(proj).reshape(slots, count * block_len, 3 * WIDE)
        unit_out, unit_lse = attend(lengths, proj, conv_taps, count)
        attended = to_tokens(unit_out)
        rest = (grad_output, token_mask, lengths) + rest[1:]
        stream_out, d_hidden, d_units, *saved = dense(stream_in, attended, *rest)
        normed2, squared, d_up, d_attn, cotangent, grad_norm2, stats = saved
        d_units = to_heads(d_units)
    d_units = d_units.reshape(slots, count * block_len, WIDE)
    saved = (squared, cotangent, normed2, d_up, attended, d_attn)
    if fitted:
        feed, far = feed_grads_send(*saved)
        same_core = [[core + 2 * chip for chip in range(4)] for core in range(2)]
        feed = lax.all_to_all(feed, "seq", 0, 0, tiled=True, axis_index_groups=same_core)
    else:
        feed = feed_grads(*saved)
    back, grad_taps = attend_back(lengths, proj, conv_taps, unit_out, d_units, unit_lse, count)

    if fitted:
        blocks = back.reshape(slots, count, block_len, 3 * WIDE)
        grad_input, qkv, feed, small = finish(
            blocks, normed1, stream_in, d_hidden, w_qkv, norm1_gain, feed, far, grad_taps, grad_norm2, stats
        )
        down, up, out, grad_qkv, taps, gain1, gain2, rms = unpack(feed, qkv, small)
        rms = rms[:3]
    else:
        pieces, grad_input, grad_norm1 = input_grads(
            to_tokens(back), normed1, stream_in, d_hidden, w_qkv, norm1_gain
        )

        def reduce(gradient):
            share = lax.psum_scatter(gradient, ("batch", "seq"), scatter_dimension=0, tiled=True)
            return lax.all_gather(share, "seq", axis=0, tiled=True).astype(F32)

        down, up, out, grad_qkv = map(reduce, plain_gradients(feed, pieces))
        small = (grad_taps[:3], grad_norm1[0], grad_norm2[0], stats[:4, 0])
        taps, gain1, gain2, stats = lax.psum(small, ("seq", "batch"))
        share = width // batches
        begin = lax.axis_index("batch") * share
        gain1, gain2 = (lax.dynamic_slice_in_dim(gain, begin, share) for gain in (gain1, gain2))
        rms = jnp.sqrt(stats[:3] / (width * stats[3]))
    return (stream_out, grad_input, gain1, grad_qkv, taps, out, gain2, up, down, rms)


def solution(mesh):
    tokens = P("batch", "seq", None)
    return jax.shard_map(
        shards,
        mesh=mesh,
        in_specs=(
            tokens,
            P("batch"),
            P("batch", "seq"),
            P(),
            P(),
            P(),
            P(),
            P(),
            P(),
            P(),
            tokens,
        ),
        out_specs=(
            tokens,
            tokens,
            P("batch"),
            P("batch", None),
            P(),
            P("batch", None),
            P("batch"),
            P("batch", None),
            P("batch", None),
            P(),
        ),
        check_vma=False,
    )
```

```python
import functools
import math

import jax
import jax.numpy as jnp
from jax import lax
from jax.experimental import pallas as pl
from jax.experimental.pallas import tpu as pltpu
from jax.sharding import PartitionSpec as P

HEADS = 12
HEAD = 64
PAIRS = HEADS // 2
WIDE = 2 * HEAD
TILE = 256
ROWS = 512
BACK = 256
STRIP = 32
LIMIT = 62 << 20
NEG = -1e30
F32 = jnp.float32
BF16 = jnp.bfloat16


def mm(left_op, right_op):
    return jnp.dot(left_op, right_op, preferred_element_type=F32)


def mm_nt(left_op, right_op):
    return lax.dot_general(
        left_op, right_op, (((1,), (1,)), ((), ())), preferred_element_type=F32
    )


def mm_tn(left_op, right_op):
    return lax.dot_general(
        left_op, right_op, (((0,), (0,)), ((), ())), preferred_element_type=F32
    )


def params():
    return pltpu.CompilerParams(vmem_limit_bytes=LIMIT)


MESH = pl.DeviceIdType.MESH
GROUP = 8
DMA = pltpu.SemaphoreType.DMA


def remote(source, target, sems, axis, peer):
    return pltpu.make_async_remote_copy(
        src_ref=source,
        dst_ref=target,
        send_sem=sems[0],
        recv_sem=sems[1],
        device_id={axis: peer},
        device_id_type=MESH,
    )


def meet_group():
    me = lax.axis_index("seq")
    barrier = pltpu.get_barrier_semaphore()
    for bit in range(1, GROUP):
        pl.semaphore_signal(barrier, inc=1, device_id={"seq": me ^ bit}, device_id_type=MESH)
    pl.semaphore_wait(barrier, GROUP - 1)


def unit_copy(blocks, inbox, sems, unit):
    me = lax.axis_index("seq")
    owner, slot = lax.rem(unit, GROUP), unit // GROUP
    return owner, remote(
        blocks.at[unit],
        inbox.at[slot, me],
        (sems[0].at[unit], sems[1].at[slot, me ^ owner]),
        "seq",
        owner,
    )


def send_unit(blocks, inbox, sems, unit):
    me = lax.axis_index("seq")
    owner, copy = unit_copy(blocks, inbox, sems, unit)

    @pl.when(owner != me)
    def _():
        copy.start()

    @pl.when(owner == me)
    def _():
        slot = unit // GROUP
        pltpu.make_async_copy(blocks.at[unit], inbox.at[slot, me], sems[1].at[slot, 0]).start()


def wait_unit(blocks, inbox, sems, slot):
    me = lax.axis_index("seq")
    unit = slot * GROUP + me
    pltpu.make_async_copy(blocks.at[unit], inbox.at[slot, me], sems[1].at[slot, 0]).wait()
    for bit in range(1, GROUP):
        remote(
            blocks.at[unit],
            inbox.at[slot, me ^ bit],
            (sems[0].at[unit], sems[1].at[slot, bit]),
            "seq",
            me ^ bit,
        ).wait_recv()


def wait_sent(blocks, inbox, sems):
    me = lax.axis_index("seq")

    def one(unit, carry):
        owner, copy = unit_copy(blocks, inbox, sems, unit)
        pl.when(owner != me)(copy.wait_send)
        return carry

    lax.fori_loop(0, blocks.shape[0], one, 0)


def wait_units(blocks, inbox, sems):
    for slot in range(blocks.shape[0] // GROUP):
        wait_unit(blocks, inbox, sems, slot)
    wait_sent(blocks, inbox, sems)


def block_copies(units, inbox, sems, slot):
    me = lax.axis_index("seq")
    return [
        remote(
            units.at[slot, me ^ bit],
            inbox.at[slot * GROUP + me],
            (sems[0].at[slot, bit], sems[1].at[slot, bit]),
            "seq",
            me ^ bit,
        )
        for bit in range(1, GROUP)
    ]


def own_block(units, inbox, sems, slot):
    me = lax.axis_index("seq")
    return pltpu.make_async_copy(
        units.at[slot, me], inbox.at[slot * GROUP + me], sems[1].at[slot, 0]
    )


def send_blocks(units, inbox, sems, slot):
    own_block(units, inbox, sems, slot).start()
    for copy in block_copies(units, inbox, sems, slot):
        copy.start()


def wait_blocks(units, inbox, sems, slot):
    own_block(units, inbox, sems, slot).wait()
    for copy in block_copies(units, inbox, sems, slot):
        copy.wait()


def group_params(number):
    return pltpu.CompilerParams(
        collective_id=number, has_side_effects=True, vmem_limit_bytes=LIMIT
    )


def gain_row(gain_ref):
    return gain_ref[...].astype(F32).reshape(1, gain_ref.shape[0])


def project_kernel(x_ref, gain_ref, w_ref, n_ref, p_ref):
    x = x_ref[0].astype(F32)
    factor = lax.rsqrt(jnp.mean(x * x, axis=-1, keepdims=True) + 1e-06)
    normed = (x * factor * gain_row(gain_ref)).astype(BF16)
    n_ref[0] = normed
    width = x.shape[1]
    for part in range(3):
        cols = mm(normed, w_ref[:, part * width : (part + 1) * width])
        for pair in range(PAIRS):
            p_ref[pair, :, part * WIDE : (part + 1) * WIDE] = cols[
                :, pair * WIDE : (pair + 1) * WIDE
            ].astype(BF16)


def project(x, gain, w_qkv):
    groups, rows, width = x.shape
    return pl.pallas_call(
        project_kernel,
        grid=(groups,),
        in_specs=[
            pl.BlockSpec((1, rows, width), lambda s: (s, 0, 0)),
            pl.BlockSpec((width,), lambda s: (0,)),
            pl.BlockSpec(w_qkv.shape, lambda s: (0, 0)),
        ],
        out_specs=[
            pl.BlockSpec((1, rows, width), lambda s: (s, 0, 0)),
            pl.BlockSpec((PAIRS, rows, 3 * WIDE), lambda s: (s, 0, 0)),
        ],
        out_shape=[
            jax.ShapeDtypeStruct(x.shape, BF16),
            jax.ShapeDtypeStruct((groups * PAIRS, rows, 3 * WIDE), BF16),
        ],
        compiler_params=params(),
        name="project",
    )(x, gain, w_qkv)


def stack_heads(rows):
    lane = lax.broadcasted_iota(jnp.int32, rows.shape, 1)
    zero = jnp.zeros_like(rows)
    first = jnp.where(lane < HEAD, rows, zero)
    second = jnp.where(lane < HEAD, zero, rows)
    return jnp.concatenate([first, second], axis=0)


def unstack_heads(rows):
    half = rows.shape[0] // 2
    lane = lax.broadcasted_iota(jnp.int32, (half, rows.shape[1]), 1)
    return jnp.where(lane < HEAD, rows[:half], rows[half:])


def step_rows(index, size):
    return pl.ds(pl.multiple_of(index * size, size), size)


def own_unit(lengths, groups, count, slot):
    unit = slot * count + lax.axis_index("seq")
    length = lengths[jnp.minimum(unit // PAIRS, groups - 1)]
    return jnp.where(unit < groups * PAIRS, length, 0), lax.rem(unit, PAIRS)


def pair_taps(taps_ref, taps_sc, pair):
    width = taps_ref.shape[1] // 3
    for part in range(3):
        cols = pl.ds(pl.multiple_of(part * width + pair * WIDE, WIDE), WIDE)
        taps_sc[0:3, part * WIDE : (part + 1) * WIDE] = taps_ref[:, cols].astype(F32)


def convolve(wide_ref, taps_ref, tile, cols):
    begin = 8 + tile * TILE
    total = taps_ref[0:1, cols] * wide_ref[begin : begin + TILE, cols]
    total += taps_ref[1:2, cols] * wide_ref[begin - 1 : begin - 1 + TILE, cols]
    total += taps_ref[2:3, cols] * wide_ref[begin - 2 : begin - 2 + TILE, cols]
    return total.astype(BF16)


Q_COLS, K_COLS, V_COLS = (slice(part * WIDE, (part + 1) * WIDE) for part in range(3))


def key_limits(index, length, size):
    lane = lax.broadcasted_iota(jnp.int32, (STRIP, 2 * size), 1)
    return jnp.minimum(index * size + (lane & (size - 1)) + 1, length)


def over_key_steps(index, length, size, visit, carry):
    full = jnp.minimum(index * size, length) // size
    last = (jnp.minimum((index + 1) * size, length) + size - 1) // size
    carry = lax.fori_loop(0, full, lambda step, c: visit(step, False, c), carry)
    return lax.fori_loop(full, last, lambda step, c: visit(step, True, c), carry)


def attend_kernel(
    groups, count, lengths, p_ref, taps_ref, o_ref, lse_ref, taps, wide, q_sc, k_sc, vt_sc, acc, s_sc, e_sc
):
    length, pair = own_unit(lengths, groups, count, pl.program_id(0))
    wide[0:8] = jnp.zeros((8, wide.shape[1]), F32)
    wide[8:] = p_ref[0].astype(F32)
    attend_unit(
        length, pair, False, taps_ref, o_ref.at[0], lse_ref.at[0], taps, wide, q_sc, k_sc, vt_sc, acc, s_sc, e_sc
    )


def attend_unit(
    length, pair, whole, taps_ref, o_ref, lse_ref, taps, wide, q_sc, k_sc, vt_sc, acc, s_sc, e_sc
):
    tiles = q_sc.shape[0] // TILE
    per_step = ROWS // TILE
    pair_taps(taps_ref, taps, pair)
    vt_sc[:, WIDE:] = jnp.ones((vt_sc.shape[0], vt_sc.shape[1] - WIDE, ROWS), BF16)
    for tile in range(tiles):
        rows = slice(tile * TILE, (tile + 1) * TILE)
        q_sc[rows] = convolve(wide, taps, tile, Q_COLS) * (1.0 / math.sqrt(HEAD))

        def keys_values():
            k_sc[rows] = convolve(wide, taps, tile, K_COLS)
            cols = slice(tile % per_step * TILE, (tile % per_step + 1) * TILE)
            values = convolve(wide, taps, tile, V_COLS)
            vt_sc[tile // per_step, :WIDE, cols] = values.astype(F32).T.astype(BF16)

        if whole:
            keys_values()
        else:
            pl.when(tile // per_step * ROWS < length)(keys_values)

    k_row = lax.broadcasted_iota(jnp.int32, (STRIP, 2 * ROWS), 0)

    def query_step(index, carry):
        q_stack = stack_heads(q_sc[step_rows(index, ROWS)])
        limit = key_limits(index, length, ROWS)
        acc[...] = jnp.zeros(acc.shape, F32)

        def visit(step, mask, old):
            s_sc[...] = mm_nt(k_sc[step_rows(step, ROWS)], q_stack)

            def strip_of(begin):
                scores = s_sc[begin : begin + STRIP]
                if mask == "none":
                    return scores
                if mask == "length":
                    keep = k_row[:, :WIDE] < length - (step * ROWS + begin)
                    keep = jnp.concatenate([keep] * (2 * ROWS // WIDE), axis=1)
                else:
                    keep = k_row < limit - (step * ROWS + begin)
                return jnp.where(keep, scores, NEG)

            top = jnp.full((8, 2 * ROWS), NEG, F32)
            for begin in range(0, ROWS, STRIP):
                scores = strip_of(begin)
                for low in range(0, STRIP, 8):
                    top = jnp.maximum(top, scores[low : low + 8])
            new = jnp.maximum(old, jnp.max(top, axis=0, keepdims=True))
            for begin in range(0, ROWS, STRIP):
                e_sc[begin : begin + STRIP] = jnp.exp(strip_of(begin) - new).astype(BF16)
            acc[...] = acc[...] * jnp.exp(old - new) + mm(vt_sc[step], e_sc[...])
            return new

        top = jnp.full((1, 2 * ROWS), NEG, F32)
        if whole:
            top = lax.fori_loop(0, index, lambda step, c: visit(step, "length", c), top)
            top = visit(index, "both", top)
        else:

            def either(step, masked, top):
                return visit(step, "both" if masked else "none", top)

            top = over_key_steps(index, length, ROWS, either, top)
        total = acc[WIDE : WIDE + 1]
        out = (acc[:WIDE] / total).T
        o_ref[step_rows(index, ROWS)] = unstack_heads(out).astype(BF16)
        lse_ref[pl.ds(index, 1)] = top + jnp.log(total)
        return carry

    lax.fori_loop(0, q_sc.shape[0] // ROWS, query_step, 0)


def attend(lengths, proj, taps, count):
    slots, rows = proj.shape[:2]
    steps = rows // ROWS
    own = lambda i, lengths: (i, 0, 0)
    return pl.pallas_call(
        functools.partial(attend_kernel, lengths.shape[0], count),
        grid_spec=pltpu.PrefetchScalarGridSpec(
            num_scalar_prefetch=1,
            grid=(slots,),
            in_specs=[
                pl.BlockSpec((1, rows, 3 * WIDE), own),
                pl.BlockSpec(taps.shape, lambda i, lengths: (0, 0)),
            ],
            out_specs=[
                pl.BlockSpec((1, rows, WIDE), own),
                pl.BlockSpec((1, steps, 2 * ROWS), own),
            ],
            scratch_shapes=[
                pltpu.VMEM((8, 3 * WIDE), F32),
                pltpu.VMEM((rows + 8, 3 * WIDE), F32),
                pltpu.VMEM((rows, WIDE), BF16),
                pltpu.VMEM((rows, WIDE), BF16),
                pltpu.VMEM((steps, WIDE + 16, ROWS), BF16),
                pltpu.VMEM((WIDE + 16, 2 * ROWS), F32),
                pltpu.VMEM((ROWS, 2 * ROWS), F32),
                pltpu.VMEM((ROWS, 2 * ROWS), BF16),
            ],
        ),
        out_shape=[
            jax.ShapeDtypeStruct((slots, rows, WIDE), BF16),
            jax.ShapeDtypeStruct((slots, steps, 2 * ROWS), F32),
        ],
        compiler_params=params(),
        name="attend",
    )(lengths, proj, taps)


def row_copies(units, inbox, sems, slot, block):
    me = lax.axis_index("seq")
    return [
        remote(
            units.at[slot, pl.ds(pl.multiple_of((me ^ bit) * block, block), block)],
            inbox.at[slot * GROUP + me],
            (sems[0].at[slot, bit], sems[1].at[slot, bit]),
            "seq",
            me ^ bit,
        )
        for bit in range(1, GROUP)
    ]


def own_rows(units, inbox, sems, slot, block):
    me = lax.axis_index("seq")
    return pltpu.make_async_copy(
        units.at[slot, pl.ds(pl.multiple_of(me * block, block), block)],
        inbox.at[slot * GROUP + me],
        sems[1].at[slot, 0],
    )


def send_rows(units, inbox, sems, slot, block):
    own_rows(units, inbox, sems, slot, block).start()
    for copy in row_copies(units, inbox, sems, slot, block):
        copy.start()


def wait_rows(units, inbox, sems, slot, block):
    own_rows(units, inbox, sems, slot, block).wait()
    for copy in row_copies(units, inbox, sems, slot, block):
        copy.wait()


def attend_back_kernel(
    groups, count, lengths, p_ref, taps_ref, o_ref, do_ref, lse_ref, stream_ref, dp_ref, gt_ref, stream_out_ref,
    taps, wide, q_sc, k_sc, v_sc, kt_sc, dm, dqt, s_sc, d_sc, e_sc, f_sc,
):
    p_ref, o_ref, do_ref, lse_ref = p_ref.at[0], o_ref.at[0], do_ref.at[0], lse_ref.at[0]
    dp_ref = dp_ref.at[0]
    length, pair = own_unit(lengths, groups, count, pl.program_id(0))
    tiles = p_ref.shape[0] // TILE
    per_step = BACK // TILE
    pair_taps(taps_ref, taps, pair)
    wide[0:8] = jnp.zeros((8, wide.shape[1]), F32)
    wide[8:] = p_ref[...].astype(F32)
    dm[...] = jnp.zeros(dm.shape, F32)
    for tile in range(tiles):
        rows = slice(tile * TILE, (tile + 1) * TILE)

        @pl.when(tile // per_step * BACK < length)
        def _():
            q_sc[rows] = convolve(wide, taps, tile, Q_COLS) * (1.0 / math.sqrt(HEAD))
            keys = convolve(wide, taps, tile, K_COLS)
            k_sc[rows] = keys
            v_sc[rows] = convolve(wide, taps, tile, V_COLS)
            cols = slice(tile % per_step * TILE, (tile % per_step + 1) * TILE)
            kt_sc[tile // per_step, :, cols] = keys.astype(F32).T.astype(BF16)

    lane = lax.broadcasted_iota(jnp.int32, (8, WIDE), 1)
    row = lax.broadcasted_iota(jnp.int32, (8, WIDE), 0)
    picks = jnp.where((lane < HEAD) == (row == 0), 1.0, 0.0).astype(BF16)
    k_row = lax.broadcasted_iota(jnp.int32, (STRIP, 2 * BACK), 0)

    def query_step(index, carry):
        here = step_rows(index, BACK)
        q_stack = stack_heads(q_sc[here])
        d_rows = do_ref[here]
        d_stack = stack_heads(d_rows)
        product = d_rows.astype(F32) * o_ref[here].astype(F32)
        upper = product.astype(BF16)
        lower = (product - upper.astype(F32)).astype(BF16)
        sums = mm_nt(picks, upper) + mm_nt(picks, lower)
        delta = jnp.concatenate([sums[0:1], sums[1:2]], axis=1)
        line, begin = pl.ds(index * BACK // ROWS, 1), lax.rem(index * BACK, ROWS)
        lse = jnp.concatenate(
            [
                lse_ref[line, pl.ds(pl.multiple_of(head * ROWS + begin, BACK), BACK)]
                for head in range(2)
            ],
            axis=1,
        )
        limit = key_limits(index, length, BACK)
        dqt[...] = jnp.zeros(dqt.shape, F32)

        def visit(step, masked, carry):
            there = step_rows(step, BACK)
            s_sc[...] = mm_nt(k_sc[there], q_stack)
            d_sc[...] = mm_nt(v_sc[there], d_stack)
            for begin in range(0, BACK, STRIP):
                strip = slice(begin, begin + STRIP)
                probs = jnp.exp(s_sc[strip] - lse)
                if masked:
                    probs = jnp.where(k_row < limit - (step * BACK + begin), probs, 0.0)
                e_sc[strip] = probs.astype(BF16)
                f_sc[strip] = (probs * (d_sc[strip] - delta)).astype(BF16)
            dm[there, V_COLS] += mm(e_sc[...], d_stack)
            dm[there, K_COLS] += mm(f_sc[...], q_stack)
            dqt[...] += mm(kt_sc[step], f_sc[...])
            return carry

        over_key_steps(index, length, BACK, visit, 0)
        dm[here, Q_COLS] = unstack_heads(dqt[...].T) * (1.0 / math.sqrt(HEAD))
        return carry

    lax.fori_loop(0, (length + BACK - 1) // BACK, query_step, 0)

    @pl.when(pl.program_id(0) == 0)
    def _():
        gt_ref[...] = jnp.zeros(gt_ref.shape, F32)
        stream_out_ref[...] = stream_ref[...]

    sums = [jnp.zeros((1, 3 * WIDE), F32) for _ in range(3)]
    for tile in range(tiles):
        begin = tile * TILE
        total = taps[0:1] * dm[begin : begin + TILE]
        total += taps[1:2] * dm[begin + 1 : begin + 1 + TILE]
        total += taps[2:3] * dm[begin + 2 : begin + 2 + TILE]
        dp_ref[begin : begin + TILE] = total.astype(BF16)
        for tap in range(3):
            behind = wide[begin + 8 - tap : begin + 8 - tap + TILE]
            sums[tap] += jnp.sum(dm[begin : begin + TILE] * behind, axis=0, keepdims=True)
    width = gt_ref.shape[1] // 3
    for tap in range(3):
        for part in range(3):
            cols = pl.ds(pl.multiple_of(part * width + pair * WIDE, WIDE), WIDE)
            gt_ref[tap : tap + 1, cols] += sums[tap][:, part * WIDE : (part + 1) * WIDE]


def attend_back(lengths, proj, taps, attended, d_attended, lse, stream, count):
    all_rows = pl.BlockSpec(stream.shape, lambda i, lengths: (0, 0, 0), pipeline_mode=pl.Buffered(1))
    slots, rows = proj.shape[:2]
    steps = rows // BACK
    own = lambda i, lengths: (i, 0, 0)
    whole = lambda i, lengths: (0, 0)
    return pl.pallas_call(
        functools.partial(attend_back_kernel, lengths.shape[0], count),
        grid_spec=pltpu.PrefetchScalarGridSpec(
            num_scalar_prefetch=1,
            grid=(slots,),
            in_specs=[
                pl.BlockSpec((1, rows, 3 * WIDE), own),
                pl.BlockSpec(taps.shape, whole),
                pl.BlockSpec((1, rows, WIDE), own),
                pl.BlockSpec((1, rows, WIDE), own),
                pl.BlockSpec((1,) + lse.shape[1:], own),
                all_rows,
            ],
            out_specs=[
                pl.BlockSpec((1, rows, 3 * WIDE), own),
                pl.BlockSpec((8, taps.shape[1]), whole),
                all_rows,
            ],
            scratch_shapes=[
                pltpu.VMEM((8, 3 * WIDE), F32),
                pltpu.VMEM((rows + 8, 3 * WIDE), F32),
                pltpu.VMEM((rows, WIDE), BF16),
                pltpu.VMEM((rows, WIDE), BF16),
                pltpu.VMEM((rows, WIDE), BF16),
                pltpu.VMEM((steps, WIDE, BACK), BF16),
                pltpu.VMEM((rows + 8, 3 * WIDE), F32),
                pltpu.VMEM((WIDE, 2 * BACK), F32),
                pltpu.VMEM((BACK, 2 * BACK), F32),
                pltpu.VMEM((BACK, 2 * BACK), F32),
                pltpu.VMEM((BACK, 2 * BACK), BF16),
                pltpu.VMEM((BACK, 2 * BACK), BF16),
            ],
        ),
        out_shape=[
            jax.ShapeDtypeStruct((slots, rows, 3 * WIDE), BF16),
            jax.ShapeDtypeStruct((8, taps.shape[1]), F32),
            jax.ShapeDtypeStruct(stream.shape, stream.dtype),
        ],
        compiler_params=params(),
        name="attend_back",
    )(lengths, proj, taps, attended, d_attended, lse, stream)


def dense_kernel(
    group, x_ref, att_ref, cot_ref, mask_ref, lengths, gain_ref, wo_ref, wu_ref, wd_ref,
    out_ref, dh_ref, datt_ref, n2_ref, sq_ref, du_ref, da_ref, cz_ref, gain_grad_ref, stats_ref,
    act_sc, att_sc,
):
    rows, width = x_ref.shape[1:]
    hidden_units = wu_ref.shape[1]
    step = width
    for pair in range(PAIRS):
        att_sc[:, pair * WIDE : (pair + 1) * WIDE] = att_ref[pair]
    spot = lax.axis_index("seq") * rows + lax.broadcasted_iota(jnp.int32, (1, rows), 1)
    counts = jnp.where(spot < lengths[group], mask_ref[pl.ds(group, 1)].astype(F32), 0.0)
    weight = jnp.broadcast_to(counts, (WIDE, rows)).T[:, :1]
    gain = gain_row(gain_ref)
    branch = mm(att_sc[...], wo_ref[...])
    hidden = x_ref[0].astype(F32) + branch
    factor = lax.rsqrt(jnp.mean(hidden * hidden, axis=-1, keepdims=True) + 1e-06)
    normed = (hidden * factor * gain).astype(BF16)
    n2_ref[0] = normed
    total = jnp.zeros((rows, width), F32)
    for begin in range(0, hidden_units, step):
        cols = slice(begin, begin + step)
        active = jnp.maximum(mm(normed, wu_ref[:, cols]), 0.0)
        act_sc[:, cols] = active
        squared = (active * active).astype(BF16)
        sq_ref[0, :, cols] = squared
        total += mm(squared, wd_ref[cols])
    full = hidden + total
    out_ref[0] = full.astype(BF16)

    def masked(values):
        per_row = jnp.sum(values * values, axis=-1, keepdims=True)
        return jnp.sum(weight * per_row, axis=0, keepdims=True)

    @pl.when(group == 0)
    def _():
        stats_ref[...] = jnp.zeros(stats_ref.shape, F32)
        gain_grad_ref[...] = jnp.zeros(gain_grad_ref.shape, F32)

    parts = [masked(full), masked(branch), masked(total), jnp.sum(weight, axis=0, keepdims=True)]
    for place, part in enumerate(parts):
        stats_ref[place : place + 1] += jnp.broadcast_to(part, (1, WIDE))
    cotangent = (cot_ref[0].astype(F32) * weight).astype(BF16)
    cz_ref[0] = cotangent
    d_normed = jnp.zeros((rows, width), F32)
    for begin in range(0, hidden_units, step):
        cols = slice(begin, begin + step)
        d_squared = mm_nt(cotangent, wd_ref[cols])
        d_up = (2.0 * act_sc[:, cols] * d_squared).astype(BF16)
        du_ref[0, :, cols] = d_up
        d_normed += mm_nt(d_up, wu_ref[:, cols])
    weighted = d_normed * gain
    inner = jnp.mean(weighted * hidden, axis=-1, keepdims=True)
    d_hidden = cotangent.astype(F32) + factor * weighted - hidden * (factor * factor * factor) * inner
    gain_grad_ref[...] += jnp.sum(d_normed * hidden * factor, axis=0, keepdims=True)
    dh_ref[0] = d_hidden
    d_attn = d_hidden.astype(BF16)
    da_ref[0] = d_attn
    d_att = mm_nt(d_attn, wo_ref[...]).astype(BF16)
    for pair in range(PAIRS):
        datt_ref[pair] = d_att[:, pair * WIDE : (pair + 1) * WIDE]


def dense(x, attended, grad_output, token_mask, lengths, gain, w_out, w_up, w_down):
    groups, rows, width = x.shape
    hidden_units = w_up.shape[1]
    per_group = lambda s: (s, 0, 0)
    fixed = lambda s: (0, 0)
    once = pl.Buffered(1)
    row_block = pl.BlockSpec((1, rows, width), per_group)
    wide_block = pl.BlockSpec((1, rows, hidden_units), per_group)
    unit_block = pl.BlockSpec((PAIRS, rows, WIDE), per_group)
    low = jax.ShapeDtypeStruct(x.shape, BF16)
    wide_low = jax.ShapeDtypeStruct((groups, rows, hidden_units), BF16)
    return pl.pallas_call(
        lambda *refs: dense_kernel(pl.program_id(0), *refs),
        grid=(groups,),
        in_specs=[
            row_block,
            unit_block,
            row_block,
            pl.BlockSpec(token_mask.shape, fixed),
            pl.BlockSpec(memory_space=pltpu.SMEM),
            pl.BlockSpec((width,), lambda s: (0,)),
            pl.BlockSpec(w_out.shape, fixed, pipeline_mode=once),
            pl.BlockSpec(w_up.shape, fixed, pipeline_mode=once),
            pl.BlockSpec(w_down.shape, fixed, pipeline_mode=once),
        ],
        out_specs=[
            row_block,
            row_block,
            unit_block,
            row_block,
            wide_block,
            wide_block,
            row_block,
            row_block,
            pl.BlockSpec((1, width), fixed),
            pl.BlockSpec((8, WIDE), fixed),
        ],
        out_shape=[
            low,
            jax.ShapeDtypeStruct(x.shape, F32),
            jax.ShapeDtypeStruct((groups * PAIRS, rows, WIDE), BF16),
            low,
            wide_low,
            wide_low,
            low,
            low,
            jax.ShapeDtypeStruct((1, width), F32),
            jax.ShapeDtypeStruct((8, WIDE), F32),
        ],
        scratch_shapes=[pltpu.VMEM((rows, hidden_units), F32), pltpu.VMEM((rows, width), BF16)],
        compiler_params=params(),
        name="dense",
    )(x, attended, grad_output, token_mask, lengths, gain, w_out, w_up, w_down)


def front_kernel(
    lengths, x_ref, gain_ref, w_ref, taps_ref, cot_ref, mask_ref, gain2_ref, wo_ref, wu_ref, wd_ref,
    n1_out, proj_out, units_out, att_out, lse_ref, inbox, gain_grad_ref, stats_ref,
    out_ref, dh_ref, n2_ref, sq_ref, du_ref, da_ref, cz_ref,
    x_v, w_v, n1_v, blocks, proj, units, att, taps, wide, q_sc, k_sc, vt_sc, acc, s_sc, e_sc,
    cot_v, wo_v, wu_v, wd_v, act_sc, att_sc, d_blocks,
    out_b, dh_b, n2_b, sq_b, du_b, da_b, cz_b,
    load_s, store_s, keep_s, send_s, send_r, att_s, att_r, back_s, back_r,
):
    groups, block = x_v.shape[:2]
    slots = proj.shape[0]
    sems, att_sems, back_sems = (send_s, send_r), (att_s, att_r), (back_s, back_r)
    loads = [
        pltpu.make_async_copy(source, target, load_s.at[place])
        for place, (source, target) in enumerate(
            [
                (w_ref, w_v),
                (x_ref, x_v),
                (wo_ref, wo_v),
                (wu_ref, wu_v),
                (wd_ref, wd_v),
                (cot_ref, cot_v),
            ]
        )
    ]
    keeps = [
        pltpu.make_async_copy(source, target, keep_s.at[place])
        for place, (source, target) in enumerate(
            [(n1_v, n1_out), (proj, proj_out), (units, units_out), (att, att_out)]
        )
    ]
    buffers = (out_b, dh_b, n2_b, sq_b, du_b, da_b, cz_b)
    targets = (out_ref, dh_ref, n2_ref, sq_ref, du_ref, da_ref, cz_ref)

    def stores(group):
        side = lax.rem(group, 2)
        return [
            pltpu.make_async_copy(buffer.at[side], target.at[group], store_s.at[place, side])
            for place, (buffer, target) in enumerate(zip(buffers, targets))
        ]

    for copy in loads:
        copy.start()
    meet_group()
    for copy in loads[:2]:
        copy.wait()

    def sequence(group, carry):
        here = pl.ds(group, 1)
        project_kernel(
            x_v.at[here], gain_ref, w_v, n1_v.at[here], blocks.at[pl.ds(group * PAIRS, PAIRS)]
        )
        for pair in range(PAIRS):
            send_unit(blocks, proj, sems, group * PAIRS + pair)
        return carry

    lax.fori_loop(0, groups, sequence, 0)
    keeps[0].start()

    def one_slot(slot, carry):
        wait_unit(blocks, proj, sems, slot)

        @pl.when(slot == slots - 1)
        def _():
            for done in range(slots - 1):
                send_rows(units, att, att_sems, done, block)

        length, pair = own_unit(lengths, groups, GROUP, slot)
        wide[0:8] = jnp.zeros((8, wide.shape[1]), F32)
        for place in range(GROUP):
            wide[8 + place * block : 8 + (place + 1) * block] = proj[slot, place].astype(F32)
        attend_unit(
            length, pair, True, taps_ref, units.at[slot], lse_ref.at[slot],
            taps, wide, q_sc, k_sc, vt_sc, acc, s_sc, e_sc,
        )
        return carry

    lax.fori_loop(0, slots, one_slot, 0)
    send_rows(units, att, att_sems, slots - 1, block)
    keeps[1].start()
    keeps[2].start()
    for copy in loads[2:]:
        copy.wait()

    def dense_group(group, carry):
        for slot in range(slots):

            @pl.when(group == slot * GROUP // PAIRS)
            def _():
                wait_rows(units, att, att_sems, slot, block)
                if slot == slots - 1:
                    keeps[3].start()

        @pl.when(group >= 2)
        def _():
            for copy in stores(group - 2):
                copy.wait()

        here, side = pl.ds(group, 1), pl.ds(lax.rem(group, 2), 1)
        unit = pl.ds(group * PAIRS, PAIRS)
        dense_kernel(
            group, x_v.at[here], att.at[unit], cot_v.at[here], mask_ref, lengths, gain2_ref,
            wo_v, wu_v, wd_v, out_b.at[side], dh_b.at[side], d_blocks.at[unit], n2_b.at[side],
            sq_b.at[side], du_b.at[side], da_b.at[side], cz_b.at[side], gain_grad_ref, stats_ref,
            act_sc, att_sc,
        )
        for pair in range(PAIRS):
            send_unit(d_blocks, inbox, back_sems, group * PAIRS + pair)
        for copy in stores(group):
            copy.start()
        return carry

    lax.fori_loop(0, groups, dense_group, 0)
    wait_sent(blocks, proj, sems)
    wait_units(d_blocks, inbox, back_sems)
    for group in (groups - 2, groups - 1):
        for copy in stores(group):
            copy.wait()
    for copy in keeps:
        copy.wait()


def front(x, gain, w_qkv, taps, lengths, grad_output, token_mask, gain2, w_out, w_up, w_down):
    groups, block, width = x.shape
    hidden_units = w_up.shape[1]
    units = groups * PAIRS
    slots = units // GROUP
    rows = GROUP * block
    steps = rows // ROWS
    anywhere = pl.BlockSpec(memory_space=pl.ANY)
    vmem = pl.BlockSpec(memory_space=pltpu.VMEM)
    low = lambda *shape: pltpu.VMEM(shape, BF16)
    low_out = lambda *shape: jax.ShapeDtypeStruct(shape, BF16)
    wide_out = (groups, block, hidden_units)
    return pl.pallas_call(
        front_kernel,
        in_specs=[pl.BlockSpec(memory_space=pltpu.SMEM), anywhere, vmem, anywhere, vmem]
        + [anywhere, vmem, vmem, anywhere, anywhere, anywhere],
        out_specs=[anywhere] * 4 + [vmem, anywhere, vmem, vmem] + [anywhere] * 7,
        out_shape=[
            low_out(*x.shape),
            low_out(slots, GROUP, block, 3 * WIDE),
            low_out(slots, rows, WIDE),
            low_out(units, block, WIDE),
            jax.ShapeDtypeStruct((slots, steps, 2 * ROWS), F32),
            low_out(slots, GROUP, block, WIDE),
            jax.ShapeDtypeStruct((1, width), F32),
            jax.ShapeDtypeStruct((8, WIDE), F32),
            low_out(*x.shape),
            jax.ShapeDtypeStruct(x.shape, F32),
            low_out(*x.shape),
            low_out(*wide_out),
            low_out(*wide_out),
            low_out(*x.shape),
            low_out(*x.shape),
        ],
        scratch_shapes=[
            low(*x.shape),
            low(*w_qkv.shape),
            low(*x.shape),
            low(units, block, 3 * WIDE),
            low(slots, GROUP, block, 3 * WIDE),
            low(slots, rows, WIDE),
            low(units, block, WIDE),
            pltpu.VMEM((8, 3 * WIDE), F32),
            pltpu.VMEM((rows + 8, 3 * WIDE), F32),
            low(rows, WIDE),
            low(rows, WIDE),
            low(steps, WIDE + 16, ROWS),
            pltpu.VMEM((WIDE + 16, 2 * ROWS), F32),
            pltpu.VMEM((ROWS, 2 * ROWS), F32),
            low(ROWS, 2 * ROWS),
            low(*x.shape),
            low(*w_out.shape),
            low(*w_up.shape),
            low(*w_down.shape),
            pltpu.VMEM((block, hidden_units), F32),
            low(block, width),
            low(units, block, WIDE),
            low(2, block, width),
            pltpu.VMEM((2, block, width), F32),
            low(2, block, width),
            low(2, block, hidden_units),
            low(2, block, hidden_units),
            low(2, block, width),
            low(2, block, width),
            DMA((6,)),
            DMA((7, 2)),
            DMA((4,)),
            DMA((units,)),
            DMA((slots, GROUP)),
            DMA((slots, GROUP)),
            DMA((slots, GROUP)),
            DMA((units,)),
            DMA((slots, GROUP)),
        ],
        compiler_params=group_params(1),
        name="front",
    )(lengths, x, gain, w_qkv, taps, grad_output, token_mask, gain2, w_out, w_up, w_down)


PART = 384
BY_CHIP = 288


def feed_grads_kernel(sq_ref, cz_ref, n2_ref, du_ref, att_ref, da_ref, out_ref):
    half, sub = pl.program_id(0), pl.program_id(1)
    groups, rows, width = n2_ref.shape
    tokens = groups * rows

    down = mm_tn(sq_ref[...].reshape(tokens, PART), cz_ref[...].reshape(tokens, width))
    for place in range(4):
        for side in range(2):
            out_ref[place, pl.ds(sub, 1), side * 96 : side * 96 + 96] = down[
                place * 96 : (place + 1) * 96, side * PART : (side + 1) * PART
            ].astype(BF16)[None]
    up = mm_tn(n2_ref[...].reshape(tokens, width), du_ref[...].reshape(tokens, PART))
    out_ref[pl.ds(sub, 1), :, 192:384] = up.astype(BF16).reshape(1, 4, 192, PART)

    @pl.when(sub == 0)
    def _():
        att = jnp.concatenate(
            [att_ref[:, pair].reshape(tokens, WIDE) for pair in range(PAIRS)], axis=1
        )
        out = mm_tn(att, da_ref[...].reshape(tokens, PART)).astype(BF16)
        for batch in range(4):
            for q in range(4):
                begin = batch * 192 + q * 48
                out_ref[q, batch, 384:432] = out[begin : begin + 48]


def feed_grads(squared, cotangent, normed2, d_up, attended, d_attn):
    groups, rows, width = normed2.shape
    whole = lambda h, b: (0, 0, 0)
    return pl.pallas_call(
        feed_grads_kernel,
        grid=(2, 4),
        in_specs=[
            pl.BlockSpec((groups, rows, PART), lambda h, b: (0, 0, 2 * b + h)),
            pl.BlockSpec((groups, rows, width), whole, pipeline_mode=pl.Buffered(1)),
            pl.BlockSpec((groups, rows, width), whole, pipeline_mode=pl.Buffered(1)),
            pl.BlockSpec((groups, rows, PART), lambda h, b: (0, 0, 4 * h + b)),
            pl.BlockSpec(
                (groups, PAIRS, rows, WIDE), lambda h, b: (0, 0, 0, 0), pipeline_mode=pl.Buffered(1)
            ),
            pl.BlockSpec((groups, rows, PART), lambda h, b: (0, 0, h)),
        ],
        out_specs=pl.BlockSpec((4, 4, 432, PART), lambda h, b: (h, 0, 0, 0)),
        out_shape=jax.ShapeDtypeStruct((8, 4, 432, PART), BF16),
        compiler_params=params(),
        name="feed_grads",
    )(squared, cotangent, normed2, d_up, attended.reshape(groups, PAIRS, rows, WIDE), d_attn)


def feed_grads_send_kernel(
    sq_ref, cz_ref, n2_ref, du_ref, att_ref, da_ref, chip_ref, z_ref,
    pieces, core_in, down_s, down_r, up_s, up_r, out_s, out_r,
):
    half, sub = pl.program_id(0), pl.program_id(1)
    me = lax.axis_index("seq")
    core = lax.rem(me, 2)
    other = 1 - core

    @pl.when((half == 0) & (sub == 0))
    def _():
        barrier = pltpu.get_barrier_semaphore()
        pl.semaphore_signal(barrier, inc=1, device_id={"seq": me ^ 1}, device_id_type=MESH)
        pl.semaphore_wait(barrier, 1)

    feed_grads_kernel(
        sq_ref, cz_ref, n2_ref, du_ref, att_ref, da_ref, pieces.at[pl.ds(half * 4, 4)]
    )

    def down(part, batch, side):
        chip = part * 2 + side
        return remote(
            pieces.at[chip * 2 + other, batch, 0:192],
            core_in.at[chip, batch, 0:192],
            (down_s.at[part, batch, side], down_r.at[part, batch, side]),
            "seq",
            me ^ 1,
        )

    def up(chip):
        return remote(
            pieces.at[chip * 2 + other, :, 192:384],
            core_in.at[chip, :, 192:384],
            (up_s.at[chip], up_r.at[chip]),
            "seq",
            me ^ 1,
        )

    def out(chip):
        return remote(
            pieces.at[chip * 2 + other, :, 384:432],
            core_in.at[chip, :, 384:432],
            (out_s.at[chip], out_r.at[chip]),
            "seq",
            me ^ 1,
        )

    for side in range(2):
        down(half, sub, side).start()

    @pl.when(sub == 0)
    def _():
        for side in range(2):
            out(half * 2 + side).start()

    @pl.when(lax.rem(sub, 2) == other)
    def _():
        up(half * 2 + sub // 2).start()

    @pl.when((half == 1) & (sub == 3))
    def _():
        for part in range(2):
            for side in range(2):
                chip = part * 2 + side
                for batch in range(4):
                    down(part, batch, side).wait()
                up(chip).wait()
                out(chip).wait()
                for batch in range(4):
                    both = pieces[chip * 2 + core, batch].astype(F32) + core_in[chip, batch].astype(F32)
                    chip_ref[chip, batch] = both[:BY_CHIP].astype(BF16)
                    z_ref[batch, chip] = both[BY_CHIP:].astype(BF16)


def feed_grads_send(squared, cotangent, normed2, d_up, attended, d_attn):
    groups, rows, width = normed2.shape
    whole = lambda h, b: (0, 0, 0)
    once = pl.Buffered(1)
    quarter = (4, 4, 432, PART)
    return pl.pallas_call(
        feed_grads_send_kernel,
        grid=(2, 4),
        in_specs=[
            pl.BlockSpec((groups, rows, PART), lambda h, b: (0, 0, 2 * b + h)),
            pl.BlockSpec((groups, rows, width), whole, pipeline_mode=once),
            pl.BlockSpec((groups, rows, width), whole, pipeline_mode=once),
            pl.BlockSpec((groups, rows, PART), lambda h, b: (0, 0, 4 * h + b)),
            pl.BlockSpec((groups, PAIRS, rows, WIDE), lambda h, b: (0, 0, 0, 0), pipeline_mode=once),
            pl.BlockSpec((groups, rows, PART), lambda h, b: (0, 0, h)),
        ],
        out_specs=[
            pl.BlockSpec((4, 4, BY_CHIP, PART), lambda h, b: (0, 0, 0, 0), pipeline_mode=once),
            pl.BlockSpec((4, 4, 432 - BY_CHIP, PART), lambda h, b: (0, 0, 0, 0), pipeline_mode=once),
        ],
        out_shape=[
            jax.ShapeDtypeStruct((4, 4, BY_CHIP, PART), BF16),
            jax.ShapeDtypeStruct((4, 4, 432 - BY_CHIP, PART), BF16),
        ],
        scratch_shapes=[
            pltpu.VMEM((8, 4, 432, PART), BF16),
            pltpu.VMEM(quarter, BF16),
            DMA((2, 4, 2)),
            DMA((2, 4, 2)),
            DMA((4,)),
            DMA((4,)),
            DMA((4,)),
            DMA((4,)),
        ],
        compiler_params=group_params(3),
        name="feed_grads_send",
    )(squared, cotangent, normed2, d_up, attended.reshape(groups, PAIRS, rows, WIDE), d_attn)


def input_grads_kernel(
    dp_ref, n1_ref, x_ref, dh_ref, w_ref, gain_ref, out_ref, gx_ref, gain_grad_ref, n1_t, total, w_sc
):
    pair = pl.program_id(0)
    groups, rows, width = n1_ref.shape
    tokens = groups * rows

    @pl.when(pair == 0)
    def _():
        for group in range(groups):
            n1_t[:, group * rows : (group + 1) * rows] = n1_ref[group].astype(F32).T.astype(BF16)
        total[...] = jnp.zeros(total.shape, F32)

    d_proj = dp_ref[...].reshape(tokens, 3 * WIDE)
    grad = mm(n1_t[...], d_proj).astype(BF16)
    for batch in range(4):
        for chip in range(4):
            begin = batch * 192 + chip * 48
            out_ref[0, 0, chip, batch] = grad[begin : begin + 48]
    for part in range(3):
        cols = pl.ds(pl.multiple_of(part * width + pair * WIDE, WIDE), WIDE)
        w_sc[:, part * WIDE : (part + 1) * WIDE] = w_ref[:, cols]
    total[...] += mm_nt(d_proj, w_sc[...])

    @pl.when(pair == PAIRS - 1)
    def _():
        gain = gain_row(gain_ref)
        gain_sum = jnp.zeros((1, width), F32)
        for group in range(groups):
            x = x_ref[group].astype(F32)
            d_normed = total[group * rows : (group + 1) * rows]
            factor = lax.rsqrt(jnp.mean(x * x, axis=-1, keepdims=True) + 1e-06)
            weighted = d_normed * gain
            inner = jnp.mean(weighted * x, axis=-1, keepdims=True)
            gx_ref[group] = (
                dh_ref[group] + factor * weighted - x * (factor * factor * factor) * inner
            )
            gain_sum += jnp.sum(d_normed * x * factor, axis=0, keepdims=True)
        gain_grad_ref[...] = gain_sum


def input_grads(d_proj, normed1, x, d_hidden, w_qkv, gain):
    groups, rows, width = x.shape
    whole = lambda p: (0, 0, 0)
    once = pl.Buffered(1)
    tokens = pl.BlockSpec((groups, rows, width), whole, pipeline_mode=once)
    return pl.pallas_call(
        input_grads_kernel,
        grid=(PAIRS,),
        in_specs=[
            pl.BlockSpec((groups, 1, rows, 3 * WIDE), lambda p: (0, p, 0, 0)),
            tokens,
            tokens,
            tokens,
            pl.BlockSpec(w_qkv.shape, lambda p: (0, 0), pipeline_mode=once),
            pl.BlockSpec((width,), lambda p: (0,)),
        ],
        out_specs=[
            pl.BlockSpec((1, 1, 4, 4, 48, PART), lambda p: (p % 3, p // 3, 0, 0, 0, 0)),
            tokens,
            pl.BlockSpec((1, width), lambda p: (0, 0)),
        ],
        out_shape=[
            jax.ShapeDtypeStruct((3, 2, 4, 4, 48, PART), BF16),
            jax.ShapeDtypeStruct(x.shape, F32),
            jax.ShapeDtypeStruct((1, width), F32),
        ],
        scratch_shapes=[
            pltpu.VMEM((width, groups * rows), BF16),
            pltpu.VMEM((groups * rows, width), F32),
            pltpu.VMEM((width, 3 * WIDE), BF16),
        ],
        compiler_params=params(),
        name="input_grads",
    )(d_proj.reshape(groups, PAIRS, rows, 3 * WIDE), normed1, x, d_hidden, w_qkv, gain)


def finish_kernel(
    units_ref, n1_ref, x_ref, dh_ref, w_ref, gain_ref, feed_ref, far_ref, gt_ref, gain2_ref, stats_ref,
    gx_ref, qkv_out, feed_out, small_out,
    dp_in, n1_v, n1_t, x_v, dh_v, w_v, feed_v, far_v, far_mine, far_in, dn, grads, pieces,
    core_in, here, chip_in, mine, z_in, qkv_all, feed_mine, feed_in, feed_all,
    row_own, row_in, row_sum, col_in,
    load_s, far_s, far_r, dp_s, dp_r, core_s, core_r, chip_s, chip_r, z_s, z_r, qkv_s, qkv_r, fz_s, fz_r, fa_s, fa_r,
    row_s, row_r, col_s, col_r,
):
    me = lax.axis_index("seq")
    z = lax.axis_index("batch")
    core, chip = lax.rem(me, 2), me // 2
    groups, block, width = n1_v.shape
    tokens = groups * block
    middle = tokens // 2
    chunks = pieces.shape[0]
    slots = units_ref.shape[0]
    rows = feed_in.shape[2]
    barrier = pltpu.get_barrier_semaphore()
    for bit in range(1, 8):
        pl.semaphore_signal(barrier, inc=1, device_id={"seq": me ^ bit}, device_id_type=MESH)
    for bit in range(1, 4):
        pl.semaphore_signal(barrier, inc=1, device_id={"batch": z ^ bit}, device_id_type=MESH)
    pl.semaphore_wait(barrier, 10)

    def send(source, target, sems, axis, peer):
        copy = remote(source, target, sems, axis, peer)
        copy.start()
        return copy

    across, along = me ^ 2, me ^ 4

    def spread(ref, s, r):
        return [
            send(ref.at[me], ref.at[me], (s.at[step], r.at[step]), "seq", peer)
            for step, peer in enumerate((me ^ 1, across, along))
        ]

    def relay(ref, first, s, r):
        rows = ref.shape[1]
        cut = (rows // 2 + 15) // 16 * 16
        first[1].wait()
        first[2].wait()
        upper, lower = pl.ds(0, cut), pl.ds(cut, rows - cut)
        on = [
            send(ref.at[across, upper], ref.at[across, upper], (s.at[3], r.at[3]), "seq", along),
            send(ref.at[along, lower], ref.at[along, lower], (s.at[4], r.at[4]), "seq", across),
        ]
        more = [
            send(ref.at[slot], ref.at[slot], (s.at[5 + step], r.at[5 + step]), "seq", me ^ 1)
            for step, slot in enumerate((across, along))
        ]
        return [first[0]] + more, on

    def finish_relay(ref, on, s, r):
        for copy in on:
            copy.wait()
        slot = me ^ 6
        return [send(ref.at[slot], ref.at[slot], (s.at[7], r.at[7]), "seq", me ^ 1)]

    for slot in range(slots):
        send_blocks(units_ref, dp_in, (dp_s, dp_r), slot)
    loads = [
        pltpu.make_async_copy(source, target, load_s.at[place])
        for place, (source, target) in enumerate(
            [
                (feed_ref, feed_v),
                (far_ref.at[z], far_v.at[0]),
                (n1_ref, n1_v),
                (w_ref, w_v),
                (x_ref, x_v),
                (dh_ref, dh_v),
            ]
        )
    ]
    for copy in loads:
        copy.start()
    far_z = [
        send(far_ref.at[z ^ bit], far_v.at[bit], (far_s.at[2 + bit], far_r.at[2 + bit]), "batch", z ^ bit)
        for bit in range(1, 4)
    ]

    loads[0].wait()
    for batch in range(4):
        both = feed_v[0, batch].astype(F32)
        for q in range(1, 4):
            both = both + feed_v[q, batch].astype(F32)
        feed_mine[batch] = both.astype(BF16)
    near = feed_mine.shape[1] // rows
    feed_z = [
        [
            send(
                feed_mine.at[z ^ bit, c * rows : (c + 1) * rows],
                feed_in.at[c, bit - 1],
                (fz_s.at[c, bit - 1], fz_r.at[c, bit - 1]),
                "batch",
                z ^ bit,
            )
            for bit in range(1, 4)
        ]
        for c in range(near)
    ]
    loads[2].wait()
    for group in range(groups):
        n1_t[:, group * block : (group + 1) * block] = n1_v[group].astype(F32).T.astype(BF16)
    for copy in loads[3:]:
        copy.wait()
    gain = gain_row(gain_ref)

    def unit_rows(pair, first):
        return jnp.concatenate(
            [dp_in[(first + more) * PAIRS + pair] for more in range(groups // 2)], axis=0
        )

    def pair_weights(pair):
        return jnp.concatenate(
            [
                w_v[:, pl.ds(pl.multiple_of(part * width + pair * WIDE, WIDE), WIDE)]
                for part in range(3)
            ],
            axis=1,
        )

    def input_half(first):
        gain_sum = jnp.zeros((1, width), F32)
        for more in range(groups // 2):
            group = first + more
            x = x_v[group].astype(F32)
            d_normed = dn[group * block : (group + 1) * block]
            factor = lax.rsqrt(jnp.mean(x * x, axis=-1, keepdims=True) + 1e-06)
            weighted = d_normed * gain
            inner = jnp.mean(weighted * x, axis=-1, keepdims=True)
            dh_v[group] += factor * weighted - x * (factor * factor * factor) * inner
            gain_sum += jnp.sum(d_normed * x * factor, axis=0, keepdims=True)
        return gain_sum

    for slot in range(slots):
        if (slot * GROUP) // PAIRS < groups // 2:
            wait_blocks(units_ref, dp_in, (dp_s, dp_r), slot)
    dn[...] = jnp.zeros(dn.shape, F32)

    def first_half(pair, carry):
        d_rows = unit_rows(pair, 0)
        grads[pair] = mm(n1_t[:, :middle], d_rows)
        dn[:middle] += mm_nt(d_rows, pair_weights(pair))
        return carry

    lax.fori_loop(0, PAIRS, first_half, 0)
    gain_sum = input_half(0)
    loads[1].wait()
    for copy in far_z:
        copy.wait()
    for q in range(4):
        both = far_v[0, q].astype(F32)
        for place in range(1, 4):
            both = both + far_v[place, q].astype(F32)
        far_mine[q] = both.astype(BF16)
    far_chips = [
        send(
            far_mine.at[chip ^ bit],
            far_in.at[bit - 1],
            (far_s.at[bit - 1], far_r.at[bit - 1]),
            "seq",
            me ^ (2 * bit),
        )
        for bit in range(1, 4)
    ]
    for slot in range(slots):
        if (slot * GROUP) // PAIRS >= groups // 2:
            wait_blocks(units_ref, dp_in, (dp_s, dp_r), slot)

    feed_first = []

    def spread_feed(c):
        for copy in feed_z[c] if c < near else far_chips:
            copy.wait()
        if c < near:
            both = feed_mine[z, c * rows : (c + 1) * rows].astype(F32)
            for bit in range(3):
                both = both + feed_in[c, bit].astype(F32)
        else:
            both = far_mine[chip].astype(F32)
            for bit in range(3):
                both = both + far_in[bit].astype(F32)
        feed_all[c, pl.ds(me, 1)] = both.astype(BF16)[None]
        feed_first.append(spread(feed_all.at[c], fa_s.at[c], fa_r.at[c]))

    spread_feed(0)
    to_core, to_chip = [], []

    def pass_on(c):
        to_core[c].wait()
        for q in range(4):
            both = pieces[c, core, q].astype(F32) + core_in[c, q].astype(F32)
            here[c, q] = both.astype(BF16)
        to_chip.append(
            [
                send(
                    here.at[c, q, half],
                    chip_in.at[c, place],
                    (chip_s.at[c, place], chip_r.at[c, place]),
                    "seq",
                    peer,
                )
                for place, (q, half, peer) in enumerate(
                    (
                        (chip ^ 1, first_two, across),
                        (chip ^ 3, first_two, across),
                        (chip ^ 2, last_two, along),
                        (chip ^ 3, last_two, along),
                    )
                )
            ]
        )

    first_two, last_two = pl.ds(0, 2), pl.ds(2, 2)

    def pass_again(c):
        for place, (q, half) in enumerate(
            ((chip, first_two), (chip ^ 2, first_two), (chip, last_two), (chip ^ 1, last_two))
        ):
            to_chip[c][place].wait()
            both = here[c, q, half].astype(F32) + chip_in[c, place].astype(F32)
            here[c, q, half] = both.astype(BF16)
        return [
            send(
                here.at[c, q, half],
                chip_in.at[c, place],
                (chip_s.at[c, place], chip_r.at[c, place]),
                "seq",
                peer,
            )
            for place, (q, half, peer) in (
                (4, (chip ^ 2, first_two, along)),
                (5, (chip ^ 1, last_two, across)),
            )
        ]

    for c in range(chunks):

        def second_half(side, carry, c=c):
            pair = side * chunks + c
            grad = (grads[pair] + mm(n1_t[:, middle:], unit_rows(pair, groups // 2))).astype(BF16)
            for batch in range(4):
                for q in range(4):
                    begin = batch * 192 + q * 48
                    pieces[c, side, q, batch] = grad[begin : begin + 48]
            return carry

        lax.fori_loop(0, 2, second_half, 0)
        to_core.append(
            send(
                pieces.at[c, 1 - core], core_in.at[c], (core_s.at[c], core_r.at[c]), "seq", me ^ 1
            )
        )
        if c > 0:
            pass_on(c - 1)

    def second_rows(pair, carry):
        dn[middle:] += mm_nt(unit_rows(pair, groups // 2), pair_weights(pair))
        return carry

    lax.fori_loop(0, 2, second_rows, 0)
    pass_on(chunks - 1)
    again = [pass_again(0)]
    lax.fori_loop(2, 4, second_rows, 0)
    again.append(pass_again(1))
    lax.fori_loop(4, PAIRS, second_rows, 0)
    again.append(pass_again(2))
    for c in range(1, chunks):
        spread_feed(c)
    gain_sum = gain_sum + input_half(groups // 2)
    gx_copy = pltpu.make_async_copy(dh_v, gx_ref, load_s.at[len(loads)])
    gx_copy.start()
    row_own[...] = jnp.zeros(row_own.shape, F32)
    for tap in range(3):
        for part in range(3):
            row = tap * 3 + part
            row_own[row : row + 1] = gt_ref[tap : tap + 1, part * width : (part + 1) * width]
    row_own[9:10] = gain_sum
    row_own[10:11] = gain2_ref[...]
    for place in range(4):
        row_own[11:12, place * WIDE : (place + 1) * WIDE] = stats_ref[place : place + 1]
    row_in[pl.ds(me, 1)] = row_own[...][None]
    rows_out = [
        send(row_own, row_in.at[me], (row_s.at[bit - 1], row_r.at[bit - 1]), "seq", me ^ bit)
        for bit in range(1, 8)
    ]
    to_z = []
    for c in range(chunks):
        for copy in again[c]:
            copy.wait()
        for half, place in ((first_two, 4), (last_two, 5)):
            both = here[c, chip, half].astype(F32) + chip_in[c, place].astype(F32)
            mine[c, half] = both.astype(BF16)
        to_z.append(
            [
                send(
                    mine.at[c, z ^ bit],
                    z_in.at[c, bit - 1],
                    (z_s.at[c, bit - 1], z_r.at[c, bit - 1]),
                    "batch",
                    z ^ bit,
                )
                for bit in range(1, 4)
            ]
        )
    for copy in rows_out:
        copy.wait()
    total = row_in[0]
    for place in range(1, 8):
        total = total + row_in[place]
    row_sum[...] = total
    col_in[pl.ds(z, 1)] = total[None]
    cols_out = [
        send(row_sum, col_in.at[z], (col_s.at[bit - 1], col_r.at[bit - 1]), "batch", z ^ bit)
        for bit in range(1, 4)
    ]
    last, feed_on, qkv_on = [], [], []
    for c in range(chunks):
        more, on = relay(feed_all.at[c], feed_first[c], fa_s.at[c], fa_r.at[c])
        last += more
        feed_on.append(on)
    qkv_first = []
    for c in range(chunks):
        for copy in to_z[c]:
            copy.wait()
        both = mine[c, z].astype(F32)
        for bit in range(3):
            both = both + z_in[c, bit].astype(F32)
        qkv_all[c, pl.ds(me, 1)] = both.astype(BF16)[None]
        qkv_first.append(spread(qkv_all.at[c], qkv_s.at[c], qkv_r.at[c]))
    for c in range(chunks):
        more, on = relay(qkv_all.at[c], qkv_first[c], qkv_s.at[c], qkv_r.at[c])
        last += more
        qkv_on.append(on)
    for c in range(chunks):
        last += finish_relay(feed_all.at[c], feed_on[c], fa_s.at[c], fa_r.at[c])
    for c in range(chunks):
        last += finish_relay(qkv_all.at[c], qkv_on[c], qkv_s.at[c], qkv_r.at[c])
    for copy in cols_out:
        copy.wait()
    small_out[...] = ((col_in[0] + col_in[1]) + col_in[2]) + col_in[3]
    for copy in last:
        copy.wait()
    qkv_out[...] = qkv_all[...]
    feed_out[...] = feed_all[...]
    gx_copy.wait()


def finish(units, normed1, x, d_hidden, w_qkv, gain, feed, far, grad_taps, grad_norm2, stats):
    groups, block, width = x.shape
    chunks, rows, feed_rows = 3, 48, 144
    small_shape = (16, width)
    tokens = groups * block
    slots = units.shape[0]
    vmem = pl.BlockSpec(memory_space=pltpu.VMEM)
    anywhere = pl.BlockSpec(memory_space=pl.ANY)
    pairs = [DMA((slots, GROUP)), DMA((slots, GROUP))]
    for shape in [(), (6,), (3,), (8,), (3,), (8,)]:
        pairs += [DMA((chunks,) + shape), DMA((chunks,) + shape)]
    low = lambda *shape: pltpu.VMEM(shape, BF16)
    return pl.pallas_call(
        finish_kernel,
        in_specs=[anywhere] * 5 + [vmem, anywhere, anywhere] + [vmem] * 3,
        out_specs=[anywhere, vmem, vmem, vmem],
        out_shape=[
            jax.ShapeDtypeStruct(x.shape, F32),
            jax.ShapeDtypeStruct((chunks, 8, rows, PART), BF16),
            jax.ShapeDtypeStruct((chunks, 8, feed_rows, PART), BF16),
            jax.ShapeDtypeStruct(small_shape, F32),
        ],
        scratch_shapes=[
            low(groups * PAIRS, block, 3 * WIDE),
            low(groups, block, width),
            low(width, tokens),
            low(groups, block, width),
            pltpu.VMEM((groups, block, width), F32),
            low(*w_qkv.shape),
            low(*feed.shape),
            low(*far.shape),
            low(*far.shape[1:]),
            low(3, *far.shape[2:]),
            pltpu.VMEM((tokens, width), F32),
            pltpu.VMEM((PAIRS, width, 3 * WIDE), F32),
            low(chunks, 2, 4, 4, rows, PART),
            low(chunks, 4, 4, rows, PART),
            low(chunks, 4, 4, rows, PART),
            low(chunks, 6, 2, rows, PART),
            low(chunks, 4, rows, PART),
            low(chunks, 3, rows, PART),
            low(chunks, 8, rows, PART),
            low(*feed.shape[1:]),
            low(chunks, 3, feed_rows, PART),
            low(chunks, 8, feed_rows, PART),
            pltpu.VMEM(small_shape, F32),
            pltpu.VMEM((8,) + small_shape, F32),
            pltpu.VMEM(small_shape, F32),
            pltpu.VMEM((4,) + small_shape, F32),
            DMA((7,)),
            DMA((6,)),
            DMA((6,)),
        ]
        + pairs
        + [DMA((7,)), DMA((7,)), DMA((3,)), DMA((3,))],
        compiler_params=group_params(0),
        name="finish",
    )(units, normed1, x, d_hidden, w_qkv, gain, feed, far, grad_taps, grad_norm2, stats)


def unpack_kernel(
    feed_ref, qkv_ref, small_ref, rows_ref, rows_out_ref, down_ref, up_ref, out_ref, grad_ref, taps_ref, gain1_ref, gain2_ref, rms_ref
):
    rows_out_ref[...] = rows_ref[...]
    for r in range(2):
        rows, cols = slice(r * 96, r * 96 + 96), slice(r * PART, (r + 1) * PART)
        down_ref[rows, :PART] = feed_ref[0, r, :96].astype(F32)
        down_ref[r * 96 : r * 96 + 48, PART:] = feed_ref[0, r, 96:].astype(F32)
        down_ref[r * 96 + 48 : r * 96 + 96, PART:] = feed_ref[1, r, :48].astype(F32)
        up_ref[:96, cols] = feed_ref[1, r, 48:].astype(F32)
        up_ref[96:, cols] = feed_ref[2, r, :96].astype(F32)
        out_ref[r * 48 : r * 48 + 48] = feed_ref[2, r, 96:].astype(F32)
        for c in range(3):
            for part in range(3):
                begin = part * PAIRS * WIDE + (r * 3 + c) * WIDE
                grad_ref[:, begin : begin + WIDE] = qkv_ref[
                    c, r, :, part * WIDE : (part + 1) * WIDE
                ].astype(F32)

    @pl.when(pl.program_id(0) == 0)
    def _():
        width = small_ref.shape[1]
        for tap in range(3):
            for part in range(3):
                row = tap * 3 + part
                taps_ref[tap : tap + 1, part * width : (part + 1) * width] = small_ref[row : row + 1]
        z = lax.axis_index("batch")
        for row, ref in ((9, gain1_ref), (10, gain2_ref)):
            own = jnp.zeros((1, width // 4), F32)
            for batch in range(4):
                share = small_ref[row : row + 1, batch * width // 4 : (batch + 1) * width // 4]
                own = jnp.where(z == batch, share, own)
            ref[...] = own.reshape(ref.shape)
        count = small_ref[11:12, 3 * WIDE : 4 * WIDE]
        lane = lax.broadcasted_iota(jnp.int32, (1, WIDE), 1)
        total = jnp.zeros((1, WIDE), F32)
        for place in range(3):
            total = jnp.where(lane == place, small_ref[11:12, place * WIDE : (place + 1) * WIDE], total)
        rms_ref[...] = jnp.sqrt(total / (width * count)).reshape(rms_ref.shape)


def unpack(feed, qkv, small, rows):
    wide = 3 * PAIRS * WIDE
    row_block = pl.BlockSpec((1,) + rows.shape[1:], lambda i: (i, 0, 0))
    return pl.pallas_call(
        unpack_kernel,
        grid=(4,),
        in_specs=[
            pl.BlockSpec((3, 2, 144, PART), lambda i: (0, i, 0, 0)),
            pl.BlockSpec((3, 2, 48, PART), lambda i: (0, i, 0, 0)),
            pl.BlockSpec(small.shape, lambda i: (0, 0)),
            row_block,
        ],
        out_specs=[
            row_block,
            pl.BlockSpec((192, 2 * PART), lambda i: (i, 0)),
            pl.BlockSpec((192, 2 * PART), lambda i: (0, i)),
            pl.BlockSpec((96, PART), lambda i: (i % 2, i // 2)),
            pl.BlockSpec((48, wide), lambda i: (i, 0)),
            pl.BlockSpec((3, wide), lambda i: (0, 0)),
            pl.BlockSpec((192,), lambda i: (0,)),
            pl.BlockSpec((192,), lambda i: (0,)),
            pl.BlockSpec((WIDE,), lambda i: (0,)),
        ],
        out_shape=[
            jax.ShapeDtypeStruct(rows.shape, F32),
            jax.ShapeDtypeStruct((768, 2 * PART), F32),
            jax.ShapeDtypeStruct((192, 8 * PART), F32),
            jax.ShapeDtypeStruct((192, 2 * PART), F32),
            jax.ShapeDtypeStruct((192, wide), F32),
            jax.ShapeDtypeStruct((3, wide), F32),
            jax.ShapeDtypeStruct((192,), F32),
            jax.ShapeDtypeStruct((192,), F32),
            jax.ShapeDtypeStruct((WIDE,), F32),
        ],
        compiler_params=params(),
        name="unpack",
    )(feed, qkv, small, rows)


def exchange(blocks):
    return lax.all_to_all(blocks, "seq", 0, 0, tiled=True)


def plain_gradients(feed, qkv):
    down = feed[:, :, :192].reshape(8, 4, 2, 96, PART).transpose(1, 0, 3, 2, 4)
    up = feed[:, :, 192:384].transpose(1, 2, 0, 3)
    out = feed[:, :, 384:].reshape(2, 4, 4, 48, PART).transpose(2, 1, 3, 0, 4)
    grad = qkv.reshape(3, 2, 4, 4, 48, 3, WIDE).transpose(3, 2, 4, 5, 1, 0, 6)
    return (
        down.reshape(3072, 768),
        up.reshape(768, 3072),
        out.reshape(768, 768),
        grad.reshape(768, 2304),
    )


def shards(
    stream_in,
    lengths,
    token_mask,
    norm1_gain,
    w_qkv,
    conv_taps,
    w_out,
    norm2_gain,
    w_up,
    w_down,
    grad_output,
):
    groups, block_len, width = stream_in.shape
    count = lax.axis_size("seq")
    batches = lax.axis_size("batch")
    units = groups * PAIRS
    slots = -(-units // count)
    spare = slots * count - units
    fitted = count == GROUP and batches == 4 and units % GROUP == 0

    def to_heads(blocks):
        blocks = jnp.pad(blocks, ((0, spare), (0, 0), (0, 0)))
        blocks = blocks.reshape((slots, count) + blocks.shape[1:])
        return jnp.stack([exchange(blocks[slot]) for slot in range(slots)])

    def to_tokens(rows):
        rows = rows.reshape(slots, count, block_len, rows.shape[2])
        return jnp.concatenate([exchange(rows[slot]) for slot in range(slots)])[:units]

    rest = (token_mask, norm2_gain, w_out, w_up, w_down)
    if fitted:
        normed1, proj, unit_out, attended, unit_lse, d_units, grad_norm2, stats, *saved = front(
            stream_in, norm1_gain, w_qkv, conv_taps, lengths, grad_output, *rest
        )
        stream_out, d_hidden, normed2, squared, d_up, d_attn, cotangent = saved
        proj = proj.reshape(slots, count * block_len, 3 * WIDE)
    else:
        normed1, proj = project(stream_in, norm1_gain, w_qkv)
        proj = to_heads(proj).reshape(slots, count * block_len, 3 * WIDE)
        unit_out, unit_lse = attend(lengths, proj, conv_taps, count)
        attended = to_tokens(unit_out)
        rest = (grad_output, token_mask, lengths) + rest[1:]
        stream_out, d_hidden, d_units, *saved = dense(stream_in, attended, *rest)
        normed2, squared, d_up, d_attn, cotangent, grad_norm2, stats = saved
        d_units = to_heads(d_units)
    d_units = d_units.reshape(slots, count * block_len, WIDE)
    saved = (squared, cotangent, normed2, d_up, attended, d_attn)
    if fitted:
        feed, far = feed_grads_send(*saved)
        same_core = [[core + 2 * chip for chip in range(4)] for core in range(2)]
        feed = lax.all_to_all(feed, "seq", 0, 0, tiled=True, axis_index_groups=same_core)
    else:
        feed = feed_grads(*saved)
    back, grad_taps, stream_out = attend_back(
        lengths, proj, conv_taps, unit_out, d_units, unit_lse, stream_out, count
    )

    if fitted:
        blocks = back.reshape(slots, count, block_len, 3 * WIDE)
        grad_input, qkv, feed, small = finish(
            blocks, normed1, stream_in, d_hidden, w_qkv, norm1_gain, feed, far, grad_taps, grad_norm2, stats
        )
        grad_input, down, up, out, grad_qkv, taps, gain1, gain2, rms = unpack(
            feed, qkv, small, grad_input
        )
        rms = rms[:3]
    else:
        pieces, grad_input, grad_norm1 = input_grads(
            to_tokens(back), normed1, stream_in, d_hidden, w_qkv, norm1_gain
        )

        def reduce(gradient):
            share = lax.psum_scatter(gradient, ("batch", "seq"), scatter_dimension=0, tiled=True)
            return lax.all_gather(share, "seq", axis=0, tiled=True).astype(F32)

        down, up, out, grad_qkv = map(reduce, plain_gradients(feed, pieces))
        small = (grad_taps[:3], grad_norm1[0], grad_norm2[0], stats[:4, 0])
        taps, gain1, gain2, stats = lax.psum(small, ("seq", "batch"))
        share = width // batches
        begin = lax.axis_index("batch") * share
        gain1, gain2 = (lax.dynamic_slice_in_dim(gain, begin, share) for gain in (gain1, gain2))
        rms = jnp.sqrt(stats[:3] / (width * stats[3]))
    return (stream_out, grad_input, gain1, grad_qkv, taps, out, gain2, up, down, rms)


def solution(mesh):
    tokens = P("batch", "seq", None)
    return jax.shard_map(
        shards,
        mesh=mesh,
        in_specs=(
            tokens,
            P("batch"),
            P("batch", "seq"),
            P(),
            P(),
            P(),
            P(),
            P(),
            P(),
            P(),
            tokens,
        ),
        out_specs=(
            tokens,
            tokens,
            P("batch"),
            P("batch", None),
            P(),
            P("batch", None),
            P("batch"),
            P("batch", None),
            P("batch", None),
            P(),
        ),
        check_vma=False,
    )
```
